32 devices in a mesh: batch: 4 (over z), gy: 2 (over x), gx: 4 (over y, core).
Axes of the slice: x: 2, y: 2, z: 4, core: 2. Of those that a mesh axis runs over, the one named last changes fastest.
Arguments:
- tokens: bfloat16 [16, 32, 32, 768], P('batch', 'gy', 'gx'), may hold values from -6 to 6
- timesteps: int32 [16], P('batch'), may hold values from 0 to 999
- labels: int32 [16], P('batch'), may hold values from 0 to 1000
- class_table: bfloat16 [1001, 768], replicated, may hold values from -3 to 3
- modulate_weight: bfloat16 [768, 4608], replicated, may hold values from -0.21875 to 0.21875
- modulate_bias: bfloat16 [4608], replicated, may hold values from -1.796875 to 1.796875
- inproj_weight: bfloat16 [768, 2304], replicated, may hold values from -0.21875 to 0.21875
- inproj_bias: bfloat16 [2304], replicated, may hold values from -3 to 3
- query_gain: bfloat16 [64], replicated, may hold values from 0.796875 to 1.796875
- key_gain: bfloat16 [64], replicated, may hold values from 0.796875 to 1.796875
- outproj_weight: bfloat16 [768, 768], replicated, may hold values from -0.875 to 0.875
- outproj_bias: bfloat16 [768], replicated, may hold values from -1.796875 to 1.796875
- gate_up_weight: bfloat16 [768, 4096], replicated, may hold values from -0.21875 to 0.21875
- gate_up_bias: bfloat16 [4096], replicated, may hold values from -3 to 3
- down_weight: bfloat16 [2048, 768], replicated, may hold values from -0.125 to 0.125
- down_bias: bfloat16 [768], replicated, may hold values from -1.796875 to 1.796875
- cotangent: bfloat16 [16, 32, 32, 768], P('batch', 'gy', 'gx'), may hold values from -6 to 6
Outputs:
- output: bfloat16 [16, 32, 32, 768], P('batch', 'gy', 'gx')
- grad_tokens: bfloat16 [16, 32, 32, 768], P('batch', 'gy', 'gx')
- grad_condition: float32 [16, 768], P('batch')
- grad_class_table: float32 [1001, 768], replicated
- grad_modulate_weight: float32 [768, 4608], P('batch')
- grad_modulate_bias: float32 [4608], P('batch')
- grad_inproj_weight: float32 [768, 2304], P('batch')
- grad_inproj_bias: float32 [2304], P('batch')
- grad_query_gain: float32 [64], P('batch')
- grad_key_gain: float32 [64], P('batch')
- grad_outproj_weight: float32 [768, 768], P('batch')
- grad_outproj_bias: float32 [768], P('batch')
- grad_gate_up_weight: float32 [768, 4096], P('batch')
- grad_gate_up_bias: float32 [4096], P('batch')
- grad_down_weight: float32 [2048, 768], P('batch')
- grad_down_bias: float32 [768], P('batch')
The draws below stay inside these ranges and needn't reach their ends.
All inputs are finite; a program needn't handle non-finite values.
Results may differ from the reference program's by a relative error of at most 0.025.
Values may be sent and summed in bfloat16 or wider, within the bound.
A program may use at most 256 MiB of HBM per device.

```python
import math
import jax
import jax.numpy as jnp
from jax import lax

D = 768
HEAD = 64
FF = 2048
CLASSES = 1001
GRID = 32
IMAGES = 16


def place_ends(values, stream_key, smallest, high):
    longest = values.shape.index(max(values.shape))
    spots = []
    for shift in (0, 1):
        where = [jax.random.randint(jax.random.fold_in(stream_key, axis), (), 0, length) for axis, length in enumerate(values.shape)]
        where[longest] = (where[longest] + shift) % values.shape[longest]
        spots.append(tuple(where))
    return values.at[spots[0]].set(smallest).at[spots[1]].set(high)


def shard_levels(key, shape, cuts, smallest, high):
    gain = 1.0
    for position, shards_of in cuts:
        draws = jax.random.uniform(jax.random.fold_in(jax.random.fold_in(key, 6), position), (shards_of,), jnp.float32, smallest / len(cuts), high / len(cuts))
        gain = gain * jnp.repeat(jnp.exp(draws), shape[position] // shards_of).reshape((-1,) + (1,) * (len(shape) - 1 - position))
    return gain


def centred(own_key, extent, scale, reach, cuts=(), held_as=jnp.bfloat16):
    entries = scale * jax.random.normal(own_key, extent, jnp.float32)
    if cuts:
        entries = entries * shard_levels(own_key, extent, cuts, -0.22, 0.18)
    return jnp.clip(entries, -reach, reach).astype(held_as)


def setup_inputs(seed: int = 0) -> dict:
    streams_of = jax.random.split(jax.random.key(seed), 18)
    tokens = centred(streams_of[0], (IMAGES, GRID, GRID, D), 1.0, 6.0, ((0, 4), (1, 2), (2, 4)))
    timesteps = place_ends(jax.random.randint(streams_of[1], (IMAGES,), 0, 1000), jax.random.fold_in(streams_of[1], 1), 0, 999).astype(jnp.int32)
    labels = place_ends(jax.random.randint(streams_of[2], (IMAGES,), 0, CLASSES), jax.random.fold_in(streams_of[2], 1), 0, CLASSES - 1).astype(jnp.int32)
    class_table = centred(streams_of[3], (CLASSES, D), 0.5, 3.0)
    modulate_weight = centred(streams_of[4], (D, 6 * D), D ** -0.5, 0.21875)
    modulate_bias = centred(streams_of[5], (6 * D,), 0.3, 1.796875)
    inproj_weight = centred(streams_of[6], (D, 3 * D), D ** -0.5, 0.21875)
    inproj_bias = centred(streams_of[7], (3 * D,), 0.5, 3.0)
    query_gain = jnp.clip(jax.random.uniform(streams_of[8], (HEAD,), jnp.float32, 0.796875, 1.796875), 0.796875, 1.796875).astype(jnp.bfloat16)
    key_gain = jnp.clip(jax.random.uniform(streams_of[9], (HEAD,), jnp.float32, 0.796875, 1.796875), 0.796875, 1.796875).astype(jnp.bfloat16)
    outproj_weight = centred(streams_of[10], (D, D), (D // 16) ** -0.5, 0.875)
    outproj_bias = centred(streams_of[11], (D,), 0.3, 1.796875)
    gate_up_weight = centred(streams_of[12], (D, 2 * FF), D ** -0.5, 0.21875)
    gate_up_bias = centred(streams_of[13], (2 * FF,), 0.5, 3.0)
    down_weight = centred(streams_of[14], (FF, D), FF ** -0.5, 0.125)
    down_bias = centred(streams_of[15], (D,), 0.3, 1.796875)
    cotangent = centred(streams_of[16], (IMAGES, GRID, GRID, D), 1.0, 6.0, ((0, 4), (1, 2), (2, 4)))
    return dict(tokens=tokens, timesteps=timesteps, labels=labels, class_table=class_table, modulate_weight=modulate_weight, modulate_bias=modulate_bias, inproj_weight=inproj_weight, inproj_bias=inproj_bias, query_gain=query_gain, key_gain=key_gain, outproj_weight=outproj_weight, outproj_bias=outproj_bias, gate_up_weight=gate_up_weight, gate_up_bias=gate_up_bias, down_weight=down_weight, down_bias=down_bias, cotangent=cotangent)


@jax.custom_vjp
def low(v):
    return lax.optimization_barrier(v.astype(jnp.bfloat16)).astype(jnp.float32)

@jax.custom_vjp
def low_back(v):
    return v

def low_keep(v):
    return (low(v), None)

def low_pass(kept, grad):
    return (grad,)

def back_keep(v):
    return (v, None)

def back_low(kept, grad):
    return (low(grad),)
low.defvjp(low_keep, low_pass)
low_back.defvjp(back_keep, back_low)
NORM_EPSILON = 1e-06

def mean_norm(values):
    return values * lax.rsqrt(lax.optimization_barrier(jnp.mean(values * values, axis=-1, keepdims=True)) + NORM_EPSILON)

def time_features(step_values, model_width):
    half_width = model_width // 2
    frequencies = jnp.exp(-math.log(10000.0) * jnp.arange(half_width, dtype=jnp.float32) / half_width)
    angles = step_values.astype(jnp.float32)[:, None] * frequencies[None, :]
    return jnp.concatenate([jnp.cos(angles), jnp.sin(angles)], axis=-1)

def rotary_tables(row_places, column_places, head_size):
    quarter = head_size // 4
    frequencies = jnp.exp(-math.log(10000.0) * jnp.arange(quarter, dtype=jnp.float32) / quarter)
    angles = jnp.stack([row_places[:, None] * frequencies[None, :], column_places[:, None] * frequencies[None, :]], axis=1)
    return (jnp.cos(angles)[:, None], jnp.sin(angles)[:, None])

def rotate(values, cosine_table, sine_table):
    full_shape = values.shape
    split_parts = values.reshape(full_shape[:-1] + (2, 2, full_shape[-1] // 4))
    leading = split_parts[..., 0, :]
    trailing = split_parts[..., 1, :]
    turned = jnp.stack([leading * cosine_table - trailing * sine_table, trailing * cosine_table + leading * sine_table], axis=-2)
    return turned.reshape(full_shape)

def forward(inputs, condition, params, cosine_table, sine_table):
    modulate_weight, modulate_bias, inproj_weight, inproj_bias, query_gain, key_gain, outproj_weight, outproj_bias, gate_up_weight, gate_up_bias, down_weight, down_bias = params
    highest = lax.Precision.HIGHEST
    image_count, cell_count, model_width = inputs.shape
    head_size = query_gain.shape[0]
    head_count = model_width // head_size
    hidden_width = down_weight.shape[0]
    modulation = jnp.dot(low(jax.nn.silu(condition)), modulate_weight, precision=highest) + modulate_bias
    shift_one, scale_one, gate_one, shift_two, scale_two, gate_two = [portion[:, None, :] for portion in jnp.split(modulation, 6, axis=-1)]
    hidden_one = low(mean_norm(inputs) * (1.0 + scale_one) + shift_one)
    projected = low_back(jnp.einsum('gsd,de->gse', hidden_one, inproj_weight, precision=highest) + inproj_bias)
    projected = projected.reshape(image_count, cell_count, 3, head_count, head_size)
    queries = low(rotate(mean_norm(projected[:, :, 0]) * query_gain, cosine_table, sine_table))
    key_rows = low(rotate(mean_norm(projected[:, :, 1]) * key_gain, cosine_table, sine_table))
    value_rows = low(projected[:, :, 2])
    scores = low_back(jnp.einsum('gqhd,gkhd->ghqk', queries, key_rows, precision=highest) * head_size ** (-0.5))
    probabilities = low(jax.nn.softmax(scores, axis=-1))
    mixed_heads = jnp.einsum('ghqk,gkhd->gqhd', probabilities, value_rows, precision=highest)
    mixed_heads = low(low_back(mixed_heads)).reshape(image_count, cell_count, model_width)
    attended = low_back(jnp.einsum('gsd,de->gse', mixed_heads, outproj_weight, precision=highest) + outproj_bias)
    middle = inputs + gate_one * attended
    hidden_two = low(mean_norm(middle) * (1.0 + scale_two) + shift_two)
    gate_up = low_back(jnp.einsum('gsd,de->gse', hidden_two, gate_up_weight, precision=highest) + gate_up_bias)
    product = low(jax.nn.silu(gate_up[..., :hidden_width]) * gate_up[..., hidden_width:])
    feed_out = low_back(jnp.einsum('gsf,fd->gsd', product, down_weight, precision=highest) + down_bias)
    return middle + gate_two * feed_out

def reference(tokens, timesteps, labels, class_table, modulate_weight, modulate_bias, inproj_weight, inproj_bias, query_gain, key_gain, outproj_weight, outproj_bias, gate_up_weight, gate_up_bias, down_weight, down_bias, cotangent):
    image_count = tokens.shape[0]
    model_width = tokens.shape[-1]
    cell_count = GRID * GRID
    inputs = tokens.astype(jnp.float32).reshape(image_count, cell_count, model_width)
    grad_out = cotangent.astype(jnp.float32).reshape(image_count, cell_count, model_width)
    table_full = class_table.astype(jnp.float32)
    params = tuple((weight_arr.astype(jnp.float32) for weight_arr in (modulate_weight, modulate_bias, inproj_weight, inproj_bias, query_gain, key_gain, outproj_weight, outproj_bias, gate_up_weight, gate_up_bias, down_weight, down_bias)))
    step_features = time_features(timesteps, model_width)
    condition, table_back = jax.vjp(lambda table_arg: step_features + table_arg[labels], table_full)
    positions = jnp.arange(cell_count, dtype=jnp.int32)
    cosine_table, sine_table = rotary_tables((positions // GRID).astype(jnp.float32), (positions % GRID).astype(jnp.float32), query_gain.shape[0])
    group_size = math.gcd(image_count, 4)
    group_count = image_count // group_size

    def one_group(totals, operands):
        group_inputs, group_condition, group_grad = operands
        result, back_fn = jax.vjp(lambda first_arg, second_arg, third_arg: forward(first_arg, second_arg, third_arg, cosine_table, sine_table), group_inputs, group_condition, params)
        grad_inputs, grad_cond, grad_params = back_fn(group_grad)
        totals = jax.tree.map(lambda left_side, right_side: left_side + right_side, totals, grad_params)
        return (totals, (result, grad_inputs, grad_cond))
    zero_totals = jax.tree.map(jnp.zeros_like, params)
    totals, (results, grad_inputs, grad_conds) = lax.scan(one_group, zero_totals, (inputs.reshape(group_count, group_size, cell_count, model_width), condition.reshape(group_count, group_size, model_width), grad_out.reshape(group_count, group_size, cell_count, model_width)))
    grad_condition = grad_conds.reshape(image_count, model_width)
    grad_table, = table_back(grad_condition)
    output = results.reshape(tokens.shape).astype(jnp.bfloat16)
    grad_tokens = grad_inputs.reshape(tokens.shape).astype(jnp.bfloat16)
    return (output, grad_tokens, grad_condition, grad_table, totals[0], totals[1], totals[2], totals[3], totals[4], totals[5], totals[6], totals[7], totals[8], totals[9], totals[10], totals[11])
```

```python
import functools
import math

import jax
import jax.numpy as jnp
from jax import lax
from jax.experimental import pallas as pl
from jax.experimental.pallas import tpu as pltpu
from jax.sharding import PartitionSpec as P

NORM_EPSILON = 1e-06
AXES = ("batch", "gy", "gx")
BF16 = jnp.bfloat16
F32 = jnp.float32
VMEM_LIMIT = 60 * 1024 * 1024


def mm(left, right):
    return lax.dot_general(left, right, (((1,), (0,)), ((), ())), preferred_element_type=F32)


def mm_nt(left, right):
    return lax.dot_general(left, right, (((1,), (1,)), ((), ())), preferred_element_type=F32)


def mm_tn(left, right):
    return lax.dot_general(left, right, (((0,), (0,)), ((), ())), preferred_element_type=F32)


def params():
    return pltpu.CompilerParams(vmem_limit_bytes=VMEM_LIMIT)


def full(shape):
    return pl.BlockSpec(shape, lambda *_: (0,) * len(shape))


def col_sum(values):
    return jnp.sum(values, axis=0, keepdims=True)


def modulation_kernel(act_ref, weight_ref, bias_ref, out_ref):
    out_ref[...] = mm(act_ref[...], weight_ref[...]) + bias_ref[...].astype(F32)


def modulation_call(act, weight, bias):
    rows, width = act.shape
    wide = weight.shape[1]
    return pl.pallas_call(
        modulation_kernel,
        grid=(wide // width,),
        in_specs=[
            full((rows, width)),
            pl.BlockSpec((width, width), lambda j: (0, j)),
            pl.BlockSpec((1, width), lambda j: (0, j)),
        ],
        out_specs=pl.BlockSpec((rows, width), lambda j: (0, j)),
        out_shape=jax.ShapeDtypeStruct((rows, wide), F32),
        compiler_params=params(),
        name="modulation",
    )(act, weight, bias)


def head_sum(values, head):
    width = 256
    row = lax.broadcasted_iota(jnp.int32, (width, width), 0) // head
    col = lax.broadcasted_iota(jnp.int32, (width, width), 1) // head
    ones = jnp.where(row == col, 1.0, 0.0).astype(BF16)
    parts = [
        mm(values[:, i : i + width].astype(BF16), ones) for i in range(0, values.shape[1], width)
    ]
    return jnp.concatenate(parts, axis=1)


def turn(values, cosine, sine, head):
    quarter = head // 4
    lane = lax.broadcasted_iota(jnp.int32, (1, 128), 1)
    first = (lane % (2 * quarter)) < quarter
    parts = []
    for i in range(0, values.shape[1], 128):
        part = values[:, i : i + 128]
        partner = jnp.where(
            first, pltpu.roll(part, 128 - quarter, 1), pltpu.roll(part, quarter, 1)
        )
        parts.append(part * cosine + partner * sine)
    return jnp.concatenate(parts, axis=1)


def project_kernel(
    head, x_ref, mod_ref, weight_ref, bias_ref, qgain_ref, kgain_ref, cos_ref, sin_ref,
    hid_ref, q_ref, k_ref, v_ref, raw_ref,
):
    width = x_ref.shape[1]
    x = x_ref[...].astype(F32)
    normed = x * lax.rsqrt(jnp.mean(x * x, axis=-1, keepdims=True) + NORM_EPSILON)
    hidden = (normed * (1.0 + mod_ref[:, width : 2 * width]) + mod_ref[:, :width]).astype(BF16)
    hid_ref[...] = hidden
    for part, (out_ref, gain_ref) in enumerate(((q_ref, qgain_ref), (k_ref, kgain_ref))):
        raw = mm(hidden, weight_ref[:, part * width : (part + 1) * width])
        raw = raw + bias_ref[:, part * width : (part + 1) * width].astype(F32)
        raw_ref[:, part * width : (part + 1) * width] = raw.astype(BF16)
        factor = lax.rsqrt(head_sum(raw * raw, head) * (1.0 / head) + NORM_EPSILON)
        scaled = raw * factor * gain_ref[...]
        out_ref[...] = turn(scaled, cos_ref[...], sin_ref[...], head).astype(BF16)
    value = mm(hidden, weight_ref[:, 2 * width :]) + bias_ref[:, 2 * width :].astype(F32)
    v_ref[...] = value.astype(BF16)


def project_call(x, mod, weight, bias, qgain, kgain, cosine, sine, head):
    rows, width = x.shape
    block = rows // 2
    by_row = lambda wide: pl.BlockSpec((block, wide), lambda i: (i, 0))
    shape = jax.ShapeDtypeStruct((rows, width), BF16)
    return pl.pallas_call(
        functools.partial(project_kernel, head),
        grid=(2,),
        in_specs=[
            by_row(width),
            full(mod.shape),
            full(weight.shape),
            full(bias.shape),
            full(qgain.shape),
            full(kgain.shape),
            by_row(128),
            by_row(128),
        ],
        out_specs=[by_row(width)] * 4 + [by_row(2 * width)],
        out_shape=[shape] * 4 + [jax.ShapeDtypeStruct((rows, 2 * width), BF16)],
        compiler_params=params(),
        name="project",
    )(x, mod, weight, bias, qgain, kgain, cosine, sine)


def attend_kernel(scale, q_ref, k0_ref, k1_ref, v0_ref, v1_ref, mix_ref, e_ref, rl_ref):
    lane = lax.broadcasted_iota(jnp.int32, (1, 128), 1)
    q = q_ref[...]
    keys = jnp.concatenate([k0_ref[...], k1_ref[...]], axis=0)
    values = jnp.concatenate([v0_ref[...], v1_ref[...]], axis=0)
    values = jnp.concatenate([values, jnp.ones_like(values)], axis=1)
    outs = []
    for h in range(2):
        mine = (lane >= 64) if h else (lane < 64)
        scores = mm_nt(jnp.where(mine, q, jnp.zeros_like(q)), keys)
        grown = jnp.exp(scores * scale).astype(BF16)
        e_ref[h] = grown
        outs.append(mm(grown, values))
    inverse = 1.0 / jnp.where(lane < 64, outs[0][:, 128:], outs[1][:, 128:])
    mix_ref[...] = (jnp.where(lane < 64, outs[0][:, :128], outs[1][:, :128]) * inverse).astype(BF16)
    rl_ref[...] = inverse


def attend_call(q, k0, k1, v0, v1, head):
    rows, width = q.shape
    pair = pl.BlockSpec((rows, 128), lambda p: (0, p))
    return pl.pallas_call(
        functools.partial(attend_kernel, head**-0.5),
        grid=(width // 128,),
        in_specs=[pair] * 5,
        out_specs=[pair, pl.BlockSpec((2, rows, 2 * rows), lambda p: (p, 0, 0)), pair],
        out_shape=[
            jax.ShapeDtypeStruct((rows, width), BF16),
            jax.ShapeDtypeStruct((width // head, rows, 2 * rows), BF16),
            jax.ShapeDtypeStruct((rows, width), F32),
        ],
        compiler_params=params(),
        name="attend",
    )(q, k0, k1, v0, v1)


def attend_back_kernel(
    scale, q_ref, k0_ref, k1_ref, v0_ref, v1_ref, e_ref, gm_ref, mix_ref, rl_ref,
    dq_ref, dk0_ref, dk1_ref, dv0_ref, dv1_ref,
):
    rows = q_ref.shape[0]
    lane = lax.broadcasted_iota(jnp.int32, (1, 128), 1)
    keys = jnp.concatenate([k0_ref[...], k1_ref[...]], axis=0)
    values = jnp.concatenate([v0_ref[...], v1_ref[...]], axis=0)
    scaled = gm_ref[...].astype(F32) * rl_ref[...]
    products = scaled * mix_ref[...].astype(F32)
    scaled = scaled.astype(BF16)
    q_t = q_ref[...].T
    scaled_t = scaled.T
    dqs, dks, dvs = [], [], []
    for h in range(2):
        mine = (lane >= 64) if h else (lane < 64)
        inner = jnp.sum(jnp.where(mine, products, 0.0), axis=1, keepdims=True)
        grad_probs = mm_nt(jnp.where(mine, scaled, jnp.zeros_like(scaled)), values)
        grown = e_ref[h]
        grad_scores = (grown.astype(F32) * (grad_probs - inner) * scale).astype(BF16)
        dqs.append(mm(grad_scores, keys))
        dks.append(mm(q_t[64 * h : 64 * h + 64], grad_scores))
        dvs.append(mm(scaled_t[64 * h : 64 * h + 64], grown))
    dq_ref[...] = jnp.where(lane < 64, dqs[0], dqs[1]).astype(BF16)
    dk = jnp.concatenate(dks, axis=0).T.astype(BF16)
    dv = jnp.concatenate(dvs, axis=0).T.astype(BF16)
    dk0_ref[...] = dk[:rows]
    dk1_ref[...] = dk[rows:]
    dv0_ref[...] = dv[:rows]
    dv1_ref[...] = dv[rows:]


def attend_back_call(q, k0, k1, v0, v1, grown, grad_mixed, mixed, inverse, head):
    rows, width = q.shape
    pair = pl.BlockSpec((rows, 128), lambda p: (0, p))
    return pl.pallas_call(
        functools.partial(attend_back_kernel, head**-0.5),
        grid=(width // 128,),
        in_specs=[pair] * 5
        + [pl.BlockSpec((2, rows, 2 * rows), lambda p: (p, 0, 0))]
        + [pair] * 3,
        out_specs=[pair] * 5,
        out_shape=[jax.ShapeDtypeStruct((rows, width), BF16)] * 5,
        compiler_params=params(),
        name="attend_back",
    )(q, k0, k1, v0, v1, grown, grad_mixed, mixed, inverse)


def middle_kernel(
    mix_ref, x_ref, dy_ref, mod_ref, weight_ref, bias_ref, att_ref, mid_ref, h2_ref, h2t_ref, gf_ref
):
    width = x_ref.shape[1]
    attended = mm(mix_ref[...], weight_ref[...]) + bias_ref[...].astype(F32)
    middle = x_ref[...].astype(F32) + mod_ref[:, 2 * width : 3 * width] * attended
    normed = middle * lax.rsqrt(jnp.mean(middle * middle, axis=-1, keepdims=True) + NORM_EPSILON)
    hidden = normed * (1.0 + mod_ref[:, 4 * width : 5 * width]) + mod_ref[:, 3 * width : 4 * width]
    hidden = hidden.astype(BF16)
    att_ref[...] = attended.astype(BF16)
    mid_ref[...] = middle
    h2_ref[...] = hidden
    h2t_ref[...] = hidden.T
    gf_ref[...] = (mod_ref[:, 5 * width :] * dy_ref[...].astype(F32)).astype(BF16)


def middle_call(mixed, x, dy, mod, weight, bias):
    rows, width = x.shape
    block = rows // 2
    by_row = pl.BlockSpec((block, width), lambda i: (i, 0))
    low = jax.ShapeDtypeStruct((rows, width), BF16)
    return pl.pallas_call(
        middle_kernel,
        grid=(2,),
        in_specs=[by_row] * 3 + [full(mod.shape), full(weight.shape), full(bias.shape)],
        out_specs=[by_row] * 3 + [pl.BlockSpec((width, block), lambda i: (0, i)), by_row],
        out_shape=[low, jax.ShapeDtypeStruct((rows, width), F32), low]
        + [jax.ShapeDtypeStruct((width, rows), BF16), low],
        compiler_params=params(),
        name="middle",
    )(mixed, x, dy, mod, weight, bias)


def feed_kernel(
    h2_ref, h2t_ref, gf_ref, wg_ref, wu_ref, bg_ref, bu_ref, wd_ref, feed_in_ref, gh_in_ref,
    feed_ref, gh_ref, dd_ref, dg_ref, db_ref,
):
    @pl.when(pl.program_id(0) == 0)
    def _():
        feed_ref[...] = feed_in_ref[...]
        gh_ref[...] = gh_in_ref[...]

    hidden = h2_ref[...]
    grad_feed = gf_ref[...]
    gate = mm(hidden, wg_ref[...]) + bg_ref[...].astype(F32)
    up = mm(hidden, wu_ref[...]) + bu_ref[...].astype(F32)
    grad_product = mm_nt(grad_feed, wd_ref[...])
    sig = 1.0 / (1.0 + jnp.exp(-gate))
    active = gate * sig
    product = (active * up).astype(BF16)
    grad_gate = (grad_product * up * sig * (1.0 + gate * (1.0 - sig))).astype(BF16)
    grad_up = (grad_product * active).astype(BF16)
    dd_ref[...] = mm_tn(product, grad_feed).astype(BF16)
    dg_ref[0] = mm(h2t_ref[...], grad_gate).astype(BF16)
    dg_ref[1] = mm(h2t_ref[...], grad_up).astype(BF16)
    db_ref[0] = col_sum(grad_gate.astype(F32))
    db_ref[1] = col_sum(grad_up.astype(F32))
    feed_ref[...] += mm(product, wd_ref[...])
    gh_ref[...] += mm_nt(grad_gate, wg_ref[...]) + mm_nt(grad_up, wu_ref[...])


def feed_call(hidden, hidden_t, grad_feed, weight, bias, down, feed, grad_hidden, first, step, unit):
    rows, width = hidden.shape
    blocks = down.shape[0] // unit
    steps = len(range(first, blocks, step))
    pick = lambda s: first + step * s
    acc = jax.ShapeDtypeStruct((rows, width), F32)
    return pl.pallas_call(
        feed_kernel,
        grid=(steps,),
        in_specs=[
            full((rows, width)),
            full((width, rows)),
            full((rows, width)),
            pl.BlockSpec((width, unit), lambda s: (0, pick(s))),
            pl.BlockSpec((width, unit), lambda s: (0, blocks + pick(s))),
            pl.BlockSpec((1, unit), lambda s: (0, pick(s))),
            pl.BlockSpec((1, unit), lambda s: (0, blocks + pick(s))),
            pl.BlockSpec((unit, width), lambda s: (pick(s), 0)),
            full((rows, width)),
            full((rows, width)),
        ],
        out_specs=[
            full((rows, width)),
            full((rows, width)),
            pl.BlockSpec((None, unit, width), lambda s: (s, 0, 0)),
            pl.BlockSpec((None, 2, width, unit), lambda s: (s, 0, 0, 0)),
            pl.BlockSpec((None, 2, 1, unit), lambda s: (s, 0, 0, 0)),
        ],
        out_shape=[
            acc,
            acc,
            jax.ShapeDtypeStruct((steps, unit, width), BF16),
            jax.ShapeDtypeStruct((steps, 2, width, unit), BF16),
            jax.ShapeDtypeStruct((steps, 2, 1, unit), F32),
        ],
        compiler_params=params(),
        name="feed",
    )(hidden, hidden_t, grad_feed, weight, weight, bias, bias, down, feed, grad_hidden)


def turn_kernel(
    feed_ref, gh_ref, mid_ref, att_ref, dy_ref, gf_ref, mix_ref, mod_ref, weight_ref, dbias_ref,
    out_ref, gmid_ref, gmix_ref, dw_ref, sums_ref,
):
    width = mid_ref.shape[1]
    half = width // 2
    dy = dy_ref[...].astype(F32)
    feed = feed_ref[...] + dbias_ref[...].astype(F32)
    middle = mid_ref[...]
    out_ref[...] = (middle + mod_ref[:, 5 * width :] * feed).astype(BF16)
    factor = lax.rsqrt(jnp.mean(middle * middle, axis=-1, keepdims=True) + NORM_EPSILON)
    normed = middle * factor
    grad_hidden = gh_ref[...]
    product = grad_hidden * normed
    grad_normed = grad_hidden * (1.0 + mod_ref[:, 4 * width : 5 * width])
    back = factor * (
        grad_normed - normed * jnp.mean(grad_normed * normed, axis=-1, keepdims=True)
    )
    grad_middle = dy + back
    gmid_ref[...] = grad_middle
    grad_attended = (mod_ref[:, 2 * width : 3 * width] * grad_middle).astype(BF16)
    sums_ref[0:1, :] = col_sum(grad_middle * att_ref[...].astype(F32))
    sums_ref[1:2, :] = col_sum(grad_hidden)
    sums_ref[2:3, :] = col_sum(product)
    sums_ref[3:4, :] = col_sum(dy * feed)
    sums_ref[4:5, :] = col_sum(grad_attended.astype(F32))
    sums_ref[5:6, :] = col_sum(gf_ref[...].astype(F32))
    sums_ref[6:8, :] = jnp.zeros((2, width), F32)
    gmix_ref[...] = mm_nt(grad_attended, weight_ref[...]).astype(BF16)
    mixed_t = mix_ref[...].T
    dw_ref[0] = mm(mixed_t, grad_attended[:, :half]).astype(BF16)
    dw_ref[1] = mm(mixed_t, grad_attended[:, half:]).astype(BF16)


def turn_call(feed, grad_hidden, middle, attended, dy, grad_feed, mixed, mod, weight, down_bias):
    rows, width = middle.shape
    low = jax.ShapeDtypeStruct((rows, width), BF16)
    return pl.pallas_call(
        turn_kernel,
        out_shape=[
            low,
            jax.ShapeDtypeStruct((rows, width), F32),
            low,
            jax.ShapeDtypeStruct((2, width, width // 2), BF16),
            jax.ShapeDtypeStruct((8, width), F32),
        ],
        compiler_params=params(),
        name="turn",
    )(feed, grad_hidden, middle, attended, dy, grad_feed, mixed, mod, weight, down_bias)


def project_back_kernel(
    head, dq_ref, dk0_ref, dk1_ref, dv0_ref, dv1_ref, raw_ref, hid_ref, x_ref, gmid_ref, mod_ref,
    weight_ref, qgain_ref, kgain_ref, cos_ref, sin_ref,
    gx_ref, dw_ref, sums_ref, bias_ref, proj_ref,
):
    width = x_ref.shape[1]
    cosine, sine = cos_ref[...], -sin_ref[...]
    for part in range(3):
        span = slice(part * width, (part + 1) * width)
        if part == 2:
            grad = dv0_ref[...].astype(F32) + dv1_ref[...].astype(F32)
        else:
            grad = dq_ref[...].astype(F32)
            if part == 1:
                grad = dk0_ref[...].astype(F32) + dk1_ref[...].astype(F32)
            gain = (qgain_ref, kgain_ref)[part][...]
            raw = raw_ref[:, span].astype(F32)
            factor = lax.rsqrt(head_sum(raw * raw, head) * (1.0 / head) + NORM_EPSILON)
            normed = raw * factor
            turned = turn(grad, cosine, sine, head)
            sums_ref[2 + part : 3 + part, :] = col_sum(turned * normed)
            turned = turned * gain
            mean = head_sum(turned * normed, head) * (1.0 / head)
            grad = factor * (turned - normed * mean)
        low = grad.astype(BF16)
        proj_ref[:, span] = low
        bias_ref[:, span] = col_sum(low.astype(F32))
    hidden_t = hid_ref[...].T
    half = 3 * width // 2
    dw_ref[0] = mm(hidden_t, proj_ref[:, :half]).astype(BF16)
    dw_ref[1] = mm(hidden_t, proj_ref[:, half:]).astype(BF16)
    grad_hidden = mm_nt(proj_ref[...], weight_ref[...])
    x = x_ref[...].astype(F32)
    factor = lax.rsqrt(jnp.mean(x * x, axis=-1, keepdims=True) + NORM_EPSILON)
    normed = x * factor
    sums_ref[0:1, :] = col_sum(grad_hidden)
    sums_ref[1:2, :] = col_sum(grad_hidden * normed)
    sums_ref[4:8, :] = jnp.zeros((4, width), F32)
    grad_normed = grad_hidden * (1.0 + mod_ref[:, width : 2 * width])
    back = factor * (
        grad_normed - normed * jnp.mean(grad_normed * normed, axis=-1, keepdims=True)
    )
    gx_ref[...] = (gmid_ref[...] + back).astype(BF16)


def project_back_call(
    dq, dk0, dk1, dv0, dv1, raw, hidden, x, grad_middle, mod, weight, qgain, kgain, cosine, sine, head
):
    rows, width = x.shape
    return pl.pallas_call(
        functools.partial(project_back_kernel, head),
        out_shape=[
            jax.ShapeDtypeStruct((rows, width), BF16),
            jax.ShapeDtypeStruct((2, width, 3 * width // 2), BF16),
            jax.ShapeDtypeStruct((8, width), F32),
            jax.ShapeDtypeStruct((1, 3 * width), F32),
        ],
        scratch_shapes=[pltpu.VMEM((rows, 3 * width), BF16)],
        compiler_params=params(),
        name="project_back",
    )(dq, dk0, dk1, dv0, dv1, raw, hidden, x, grad_middle, mod, weight, qgain, kgain, cosine, sine)


def take(array_in, index, axis=0):
    return lax.dynamic_index_in_dim(array_in, index, axis, keepdims=False)


def add(*terms):
    return sum(term.astype(F32) for term in terms)


class Moves:
    def __init__(self, mesh):
        self.sizes = tuple(mesh.shape[name] for name in AXES)

    def flip(self, value, batch=0, gy=0, gx=0):
        nb, ny, nx = self.sizes
        pairs = []
        for b in range(nb):
            for y in range(ny):
                for x in range(nx):
                    here = (b * ny + y) * nx + x
                    there = ((b ^ batch) * ny + (y ^ gy)) * nx + (x ^ gx)
                    pairs.append((here, there))
        return lax.ppermute(value, AXES, pairs)

    def plane(self, value, k):
        return self.flip(value, gy=k >> 1, gx=2 * (k & 1))

    def pair(self, value):
        return self.flip(value, gx=1)

    def gather(self, value):
        value = value[None]
        value = jnp.concatenate([value, self.plane(value, 1)], axis=0)
        value = jnp.concatenate([value, self.plane(value, 2)], axis=0)
        bit = 1
        while bit < self.sizes[0]:
            value = jnp.concatenate([value, self.flip(value, batch=bit)], axis=0)
            bit *= 2
        return value


def regroup(parts, place):
    stacked = jnp.stack(parts)
    return jnp.stack([take(stacked, place ^ k) for k in range(len(parts))])


def reduce_pieces(moves, pieces, c, first, second, order, z):
    one, two = order
    arrived = moves.pair(take(pieces, 1 - c))
    mine = take(pieces, c)
    near = moves.plane(add(take(mine, 1 - first), take(arrived, 1 - first)).astype(BF16), one)
    mine, arrived = take(mine, first), take(arrived, first)
    far = moves.plane(
        add(take(mine, 1 - second), take(arrived, 1 - second), take(near, 1 - second)).astype(BF16),
        two,
    )
    total = add(take(mine, second), take(arrived, second), take(near, second), far)
    low = total.astype(BF16)
    own = take(total, z)
    for d in range(1, moves.sizes[0]):
        own = add(own, moves.flip(take(low, z ^ d), batch=d))
    own = own.astype(BF16)
    quarter = [own, moves.plane(own, two), moves.plane(own, one), moves.plane(own, one ^ two)]
    quarter = regroup(quarter, 2 * first + second)
    halves = [quarter, moves.pair(quarter)]
    return regroup(halves, c)


def body(mesh, *operands):
    (
        tokens, timesteps, labels, class_table, modulate_weight, modulate_bias, inproj_weight,
        inproj_bias, query_gain, key_gain, outproj_weight, outproj_bias, gate_up_weight,
        gate_up_bias, down_weight, down_bias, cotangent,
    ) = operands
    image_count, tile_rows, tile_cols, width = tokens.shape
    cells = tile_rows * tile_cols
    rows = image_count * cells
    head = query_gain.shape[0]
    heads = width // head
    hidden_width = down_weight.shape[0]
    class_count = class_table.shape[0]
    highest = lax.Precision.HIGHEST
    moves = Moves(mesh)
    nb, ny, nx = moves.sizes
    assert ny == 2 and nx == 4 and image_count == 4
    z, gy, gx = (lax.axis_index(name) for name in AXES)
    side, core = gx // 2, gx % 2
    place = 2 * gy + side

    tiles = tokens.reshape(image_count, cells, width)
    grads = cotangent.reshape(image_count, cells, width)

    def exchange(blocks):
        return [take(blocks, place)] + [
            moves.plane(take(blocks, place ^ k), k) for k in range(1, 4)
        ]

    x = jnp.concatenate(exchange(tiles), axis=0)

    half_width = width // 2
    step = take(timesteps, place).astype(F32)
    label = take(labels, place)
    rates = jnp.exp(-math.log(10000.0) * jnp.arange(half_width, dtype=F32) / half_width)
    features = jnp.concatenate([jnp.cos(step * rates), jnp.sin(step * rates)])
    condition = features + take(class_table, label).astype(F32)
    cond_act = jax.nn.silu(condition).astype(BF16)
    mod = modulation_call(
        jnp.broadcast_to(cond_act[None], (16, width)), modulate_weight, modulate_bias[None]
    )[:1]

    quarter = head // 4
    cell = jnp.arange(cells, dtype=jnp.int32)
    row_places, col_places = [], []
    for k in range(4):
        there = place ^ k
        row_places.append((there // 2) * tile_rows + cell // tile_cols)
        col_places.append((2 * (there % 2) + core) * tile_cols + cell % tile_cols)
    row_places = jnp.concatenate(row_places).astype(F32)[:, None]
    col_places = jnp.concatenate(col_places).astype(F32)[:, None]
    lane = jnp.arange(128, dtype=jnp.int32)
    turn_rate = jnp.exp(-math.log(10000.0) * (lane % quarter).astype(F32) / quarter)[None]
    angles = jnp.where((lane % head)[None] < head // 2, row_places, col_places) * turn_rate
    cosine = jnp.cos(angles)
    sine = jnp.where((lane % (2 * quarter))[None] < quarter, -1.0, 1.0) * jnp.sin(angles)
    qgain = jnp.tile(query_gain.astype(F32), heads)[None]
    kgain = jnp.tile(key_gain.astype(F32), heads)[None]

    hidden_one, q, k0, v0, raw = project_call(
        x, mod, inproj_weight, inproj_bias[None], qgain, kgain, cosine, sine, head
    )
    k1, v1 = moves.pair(k0), moves.pair(v0)
    dy = jnp.concatenate(exchange(grads), axis=0)
    mixed, grown, inverse = attend_call(q, k0, k1, v0, v1, head)
    attended, middle, hidden_two, hidden_two_t, grad_feed = middle_call(
        mixed, x, dy, mod, outproj_weight, outproj_bias[None]
    )

    unit = 256
    blocks = hidden_width // unit
    quick = nb == 4
    chunks = 2 if quick else 1
    feed = jnp.zeros((rows, width), F32)
    grad_hidden = jnp.zeros((rows, width), F32)
    down_parts, gate_parts, gate_bias_parts = [], [], []
    for j in range(chunks):
        feed, grad_hidden, d_down, d_gate, d_bias = feed_call(
            hidden_two, hidden_two_t, grad_feed, gate_up_weight, gate_up_bias[None], down_weight,
            feed, grad_hidden, j, chunks, unit,
        )
        down_parts.append(d_down)
        gate_parts.append(d_gate)
        gate_bias_parts.append(d_bias)

    output_rows, grad_middle, grad_mixed, d_out, sums_two = turn_call(
        feed, grad_hidden, middle, attended, dy, grad_feed, mixed, mod, outproj_weight,
        down_bias[None],
    )
    dq, dk0, dk1, dv0, dv1 = attend_back_call(
        q, k0, k1, v0, v1, grown, grad_mixed, mixed, inverse, head
    )
    dk1, dv1 = moves.pair(dk1), moves.pair(dv1)
    grad_x, d_in, sums_one, in_bias = project_back_call(
        dq, dk0, dk1, dv0, dv1, raw, hidden_one, x, grad_middle, mod, inproj_weight, qgain, kgain,
        cosine, sine, head,
    )

    def give_back(rows_out):
        parts = rows_out.reshape(4, cells, width)
        got = [parts[0]] + [moves.plane(parts[k], k) for k in range(1, 4)]
        return regroup(got, place).reshape(tokens.shape)

    output = give_back(output_rows)
    grad_tokens = give_back(grad_x)

    slice_rows = width // nb
    if quick:
        downs, gates = [], []
        for j in range(chunks):
            order = (1, 2) if j % 2 == 0 else (2, 1)
            first, second = (side, gy) if j % 2 == 0 else (gy, side)
            d = down_parts[j].reshape(nb, 2, 2, 2, unit // 8, width).transpose(1, 2, 3, 0, 4, 5)
            g = gate_parts[j].reshape(2, 2, 2, nb, slice_rows, unit)
            d = reduce_pieces(moves, d, core, first, second, order, z)
            g = reduce_pieces(moves, g, core, first, second, order, z)
            downs.append(d.reshape(unit, width))
            gates.append(g.reshape(blocks // chunks, 2, slice_rows, unit))
        grad_down_w = jnp.stack(downs).reshape(hidden_width // nb, width).astype(F32)
        grad_gu_w = jnp.stack(gates, axis=1).reshape(blocks, 2, slice_rows, unit)
        grad_gu_w = grad_gu_w.transpose(2, 1, 0, 3).reshape(slice_rows, 2 * hidden_width).astype(F32)

        def by_rows(d, order, first, second):
            wide = d.shape[2]
            d = d.reshape(2, nb, 2, 2, slice_rows // 4, wide).transpose(0, 2, 3, 1, 4, 5)
            d = reduce_pieces(moves, d, core, first, second, order, z)
            d = d.reshape(2, slice_rows, wide)
            return jnp.concatenate([d[0], d[1]], axis=1).astype(F32)

        grad_out_w = by_rows(d_out, (1, 2), side, gy)
        grad_in_w = by_rows(d_in, (2, 1), gy, side)
    else:

        def scatter(d):
            d = lax.psum_scatter(d.astype(BF16), "batch", scatter_dimension=0, tiled=True)
            return lax.psum(d, ("gy", "gx")).astype(F32)

        def joined(d):
            return jnp.concatenate([d[0], d[1]], axis=1)

        grad_down_w = scatter(down_parts[0].reshape(hidden_width, width))
        grad_gu_w = scatter(
            gate_parts[0].transpose(2, 1, 0, 3).reshape(width, 2 * hidden_width)
        )
        grad_out_w = scatter(joined(d_out))
        grad_in_w = scatter(joined(d_in))

    gate_bias = jnp.stack(gate_bias_parts, axis=1).reshape(blocks, 2, unit).transpose(1, 0, 2)
    gain_sums = sums_one[2:4].reshape(2, heads, head).sum(axis=1)
    early = jnp.concatenate([sums_two[:6].reshape(-1), gate_bias.reshape(-1)])
    late = jnp.concatenate([sums_one[:2].reshape(-1), in_bias.reshape(-1), gain_sums.reshape(-1)])

    def everywhere(vector):
        halves = vector.reshape(2, -1)
        half = add(take(halves, core), moves.pair(take(halves, 1 - core)))
        half = moves.gather(half)
        both = regroup([half, moves.pair(half)], core)
        return both.transpose(1, 0, 2).reshape(half.shape[0], -1)

    known = jnp.concatenate([condition, jnp.broadcast_to(label.astype(F32), (128,))])
    known = moves.gather(known)
    early = everywhere(early)
    late = everywhere(late)
    grad_modulation = jnp.concatenate([late[:, : 2 * width], early[:, : 4 * width]], axis=1)
    conditions = known[:, :width]
    all_labels = known[:, width].astype(jnp.int32)
    cond_acts = jax.nn.silu(conditions).astype(BF16)
    my_acts = lax.dynamic_slice_in_dim(cond_acts, z * slice_rows, slice_rows, axis=1)
    low_mod = grad_modulation.astype(BF16)
    grad_mod_w = mm_tn(my_acts, low_mod)
    wide = 6 * width
    grad_mod_b = lax.dynamic_slice_in_dim(
        jnp.sum(grad_modulation, axis=0), z * (wide // nb), wide // nb, axis=0
    )
    grad_cond_act = mm_nt(low_mod, modulate_weight)
    sig = jax.nn.sigmoid(conditions)
    grad_conditions = grad_cond_act * sig * (1.0 + conditions * (1.0 - sig))
    grad_condition = regroup([grad_conditions[k] for k in range(4)], place)
    onehot = (all_labels[:, None] == jnp.arange(class_count, dtype=jnp.int32)[None, :]).astype(F32)
    grad_table = lax.dot_general(
        onehot, grad_conditions, (((0,), (0,)), ((), ())), precision=highest,
        preferred_element_type=F32,
    )

    early_sum = jnp.sum(early, axis=0)
    late_sum = jnp.sum(late, axis=0)

    def part(vector, start, size):
        return lax.dynamic_slice_in_dim(vector, start + z * (size // nb), size // nb, axis=0)

    grad_out_b = part(early_sum, 4 * width, width)
    grad_down_b = part(early_sum, 5 * width, width)
    grad_gu_b = part(early_sum, 6 * width, 2 * hidden_width)
    grad_in_b = part(late_sum, 2 * width, 3 * width)
    grad_q_gain = part(late_sum, 5 * width, head)
    grad_k_gain = part(late_sum, 5 * width + head, head)
    return (
        output, grad_tokens, grad_condition, grad_table, grad_mod_w, grad_mod_b, grad_in_w,
        grad_in_b, grad_q_gain, grad_k_gain, grad_out_w, grad_out_b, grad_gu_w, grad_gu_b,
        grad_down_w, grad_down_b,
    )


def solution(mesh):
    grid = P("batch", "gy", "gx", None)
    by_batch = P("batch")
    rows = P("batch", None)
    placed = (grid, by_batch, by_batch) + (P(),) * 13 + (grid,)
    return jax.shard_map(
        functools.partial(body, mesh),
        mesh=mesh,
        in_specs=placed,
        out_specs=(
            grid, grid, rows, P(), rows, by_batch, rows, by_batch, by_batch, by_batch, rows,
            by_batch, rows, by_batch, rows, by_batch,
        ),
        check_vma=False,
    )
```

```python
import functools
import math

import jax
import jax.numpy as jnp
from jax import lax
from jax.experimental import pallas as pl
from jax.experimental.pallas import tpu as pltpu
from jax.sharding import PartitionSpec as P

NORM_EPSILON = 1e-06
AXES = ("batch", "gy", "gx")
BF16 = jnp.bfloat16
F32 = jnp.float32
VMEM_LIMIT = 60 * 1024 * 1024


def mm(left, right):
    return lax.dot_general(left, right, (((1,), (0,)), ((), ())), preferred_element_type=F32)


def mm_nt(left, right):
    return lax.dot_general(left, right, (((1,), (1,)), ((), ())), preferred_element_type=F32)


def mm_tn(left, right):
    return lax.dot_general(left, right, (((0,), (0,)), ((), ())), preferred_element_type=F32)


def params():
    return pltpu.CompilerParams(vmem_limit_bytes=VMEM_LIMIT)


def full(shape):
    return pl.BlockSpec(shape, lambda *_: (0,) * len(shape))


def col_sum(values):
    return jnp.sum(values, axis=0, keepdims=True)


def modulation_kernel(act_ref, weight_ref, bias_ref, out_ref):
    out_ref[...] = mm(act_ref[...], weight_ref[...]) + bias_ref[...].astype(F32)


def modulation_call(act, weight, bias):
    rows, width = act.shape
    wide = weight.shape[1]
    return pl.pallas_call(
        modulation_kernel,
        grid=(wide // width,),
        in_specs=[
            full((rows, width)),
            pl.BlockSpec((width, width), lambda j: (0, j)),
            pl.BlockSpec((1, width), lambda j: (0, j)),
        ],
        out_specs=pl.BlockSpec((rows, width), lambda j: (0, j)),
        out_shape=jax.ShapeDtypeStruct((rows, wide), F32),
        compiler_params=params(),
        name="modulation",
    )(act, weight, bias)


def head_sum(values, head):
    width = 256
    row = lax.broadcasted_iota(jnp.int32, (width, width), 0) // head
    col = lax.broadcasted_iota(jnp.int32, (width, width), 1) // head
    ones = jnp.where(row == col, 1.0, 0.0).astype(BF16)
    parts = [
        mm(values[:, i : i + width].astype(BF16), ones) for i in range(0, values.shape[1], width)
    ]
    return jnp.concatenate(parts, axis=1)


def turn(values, cosine, sine, head):
    quarter = head // 4
    lane = lax.broadcasted_iota(jnp.int32, (1, 128), 1)
    first = (lane % (2 * quarter)) < quarter
    parts = []
    for i in range(0, values.shape[1], 128):
        part = values[:, i : i + 128]
        partner = jnp.where(
            first, pltpu.roll(part, 128 - quarter, 1), pltpu.roll(part, quarter, 1)
        )
        parts.append(part * cosine + partner * sine)
    return jnp.concatenate(parts, axis=1)


def project_kernel(
    head, x_ref, mod_ref, weight_ref, bias_ref, qgain_ref, kgain_ref, cos_ref, sin_ref,
    hid_ref, q_ref, k_ref, v_ref, raw_ref,
):
    width = x_ref.shape[1]
    x = x_ref[...].astype(F32)
    normed = x * lax.rsqrt(jnp.mean(x * x, axis=-1, keepdims=True) + NORM_EPSILON)
    hidden = (normed * (1.0 + mod_ref[:, width : 2 * width]) + mod_ref[:, :width]).astype(BF16)
    hid_ref[...] = hidden
    for part, (out_ref, gain_ref) in enumerate(((q_ref, qgain_ref), (k_ref, kgain_ref))):
        raw = mm(hidden, weight_ref[:, part * width : (part + 1) * width])
        raw = raw + bias_ref[:, part * width : (part + 1) * width].astype(F32)
        raw_ref[:, part * width : (part + 1) * width] = raw.astype(BF16)
        factor = lax.rsqrt(head_sum(raw * raw, head) * (1.0 / head) + NORM_EPSILON)
        scaled = raw * factor * gain_ref[...]
        out_ref[...] = turn(scaled, cos_ref[...], sin_ref[...], head).astype(BF16)
    value = mm(hidden, weight_ref[:, 2 * width :]) + bias_ref[:, 2 * width :].astype(F32)
    v_ref[...] = value.astype(BF16)


def project_call(x, mod, weight, bias, qgain, kgain, cosine, sine, head):
    rows, width = x.shape
    block = rows // 2
    by_row = lambda wide: pl.BlockSpec((block, wide), lambda i: (i, 0))
    shape = jax.ShapeDtypeStruct((rows, width), BF16)
    return pl.pallas_call(
        functools.partial(project_kernel, head),
        grid=(2,),
        in_specs=[
            by_row(width),
            full(mod.shape),
            full(weight.shape),
            full(bias.shape),
            full(qgain.shape),
            full(kgain.shape),
            by_row(128),
            by_row(128),
        ],
        out_specs=[by_row(width)] * 4 + [by_row(2 * width)],
        out_shape=[shape] * 4 + [jax.ShapeDtypeStruct((rows, 2 * width), BF16)],
        compiler_params=params(),
        name="project",
    )(x, mod, weight, bias, qgain, kgain, cosine, sine)


def attend_kernel(scale, q_ref, k0_ref, k1_ref, v0_ref, v1_ref, mix_ref, e_ref, rl_ref):
    lane = lax.broadcasted_iota(jnp.int32, (1, 128), 1)
    q = q_ref[...]
    keys = jnp.concatenate([k0_ref[...], k1_ref[...]], axis=0)
    values = jnp.concatenate([v0_ref[...], v1_ref[...]], axis=0)
    values = jnp.concatenate([values, jnp.ones_like(values)], axis=1)
    outs = []
    for h in range(2):
        mine = (lane >= 64) if h else (lane < 64)
        scores = mm_nt(jnp.where(mine, q, jnp.zeros_like(q)), keys)
        grown = jnp.exp(scores * scale).astype(BF16)
        e_ref[h] = grown
        outs.append(mm(grown, values))
    inverse = 1.0 / jnp.where(lane < 64, outs[0][:, 128:], outs[1][:, 128:])
    mix_ref[...] = (jnp.where(lane < 64, outs[0][:, :128], outs[1][:, :128]) * inverse).astype(BF16)
    rl_ref[...] = inverse


def attend_call(q, k0, k1, v0, v1, head):
    rows, width = q.shape
    pair = pl.BlockSpec((rows, 128), lambda p: (0, p))
    return pl.pallas_call(
        functools.partial(attend_kernel, head**-0.5),
        grid=(width // 128,),
        in_specs=[pair] * 5,
        out_specs=[pair, pl.BlockSpec((2, rows, 2 * rows), lambda p: (p, 0, 0)), pair],
        out_shape=[
            jax.ShapeDtypeStruct((rows, width), BF16),
            jax.ShapeDtypeStruct((width // head, rows, 2 * rows), BF16),
            jax.ShapeDtypeStruct((rows, width), F32),
        ],
        compiler_params=params(),
        name="attend",
    )(q, k0, k1, v0, v1)


def attend_back_kernel(
    scale, q_ref, k0_ref, k1_ref, v0_ref, v1_ref, e_ref, gm_ref, mix_ref, rl_ref,
    dq_ref, dk0_ref, dk1_ref, dv0_ref, dv1_ref,
):
    rows = q_ref.shape[0]
    lane = lax.broadcasted_iota(jnp.int32, (1, 128), 1)
    keys = jnp.concatenate([k0_ref[...], k1_ref[...]], axis=0)
    values = jnp.concatenate([v0_ref[...], v1_ref[...]], axis=0)
    scaled = gm_ref[...].astype(F32) * rl_ref[...]
    products = scaled * mix_ref[...].astype(F32)
    scaled = scaled.astype(BF16)
    q_t = q_ref[...].T
    scaled_t = scaled.T
    dqs, dks, dvs = [], [], []
    for h in range(2):
        mine = (lane >= 64) if h else (lane < 64)
        inner = jnp.sum(jnp.where(mine, products, 0.0), axis=1, keepdims=True)
        grad_probs = mm_nt(jnp.where(mine, scaled, jnp.zeros_like(scaled)), values)
        grown = e_ref[h]
        grad_scores = (grown.astype(F32) * (grad_probs - inner) * scale).astype(BF16)
        dqs.append(mm(grad_scores, keys))
        dks.append(mm(q_t[64 * h : 64 * h + 64], grad_scores))
        dvs.append(mm(scaled_t[64 * h : 64 * h + 64], grown))
    dq_ref[...] = jnp.where(lane < 64, dqs[0], dqs[1]).astype(BF16)
    dk = jnp.concatenate(dks, axis=0).T.astype(BF16)
    dv = jnp.concatenate(dvs, axis=0).T.astype(BF16)
    dk0_ref[...] = dk[:rows]
    dk1_ref[...] = dk[rows:]
    dv0_ref[...] = dv[:rows]
    dv1_ref[...] = dv[rows:]


def attend_back_call(q, k0, k1, v0, v1, grown, grad_mixed, mixed, inverse, head):
    rows, width = q.shape
    pair = pl.BlockSpec((rows, 128), lambda p: (0, p))
    return pl.pallas_call(
        functools.partial(attend_back_kernel, head**-0.5),
        grid=(width // 128,),
        in_specs=[pair] * 5
        + [pl.BlockSpec((2, rows, 2 * rows), lambda p: (p, 0, 0))]
        + [pair] * 3,
        out_specs=[pair] * 5,
        out_shape=[jax.ShapeDtypeStruct((rows, width), BF16)] * 5,
        compiler_params=params(),
        name="attend_back",
    )(q, k0, k1, v0, v1, grown, grad_mixed, mixed, inverse)


def middle_kernel(
    mix_ref, x_ref, dy_ref, mod_ref, weight_ref, bias_ref, att_ref, mid_ref, h2_ref, h2t_ref, gf_ref
):
    width = x_ref.shape[1]
    attended = mm(mix_ref[...], weight_ref[...]) + bias_ref[...].astype(F32)
    middle = x_ref[...].astype(F32) + mod_ref[:, 2 * width : 3 * width] * attended
    normed = middle * lax.rsqrt(jnp.mean(middle * middle, axis=-1, keepdims=True) + NORM_EPSILON)
    hidden = normed * (1.0 + mod_ref[:, 4 * width : 5 * width]) + mod_ref[:, 3 * width : 4 * width]
    hidden = hidden.astype(BF16)
    att_ref[...] = attended.astype(BF16)
    mid_ref[...] = middle
    h2_ref[...] = hidden
    h2t_ref[...] = hidden.T
    gf_ref[...] = (mod_ref[:, 5 * width :] * dy_ref[...].astype(F32)).astype(BF16)


def middle_call(mixed, x, dy, mod, weight, bias):
    rows, width = x.shape
    block = rows // 2
    by_row = pl.BlockSpec((block, width), lambda i: (i, 0))
    low = jax.ShapeDtypeStruct((rows, width), BF16)
    return pl.pallas_call(
        middle_kernel,
        grid=(2,),
        in_specs=[by_row] * 3 + [full(mod.shape), full(weight.shape), full(bias.shape)],
        out_specs=[by_row] * 3 + [pl.BlockSpec((width, block), lambda i: (0, i)), by_row],
        out_shape=[low, jax.ShapeDtypeStruct((rows, width), F32), low]
        + [jax.ShapeDtypeStruct((width, rows), BF16), low],
        compiler_params=params(),
        name="middle",
    )(mixed, x, dy, mod, weight, bias)


def feed_kernel(
    h2_ref, h2t_ref, gf_ref, wg_ref, wu_ref, bg_ref, bu_ref, wd_ref, feed_in_ref, gh_in_ref,
    feed_ref, gh_ref, dd_ref, dg_ref, db_ref,
):
    @pl.when(pl.program_id(0) == 0)
    def _():
        feed_ref[...] = feed_in_ref[...]
        gh_ref[...] = gh_in_ref[...]

    hidden = h2_ref[...]
    grad_feed = gf_ref[...]
    gate = mm(hidden, wg_ref[...]) + bg_ref[...].astype(F32)
    up = mm(hidden, wu_ref[...]) + bu_ref[...].astype(F32)
    grad_product = mm_nt(grad_feed, wd_ref[...])
    sig = 1.0 / (1.0 + jnp.exp(-gate))
    active = gate * sig
    product = (active * up).astype(BF16)
    grad_gate = (grad_product * up * sig * (1.0 + gate * (1.0 - sig))).astype(BF16)
    grad_up = (grad_product * active).astype(BF16)
    dd_ref[...] = mm_tn(product, grad_feed).astype(BF16)
    dg_ref[0] = mm(h2t_ref[...], grad_gate).astype(BF16)
    dg_ref[1] = mm(h2t_ref[...], grad_up).astype(BF16)
    db_ref[0] = col_sum(grad_gate.astype(F32))
    db_ref[1] = col_sum(grad_up.astype(F32))
    feed_ref[...] += mm(product, wd_ref[...])
    gh_ref[...] += mm_nt(grad_gate, wg_ref[...]) + mm_nt(grad_up, wu_ref[...])


def feed_call(hidden, hidden_t, grad_feed, weight, bias, down, feed, grad_hidden, first, step, unit):
    rows, width = hidden.shape
    blocks = down.shape[0] // unit
    steps = len(range(first, blocks, step))
    pick = lambda s: first + step * s
    acc = jax.ShapeDtypeStruct((rows, width), F32)
    return pl.pallas_call(
        feed_kernel,
        grid=(steps,),
        in_specs=[
            full((rows, width)),
            full((width, rows)),
            full((rows, width)),
            pl.BlockSpec((width, unit), lambda s: (0, pick(s))),
            pl.BlockSpec((width, unit), lambda s: (0, blocks + pick(s))),
            pl.BlockSpec((1, unit), lambda s: (0, pick(s))),
            pl.BlockSpec((1, unit), lambda s: (0, blocks + pick(s))),
            pl.BlockSpec((unit, width), lambda s: (pick(s), 0)),
            full((rows, width)),
            full((rows, width)),
        ],
        out_specs=[
            full((rows, width)),
            full((rows, width)),
            pl.BlockSpec((None, unit, width), lambda s: (s, 0, 0)),
            pl.BlockSpec((None, 2, width, unit), lambda s: (s, 0, 0, 0)),
            pl.BlockSpec((None, 2, 1, unit), lambda s: (s, 0, 0, 0)),
        ],
        out_shape=[
            acc,
            acc,
            jax.ShapeDtypeStruct((steps, unit, width), BF16),
            jax.ShapeDtypeStruct((steps, 2, width, unit), BF16),
            jax.ShapeDtypeStruct((steps, 2, 1, unit), F32),
        ],
        compiler_params=params(),
        name="feed",
    )(hidden, hidden_t, grad_feed, weight, weight, bias, bias, down, feed, grad_hidden)


def turn_kernel(
    feed_ref, gh_ref, mid_ref, att_ref, dy_ref, gf_ref, mix_ref, mod_ref, weight_ref, dbias_ref,
    out_ref, gmid_ref, gmix_ref, dw_ref, sums_ref,
):
    width = mid_ref.shape[1]
    half = width // 2
    dy = dy_ref[...].astype(F32)
    feed = feed_ref[...] + dbias_ref[...].astype(F32)
    middle = mid_ref[...]
    out_ref[...] = (middle + mod_ref[:, 5 * width :] * feed).astype(BF16)
    factor = lax.rsqrt(jnp.mean(middle * middle, axis=-1, keepdims=True) + NORM_EPSILON)
    normed = middle * factor
    grad_hidden = gh_ref[...]
    product = grad_hidden * normed
    grad_normed = grad_hidden * (1.0 + mod_ref[:, 4 * width : 5 * width])
    back = factor * (
        grad_normed - normed * jnp.mean(grad_normed * normed, axis=-1, keepdims=True)
    )
    grad_middle = dy + back
    gmid_ref[...] = grad_middle
    grad_attended = (mod_ref[:, 2 * width : 3 * width] * grad_middle).astype(BF16)
    sums_ref[0:1, :] = col_sum(grad_middle * att_ref[...].astype(F32))
    sums_ref[1:2, :] = col_sum(grad_hidden)
    sums_ref[2:3, :] = col_sum(product)
    sums_ref[3:4, :] = col_sum(dy * feed)
    sums_ref[4:5, :] = col_sum(grad_attended.astype(F32))
    sums_ref[5:6, :] = col_sum(gf_ref[...].astype(F32))
    sums_ref[6:8, :] = jnp.zeros((2, width), F32)
    gmix_ref[...] = mm_nt(grad_attended, weight_ref[...]).astype(BF16)
    mixed_t = mix_ref[...].T
    dw_ref[0] = mm(mixed_t, grad_attended[:, :half]).astype(BF16)
    dw_ref[1] = mm(mixed_t, grad_attended[:, half:]).astype(BF16)


def turn_call(feed, grad_hidden, middle, attended, dy, grad_feed, mixed, mod, weight, down_bias):
    rows, width = middle.shape
    low = jax.ShapeDtypeStruct((rows, width), BF16)
    return pl.pallas_call(
        turn_kernel,
        out_shape=[
            low,
            jax.ShapeDtypeStruct((rows, width), F32),
            low,
            jax.ShapeDtypeStruct((2, width, width // 2), BF16),
            jax.ShapeDtypeStruct((8, width), F32),
        ],
        compiler_params=params(),
        name="turn",
    )(feed, grad_hidden, middle, attended, dy, grad_feed, mixed, mod, weight, down_bias)


def project_back_kernel(
    head, dq_ref, dk0_ref, dk1_ref, dv0_ref, dv1_ref, raw_ref, hid_ref, x_ref, gmid_ref, mod_ref,
    weight_ref, qgain_ref, kgain_ref, cos_ref, sin_ref,
    gx_ref, dw_ref, sums_ref, bias_ref, proj_ref,
):
    width = x_ref.shape[1]
    cosine, sine = cos_ref[...], -sin_ref[...]
    for part in range(3):
        span = slice(part * width, (part + 1) * width)
        if part == 2:
            grad = dv0_ref[...].astype(F32) + dv1_ref[...].astype(F32)
        else:
            grad = dq_ref[...].astype(F32)
            if part == 1:
                grad = dk0_ref[...].astype(F32) + dk1_ref[...].astype(F32)
            gain = (qgain_ref, kgain_ref)[part][...]
            raw = raw_ref[:, span].astype(F32)
            factor = lax.rsqrt(head_sum(raw * raw, head) * (1.0 / head) + NORM_EPSILON)
            normed = raw * factor
            turned = turn(grad, cosine, sine, head)
            sums_ref[2 + part : 3 + part, :] = col_sum(turned * normed)
            turned = turned * gain
            mean = head_sum(turned * normed, head) * (1.0 / head)
            grad = factor * (turned - normed * mean)
        low = grad.astype(BF16)
        proj_ref[:, span] = low
        bias_ref[:, span] = col_sum(low.astype(F32))
    hidden_t = hid_ref[...].T
    half = 3 * width // 2
    dw_ref[0] = mm(hidden_t, proj_ref[:, :half]).astype(BF16)
    dw_ref[1] = mm(hidden_t, proj_ref[:, half:]).astype(BF16)
    grad_hidden = mm_nt(proj_ref[...], weight_ref[...])
    x = x_ref[...].astype(F32)
    factor = lax.rsqrt(jnp.mean(x * x, axis=-1, keepdims=True) + NORM_EPSILON)
    normed = x * factor
    sums_ref[0:1, :] = col_sum(grad_hidden)
    sums_ref[1:2, :] = col_sum(grad_hidden * normed)
    sums_ref[4:8, :] = jnp.zeros((4, width), F32)
    grad_normed = grad_hidden * (1.0 + mod_ref[:, width : 2 * width])
    back = factor * (
        grad_normed - normed * jnp.mean(grad_normed * normed, axis=-1, keepdims=True)
    )
    gx_ref[...] = (gmid_ref[...] + back).astype(BF16)


def project_back_call(
    dq, dk0, dk1, dv0, dv1, raw, hidden, x, grad_middle, mod, weight, qgain, kgain, cosine, sine, head
):
    rows, width = x.shape
    return pl.pallas_call(
        functools.partial(project_back_kernel, head),
        out_shape=[
            jax.ShapeDtypeStruct((rows, width), BF16),
            jax.ShapeDtypeStruct((2, width, 3 * width // 2), BF16),
            jax.ShapeDtypeStruct((8, width), F32),
            jax.ShapeDtypeStruct((1, 3 * width), F32),
        ],
        scratch_shapes=[pltpu.VMEM((rows, 3 * width), BF16)],
        compiler_params=params(),
        name="project_back",
    )(dq, dk0, dk1, dv0, dv1, raw, hidden, x, grad_middle, mod, weight, qgain, kgain, cosine, sine)


class Place:
    def __init__(self):
        self.z, self.gy, self.gx = (lax.axis_index(name) for name in AXES)
        self.core = lax.rem(self.gx, 2)
        self.side = self.gx // 2
        self.chip = 2 * self.gy + self.side

    def flipped(self, k):
        return 2 * lax.rem(self.gy + k // 2, 2) + lax.rem(self.side + lax.rem(k, 2), 2)

    def pair(self):
        return {"gx": self.gx + 1 - 2 * self.core}

    def plane(self, k):
        device = {}
        if k & 2:
            device["gy"] = 1 - self.gy
        if k & 1:
            device["gx"] = lax.rem(self.gx + 2, 4)
        return device

    def depth(self, d):
        return {"batch": self.flipped_z(d)}

    def flipped_z(self, d):
        return {1: self.z + 1 - 2 * lax.rem(self.z, 2), 2: lax.rem(self.z + 2, 4), 3: 3 - self.z}[d]


def meet(devices):
    barrier = pltpu.get_barrier_semaphore()
    for device in devices:
        pl.semaphore_signal(barrier, inc=1, device_id=device, device_id_type=pl.DeviceIdType.MESH)
    pl.semaphore_wait(barrier, len(devices))


def send(source, target, send_sem, recv_sem, device):
    return pltpu.make_async_remote_copy(
        src_ref=source, dst_ref=target, send_sem=send_sem, recv_sem=recv_sem, device_id=device,
        device_id_type=pl.DeviceIdType.MESH,
    )


def feed_order(step):
    owner = jnp.where(
        step < 2, 3, jnp.where((step == 2) | (step == 5), 2, jnp.where(step < 5, 1, 0))
    )
    return owner, lax.rem(step, 2)


def feed_block(step, i):
    step = jnp.minimum(step, 7)
    owner, half = feed_order(step)
    return (2 * half + i) * 4 + Place().flipped(owner)


def feed_turn_kernel(
    h2_ref, h2t_ref, gf_ref, wg0, wg1, wu0, wu1, bg0, bg1, bu0, bu1, wd0, wd1,
    mid_ref, att_ref, dy_ref, mix_ref, mod_ref, weight_ref, dbias_ref,
    out_ref, gmid_ref, gmix_ref, dw_ref, sums_ref, db_ref, total_ref,
    feed_ref, gh_ref, made, paired, near, pair_send, pair_recv, near_send, near_recv,
):
    place = Place()
    core = place.core
    step = pl.program_id(0)
    slot = lax.rem(step, 2)
    width = h2_ref.shape[1]
    unit = 128
    g_rows = width

    @pl.when(step == 0)
    def _():
        feed_ref[...] = jnp.zeros_like(feed_ref)
        gh_ref[...] = jnp.zeros_like(gh_ref)
        meet([place.pair(), place.plane(1), place.plane(2)])

    def pair_copy(of):
        return send(
            made.at[lax.rem(of, 2), 1 - core], paired.at[of], pair_send.at[lax.rem(of, 2)],
            pair_recv.at[of], place.pair(),
        )

    def near_copy(of, k):
        return send(paired.at[of], near.at[of], near_send.at[of], near_recv.at[of], place.plane(k))

    @pl.when(step >= 1)
    def _():
        pair_copy(step - 1).start()

    @pl.when(step < 8)
    def _():
        owner, half = feed_order(step)
        hidden = h2_ref[...]
        grad_feed = gf_ref[...]
        wg = jnp.concatenate([wg0[...], wg1[...]], axis=1)
        wu = jnp.concatenate([wu0[...], wu1[...]], axis=1)
        wd = jnp.concatenate([wd0[...], wd1[...]], axis=0)
        gate = mm(hidden, wg) + jnp.concatenate([bg0[...], bg1[...]], axis=1).astype(F32)
        up = mm(hidden, wu) + jnp.concatenate([bu0[...], bu1[...]], axis=1).astype(F32)
        grad_product = mm_nt(grad_feed, wd)
        sig = 1.0 / (1.0 + jnp.exp(-gate))
        active = gate * sig
        product = (active * up).astype(BF16)
        grad_gate = (grad_product * up * sig * (1.0 + gate * (1.0 - sig))).astype(BF16)
        grad_up = (grad_product * active).astype(BF16)
        feed_ref[...] += mm(product, wd)
        gh_ref[...] += mm_nt(grad_gate, wg) + mm_nt(grad_up, wu)
        for e, grad in enumerate((grad_gate, grad_up)):
            total = col_sum(grad.astype(F32))
            for i in range(2):
                row = 16 * e + (2 * half + i) * 4 + place.flipped(owner)
                db_ref[pl.ds(row, 1), :] = total[:, i * unit : (i + 1) * unit]

        @pl.when(step >= 2)
        def _():
            pair_copy(step - 2).wait_send()

        for e, grad in enumerate((grad_gate, grad_up)):
            made[slot, e, :g_rows] = mm(h2t_ref[...], grad).astype(BF16)
        product_t = product.T
        for b in range(3):
            d = mm(product_t, grad_feed[:, 256 * b : 256 * b + 256]).astype(BF16)
            for i in range(2):
                for c in range(2):
                    made[slot, c, pl.ds(g_rows + b * 128 + i * 64, 64)] = d[
                        i * 128 + c * 64 : i * 128 + c * 64 + 64
                    ]

    @pl.when(step >= 1)
    def _():
        of = step - 1
        copy = pair_copy(of)
        copy.wait_recv()
        late = (of == 4) | (of == 5)

        @pl.when(jnp.logical_not(late))
        def _():
            paired[of] = (made[1 - slot, core].astype(F32) + paired[of].astype(F32)).astype(BF16)

        @pl.when(late)
        def _():
            near_copy(of - 4, 1).wait_recv()
            paired[of] = (
                made[1 - slot, core].astype(F32)
                + paired[of].astype(F32)
                + near[of - 4].astype(F32)
            ).astype(BF16)

        @pl.when((of == 0) | (of == 2) | (of == 5))
        def _():
            near_copy(of, 2).start()

        @pl.when((of == 1) | (of == 3) | (of == 4))
        def _():
            near_copy(of, 1).start()

    @pl.when(step == 8)
    def _():
        half = width // 2
        dy = dy_ref[...].astype(F32)
        feed = feed_ref[...] + dbias_ref[...].astype(F32)
        middle = mid_ref[...]
        out_ref[...] = (middle + mod_ref[:, 5 * width :] * feed).astype(BF16)
        factor = lax.rsqrt(jnp.mean(middle * middle, axis=-1, keepdims=True) + NORM_EPSILON)
        normed = middle * factor
        grad_hidden = gh_ref[...]
        product = grad_hidden * normed
        grad_normed = grad_hidden * (1.0 + mod_ref[:, 4 * width : 5 * width])
        back = factor * (
            grad_normed - normed * jnp.mean(grad_normed * normed, axis=-1, keepdims=True)
        )
        grad_middle = dy + back
        gmid_ref[...] = grad_middle
        grad_attended = (mod_ref[:, 2 * width : 3 * width] * grad_middle).astype(BF16)
        sums_ref[0:1, :] = col_sum(grad_middle * att_ref[...].astype(F32))
        sums_ref[1:2, :] = col_sum(grad_hidden)
        sums_ref[2:3, :] = col_sum(product)
        sums_ref[3:4, :] = col_sum(dy * feed)
        sums_ref[4:5, :] = col_sum(grad_attended.astype(F32))
        sums_ref[5:6, :] = col_sum(gf_ref[...].astype(F32))
        sums_ref[6:8, :] = jnp.zeros((2, width), F32)
        gmix_ref[...] = mm_nt(grad_attended, weight_ref[...]).astype(BF16)
        mixed_t = mix_ref[...].T
        dw_ref[0] = mm(mixed_t, grad_attended[:, :half]).astype(BF16)
        dw_ref[1] = mm(mixed_t, grad_attended[:, half:]).astype(BF16)
        for of in (6, 7):
            pair_copy(of).wait_send()
        for of in (2, 3, 4, 5):
            near_copy(of, 1).wait_recv()
        for of in range(6):
            near_copy(of, 1).wait_send()
        rows = width // 4
        for f in range(2):
            for z in range(4):
                span = slice(z * rows, (z + 1) * rows)
                total_ref[z, f] = sum(
                    part.astype(F32)
                    for part in (paired[6 + f, span], near[2 + f, span], near[4 + f, span])
                ).astype(BF16)
            for i in range(2):
                for b in range(3):
                    span = slice(g_rows + b * 128 + i * 64, g_rows + b * 128 + i * 64 + 64)
                    total_ref[2 * f + i, 2, b * 64 : b * 64 + 64] = sum(
                        part.astype(F32)
                        for part in (paired[6 + f, span], near[2 + f, span], near[4 + f, span])
                    ).astype(BF16)


def once(shape):
    return pl.BlockSpec(shape, lambda *_: (0,) * len(shape), pipeline_mode=pl.Buffered(1))


def feed_turn_call(
    hidden, hidden_t, grad_feed, gate_up, gate_up_bias, down, middle, attended, dy, mixed, mod,
    weight, down_bias,
):
    rows, width = hidden.shape
    low = jax.ShapeDtypeStruct((rows, width), BF16)
    wide = jax.ShapeDtypeStruct((rows, width), F32)
    cols = lambda i, e: pl.BlockSpec((width, 128), lambda s: (0, 16 * e + feed_block(s, i)))
    bias = lambda i, e: pl.BlockSpec((1, 128), lambda s: (0, 16 * e + feed_block(s, i)))
    deep = lambda i: pl.BlockSpec((128, width), lambda s: (feed_block(s, i), 0))
    piece = (width + 384, 256)
    out_shape = [
        low, wide, low,
        jax.ShapeDtypeStruct((2, width, width // 2), BF16),
        jax.ShapeDtypeStruct((8, width), F32),
        jax.ShapeDtypeStruct((32, 128), F32),
        jax.ShapeDtypeStruct((4, 3, width // 4, 256), BF16),
    ]
    return pl.pallas_call(
        feed_turn_kernel,
        grid=(9,),
        in_specs=[once((rows, width)), once((width, rows)), once((rows, width))]
        + [cols(0, 0), cols(1, 0), cols(0, 1), cols(1, 1)]
        + [bias(0, 0), bias(1, 0), bias(0, 1), bias(1, 1)]
        + [deep(0), deep(1)]
        + [once((rows, width))] * 4
        + [once(mod.shape), once(weight.shape), once(down_bias.shape)],
        out_specs=[full(shape.shape) for shape in out_shape],
        out_shape=out_shape,
        scratch_shapes=[
            pltpu.VMEM((rows, width), F32),
            pltpu.VMEM((rows, width), F32),
            pltpu.VMEM((2, 2) + piece, BF16),
            pltpu.VMEM((8,) + piece, BF16),
            pltpu.VMEM((6,) + piece, BF16),
            pltpu.SemaphoreType.DMA((2,)),
            pltpu.SemaphoreType.DMA((8,)),
            pltpu.SemaphoreType.DMA((6,)),
            pltpu.SemaphoreType.DMA((6,)),
        ],
        compiler_params=pltpu.CompilerParams(
            vmem_limit_bytes=VMEM_LIMIT, collective_id=1, has_side_effects=True
        ),
        name="feed_turn",
    )(
        hidden, hidden_t, grad_feed, gate_up, gate_up, gate_up, gate_up, gate_up_bias,
        gate_up_bias, gate_up_bias, gate_up_bias, down, down, middle, attended, dy, mixed, mod,
        weight, down_bias,
    )


def take(array_in, index, axis=0):
    return lax.dynamic_index_in_dim(array_in, index, axis, keepdims=False)


def add(*terms):
    return sum(term.astype(F32) for term in terms)


class Moves:
    def __init__(self, mesh):
        self.sizes = tuple(mesh.shape[name] for name in AXES)

    def flip(self, value, batch=0, gy=0, gx=0):
        nb, ny, nx = self.sizes
        pairs = []
        for b in range(nb):
            for y in range(ny):
                for x in range(nx):
                    here = (b * ny + y) * nx + x
                    there = ((b ^ batch) * ny + (y ^ gy)) * nx + (x ^ gx)
                    pairs.append((here, there))
        return lax.ppermute(value, AXES, pairs)

    def plane(self, value, k):
        return self.flip(value, gy=k >> 1, gx=2 * (k & 1))

    def pair(self, value):
        return self.flip(value, gx=1)

    def gather(self, value):
        value = value[None]
        value = jnp.concatenate([value, self.plane(value, 1)], axis=0)
        value = jnp.concatenate([value, self.plane(value, 2)], axis=0)
        bit = 1
        while bit < self.sizes[0]:
            value = jnp.concatenate([value, self.flip(value, batch=bit)], axis=0)
            bit *= 2
        return value


def regroup(parts, place):
    stacked = jnp.stack(parts)
    return jnp.stack([take(stacked, place ^ k) for k in range(len(parts))])


def reduce_pieces(moves, pieces, c, first, second, order, z):
    one, two = order
    arrived = moves.pair(take(pieces, 1 - c))
    mine = take(pieces, c)
    near = moves.plane(add(take(mine, 1 - first), take(arrived, 1 - first)).astype(BF16), one)
    mine, arrived = take(mine, first), take(arrived, first)
    far = moves.plane(
        add(take(mine, 1 - second), take(arrived, 1 - second), take(near, 1 - second)).astype(BF16),
        two,
    )
    total = add(take(mine, second), take(arrived, second), take(near, second), far)
    low = total.astype(BF16)
    own = take(total, z)
    for d in range(1, moves.sizes[0]):
        own = add(own, moves.flip(take(low, z ^ d), batch=d))
    own = own.astype(BF16)
    quarter = [own, moves.plane(own, two), moves.plane(own, one), moves.plane(own, one ^ two)]
    quarter = regroup(quarter, 2 * first + second)
    halves = [quarter, moves.pair(quarter)]
    return regroup(halves, c)


def body(mesh, *operands):
    (
        tokens, timesteps, labels, class_table, modulate_weight, modulate_bias, inproj_weight,
        inproj_bias, query_gain, key_gain, outproj_weight, outproj_bias, gate_up_weight,
        gate_up_bias, down_weight, down_bias, cotangent,
    ) = operands
    image_count, tile_rows, tile_cols, width = tokens.shape
    cells = tile_rows * tile_cols
    rows = image_count * cells
    head = query_gain.shape[0]
    heads = width // head
    hidden_width = down_weight.shape[0]
    class_count = class_table.shape[0]
    highest = lax.Precision.HIGHEST
    moves = Moves(mesh)
    nb, ny, nx = moves.sizes
    assert ny == 2 and nx == 4 and image_count == 4
    z, gy, gx = (lax.axis_index(name) for name in AXES)
    side, core = gx // 2, gx % 2
    place = 2 * gy + side

    tiles = tokens.reshape(image_count, cells, width)
    grads = cotangent.reshape(image_count, cells, width)

    def exchange(blocks):
        return [take(blocks, place)] + [
            moves.plane(take(blocks, place ^ k), k) for k in range(1, 4)
        ]

    x = jnp.concatenate(exchange(tiles), axis=0)

    half_width = width // 2
    step = take(timesteps, place).astype(F32)
    label = take(labels, place)
    rates = jnp.exp(-math.log(10000.0) * jnp.arange(half_width, dtype=F32) / half_width)
    features = jnp.concatenate([jnp.cos(step * rates), jnp.sin(step * rates)])
    condition = features + take(class_table, label).astype(F32)
    cond_act = jax.nn.silu(condition).astype(BF16)
    mod = modulation_call(
        jnp.broadcast_to(cond_act[None], (16, width)), modulate_weight, modulate_bias[None]
    )[:1]

    quarter = head // 4
    cell = jnp.arange(cells, dtype=jnp.int32)
    row_places, col_places = [], []
    for k in range(4):
        there = place ^ k
        row_places.append((there // 2) * tile_rows + cell // tile_cols)
        col_places.append((2 * (there % 2) + core) * tile_cols + cell % tile_cols)
    row_places = jnp.concatenate(row_places).astype(F32)[:, None]
    col_places = jnp.concatenate(col_places).astype(F32)[:, None]
    lane = jnp.arange(128, dtype=jnp.int32)
    turn_rate = jnp.exp(-math.log(10000.0) * (lane % quarter).astype(F32) / quarter)[None]
    angles = jnp.where((lane % head)[None] < head // 2, row_places, col_places) * turn_rate
    cosine = jnp.cos(angles)
    sine = jnp.where((lane % (2 * quarter))[None] < quarter, -1.0, 1.0) * jnp.sin(angles)
    qgain = jnp.tile(query_gain.astype(F32), heads)[None]
    kgain = jnp.tile(key_gain.astype(F32), heads)[None]

    hidden_one, q, k0, v0, raw = project_call(
        x, mod, inproj_weight, inproj_bias[None], qgain, kgain, cosine, sine, head
    )
    k1, v1 = moves.pair(k0), moves.pair(v0)
    dy = jnp.concatenate(exchange(grads), axis=0)
    mixed, grown, inverse = attend_call(q, k0, k1, v0, v1, head)
    attended, middle, hidden_two, hidden_two_t, grad_feed = middle_call(
        mixed, x, dy, mod, outproj_weight, outproj_bias[None]
    )

    unit = 256
    blocks = hidden_width // unit
    quick = nb == 4 and hidden_width == 16 * 128
    if quick:
        output_rows, grad_middle, grad_mixed, d_out, sums_two, gate_bias, totals = feed_turn_call(
            hidden_two, hidden_two_t, grad_feed, gate_up_weight, gate_up_bias[None], down_weight,
            middle, attended, dy, mixed, mod, outproj_weight, down_bias[None],
        )
    else:
        feed, grad_hidden, d_down, d_gate, d_bias = feed_call(
            hidden_two, hidden_two_t, grad_feed, gate_up_weight, gate_up_bias[None], down_weight,
            jnp.zeros((rows, width), F32), jnp.zeros((rows, width), F32), 0, 1, unit,
        )
        output_rows, grad_middle, grad_mixed, d_out, sums_two = turn_call(
            feed, grad_hidden, middle, attended, dy, grad_feed, mixed, mod, outproj_weight,
            down_bias[None],
        )
        gate_bias = d_bias.reshape(blocks, 2, unit).transpose(1, 0, 2)
    dq, dk0, dk1, dv0, dv1 = attend_back_call(
        q, k0, k1, v0, v1, grown, grad_mixed, mixed, inverse, head
    )
    dk1, dv1 = moves.pair(dk1), moves.pair(dv1)
    grad_x, d_in, sums_one, in_bias = project_back_call(
        dq, dk0, dk1, dv0, dv1, raw, hidden_one, x, grad_middle, mod, inproj_weight, qgain, kgain,
        cosine, sine, head,
    )

    def give_back(rows_out):
        parts = rows_out.reshape(4, cells, width)
        got = [parts[0]] + [moves.plane(parts[k], k) for k in range(1, 4)]
        return regroup(got, place).reshape(tokens.shape)

    output = give_back(output_rows)
    grad_tokens = give_back(grad_x)

    slice_rows = width // nb
    if quick:
        own = take(totals, z).astype(F32)
        for d in range(1, nb):
            own = add(own, moves.flip(take(totals, z ^ d), batch=d))
        own = own.astype(BF16)
        own = regroup([own] + [moves.plane(own, k) for k in range(1, 4)], place)
        own = regroup([own, moves.pair(own)], core)
        gates = own[:, :, :2].reshape(2, 4, 2, slice_rows, 2, 128).transpose(3, 0, 2, 4, 1, 5)
        grad_gu_w = gates.reshape(slice_rows, 2 * hidden_width).astype(F32)
        downs = own[:, :, 2].reshape(2, 4, 3, 64, 256).transpose(1, 0, 3, 2, 4)
        grad_down_w = downs.reshape(hidden_width // nb, width).astype(F32)

        def by_rows(d, order, first, second):
            wide = d.shape[2]
            d = d.reshape(2, nb, 2, 2, slice_rows // 4, wide).transpose(0, 2, 3, 1, 4, 5)
            d = reduce_pieces(moves, d, core, first, second, order, z)
            d = d.reshape(2, slice_rows, wide)
            return jnp.concatenate([d[0], d[1]], axis=1).astype(F32)

        grad_out_w = by_rows(d_out, (1, 2), side, gy)
        grad_in_w = by_rows(d_in, (2, 1), gy, side)
    else:

        def scatter(d):
            d = lax.psum_scatter(d.astype(BF16), "batch", scatter_dimension=0, tiled=True)
            return lax.psum(d, ("gy", "gx")).astype(F32)

        def joined(d):
            return jnp.concatenate([d[0], d[1]], axis=1)

        grad_down_w = scatter(d_down.reshape(hidden_width, width))
        grad_gu_w = scatter(
            d_gate.transpose(2, 1, 0, 3).reshape(width, 2 * hidden_width)
        )
        grad_out_w = scatter(joined(d_out))
        grad_in_w = scatter(joined(d_in))

    gain_sums = sums_one[2:4].reshape(2, heads, head).sum(axis=1)
    early = jnp.concatenate([sums_two[:6].reshape(-1), gate_bias.reshape(-1)])
    late = jnp.concatenate([sums_one[:2].reshape(-1), in_bias.reshape(-1), gain_sums.reshape(-1)])

    def everywhere(vector):
        halves = vector.reshape(2, -1)
        half = add(take(halves, core), moves.pair(take(halves, 1 - core)))
        half = moves.gather(half)
        both = regroup([half, moves.pair(half)], core)
        return both.transpose(1, 0, 2).reshape(half.shape[0], -1)

    known = jnp.concatenate([condition, jnp.broadcast_to(label.astype(F32), (128,))])
    known = moves.gather(known)
    early = everywhere(early)
    late = everywhere(late)
    grad_modulation = jnp.concatenate([late[:, : 2 * width], early[:, : 4 * width]], axis=1)
    conditions = known[:, :width]
    all_labels = known[:, width].astype(jnp.int32)
    cond_acts = jax.nn.silu(conditions).astype(BF16)
    my_acts = lax.dynamic_slice_in_dim(cond_acts, z * slice_rows, slice_rows, axis=1)
    low_mod = grad_modulation.astype(BF16)
    grad_mod_w = mm_tn(my_acts, low_mod)
    wide = 6 * width
    grad_mod_b = lax.dynamic_slice_in_dim(
        jnp.sum(grad_modulation, axis=0), z * (wide // nb), wide // nb, axis=0
    )
    grad_cond_act = mm_nt(low_mod, modulate_weight)
    sig = jax.nn.sigmoid(conditions)
    grad_conditions = grad_cond_act * sig * (1.0 + conditions * (1.0 - sig))
    grad_condition = regroup([grad_conditions[k] for k in range(4)], place)
    onehot = (all_labels[:, None] == jnp.arange(class_count, dtype=jnp.int32)[None, :]).astype(F32)
    grad_table = lax.dot_general(
        onehot, grad_conditions, (((0,), (0,)), ((), ())), precision=highest,
        preferred_element_type=F32,
    )

    early_sum = jnp.sum(early, axis=0)
    late_sum = jnp.sum(late, axis=0)

    def part(vector, start, size):
        return lax.dynamic_slice_in_dim(vector, start + z * (size // nb), size // nb, axis=0)

    grad_out_b = part(early_sum, 4 * width, width)
    grad_down_b = part(early_sum, 5 * width, width)
    grad_gu_b = part(early_sum, 6 * width, 2 * hidden_width)
    grad_in_b = part(late_sum, 2 * width, 3 * width)
    grad_q_gain = part(late_sum, 5 * width, head)
    grad_k_gain = part(late_sum, 5 * width + head, head)
    return (
        output, grad_tokens, grad_condition, grad_table, grad_mod_w, grad_mod_b, grad_in_w,
        grad_in_b, grad_q_gain, grad_k_gain, grad_out_w, grad_out_b, grad_gu_w, grad_gu_b,
        grad_down_w, grad_down_b,
    )


def solution(mesh):
    grid = P("batch", "gy", "gx", None)
    by_batch = P("batch")
    rows = P("batch", None)
    placed = (grid, by_batch, by_batch) + (P(),) * 13 + (grid,)
    return jax.shard_map(
        functools.partial(body, mesh),
        mesh=mesh,
        in_specs=placed,
        out_specs=(
            grid, grid, rows, P(), rows, by_batch, rows, by_batch, by_batch, by_batch, rows,
            by_batch, rows, by_batch, rows, by_batch,
        ),
        check_vma=False,
    )
```

```python
import functools
import math

import jax
import jax.numpy as jnp
from jax import lax
from jax.experimental import pallas as pl
from jax.experimental.pallas import tpu as pltpu
from jax.sharding import PartitionSpec as P

NORM_EPSILON = 1e-06
AXES = ("batch", "gy", "gx")
BF16 = jnp.bfloat16
F32 = jnp.float32
VMEM_LIMIT = 60 * 1024 * 1024


def mm(left, right):
    return lax.dot_general(left, right, (((1,), (0,)), ((), ())), preferred_element_type=F32)


def mm_nt(left, right):
    return lax.dot_general(left, right, (((1,), (1,)), ((), ())), preferred_element_type=F32)


def mm_tn(left, right):
    return lax.dot_general(left, right, (((0,), (0,)), ((), ())), preferred_element_type=F32)


def params():
    return pltpu.CompilerParams(vmem_limit_bytes=VMEM_LIMIT)


def full(shape):
    return pl.BlockSpec(shape, lambda *_: (0,) * len(shape))


def col_sum(values):
    return jnp.sum(values, axis=0, keepdims=True)


def modulation_kernel(act_ref, weight_ref, bias_ref, out_ref):
    out_ref[...] = mm(act_ref[...], weight_ref[...]) + bias_ref[...].astype(F32)


def modulation_call(act, weight, bias):
    rows, width = act.shape
    wide = weight.shape[1]
    return pl.pallas_call(
        modulation_kernel,
        grid=(wide // width,),
        in_specs=[
            full((rows, width)),
            pl.BlockSpec((width, width), lambda j: (0, j)),
            pl.BlockSpec((1, width), lambda j: (0, j)),
        ],
        out_specs=pl.BlockSpec((rows, width), lambda j: (0, j)),
        out_shape=jax.ShapeDtypeStruct((rows, wide), F32),
        compiler_params=params(),
        name="modulation",
    )(act, weight, bias)


def head_sum(values, head):
    width = 256
    row = lax.broadcasted_iota(jnp.int32, (width, width), 0) // head
    col = lax.broadcasted_iota(jnp.int32, (width, width), 1) // head
    ones = jnp.where(row == col, 1.0, 0.0).astype(BF16)
    parts = [
        mm(values[:, i : i + width].astype(BF16), ones) for i in range(0, values.shape[1], width)
    ]
    return jnp.concatenate(parts, axis=1)


def turn(values, cosine, sine, head):
    quarter = head // 4
    lane = lax.broadcasted_iota(jnp.int32, (1, 128), 1)
    first = (lane % (2 * quarter)) < quarter
    parts = []
    for i in range(0, values.shape[1], 128):
        part = values[:, i : i + 128]
        partner = jnp.where(
            first, pltpu.roll(part, 128 - quarter, 1), pltpu.roll(part, quarter, 1)
        )
        parts.append(part * cosine + partner * sine)
    return jnp.concatenate(parts, axis=1)


def project_kernel(
    head, x_ref, mod_ref, weight_ref, bias_ref, qgain_ref, kgain_ref, cos_ref, sin_ref,
    hid_ref, q_ref, k_ref, v_ref, raw_ref,
):
    width = x_ref.shape[1]
    x = x_ref[...].astype(F32)
    normed = x * lax.rsqrt(jnp.mean(x * x, axis=-1, keepdims=True) + NORM_EPSILON)
    hidden = (normed * (1.0 + mod_ref[:, width : 2 * width]) + mod_ref[:, :width]).astype(BF16)
    hid_ref[...] = hidden
    for part, (out_ref, gain_ref) in enumerate(((q_ref, qgain_ref), (k_ref, kgain_ref))):
        raw = mm(hidden, weight_ref[:, part * width : (part + 1) * width])
        raw = raw + bias_ref[:, part * width : (part + 1) * width].astype(F32)
        raw_ref[:, part * width : (part + 1) * width] = raw.astype(BF16)
        factor = lax.rsqrt(head_sum(raw * raw, head) * (1.0 / head) + NORM_EPSILON)
        scaled = raw * factor * gain_ref[...]
        out_ref[...] = turn(scaled, cos_ref[...], sin_ref[...], head).astype(BF16)
    value = mm(hidden, weight_ref[:, 2 * width :]) + bias_ref[:, 2 * width :].astype(F32)
    v_ref[...] = value.astype(BF16)


def project_call(x, mod, weight, bias, qgain, kgain, cosine, sine, head):
    rows, width = x.shape
    block = rows // 2
    by_row = lambda wide: pl.BlockSpec((block, wide), lambda i: (i, 0))
    shape = jax.ShapeDtypeStruct((rows, width), BF16)
    return pl.pallas_call(
        functools.partial(project_kernel, head),
        grid=(2,),
        in_specs=[
            by_row(width),
            full(mod.shape),
            full(weight.shape),
            full(bias.shape),
            full(qgain.shape),
            full(kgain.shape),
            by_row(128),
            by_row(128),
        ],
        out_specs=[by_row(width)] * 4 + [by_row(2 * width)],
        out_shape=[shape] * 4 + [jax.ShapeDtypeStruct((rows, 2 * width), BF16)],
        compiler_params=params(),
        name="project",
    )(x, mod, weight, bias, qgain, kgain, cosine, sine)


def attend_kernel(scale, q_ref, k0_ref, k1_ref, v0_ref, v1_ref, mix_ref, e_ref, rl_ref):
    lane = lax.broadcasted_iota(jnp.int32, (1, 128), 1)
    q = q_ref[...]
    keys = jnp.concatenate([k0_ref[...], k1_ref[...]], axis=0)
    values = jnp.concatenate([v0_ref[...], v1_ref[...]], axis=0)
    values = jnp.concatenate([values, jnp.ones_like(values)], axis=1)
    outs = []
    for h in range(2):
        mine = (lane >= 64) if h else (lane < 64)
        scores = mm_nt(jnp.where(mine, q, jnp.zeros_like(q)), keys)
        grown = jnp.exp(scores * scale).astype(BF16)
        e_ref[h] = grown
        outs.append(mm(grown, values))
    inverse = 1.0 / jnp.where(lane < 64, outs[0][:, 128:], outs[1][:, 128:])
    mix_ref[...] = (jnp.where(lane < 64, outs[0][:, :128], outs[1][:, :128]) * inverse).astype(BF16)
    rl_ref[...] = inverse


def attend_call(q, k0, k1, v0, v1, head):
    rows, width = q.shape
    pair = pl.BlockSpec((rows, 128), lambda p: (0, p))
    return pl.pallas_call(
        functools.partial(attend_kernel, head**-0.5),
        grid=(width // 128,),
        in_specs=[pair] * 5,
        out_specs=[pair, pl.BlockSpec((2, rows, 2 * rows), lambda p: (p, 0, 0)), pair],
        out_shape=[
            jax.ShapeDtypeStruct((rows, width), BF16),
            jax.ShapeDtypeStruct((width // head, rows, 2 * rows), BF16),
            jax.ShapeDtypeStruct((rows, width), F32),
        ],
        compiler_params=params(),
        name="attend",
    )(q, k0, k1, v0, v1)


def attend_back_kernel(
    scale, q_ref, k0_ref, k1_ref, v0_ref, v1_ref, e_ref, gm_ref, mix_ref, rl_ref,
    dq_ref, dk0_ref, dk1_ref, dv0_ref, dv1_ref,
):
    rows = q_ref.shape[0]
    lane = lax.broadcasted_iota(jnp.int32, (1, 128), 1)
    keys = jnp.concatenate([k0_ref[...], k1_ref[...]], axis=0)
    values = jnp.concatenate([v0_ref[...], v1_ref[...]], axis=0)
    scaled = gm_ref[...].astype(F32) * rl_ref[...]
    products = scaled * mix_ref[...].astype(F32)
    scaled = scaled.astype(BF16)
    q_t = q_ref[...].T
    scaled_t = scaled.T
    dqs, dks, dvs = [], [], []
    for h in range(2):
        mine = (lane >= 64) if h else (lane < 64)
        inner = jnp.sum(jnp.where(mine, products, 0.0), axis=1, keepdims=True)
        grad_probs = mm_nt(jnp.where(mine, scaled, jnp.zeros_like(scaled)), values)
        grown = e_ref[h]
        grad_scores = (grown.astype(F32) * (grad_probs - inner) * scale).astype(BF16)
        dqs.append(mm(grad_scores, keys))
        dks.append(mm(q_t[64 * h : 64 * h + 64], grad_scores))
        dvs.append(mm(scaled_t[64 * h : 64 * h + 64], grown))
    dq_ref[...] = jnp.where(lane < 64, dqs[0], dqs[1]).astype(BF16)
    dk = jnp.concatenate(dks, axis=0).T.astype(BF16)
    dv = jnp.concatenate(dvs, axis=0).T.astype(BF16)
    dk0_ref[...] = dk[:rows]
    dk1_ref[...] = dk[rows:]
    dv0_ref[...] = dv[:rows]
    dv1_ref[...] = dv[rows:]


def attend_back_call(q, k0, k1, v0, v1, grown, grad_mixed, mixed, inverse, head):
    rows, width = q.shape
    pair = pl.BlockSpec((rows, 128), lambda p: (0, p))
    return pl.pallas_call(
        functools.partial(attend_back_kernel, head**-0.5),
        grid=(width // 128,),
        in_specs=[pair] * 5
        + [pl.BlockSpec((2, rows, 2 * rows), lambda p: (p, 0, 0))]
        + [pair] * 3,
        out_specs=[pair] * 5,
        out_shape=[jax.ShapeDtypeStruct((rows, width), BF16)] * 5,
        compiler_params=params(),
        name="attend_back",
    )(q, k0, k1, v0, v1, grown, grad_mixed, mixed, inverse)


def middle_kernel(
    mix_ref, x_ref, dy_ref, mod_ref, weight_ref, bias_ref, att_ref, mid_ref, h2_ref, h2t_ref, gf_ref
):
    width = x_ref.shape[1]
    attended = mm(mix_ref[...], weight_ref[...]) + bias_ref[...].astype(F32)
    middle = x_ref[...].astype(F32) + mod_ref[:, 2 * width : 3 * width] * attended
    normed = middle * lax.rsqrt(jnp.mean(middle * middle, axis=-1, keepdims=True) + NORM_EPSILON)
    hidden = normed * (1.0 + mod_ref[:, 4 * width : 5 * width]) + mod_ref[:, 3 * width : 4 * width]
    hidden = hidden.astype(BF16)
    att_ref[...] = attended.astype(BF16)
    mid_ref[...] = middle
    h2_ref[...] = hidden
    h2t_ref[...] = hidden.T
    gf_ref[...] = (mod_ref[:, 5 * width :] * dy_ref[...].astype(F32)).astype(BF16)


def middle_call(mixed, x, dy, mod, weight, bias):
    rows, width = x.shape
    block = rows // 2
    by_row = pl.BlockSpec((block, width), lambda i: (i, 0))
    low = jax.ShapeDtypeStruct((rows, width), BF16)
    return pl.pallas_call(
        middle_kernel,
        grid=(2,),
        in_specs=[by_row] * 3 + [full(mod.shape), full(weight.shape), full(bias.shape)],
        out_specs=[by_row] * 3 + [pl.BlockSpec((width, block), lambda i: (0, i)), by_row],
        out_shape=[low, jax.ShapeDtypeStruct((rows, width), F32), low]
        + [jax.ShapeDtypeStruct((width, rows), BF16), low],
        compiler_params=params(),
        name="middle",
    )(mixed, x, dy, mod, weight, bias)


def feed_kernel(
    h2_ref, h2t_ref, gf_ref, wg_ref, wu_ref, bg_ref, bu_ref, wd_ref, feed_in_ref, gh_in_ref,
    feed_ref, gh_ref, dd_ref, dg_ref, db_ref,
):
    @pl.when(pl.program_id(0) == 0)
    def _():
        feed_ref[...] = feed_in_ref[...]
        gh_ref[...] = gh_in_ref[...]

    hidden = h2_ref[...]
    grad_feed = gf_ref[...]
    gate = mm(hidden, wg_ref[...]) + bg_ref[...].astype(F32)
    up = mm(hidden, wu_ref[...]) + bu_ref[...].astype(F32)
    grad_product = mm_nt(grad_feed, wd_ref[...])
    sig = 1.0 / (1.0 + jnp.exp(-gate))
    active = gate * sig
    product = (active * up).astype(BF16)
    grad_gate = (grad_product * up * sig * (1.0 + gate * (1.0 - sig))).astype(BF16)
    grad_up = (grad_product * active).astype(BF16)
    dd_ref[...] = mm_tn(product, grad_feed).astype(BF16)
    dg_ref[0] = mm(h2t_ref[...], grad_gate).astype(BF16)
    dg_ref[1] = mm(h2t_ref[...], grad_up).astype(BF16)
    db_ref[0] = col_sum(grad_gate.astype(F32))
    db_ref[1] = col_sum(grad_up.astype(F32))
    feed_ref[...] += mm(product, wd_ref[...])
    gh_ref[...] += mm_nt(grad_gate, wg_ref[...]) + mm_nt(grad_up, wu_ref[...])


def feed_call(hidden, hidden_t, grad_feed, weight, bias, down, feed, grad_hidden, first, step, unit):
    rows, width = hidden.shape
    blocks = down.shape[0] // unit
    steps = len(range(first, blocks, step))
    pick = lambda s: first + step * s
    acc = jax.ShapeDtypeStruct((rows, width), F32)
    return pl.pallas_call(
        feed_kernel,
        grid=(steps,),
        in_specs=[
            full((rows, width)),
            full((width, rows)),
            full((rows, width)),
            pl.BlockSpec((width, unit), lambda s: (0, pick(s))),
            pl.BlockSpec((width, unit), lambda s: (0, blocks + pick(s))),
            pl.BlockSpec((1, unit), lambda s: (0, pick(s))),
            pl.BlockSpec((1, unit), lambda s: (0, blocks + pick(s))),
            pl.BlockSpec((unit, width), lambda s: (pick(s), 0)),
            full((rows, width)),
            full((rows, width)),
        ],
        out_specs=[
            full((rows, width)),
            full((rows, width)),
            pl.BlockSpec((None, unit, width), lambda s: (s, 0, 0)),
            pl.BlockSpec((None, 2, width, unit), lambda s: (s, 0, 0, 0)),
            pl.BlockSpec((None, 2, 1, unit), lambda s: (s, 0, 0, 0)),
        ],
        out_shape=[
            acc,
            acc,
            jax.ShapeDtypeStruct((steps, unit, width), BF16),
            jax.ShapeDtypeStruct((steps, 2, width, unit), BF16),
            jax.ShapeDtypeStruct((steps, 2, 1, unit), F32),
        ],
        compiler_params=params(),
        name="feed",
    )(hidden, hidden_t, grad_feed, weight, weight, bias, bias, down, feed, grad_hidden)


def turn_kernel(
    feed_ref, gh_ref, mid_ref, att_ref, dy_ref, gf_ref, mix_ref, mod_ref, weight_ref, dbias_ref,
    out_ref, gmid_ref, gmix_ref, dw_ref, sums_ref,
):
    width = mid_ref.shape[1]
    half = width // 2
    dy = dy_ref[...].astype(F32)
    feed = feed_ref[...] + dbias_ref[...].astype(F32)
    middle = mid_ref[...]
    out_ref[...] = (middle + mod_ref[:, 5 * width :] * feed).astype(BF16)
    factor = lax.rsqrt(jnp.mean(middle * middle, axis=-1, keepdims=True) + NORM_EPSILON)
    normed = middle * factor
    grad_hidden = gh_ref[...]
    product = grad_hidden * normed
    grad_normed = grad_hidden * (1.0 + mod_ref[:, 4 * width : 5 * width])
    back = factor * (
        grad_normed - normed * jnp.mean(grad_normed * normed, axis=-1, keepdims=True)
    )
    grad_middle = dy + back
    gmid_ref[...] = grad_middle
    grad_attended = (mod_ref[:, 2 * width : 3 * width] * grad_middle).astype(BF16)
    sums_ref[0:1, :] = col_sum(grad_middle * att_ref[...].astype(F32))
    sums_ref[1:2, :] = col_sum(grad_hidden)
    sums_ref[2:3, :] = col_sum(product)
    sums_ref[3:4, :] = col_sum(dy * feed)
    sums_ref[4:5, :] = col_sum(grad_attended.astype(F32))
    sums_ref[5:6, :] = col_sum(gf_ref[...].astype(F32))
    sums_ref[6:8, :] = jnp.zeros((2, width), F32)
    gmix_ref[...] = mm_nt(grad_attended, weight_ref[...]).astype(BF16)
    mixed_t = mix_ref[...].T
    dw_ref[0] = mm(mixed_t, grad_attended[:, :half]).astype(BF16)
    dw_ref[1] = mm(mixed_t, grad_attended[:, half:]).astype(BF16)


def turn_call(feed, grad_hidden, middle, attended, dy, grad_feed, mixed, mod, weight, down_bias):
    rows, width = middle.shape
    low = jax.ShapeDtypeStruct((rows, width), BF16)
    return pl.pallas_call(
        turn_kernel,
        out_shape=[
            low,
            jax.ShapeDtypeStruct((rows, width), F32),
            low,
            jax.ShapeDtypeStruct((2, width, width // 2), BF16),
            jax.ShapeDtypeStruct((8, width), F32),
        ],
        compiler_params=params(),
        name="turn",
    )(feed, grad_hidden, middle, attended, dy, grad_feed, mixed, mod, weight, down_bias)


def project_back_kernel(
    head, dq_ref, dk0_ref, dk1_ref, dv0_ref, dv1_ref, raw_ref, hid_ref, x_ref, gmid_ref, mod_ref,
    weight_ref, qgain_ref, kgain_ref, cos_ref, sin_ref,
    gx_ref, dw_ref, sums_ref, bias_ref, proj_ref,
):
    width = x_ref.shape[1]
    cosine, sine = cos_ref[...], -sin_ref[...]
    for part in range(3):
        span = slice(part * width, (part + 1) * width)
        if part == 2:
            grad = dv0_ref[...].astype(F32) + dv1_ref[...].astype(F32)
        else:
            grad = dq_ref[...].astype(F32)
            if part == 1:
                grad = dk0_ref[...].astype(F32) + dk1_ref[...].astype(F32)
            gain = (qgain_ref, kgain_ref)[part][...]
            raw = raw_ref[:, span].astype(F32)
            factor = lax.rsqrt(head_sum(raw * raw, head) * (1.0 / head) + NORM_EPSILON)
            normed = raw * factor
            turned = turn(grad, cosine, sine, head)
            sums_ref[2 + part : 3 + part, :] = col_sum(turned * normed)
            turned = turned * gain
            mean = head_sum(turned * normed, head) * (1.0 / head)
            grad = factor * (turned - normed * mean)
        low = grad.astype(BF16)
        proj_ref[:, span] = low
        bias_ref[:, span] = col_sum(low.astype(F32))
    hidden_t = hid_ref[...].T
    half = 3 * width // 2
    dw_ref[0] = mm(hidden_t, proj_ref[:, :half]).astype(BF16)
    dw_ref[1] = mm(hidden_t, proj_ref[:, half:]).astype(BF16)
    grad_hidden = mm_nt(proj_ref[...], weight_ref[...])
    x = x_ref[...].astype(F32)
    factor = lax.rsqrt(jnp.mean(x * x, axis=-1, keepdims=True) + NORM_EPSILON)
    normed = x * factor
    sums_ref[0:1, :] = col_sum(grad_hidden)
    sums_ref[1:2, :] = col_sum(grad_hidden * normed)
    sums_ref[4:8, :] = jnp.zeros((4, width), F32)
    grad_normed = grad_hidden * (1.0 + mod_ref[:, width : 2 * width])
    back = factor * (
        grad_normed - normed * jnp.mean(grad_normed * normed, axis=-1, keepdims=True)
    )
    gx_ref[...] = (gmid_ref[...] + back).astype(BF16)


def project_back_call(
    dq, dk0, dk1, dv0, dv1, raw, hidden, x, grad_middle, mod, weight, qgain, kgain, cosine, sine, head
):
    rows, width = x.shape
    return pl.pallas_call(
        functools.partial(project_back_kernel, head),
        out_shape=[
            jax.ShapeDtypeStruct((rows, width), BF16),
            jax.ShapeDtypeStruct((2, width, 3 * width // 2), BF16),
            jax.ShapeDtypeStruct((8, width), F32),
            jax.ShapeDtypeStruct((1, 3 * width), F32),
        ],
        scratch_shapes=[pltpu.VMEM((rows, 3 * width), BF16)],
        compiler_params=params(),
        name="project_back",
    )(dq, dk0, dk1, dv0, dv1, raw, hidden, x, grad_middle, mod, weight, qgain, kgain, cosine, sine)


class Place:
    def __init__(self):
        self.z, self.gy, self.gx = (lax.axis_index(name) for name in AXES)
        self.core = lax.rem(self.gx, 2)
        self.side = self.gx // 2
        self.chip = 2 * self.gy + self.side

    def flipped(self, k):
        return 2 * lax.rem(self.gy + k // 2, 2) + lax.rem(self.side + lax.rem(k, 2), 2)

    def pair(self):
        return {"gx": self.gx + 1 - 2 * self.core}

    def plane(self, k):
        device = {}
        if k & 2:
            device["gy"] = 1 - self.gy
        if k & 1:
            device["gx"] = lax.rem(self.gx + 2, 4)
        return device

    def depth(self, d):
        return {"batch": self.flipped_z(d)}

    def flipped_z(self, d):
        return {1: self.z + 1 - 2 * lax.rem(self.z, 2), 2: lax.rem(self.z + 2, 4), 3: 3 - self.z}[d]


def meet(devices):
    barrier = pltpu.get_barrier_semaphore()
    for device in devices:
        pl.semaphore_signal(barrier, inc=1, device_id=device, device_id_type=pl.DeviceIdType.MESH)
    pl.semaphore_wait(barrier, len(devices))


def send(source, target, send_sem, recv_sem, device):
    return pltpu.make_async_remote_copy(
        src_ref=source, dst_ref=target, send_sem=send_sem, recv_sem=recv_sem, device_id=device,
        device_id_type=pl.DeviceIdType.MESH,
    )


def feed_order(step):
    owner = jnp.where(
        step < 2, 3, jnp.where((step == 2) | (step == 5), 2, jnp.where(step < 5, 1, 0))
    )
    return owner, lax.rem(step, 2)


def feed_block(step, i):
    step = jnp.minimum(step, 7)
    owner, half = feed_order(step)
    return (2 * half + i) * 4 + Place().flipped(owner)


def feed_turn_kernel(
    h2_ref, h2t_ref, gf_ref, wg0, wg1, wu0, wu1, bg0, bg1, bu0, bu1, wd0, wd1,
    mid_ref, att_ref, dy_ref, mix_ref, mod_ref, weight_ref, dbias_ref,
    out_ref, gmid_ref, gmix_ref, dw_ref, sums_ref, total_ref,
    feed_ref, gh_ref, bias_ref, made, paired, near, pair_send, pair_recv, near_send, near_recv,
):
    place = Place()
    core = place.core
    step = pl.program_id(0)
    slot = lax.rem(step, 2)
    width = h2_ref.shape[1]
    unit = 128
    g_rows = width

    @pl.when(step == 0)
    def _():
        feed_ref[...] = jnp.zeros_like(feed_ref)
        sums_ref[1] = jnp.zeros((8, width), F32)
        gh_ref[...] = jnp.zeros_like(gh_ref)
        meet([place.pair(), place.plane(1), place.plane(2)])

    def pair_copy(of):
        return send(
            made.at[lax.rem(of, 2), 1 - core], paired.at[of], pair_send.at[lax.rem(of, 2)],
            pair_recv.at[of], place.pair(),
        )

    def near_copy(of, k):
        return send(paired.at[of], near.at[of], near_send.at[of], near_recv.at[of], place.plane(k))

    @pl.when(step >= 1)
    def _():
        pair_copy(step - 1).start()

    @pl.when(step < 8)
    def _():
        owner, half = feed_order(step)
        hidden = h2_ref[...]
        grad_feed = gf_ref[...]
        wg = jnp.concatenate([wg0[...], wg1[...]], axis=1)
        wu = jnp.concatenate([wu0[...], wu1[...]], axis=1)
        wd = jnp.concatenate([wd0[...], wd1[...]], axis=0)
        gate = mm(hidden, wg) + jnp.concatenate([bg0[...], bg1[...]], axis=1).astype(F32)
        up = mm(hidden, wu) + jnp.concatenate([bu0[...], bu1[...]], axis=1).astype(F32)
        grad_product = mm_nt(grad_feed, wd)
        sig = 1.0 / (1.0 + jnp.exp(-gate))
        active = gate * sig
        product = (active * up).astype(BF16)
        grad_gate = (grad_product * up * sig * (1.0 + gate * (1.0 - sig))).astype(BF16)
        grad_up = (grad_product * active).astype(BF16)
        feed_ref[...] += mm(product, wd)
        gh_ref[...] += mm_nt(grad_gate, wg) + mm_nt(grad_up, wu)
        for e, grad in enumerate((grad_gate, grad_up)):
            total = col_sum(grad.astype(F32))
            for i in range(2):
                row = 16 * e + (2 * half + i) * 4 + place.flipped(owner)
                bias_ref[pl.ds(row, 1), :] = total[:, i * unit : (i + 1) * unit]

        @pl.when(step >= 2)
        def _():
            pair_copy(step - 2).wait_send()

        for e, grad in enumerate((grad_gate, grad_up)):
            made[slot, e, :g_rows] = mm(h2t_ref[...], grad).astype(BF16)
        product_t = product.T
        for b in range(3):
            d = mm(product_t, grad_feed[:, 256 * b : 256 * b + 256]).astype(BF16)
            for i in range(2):
                for c in range(2):
                    made[slot, c, pl.ds(g_rows + b * 128 + i * 64, 64)] = d[
                        i * 128 + c * 64 : i * 128 + c * 64 + 64
                    ]

    @pl.when(step >= 1)
    def _():
        of = step - 1
        copy = pair_copy(of)
        copy.wait_recv()
        late = (of == 4) | (of == 5)

        @pl.when(jnp.logical_not(late))
        def _():
            paired[of] = (made[1 - slot, core].astype(F32) + paired[of].astype(F32)).astype(BF16)

        @pl.when(late)
        def _():
            near_copy(of - 4, 1).wait_recv()
            paired[of] = (
                made[1 - slot, core].astype(F32)
                + paired[of].astype(F32)
                + near[of - 4].astype(F32)
            ).astype(BF16)

        @pl.when((of == 0) | (of == 2) | (of == 5))
        def _():
            near_copy(of, 2).start()

        @pl.when((of == 1) | (of == 3) | (of == 4))
        def _():
            near_copy(of, 1).start()

    @pl.when(step == 8)
    def _():
        half = width // 2
        dy = dy_ref[...].astype(F32)
        feed = feed_ref[...] + dbias_ref[...].astype(F32)
        middle = mid_ref[...]
        out_ref[...] = (middle + mod_ref[:, 5 * width :] * feed).astype(BF16)
        factor = lax.rsqrt(jnp.mean(middle * middle, axis=-1, keepdims=True) + NORM_EPSILON)
        normed = middle * factor
        grad_hidden = gh_ref[...]
        product = grad_hidden * normed
        grad_normed = grad_hidden * (1.0 + mod_ref[:, 4 * width : 5 * width])
        back = factor * (
            grad_normed - normed * jnp.mean(grad_normed * normed, axis=-1, keepdims=True)
        )
        grad_middle = dy + back
        gmid_ref[...] = grad_middle
        grad_attended = (mod_ref[:, 2 * width : 3 * width] * grad_middle).astype(BF16)
        sums_ref[0, 0:1, :] = col_sum(grad_middle * att_ref[...].astype(F32))
        sums_ref[0, 1:2, :] = col_sum(grad_hidden)
        sums_ref[0, 2:3, :] = col_sum(product)
        sums_ref[0, 3:4, :] = col_sum(dy * feed)
        sums_ref[0, 4:5, :] = col_sum(grad_attended.astype(F32))
        sums_ref[0, 5:6, :] = col_sum(gf_ref[...].astype(F32))
        sums_ref[0, 6:8, :] = jnp.zeros((2, width), F32)
        for row in range(32):
            col = (row % 6) * unit
            sums_ref[1, row // 6 : row // 6 + 1, col : col + unit] = bias_ref[row : row + 1, :]
        gmix_ref[...] = mm_nt(grad_attended, weight_ref[...]).astype(BF16)
        mixed_t = mix_ref[...].T
        dw_ref[0] = mm(mixed_t, grad_attended[:, :half]).astype(BF16)
        dw_ref[1] = mm(mixed_t, grad_attended[:, half:]).astype(BF16)
        for of in (6, 7):
            pair_copy(of).wait_send()
        for of in (2, 3, 4, 5):
            near_copy(of, 1).wait_recv()
        for of in range(6):
            near_copy(of, 1).wait_send()
        rows = width // 4
        for f in range(2):
            for z in range(4):
                span = slice(z * rows, (z + 1) * rows)
                total_ref[z, f] = sum(
                    part.astype(F32)
                    for part in (paired[6 + f, span], near[2 + f, span], near[4 + f, span])
                ).astype(BF16)
            for i in range(2):
                for b in range(3):
                    span = slice(g_rows + b * 128 + i * 64, g_rows + b * 128 + i * 64 + 64)
                    total_ref[2 * f + i, 2, b * 64 : b * 64 + 64] = sum(
                        part.astype(F32)
                        for part in (paired[6 + f, span], near[2 + f, span], near[4 + f, span])
                    ).astype(BF16)


def once(shape):
    return pl.BlockSpec(shape, lambda *_: (0,) * len(shape), pipeline_mode=pl.Buffered(1))


def feed_turn_call(
    hidden, hidden_t, grad_feed, gate_up, gate_up_bias, down, middle, attended, dy, mixed, mod,
    weight, down_bias,
):
    rows, width = hidden.shape
    low = jax.ShapeDtypeStruct((rows, width), BF16)
    wide = jax.ShapeDtypeStruct((rows, width), F32)
    cols = lambda i, e: pl.BlockSpec((width, 128), lambda s: (0, 16 * e + feed_block(s, i)))
    bias = lambda i, e: pl.BlockSpec((1, 128), lambda s: (0, 16 * e + feed_block(s, i)))
    deep = lambda i: pl.BlockSpec((128, width), lambda s: (feed_block(s, i), 0))
    piece = (width + 384, 256)
    out_shape = [
        low, wide, low,
        jax.ShapeDtypeStruct((2, width, width // 2), BF16),
        jax.ShapeDtypeStruct((2, 8, width), F32),
        jax.ShapeDtypeStruct((4, 3, width // 4, 256), BF16),
    ]
    return pl.pallas_call(
        feed_turn_kernel,
        grid=(9,),
        in_specs=[once((rows, width)), once((width, rows)), once((rows, width))]
        + [cols(0, 0), cols(1, 0), cols(0, 1), cols(1, 1)]
        + [bias(0, 0), bias(1, 0), bias(0, 1), bias(1, 1)]
        + [deep(0), deep(1)]
        + [once((rows, width))] * 4
        + [once(mod.shape), once(weight.shape), once(down_bias.shape)],
        out_specs=[full(shape.shape) for shape in out_shape],
        out_shape=out_shape,
        scratch_shapes=[
            pltpu.VMEM((rows, width), F32),
            pltpu.VMEM((rows, width), F32),
            pltpu.VMEM((32, 128), F32),
            pltpu.VMEM((2, 2) + piece, BF16),
            pltpu.VMEM((8,) + piece, BF16),
            pltpu.VMEM((6,) + piece, BF16),
            pltpu.SemaphoreType.DMA((2,)),
            pltpu.SemaphoreType.DMA((8,)),
            pltpu.SemaphoreType.DMA((6,)),
            pltpu.SemaphoreType.DMA((6,)),
        ],
        compiler_params=pltpu.CompilerParams(
            vmem_limit_bytes=VMEM_LIMIT, collective_id=1, has_side_effects=True
        ),
        name="feed_turn",
    )(
        hidden, hidden_t, grad_feed, gate_up, gate_up, gate_up, gate_up, gate_up_bias,
        gate_up_bias, gate_up_bias, gate_up_bias, down, down, middle, attended, dy, mixed, mod,
        weight, down_bias,
    )


Z_FIRST = (False, False, False, False)
GROUPS = 4


def back_kernel(
    head, q_ref, k0_ref, k1_ref, v0_ref, v1_ref, gm_ref, mix_ref, rl_ref, e_ref,
    mod_ref, qgain_ref, kgain_ref, cos_ref, sin_ref, dout_ref, totals_ref, early_ref,
    raw_hbm, hid_hbm, x_hbm, gmid_hbm, weight_hbm, rows_hbm,
    output_ref, gtok_ref, feeds_hbm, projs_hbm, early_hbm, late_hbm,
    feeds_ref, projs_ref, early_all, late_all, raw_ref, hid_ref, x_ref, gmid_ref, weight_ref, hidt_ref, gh_ref, gx_ref, late_ref,
    dq_s, dk0_s, dv0_s, dk1_s, dv1_s, dk_in, dv_in,
    made, paired, first_out, first_in, second_out, second_in, z_in, early_in, late_in,
    load_sem, own_sem, kv_send, kv_recv, pair_send, pair_recv, first_send, first_recv,
    second_send, second_recv, z_send, z_recv, tok_send, tok_recv, feed_send, feed_recv,
    proj_send, proj_recv, small_send, small_recv,
):
    place = Place()
    core, chip, z = place.core, place.chip, place.z
    step = pl.program_id(0)
    rows, width = x_ref.shape
    cells = rows // 4
    scale = head**-0.5
    lane = lax.broadcasted_iota(jnp.int32, (1, 128), 1)

    loads = [
        pltpu.make_async_copy(source, target, load_sem.at[i])
        for i, (source, target) in enumerate(
            (
                (hid_hbm, hid_ref), (raw_hbm, raw_ref), (weight_hbm, weight_ref),
                (x_hbm, x_ref), (gmid_hbm, gmid_ref),
            )
        )
    ]

    stores = [
        pltpu.make_async_copy(source, target, load_sem.at[5 + i])
        for i, (source, target) in enumerate(
            (
                (early_all, early_hbm), (late_all, late_hbm), (feeds_ref, feeds_hbm),
                (projs_ref, projs_hbm),
            )
        )
    ]

    def z_copy(d):
        return send(
            totals_ref.at[place.flipped_z(d)], z_in.at[d - 1], z_send.at[d - 1], z_recv.at[d - 1],
            place.depth(d),
        )

    def token_copy(which, k):
        source, target = ((rows_hbm, output_ref), (gx_ref, gtok_ref))[which]
        return send(
            source.at[pl.ds(k * cells, cells)], target.at[chip], tok_send.at[which, k - 1],
            tok_recv.at[which, k - 1], place.plane(k),
        )

    def own_tokens(which):
        source, target = ((rows_hbm, output_ref), (gx_ref, gtok_ref))[which]
        return pltpu.make_async_copy(source.at[pl.ds(0, cells)], target.at[chip], own_sem.at[which])

    def kv_copy(which, p):
        source, target = ((dk1_s, dk_in), (dv1_s, dv_in))[which]
        return send(
            source.at[p], target.at[p], kv_send.at[which, p], kv_recv.at[which, p], place.pair()
        )

    def pair_copy(g):
        source = dout_ref.at[1 - core] if g == 3 else made.at[g % 2, 1 - core]
        return send(source, paired.at[g], pair_send.at[g], pair_recv.at[g], place.pair())

    def first_copy(g, k):
        other = place.flipped_z(k) if Z_FIRST[g] else place.flipped(k)
        device = place.depth(k) if Z_FIRST[g] else place.plane(k)
        return send(
            first_out.at[g, other], first_in.at[g, k - 1], first_send.at[g, k - 1],
            first_recv.at[g, k - 1], device,
        )

    def second_copy(g, k):
        other = place.flipped(k) if Z_FIRST[g] else place.flipped_z(k)
        device = place.plane(k) if Z_FIRST[g] else place.depth(k)
        return send(
            second_out.at[g, other], second_in.at[g, k - 1], second_send.at[g, k - 1],
            second_recv.at[g, k - 1], device,
        )

    def feed_copy(k):
        here = feeds_ref.at[core, chip]
        return send(here, here, feed_send.at[k - 1], feed_recv.at[k - 1], place.plane(k))

    def feed_pair():
        here = feeds_ref.at[core]
        return send(here, here, feed_send.at[3], feed_recv.at[3], place.pair())

    def proj_copy(k):
        here = projs_ref.at[core, chip]
        return send(here, here, proj_send.at[k - 1], proj_recv.at[k - 1], place.plane(k))

    def proj_pair():
        here = projs_ref.at[core]
        return send(here, here, proj_send.at[3], proj_recv.at[3], place.pair())

    smalls = ((early_ref, early_in, early_all, 8), (late_ref, late_in, late_all, 4))
    hops = [place.plane(1), place.plane(2), place.depth(1), place.depth(2)]

    def small_pair(which):
        source, target, _, count = smalls[which]
        return send(
            source.at[1 - core], target, small_send.at[which, 0], small_recv.at[which, 0],
            place.pair(),
        )

    def small_hop(which, i):
        _, _, full_ref, _ = smalls[which]
        have = 1 << i
        return send(
            full_ref.at[core, pl.ds(0, have)], full_ref.at[core, pl.ds(have, have)],
            small_send.at[which, 1 + i], small_recv.at[which, 1 + i], hops[i],
        )

    def small_last(which):
        here = smalls[which][2].at[core]
        return send(
            here, here, small_send.at[which, 5], small_recv.at[which, 5], place.pair()
        )

    def small_begin(which):
        source, target, full_ref, _ = smalls[which]
        small_pair(which).wait_recv()
        full_ref[core, 0] = source[core] + target[...]
        small_hop(which, 0).start()

    def small_next(which, i):
        small_hop(which, i).wait_recv()
        (small_hop(which, i + 1) if i < 3 else small_last(which)).start()

    def start_group(g):
        pair_copy(g).wait_recv()
        mine = dout_ref.at[core] if g == 3 else made.at[g % 2, core]
        part = width // 16
        for a in range(4):
            for b in range(4):
                span = pl.ds((a * 4 + b) * part, part)
                total = (mine[span, :].astype(F32) + paired[g, span].astype(F32)).astype(BF16)
                if Z_FIRST[g]:
                    first_out[g, a, b] = total
                else:
                    first_out[g, b, a] = total
        for k in (1, 2, 3):
            first_copy(g, k).start()

    def go_on(g):
        for k in (1, 2, 3):
            first_copy(g, k).wait_recv()
        here = z if Z_FIRST[g] else chip
        second_out[g] = (
            first_out[g, here].astype(F32)
            + first_in[g, 0].astype(F32)
            + first_in[g, 1].astype(F32)
            + first_in[g, 2].astype(F32)
        ).astype(BF16)
        for k in (1, 2, 3):
            second_copy(g, k).start()

    def finish(g):
        for k in (1, 2, 3):
            second_copy(g, k).wait_recv()
        here = chip if Z_FIRST[g] else z
        projs_ref[core, chip, g] = (
            second_out[g, here].astype(F32)
            + second_in[g, 0].astype(F32)
            + second_in[g, 1].astype(F32)
            + second_in[g, 2].astype(F32)
        ).astype(BF16)

    @pl.when(step == 0)
    def _():
        for load in loads:
            load.start()
        meet(
            [place.pair()]
            + [place.plane(k) for k in (1, 2, 3)]
            + [place.depth(d) for d in (1, 2, 3)]
        )
        pair_copy(3).start()
        small_pair(0).start()
        for d in (1, 2, 3):
            z_copy(d).start()
        for k in (1, 2, 3):
            token_copy(0, k).start()
        own_tokens(0).start()
        gh_ref[...] = jnp.zeros_like(gh_ref)

    @pl.when(step >= 1)
    def _():
        for which in (0, 1):
            kv_copy(which, step - 1).start()

    @pl.when(step == 3)
    def _():
        pair_copy(0).start()

    @pl.when(step == 5)
    def _():
        pair_copy(1).start()

    @pl.when(step < 6)
    def _():
        keys = jnp.concatenate([k0_ref[...], k1_ref[...]], axis=0)
        values = jnp.concatenate([v0_ref[...], v1_ref[...]], axis=0)
        scaled = gm_ref[...].astype(F32) * rl_ref[...]
        products = scaled * mix_ref[...].astype(F32)
        scaled = scaled.astype(BF16)
        q_t = q_ref[...].T
        scaled_t = scaled.T
        dqs, dks, dvs = [], [], []
        for h in range(2):
            mine = (lane >= 64) if h else (lane < 64)
            inner = jnp.sum(jnp.where(mine, products, 0.0), axis=1, keepdims=True)
            grad_probs = mm_nt(jnp.where(mine, scaled, jnp.zeros_like(scaled)), values)
            grown = e_ref[h]
            grad_scores = (grown.astype(F32) * (grad_probs - inner) * scale).astype(BF16)
            dqs.append(mm(grad_scores, keys))
            dks.append(mm(q_t[64 * h : 64 * h + 64], grad_scores))
            dvs.append(mm(scaled_t[64 * h : 64 * h + 64], grown))
        dq_s[step] = jnp.where(lane < 64, dqs[0], dqs[1]).astype(BF16)
        dk = jnp.concatenate(dks, axis=0).T.astype(BF16)
        dv = jnp.concatenate(dvs, axis=0).T.astype(BF16)
        dk0_s[step] = dk[:rows]
        dk1_s[step] = dk[rows:]
        dv0_s[step] = dv[:rows]
        dv1_s[step] = dv[rows:]

    @pl.when(step == 0)
    def _():
        loads[0].wait()
        hidt_ref[...] = hid_ref[...].T

    @pl.when(step == 1)
    def _():
        loads[1].wait()
        loads[2].wait()
        start_group(3)
        small_begin(0)

    for i in range(4):

        @pl.when(step == 2 + i)
        def _(i=i):
            small_next(0, i)

    @pl.when(step == 3)
    def _():
        start_group(0)

    @pl.when(step == 5)
    def _():
        start_group(1)
        go_on(3)

    @pl.when(step == 6)
    def _():
        for d in (1, 2, 3):
            z_copy(d).wait_recv()
        for i in range(3):
            feeds_ref[core, chip, i] = (
                totals_ref[z, i].astype(F32)
                + z_in[0, i].astype(F32)
                + z_in[1, i].astype(F32)
                + z_in[2, i].astype(F32)
            ).astype(BF16)
        for k in (1, 2, 3):
            feed_copy(k).start()

    @pl.when((step >= 2) & (lax.rem(step, 2) == 0))
    def _():
        g = (step - 2) // 2
        slot = lax.rem(g, 2)
        cosine, sine = cos_ref[...], -sin_ref[...]
        for i in range(2):
            for which in (0, 1):
                kv_copy(which, 2 * g + i).wait_recv()

        def both(ref):
            return jnp.concatenate([ref[2 * g], ref[2 * g + 1]], axis=1).astype(F32)

        lows = []
        for part in range(3):
            span = pl.ds(pl.multiple_of(part * width + g * 256, 256), 256)
            if part == 2:
                grad = both(dv0_s) + both(dv_in)
            else:
                grad = both(dq_s) if part == 0 else both(dk0_s) + both(dk_in)
                gain = (qgain_ref, kgain_ref)[part][:, :256]
                raw = raw_ref[:, span].astype(F32)
                factor = lax.rsqrt(head_sum(raw * raw, head) * (1.0 / head) + NORM_EPSILON)
                normed = raw * factor
                turned = turn(grad, cosine, sine, head)
                late_ref[1, part : part + 1, pl.ds(pl.multiple_of(g * 256, 256), 256)] = col_sum(
                    turned * normed
                )
                turned = turned * gain
                mean = head_sum(turned * normed, head) * (1.0 / head)
                grad = factor * (turned - normed * mean)
            low = grad.astype(BF16)
            lows.append(low)
            total = col_sum(low.astype(F32))
            where = pl.ds(pl.multiple_of(g * 256, 256), 256)
            if part < 2:
                late_ref[0, 2 + part : 3 + part, where] = total
            else:
                late_ref[1, 2:3, where] = total
            gh_ref[...] += mm_nt(low, weight_ref[:, span])
        grads = jnp.concatenate(
            [low[:, 128 * c : 128 * c + 128] for c in range(2) for low in lows], axis=1
        )

        @pl.when(step == 6)
        def _():
            pair_copy(0).wait_send()

        half = width // 2
        made[slot, 0] = mm(hidt_ref[...], grads[:, :half]).astype(BF16)
        made[slot, 1] = mm(hidt_ref[...], grads[:, half:]).astype(BF16)

    @pl.when(step == 6)
    def _():
        pair_copy(2).start()
        go_on(0)
        go_on(1)
        loads[3].wait()
        loads[4].wait()
        grad_hidden = gh_ref[...]
        x = x_ref[...].astype(F32)
        factor = lax.rsqrt(jnp.mean(x * x, axis=-1, keepdims=True) + NORM_EPSILON)
        normed = x * factor
        late_ref[0, 0:1, :] = col_sum(grad_hidden)
        late_ref[0, 1:2, :] = col_sum(grad_hidden * normed)
        late_ref[1, 3:4, :] = jnp.zeros((1, width), F32)
        grad_normed = grad_hidden * (1.0 + mod_ref[:, width : 2 * width])
        back = factor * (
            grad_normed - normed * jnp.mean(grad_normed * normed, axis=-1, keepdims=True)
        )
        small_pair(1).start()
        start_group(2)
        gx_ref[...] = (gmid_ref[...] + back).astype(BF16)
        small_begin(1)
        for k in (1, 2, 3):
            token_copy(1, k).start()
        own_tokens(1).start()
        finish(3)
        small_next(1, 0)
        finish(0)
        finish(1)
        small_next(1, 1)
        go_on(2)
        small_next(1, 2)
        for k in (1, 2, 3):
            feed_copy(k).wait_recv()
        for k in (1, 2, 3):
            feed_copy(k).wait_send()
        feed_pair().start()
        finish(2)
        for k in (1, 2, 3):
            proj_copy(k).start()
        small_next(1, 3)
        for k in (1, 2, 3):
            proj_copy(k).wait()
        proj_pair().start()
        for which in (0, 1):
            own_tokens(which).wait()
            for k in (1, 2, 3):
                token_copy(which, k).wait()
            small_pair(which).wait_send()
            for i in range(4):
                small_hop(which, i).wait_send()
            small_last(which).wait()
            stores[which].start()
            for p in range(6):
                kv_copy(which, p).wait_send()
        for k in (1, 2, 3):
            z_copy(k).wait_send()
            for g in range(4):
                first_copy(g, k).wait_send()
                second_copy(g, k).wait_send()
        for g in (1, 2, 3):
            pair_copy(g).wait_send()
        feed_pair().wait()
        stores[2].start()
        proj_pair().wait()
        stores[3].start()
        for store in stores:
            store.wait()


def back_call(
    q, k0, k1, v0, v1, grad_mixed, mixed, inverse, grown, mod, qgain, kgain, cosine, sine, d_out,
    totals, early, raw, hidden, x, grad_middle, weight, output_rows, head,
):
    rows, width = q.shape
    half, part = width // 2, width // 16
    low = lambda *shape: jax.ShapeDtypeStruct(shape, BF16)
    pair = pl.BlockSpec((rows, 128), lambda s: (0, jnp.minimum(s, 5)))
    anywhere = pl.BlockSpec(memory_space=pl.ANY)
    small = [mod, qgain, kgain, cosine, sine, d_out, totals, early]
    out_shape = [
        low(4, rows // 4, width), low(4, rows // 4, width),
        low(2, 4, 3, width // 4, 256), low(2, 4, GROUPS, part, half),
        jax.ShapeDtypeStruct((2, 16, 8, width), F32), jax.ShapeDtypeStruct((2, 16, 4, width), F32),
    ]
    vmem = lambda *shape: pltpu.VMEM(shape, BF16)
    sems = lambda *shape: pltpu.SemaphoreType.DMA(shape)
    return pl.pallas_call(
        functools.partial(back_kernel, head),
        grid=(7,),
        in_specs=[pair] * 8
        + [pl.BlockSpec((2, rows, 2 * rows), lambda s: (jnp.minimum(s, 5), 0, 0))]
        + [once(each.shape) for each in small]
        + [anywhere] * 6,
        out_specs=[anywhere] * 6,
        out_shape=out_shape,
        scratch_shapes=[pltpu.VMEM(shape.shape, shape.dtype) for shape in out_shape[2:]]
        + [
            vmem(rows, 2 * width), vmem(rows, width), vmem(rows, width),
            pltpu.VMEM((rows, width), F32), vmem(width, 3 * width), vmem(width, rows),
            pltpu.VMEM((rows, width), F32), vmem(rows, width), pltpu.VMEM((2, 4, width), F32),
        ]
        + [vmem(6, rows, 128)] * 7
        + [
            vmem(2, 2, width, half), vmem(GROUPS, width, half),
            vmem(GROUPS, 4, 4, part, half), vmem(GROUPS, 3, 4, part, half),
            vmem(GROUPS, 4, part, half), vmem(GROUPS, 3, part, half),
            vmem(3, 3, width // 4, 256),
            pltpu.VMEM((8, width), F32), pltpu.VMEM((4, width), F32),
            sems(9), sems(2), sems(2, 6), sems(2, 6), sems(GROUPS), sems(GROUPS),
            sems(GROUPS, 3), sems(GROUPS, 3), sems(GROUPS, 3), sems(GROUPS, 3),
            sems(3), sems(3), sems(2, 3), sems(2, 3), sems(4), sems(4), sems(4), sems(4),
            sems(2, 6), sems(2, 6),
        ],
        compiler_params=pltpu.CompilerParams(
            vmem_limit_bytes=VMEM_LIMIT, collective_id=2, has_side_effects=True
        ),
        name="back",
    )(
        q, k0, k1, v0, v1, grad_mixed, mixed, inverse, grown, *small, raw, hidden, x, grad_middle,
        weight, output_rows,
    )


def take(array_in, index, axis=0):
    return lax.dynamic_index_in_dim(array_in, index, axis, keepdims=False)


def add(*terms):
    return sum(term.astype(F32) for term in terms)


class Moves:
    def __init__(self, mesh):
        self.sizes = tuple(mesh.shape[name] for name in AXES)

    def flip(self, value, batch=0, gy=0, gx=0):
        nb, ny, nx = self.sizes
        pairs = []
        for b in range(nb):
            for y in range(ny):
                for x in range(nx):
                    here = (b * ny + y) * nx + x
                    there = ((b ^ batch) * ny + (y ^ gy)) * nx + (x ^ gx)
                    pairs.append((here, there))
        return lax.ppermute(value, AXES, pairs)

    def plane(self, value, k):
        return self.flip(value, gy=k >> 1, gx=2 * (k & 1))

    def pair(self, value):
        return self.flip(value, gx=1)

    def gather(self, value):
        value = value[None]
        value = jnp.concatenate([value, self.plane(value, 1)], axis=0)
        value = jnp.concatenate([value, self.plane(value, 2)], axis=0)
        bit = 1
        while bit < self.sizes[0]:
            value = jnp.concatenate([value, self.flip(value, batch=bit)], axis=0)
            bit *= 2
        return value


def regroup(parts, place):
    stacked = jnp.stack(parts)
    return jnp.stack([take(stacked, place ^ k) for k in range(len(parts))])


def body(mesh, *operands):
    (
        tokens, timesteps, labels, class_table, modulate_weight, modulate_bias, inproj_weight,
        inproj_bias, query_gain, key_gain, outproj_weight, outproj_bias, gate_up_weight,
        gate_up_bias, down_weight, down_bias, cotangent,
    ) = operands
    image_count, tile_rows, tile_cols, width = tokens.shape
    cells = tile_rows * tile_cols
    rows = image_count * cells
    head = query_gain.shape[0]
    heads = width // head
    hidden_width = down_weight.shape[0]
    class_count = class_table.shape[0]
    highest = lax.Precision.HIGHEST
    moves = Moves(mesh)
    nb, ny, nx = moves.sizes
    assert ny == 2 and nx == 4 and image_count == 4
    z, gy, gx = (lax.axis_index(name) for name in AXES)
    side, core = gx // 2, gx % 2
    place = 2 * gy + side

    tiles = tokens.reshape(image_count, cells, width)
    grads = cotangent.reshape(image_count, cells, width)

    def exchange(blocks):
        return [take(blocks, place)] + [
            moves.plane(take(blocks, place ^ k), k) for k in range(1, 4)
        ]

    x = jnp.concatenate(exchange(tiles), axis=0)

    half_width = width // 2
    step = take(timesteps, place).astype(F32)
    label = take(labels, place)
    rates = jnp.exp(-math.log(10000.0) * jnp.arange(half_width, dtype=F32) / half_width)
    features = jnp.concatenate([jnp.cos(step * rates), jnp.sin(step * rates)])
    condition = features + take(class_table, label).astype(F32)
    cond_act = jax.nn.silu(condition).astype(BF16)
    mod = modulation_call(
        jnp.broadcast_to(cond_act[None], (16, width)), modulate_weight, modulate_bias[None]
    )[:1]

    quarter = head // 4
    cell = jnp.arange(cells, dtype=jnp.int32)
    row_places, col_places = [], []
    for k in range(4):
        there = place ^ k
        row_places.append((there // 2) * tile_rows + cell // tile_cols)
        col_places.append((2 * (there % 2) + core) * tile_cols + cell % tile_cols)
    row_places = jnp.concatenate(row_places).astype(F32)[:, None]
    col_places = jnp.concatenate(col_places).astype(F32)[:, None]
    lane = jnp.arange(128, dtype=jnp.int32)
    turn_rate = jnp.exp(-math.log(10000.0) * (lane % quarter).astype(F32) / quarter)[None]
    angles = jnp.where((lane % head)[None] < head // 2, row_places, col_places) * turn_rate
    cosine = jnp.cos(angles)
    sine = jnp.where((lane % (2 * quarter))[None] < quarter, -1.0, 1.0) * jnp.sin(angles)
    qgain = jnp.tile(query_gain.astype(F32), heads)[None]
    kgain = jnp.tile(key_gain.astype(F32), heads)[None]

    hidden_one, q, k0, v0, raw = project_call(
        x, mod, inproj_weight, inproj_bias[None], qgain, kgain, cosine, sine, head
    )
    k1, v1 = moves.pair(k0), moves.pair(v0)
    dy = jnp.concatenate(exchange(grads), axis=0)
    mixed, grown, inverse = attend_call(q, k0, k1, v0, v1, head)
    attended, middle, hidden_two, hidden_two_t, grad_feed = middle_call(
        mixed, x, dy, mod, outproj_weight, outproj_bias[None]
    )

    unit = 256
    blocks = hidden_width // unit
    quick = nb == 4 and hidden_width == 16 * 128
    if quick:
        output_rows, grad_middle, grad_mixed, d_out, sums_two, totals = feed_turn_call(
            hidden_two, hidden_two_t, grad_feed, gate_up_weight, gate_up_bias[None], down_weight,
            middle, attended, dy, mixed, mod, outproj_weight, down_bias[None],
        )
        output, grad_tokens, feeds, projs, early, late = back_call(
            q, k0, k1, v0, v1, grad_mixed, mixed, inverse, grown, mod, qgain, kgain, cosine, sine,
            d_out, totals, sums_two, raw, hidden_one, x, grad_middle, inproj_weight, output_rows,
            head,
        )
        output = output.reshape(tokens.shape)
        grad_tokens = grad_tokens.reshape(tokens.shape)
        slice_rows = width // nb
        gates = feeds[:, :, :2].reshape(2, 4, 2, slice_rows, 2, 128).transpose(3, 0, 2, 4, 1, 5)
        grad_gu_w = gates.reshape(slice_rows, 2 * hidden_width).astype(F32)
        downs = feeds[:, :, 2].reshape(2, 4, 3, 64, 256).transpose(1, 0, 3, 2, 4)
        grad_down_w = downs.reshape(hidden_width // nb, width).astype(F32)
        part = width // 16
        ins = projs[:, :, :3].reshape(2, 4, 3, part, 3, 128).transpose(1, 3, 4, 2, 0, 5)
        grad_in_w = ins.reshape(slice_rows, 3 * width).astype(F32)
        outs = projs[:, :, 3].transpose(1, 2, 0, 3)
        grad_out_w = outs.reshape(slice_rows, width).astype(F32)
        count = early.shape[1]
        early = jnp.concatenate(
            [early[0, :, :6].reshape(count, -1), early[1].reshape(count, -1)[:, : 2 * hidden_width]],
            axis=1,
        )
        gain_sums = late[1, :, :2].reshape(count, 2, heads, head).sum(axis=2)
        late = jnp.concatenate(
            [
                late[0].reshape(count, -1), late[1, :, 2], gain_sums.reshape(count, -1),
            ],
            axis=1,
        )
    else:
        feed, grad_hidden, d_down, d_gate, d_bias = feed_call(
            hidden_two, hidden_two_t, grad_feed, gate_up_weight, gate_up_bias[None], down_weight,
            jnp.zeros((rows, width), F32), jnp.zeros((rows, width), F32), 0, 1, unit,
        )
        output_rows, grad_middle, grad_mixed, d_out, sums_two = turn_call(
            feed, grad_hidden, middle, attended, dy, grad_feed, mixed, mod, outproj_weight,
            down_bias[None],
        )
        gate_bias = d_bias.reshape(blocks, 2, unit).transpose(1, 0, 2)
        dq, dk0, dk1, dv0, dv1 = attend_back_call(
            q, k0, k1, v0, v1, grown, grad_mixed, mixed, inverse, head
        )
        dk1, dv1 = moves.pair(dk1), moves.pair(dv1)
        grad_x, d_in, sums_one, in_bias = project_back_call(
            dq, dk0, dk1, dv0, dv1, raw, hidden_one, x, grad_middle, mod, inproj_weight, qgain,
            kgain, cosine, sine, head,
        )

        def give_back(rows_out):
            parts = rows_out.reshape(4, cells, width)
            got = [parts[0]] + [moves.plane(parts[k], k) for k in range(1, 4)]
            return regroup(got, place).reshape(tokens.shape)

        output = give_back(output_rows)
        grad_tokens = give_back(grad_x)
        slice_rows = width // nb

        def scatter(d):
            d = lax.psum_scatter(d.astype(BF16), "batch", scatter_dimension=0, tiled=True)
            return lax.psum(d, ("gy", "gx")).astype(F32)

        def joined(d):
            return jnp.concatenate([d[0], d[1]], axis=1)

        grad_down_w = scatter(d_down.reshape(hidden_width, width))
        grad_gu_w = scatter(
            d_gate.transpose(2, 1, 0, 3).reshape(width, 2 * hidden_width)
        )
        grad_out_w = scatter(joined(d_out))
        grad_in_w = scatter(joined(d_in))
        gain_sums = sums_one[2:4].reshape(2, heads, head).sum(axis=1)
        early = jnp.concatenate([sums_two[:6].reshape(-1), gate_bias.reshape(-1)])
        late = jnp.concatenate(
            [sums_one[:2].reshape(-1), in_bias.reshape(-1), gain_sums.reshape(-1)]
        )

    def everywhere(vector):
        halves = vector.reshape(2, -1)
        half = add(take(halves, core), moves.pair(take(halves, 1 - core)))
        half = moves.gather(half)
        both = regroup([half, moves.pair(half)], core)
        return both.transpose(1, 0, 2).reshape(half.shape[0], -1)

    known = jnp.concatenate([condition, jnp.broadcast_to(label.astype(F32), (128,))])
    known = moves.gather(known)
    if not quick:
        early, late = everywhere(early), everywhere(late)
    grad_modulation = jnp.concatenate([late[:, : 2 * width], early[:, : 4 * width]], axis=1)
    conditions = known[:, :width]
    all_labels = known[:, width].astype(jnp.int32)
    cond_acts = jax.nn.silu(conditions).astype(BF16)
    my_acts = lax.dynamic_slice_in_dim(cond_acts, z * slice_rows, slice_rows, axis=1)
    low_mod = grad_modulation.astype(BF16)
    grad_mod_w = mm_tn(my_acts, low_mod)
    wide = 6 * width
    grad_mod_b = lax.dynamic_slice_in_dim(
        jnp.sum(grad_modulation, axis=0), z * (wide // nb), wide // nb, axis=0
    )
    grad_cond_act = mm_nt(low_mod, modulate_weight)
    sig = jax.nn.sigmoid(conditions)
    grad_conditions = grad_cond_act * sig * (1.0 + conditions * (1.0 - sig))
    grad_condition = regroup([grad_conditions[k] for k in range(4)], place)
    onehot = (all_labels[:, None] == jnp.arange(class_count, dtype=jnp.int32)[None, :]).astype(F32)
    grad_table = lax.dot_general(
        onehot, grad_conditions, (((0,), (0,)), ((), ())), precision=highest,
        preferred_element_type=F32,
    )

    early_sum = jnp.sum(early, axis=0)
    late_sum = jnp.sum(late, axis=0)

    def part(vector, start, size):
        return lax.dynamic_slice_in_dim(vector, start + z * (size // nb), size // nb, axis=0)

    grad_out_b = part(early_sum, 4 * width, width)
    grad_down_b = part(early_sum, 5 * width, width)
    grad_gu_b = part(early_sum, 6 * width, 2 * hidden_width)
    grad_in_b = part(late_sum, 2 * width, 3 * width)
    grad_q_gain = part(late_sum, 5 * width, head)
    grad_k_gain = part(late_sum, 5 * width + head, head)
    return (
        output, grad_tokens, grad_condition, grad_table, grad_mod_w, grad_mod_b, grad_in_w,
        grad_in_b, grad_q_gain, grad_k_gain, grad_out_w, grad_out_b, grad_gu_w, grad_gu_b,
        grad_down_w, grad_down_b,
    )


def solution(mesh):
    grid = P("batch", "gy", "gx", None)
    by_batch = P("batch")
    rows = P("batch", None)
    placed = (grid, by_batch, by_batch) + (P(),) * 13 + (grid,)
    return jax.shard_map(
        functools.partial(body, mesh),
        mesh=mesh,
        in_specs=placed,
        out_specs=(
            grid, grid, rows, P(), rows, by_batch, rows, by_batch, by_batch, by_batch, rows,
            by_batch, rows, by_batch, rows, by_batch,
        ),
        check_vma=False,
    )
```

```python
import functools
import math

import jax
import jax.numpy as jnp
from jax import lax
from jax.experimental import pallas as pl
from jax.experimental.pallas import tpu as pltpu
from jax.sharding import PartitionSpec as P

NORM_EPSILON = 1e-06
AXES = ("batch", "gy", "gx")
BF16 = jnp.bfloat16
F32 = jnp.float32
VMEM_LIMIT = 60 * 1024 * 1024


def mm(left, right):
    return lax.dot_general(left, right, (((1,), (0,)), ((), ())), preferred_element_type=F32)


def mm_nt(left, right):
    return lax.dot_general(left, right, (((1,), (1,)), ((), ())), preferred_element_type=F32)


def mm_tn(left, right):
    return lax.dot_general(left, right, (((0,), (0,)), ((), ())), preferred_element_type=F32)


def params():
    return pltpu.CompilerParams(vmem_limit_bytes=VMEM_LIMIT)


def full(shape):
    return pl.BlockSpec(shape, lambda *_: (0,) * len(shape))


def col_sum(values):
    return jnp.sum(values, axis=0, keepdims=True)


def modulation_kernel(act_ref, weight_ref, bias_ref, out_ref):
    out_ref[...] = mm(act_ref[...], weight_ref[...]) + bias_ref[...].astype(F32)


def modulation_call(act, weight, bias):
    rows, width = act.shape
    wide = weight.shape[1]
    return pl.pallas_call(
        modulation_kernel,
        grid=(wide // width,),
        in_specs=[
            full((rows, width)),
            pl.BlockSpec((width, width), lambda j: (0, j)),
            pl.BlockSpec((1, width), lambda j: (0, j)),
        ],
        out_specs=pl.BlockSpec((rows, width), lambda j: (0, j)),
        out_shape=jax.ShapeDtypeStruct((rows, wide), F32),
        compiler_params=params(),
        name="modulation",
    )(act, weight, bias)


def head_sum(values, head):
    width = 256
    row = lax.broadcasted_iota(jnp.int32, (width, width), 0) // head
    col = lax.broadcasted_iota(jnp.int32, (width, width), 1) // head
    ones = jnp.where(row == col, 1.0, 0.0).astype(BF16)
    parts = [
        mm(values[:, i : i + width].astype(BF16), ones) for i in range(0, values.shape[1], width)
    ]
    return jnp.concatenate(parts, axis=1)


def turn(values, cosine, sine, head):
    quarter = head // 4
    lane = lax.broadcasted_iota(jnp.int32, (1, 128), 1)
    first = (lane % (2 * quarter)) < quarter
    parts = []
    for i in range(0, values.shape[1], 128):
        part = values[:, i : i + 128]
        partner = jnp.where(
            first, pltpu.roll(part, 128 - quarter, 1), pltpu.roll(part, quarter, 1)
        )
        parts.append(part * cosine + partner * sine)
    return jnp.concatenate(parts, axis=1)


def project_kernel(
    head, x_ref, mod_ref, weight_ref, bias_ref, qgain_ref, kgain_ref, cos_ref, sin_ref,
    hid_ref, q_ref, k_ref, v_ref, raw_ref,
):
    width = x_ref.shape[1]
    x = x_ref[...].astype(F32)
    normed = x * lax.rsqrt(jnp.mean(x * x, axis=-1, keepdims=True) + NORM_EPSILON)
    hidden = (normed * (1.0 + mod_ref[:, width : 2 * width]) + mod_ref[:, :width]).astype(BF16)
    hid_ref[...] = hidden
    for part, (out_ref, gain_ref) in enumerate(((q_ref, qgain_ref), (k_ref, kgain_ref))):
        raw = mm(hidden, weight_ref[:, part * width : (part + 1) * width])
        raw = raw + bias_ref[:, part * width : (part + 1) * width].astype(F32)
        raw_ref[:, part * width : (part + 1) * width] = raw.astype(BF16)
        factor = lax.rsqrt(head_sum(raw * raw, head) * (1.0 / head) + NORM_EPSILON)
        scaled = raw * factor * gain_ref[...]
        out_ref[...] = turn(scaled, cos_ref[...], sin_ref[...], head).astype(BF16)
    value = mm(hidden, weight_ref[:, 2 * width :]) + bias_ref[:, 2 * width :].astype(F32)
    v_ref[...] = value.astype(BF16)


def project_call(x, mod, weight, bias, qgain, kgain, cosine, sine, head):
    rows, width = x.shape
    block = rows // 2
    by_row = lambda wide: pl.BlockSpec((block, wide), lambda i: (i, 0))
    shape = jax.ShapeDtypeStruct((rows, width), BF16)
    return pl.pallas_call(
        functools.partial(project_kernel, head),
        grid=(2,),
        in_specs=[
            by_row(width),
            full(mod.shape),
            full(weight.shape),
            full(bias.shape),
            full(qgain.shape),
            full(kgain.shape),
            by_row(128),
            by_row(128),
        ],
        out_specs=[by_row(width)] * 4 + [by_row(2 * width)],
        out_shape=[shape] * 4 + [jax.ShapeDtypeStruct((rows, 2 * width), BF16)],
        compiler_params=params(),
        name="project",
    )(x, mod, weight, bias, qgain, kgain, cosine, sine)


def attend_kernel(scale, q_ref, k0_ref, k1_ref, v0_ref, v1_ref, mix_ref, e_ref, rl_ref):
    lane = lax.broadcasted_iota(jnp.int32, (1, 128), 1)
    q = q_ref[...]
    keys = jnp.concatenate([k0_ref[...], k1_ref[...]], axis=0)
    values = jnp.concatenate([v0_ref[...], v1_ref[...]], axis=0)
    values = jnp.concatenate([values, jnp.ones_like(values)], axis=1)
    outs = []
    for h in range(2):
        mine = (lane >= 64) if h else (lane < 64)
        scores = mm_nt(jnp.where(mine, q, jnp.zeros_like(q)), keys)
        grown = jnp.exp(scores * scale).astype(BF16)
        e_ref[h] = grown
        outs.append(mm(grown, values))
    inverse = 1.0 / jnp.where(lane < 64, outs[0][:, 128:], outs[1][:, 128:])
    mix_ref[...] = (jnp.where(lane < 64, outs[0][:, :128], outs[1][:, :128]) * inverse).astype(BF16)
    rl_ref[...] = inverse


def attend_call(q, k0, k1, v0, v1, head):
    rows, width = q.shape
    pair = pl.BlockSpec((rows, 128), lambda p: (0, p))
    return pl.pallas_call(
        functools.partial(attend_kernel, head**-0.5),
        grid=(width // 128,),
        in_specs=[pair] * 5,
        out_specs=[pair, pl.BlockSpec((2, rows, 2 * rows), lambda p: (p, 0, 0)), pair],
        out_shape=[
            jax.ShapeDtypeStruct((rows, width), BF16),
            jax.ShapeDtypeStruct((width // head, rows, 2 * rows), BF16),
            jax.ShapeDtypeStruct((rows, width), F32),
        ],
        compiler_params=params(),
        name="attend",
    )(q, k0, k1, v0, v1)


def attend_back_kernel(
    scale, q_ref, k0_ref, k1_ref, v0_ref, v1_ref, e_ref, gm_ref, mix_ref, rl_ref,
    dq_ref, dk0_ref, dk1_ref, dv0_ref, dv1_ref,
):
    rows = q_ref.shape[0]
    lane = lax.broadcasted_iota(jnp.int32, (1, 128), 1)
    keys = jnp.concatenate([k0_ref[...], k1_ref[...]], axis=0)
    values = jnp.concatenate([v0_ref[...], v1_ref[...]], axis=0)
    scaled = gm_ref[...].astype(F32) * rl_ref[...]
    products = scaled * mix_ref[...].astype(F32)
    scaled = scaled.astype(BF16)
    q_t = q_ref[...].T
    scaled_t = scaled.T
    dqs, dks, dvs = [], [], []
    for h in range(2):
        mine = (lane >= 64) if h else (lane < 64)
        inner = jnp.sum(jnp.where(mine, products, 0.0), axis=1, keepdims=True)
        grad_probs = mm_nt(jnp.where(mine, scaled, jnp.zeros_like(scaled)), values)
        grown = e_ref[h]
        grad_scores = (grown.astype(F32) * (grad_probs - inner) * scale).astype(BF16)
        dqs.append(mm(grad_scores, keys))
        dks.append(mm(q_t[64 * h : 64 * h + 64], grad_scores))
        dvs.append(mm(scaled_t[64 * h : 64 * h + 64], grown))
    dq_ref[...] = jnp.where(lane < 64, dqs[0], dqs[1]).astype(BF16)
    dk = jnp.concatenate(dks, axis=0).T.astype(BF16)
    dv = jnp.concatenate(dvs, axis=0).T.astype(BF16)
    dk0_ref[...] = dk[:rows]
    dk1_ref[...] = dk[rows:]
    dv0_ref[...] = dv[:rows]
    dv1_ref[...] = dv[rows:]


def attend_back_call(q, k0, k1, v0, v1, grown, grad_mixed, mixed, inverse, head):
    rows, width = q.shape
    pair = pl.BlockSpec((rows, 128), lambda p: (0, p))
    return pl.pallas_call(
        functools.partial(attend_back_kernel, head**-0.5),
        grid=(width // 128,),
        in_specs=[pair] * 5
        + [pl.BlockSpec((2, rows, 2 * rows), lambda p: (p, 0, 0))]
        + [pair] * 3,
        out_specs=[pair] * 5,
        out_shape=[jax.ShapeDtypeStruct((rows, width), BF16)] * 5,
        compiler_params=params(),
        name="attend_back",
    )(q, k0, k1, v0, v1, grown, grad_mixed, mixed, inverse)


def middle_kernel(
    mix_ref, x_ref, dy_ref, mod_ref, weight_ref, bias_ref, att_ref, mid_ref, h2_ref, h2t_ref, gf_ref
):
    width = x_ref.shape[1]
    attended = mm(mix_ref[...], weight_ref[...]) + bias_ref[...].astype(F32)
    middle = x_ref[...].astype(F32) + mod_ref[:, 2 * width : 3 * width] * attended
    normed = middle * lax.rsqrt(jnp.mean(middle * middle, axis=-1, keepdims=True) + NORM_EPSILON)
    hidden = normed * (1.0 + mod_ref[:, 4 * width : 5 * width]) + mod_ref[:, 3 * width : 4 * width]
    hidden = hidden.astype(BF16)
    att_ref[...] = attended.astype(BF16)
    mid_ref[...] = middle
    h2_ref[...] = hidden
    h2t_ref[...] = hidden.T
    gf_ref[...] = (mod_ref[:, 5 * width :] * dy_ref[...].astype(F32)).astype(BF16)


def middle_call(mixed, x, dy, mod, weight, bias):
    rows, width = x.shape
    block = rows // 2
    by_row = pl.BlockSpec((block, width), lambda i: (i, 0))
    low = jax.ShapeDtypeStruct((rows, width), BF16)
    return pl.pallas_call(
        middle_kernel,
        grid=(2,),
        in_specs=[by_row] * 3 + [full(mod.shape), full(weight.shape), full(bias.shape)],
        out_specs=[by_row] * 3 + [pl.BlockSpec((width, block), lambda i: (0, i)), by_row],
        out_shape=[low, jax.ShapeDtypeStruct((rows, width), F32), low]
        + [jax.ShapeDtypeStruct((width, rows), BF16), low],
        compiler_params=params(),
        name="middle",
    )(mixed, x, dy, mod, weight, bias)


def feed_kernel(
    h2_ref, h2t_ref, gf_ref, wg_ref, wu_ref, bg_ref, bu_ref, wd_ref, feed_in_ref, gh_in_ref,
    feed_ref, gh_ref, dd_ref, dg_ref, db_ref,
):
    @pl.when(pl.program_id(0) == 0)
    def _():
        feed_ref[...] = feed_in_ref[...]
        gh_ref[...] = gh_in_ref[...]

    hidden = h2_ref[...]
    grad_feed = gf_ref[...]
    gate = mm(hidden, wg_ref[...]) + bg_ref[...].astype(F32)
    up = mm(hidden, wu_ref[...]) + bu_ref[...].astype(F32)
    grad_product = mm_nt(grad_feed, wd_ref[...])
    sig = 1.0 / (1.0 + jnp.exp(-gate))
    active = gate * sig
    product = (active * up).astype(BF16)
    grad_gate = (grad_product * up * sig * (1.0 + gate * (1.0 - sig))).astype(BF16)
    grad_up = (grad_product * active).astype(BF16)
    dd_ref[...] = mm_tn(product, grad_feed).astype(BF16)
    dg_ref[0] = mm(h2t_ref[...], grad_gate).astype(BF16)
    dg_ref[1] = mm(h2t_ref[...], grad_up).astype(BF16)
    db_ref[0] = col_sum(grad_gate.astype(F32))
    db_ref[1] = col_sum(grad_up.astype(F32))
    feed_ref[...] += mm(product, wd_ref[...])
    gh_ref[...] += mm_nt(grad_gate, wg_ref[...]) + mm_nt(grad_up, wu_ref[...])


def feed_call(hidden, hidden_t, grad_feed, weight, bias, down, feed, grad_hidden, first, step, unit):
    rows, width = hidden.shape
    blocks = down.shape[0] // unit
    steps = len(range(first, blocks, step))
    pick = lambda s: first + step * s
    acc = jax.ShapeDtypeStruct((rows, width), F32)
    return pl.pallas_call(
        feed_kernel,
        grid=(steps,),
        in_specs=[
            full((rows, width)),
            full((width, rows)),
            full((rows, width)),
            pl.BlockSpec((width, unit), lambda s: (0, pick(s))),
            pl.BlockSpec((width, unit), lambda s: (0, blocks + pick(s))),
            pl.BlockSpec((1, unit), lambda s: (0, pick(s))),
            pl.BlockSpec((1, unit), lambda s: (0, blocks + pick(s))),
            pl.BlockSpec((unit, width), lambda s: (pick(s), 0)),
            full((rows, width)),
            full((rows, width)),
        ],
        out_specs=[
            full((rows, width)),
            full((rows, width)),
            pl.BlockSpec((None, unit, width), lambda s: (s, 0, 0)),
            pl.BlockSpec((None, 2, width, unit), lambda s: (s, 0, 0, 0)),
            pl.BlockSpec((None, 2, 1, unit), lambda s: (s, 0, 0, 0)),
        ],
        out_shape=[
            acc,
            acc,
            jax.ShapeDtypeStruct((steps, unit, width), BF16),
            jax.ShapeDtypeStruct((steps, 2, width, unit), BF16),
            jax.ShapeDtypeStruct((steps, 2, 1, unit), F32),
        ],
        compiler_params=params(),
        name="feed",
    )(hidden, hidden_t, grad_feed, weight, weight, bias, bias, down, feed, grad_hidden)


def turn_kernel(
    feed_ref, gh_ref, mid_ref, att_ref, dy_ref, gf_ref, mix_ref, mod_ref, weight_ref, dbias_ref,
    out_ref, gmid_ref, gmix_ref, dw_ref, sums_ref,
):
    width = mid_ref.shape[1]
    half = width // 2
    dy = dy_ref[...].astype(F32)
    feed = feed_ref[...] + dbias_ref[...].astype(F32)
    middle = mid_ref[...]
    out_ref[...] = (middle + mod_ref[:, 5 * width :] * feed).astype(BF16)
    factor = lax.rsqrt(jnp.mean(middle * middle, axis=-1, keepdims=True) + NORM_EPSILON)
    normed = middle * factor
    grad_hidden = gh_ref[...]
    product = grad_hidden * normed
    grad_normed = grad_hidden * (1.0 + mod_ref[:, 4 * width : 5 * width])
    back = factor * (
        grad_normed - normed * jnp.mean(grad_normed * normed, axis=-1, keepdims=True)
    )
    grad_middle = dy + back
    gmid_ref[...] = grad_middle
    grad_attended = (mod_ref[:, 2 * width : 3 * width] * grad_middle).astype(BF16)
    sums_ref[0:1, :] = col_sum(grad_middle * att_ref[...].astype(F32))
    sums_ref[1:2, :] = col_sum(grad_hidden)
    sums_ref[2:3, :] = col_sum(product)
    sums_ref[3:4, :] = col_sum(dy * feed)
    sums_ref[4:5, :] = col_sum(grad_attended.astype(F32))
    sums_ref[5:6, :] = col_sum(gf_ref[...].astype(F32))
    sums_ref[6:8, :] = jnp.zeros((2, width), F32)
    gmix_ref[...] = mm_nt(grad_attended, weight_ref[...]).astype(BF16)
    mixed_t = mix_ref[...].T
    dw_ref[0] = mm(mixed_t, grad_attended[:, :half]).astype(BF16)
    dw_ref[1] = mm(mixed_t, grad_attended[:, half:]).astype(BF16)


def turn_call(feed, grad_hidden, middle, attended, dy, grad_feed, mixed, mod, weight, down_bias):
    rows, width = middle.shape
    low = jax.ShapeDtypeStruct((rows, width), BF16)
    return pl.pallas_call(
        turn_kernel,
        out_shape=[
            low,
            jax.ShapeDtypeStruct((rows, width), F32),
            low,
            jax.ShapeDtypeStruct((2, width, width // 2), BF16),
            jax.ShapeDtypeStruct((8, width), F32),
        ],
        compiler_params=params(),
        name="turn",
    )(feed, grad_hidden, middle, attended, dy, grad_feed, mixed, mod, weight, down_bias)


def project_back_kernel(
    head, dq_ref, dk0_ref, dk1_ref, dv0_ref, dv1_ref, raw_ref, hid_ref, x_ref, gmid_ref, mod_ref,
    weight_ref, qgain_ref, kgain_ref, cos_ref, sin_ref,
    gx_ref, dw_ref, sums_ref, bias_ref, proj_ref,
):
    width = x_ref.shape[1]
    cosine, sine = cos_ref[...], -sin_ref[...]
    for part in range(3):
        span = slice(part * width, (part + 1) * width)
        if part == 2:
            grad = dv0_ref[...].astype(F32) + dv1_ref[...].astype(F32)
        else:
            grad = dq_ref[...].astype(F32)
            if part == 1:
                grad = dk0_ref[...].astype(F32) + dk1_ref[...].astype(F32)
            gain = (qgain_ref, kgain_ref)[part][...]
            raw = raw_ref[:, span].astype(F32)
            factor = lax.rsqrt(head_sum(raw * raw, head) * (1.0 / head) + NORM_EPSILON)
            normed = raw * factor
            turned = turn(grad, cosine, sine, head)
            sums_ref[2 + part : 3 + part, :] = col_sum(turned * normed)
            turned = turned * gain
            mean = head_sum(turned * normed, head) * (1.0 / head)
            grad = factor * (turned - normed * mean)
        low = grad.astype(BF16)
        proj_ref[:, span] = low
        bias_ref[:, span] = col_sum(low.astype(F32))
    hidden_t = hid_ref[...].T
    half = 3 * width // 2
    dw_ref[0] = mm(hidden_t, proj_ref[:, :half]).astype(BF16)
    dw_ref[1] = mm(hidden_t, proj_ref[:, half:]).astype(BF16)
    grad_hidden = mm_nt(proj_ref[...], weight_ref[...])
    x = x_ref[...].astype(F32)
    factor = lax.rsqrt(jnp.mean(x * x, axis=-1, keepdims=True) + NORM_EPSILON)
    normed = x * factor
    sums_ref[0:1, :] = col_sum(grad_hidden)
    sums_ref[1:2, :] = col_sum(grad_hidden * normed)
    sums_ref[4:8, :] = jnp.zeros((4, width), F32)
    grad_normed = grad_hidden * (1.0 + mod_ref[:, width : 2 * width])
    back = factor * (
        grad_normed - normed * jnp.mean(grad_normed * normed, axis=-1, keepdims=True)
    )
    gx_ref[...] = (gmid_ref[...] + back).astype(BF16)


def project_back_call(
    dq, dk0, dk1, dv0, dv1, raw, hidden, x, grad_middle, mod, weight, qgain, kgain, cosine, sine, head
):
    rows, width = x.shape
    return pl.pallas_call(
        functools.partial(project_back_kernel, head),
        out_shape=[
            jax.ShapeDtypeStruct((rows, width), BF16),
            jax.ShapeDtypeStruct((2, width, 3 * width // 2), BF16),
            jax.ShapeDtypeStruct((8, width), F32),
            jax.ShapeDtypeStruct((1, 3 * width), F32),
        ],
        scratch_shapes=[pltpu.VMEM((rows, 3 * width), BF16)],
        compiler_params=params(),
        name="project_back",
    )(dq, dk0, dk1, dv0, dv1, raw, hidden, x, grad_middle, mod, weight, qgain, kgain, cosine, sine)


class Place:
    def __init__(self):
        self.z, self.gy, self.gx = (lax.axis_index(name) for name in AXES)
        self.core = lax.rem(self.gx, 2)
        self.side = self.gx // 2
        self.chip = 2 * self.gy + self.side

    def flipped(self, k):
        return 2 * lax.rem(self.gy + k // 2, 2) + lax.rem(self.side + lax.rem(k, 2), 2)

    def pair(self):
        return {"gx": self.gx + 1 - 2 * self.core}

    def plane(self, k):
        device = {}
        if k & 2:
            device["gy"] = 1 - self.gy
        if k & 1:
            device["gx"] = lax.rem(self.gx + 2, 4)
        return device

    def depth(self, d):
        return {"batch": self.flipped_z(d)}

    def flipped_z(self, d):
        return {1: self.z + 1 - 2 * lax.rem(self.z, 2), 2: lax.rem(self.z + 2, 4), 3: 3 - self.z}[d]


def meet(devices):
    barrier = pltpu.get_barrier_semaphore()
    for device in devices:
        pl.semaphore_signal(barrier, inc=1, device_id=device, device_id_type=pl.DeviceIdType.MESH)
    pl.semaphore_wait(barrier, len(devices))


def send(source, target, send_sem, recv_sem, device):
    return pltpu.make_async_remote_copy(
        src_ref=source, dst_ref=target, send_sem=send_sem, recv_sem=recv_sem, device_id=device,
        device_id_type=pl.DeviceIdType.MESH,
    )


def feed_order(step):
    owner = jnp.where(
        step < 2, 3, jnp.where((step == 2) | (step == 5), 2, jnp.where(step < 5, 1, 0))
    )
    return owner, lax.rem(step, 2)


def feed_block(step, i):
    step = jnp.minimum(step, 7)
    owner, half = feed_order(step)
    return (2 * half + i) * 4 + Place().flipped(owner)


def feed_turn_kernel(
    h2_ref, h2t_ref, gf_ref, wg0, wg1, wu0, wu1, bg0, bg1, bu0, bu1, wd0, wd1,
    mid_ref, att_ref, dy_ref, mix_ref, mod_ref, weight_ref, dbias_ref, known_ref,
    out_ref, gmid_ref, gmix_ref, dw_ref, sums_ref, total_ref,
    feed_ref, gh_ref, bias_ref, made, paired, near, pair_send, pair_recv, near_send, near_recv,
):
    place = Place()
    core = place.core
    step = pl.program_id(0)
    slot = lax.rem(step, 2)
    width = h2_ref.shape[1]
    unit = 128
    g_rows = width

    @pl.when(step == 0)
    def _():
        feed_ref[...] = jnp.zeros_like(feed_ref)
        sums_ref[1] = jnp.zeros((8, width), F32)
        gh_ref[...] = jnp.zeros_like(gh_ref)
        meet([place.pair(), place.plane(1), place.plane(2)])

    def pair_copy(of):
        return send(
            made.at[lax.rem(of, 2), 1 - core], paired.at[of], pair_send.at[lax.rem(of, 2)],
            pair_recv.at[of], place.pair(),
        )

    def near_copy(of, k):
        return send(paired.at[of], near.at[of], near_send.at[of], near_recv.at[of], place.plane(k))

    @pl.when(step >= 1)
    def _():
        pair_copy(step - 1).start()

    @pl.when(step < 8)
    def _():
        owner, half = feed_order(step)
        hidden = h2_ref[...]
        grad_feed = gf_ref[...]
        wg = jnp.concatenate([wg0[...], wg1[...]], axis=1)
        wu = jnp.concatenate([wu0[...], wu1[...]], axis=1)
        wd = jnp.concatenate([wd0[...], wd1[...]], axis=0)
        gate = mm(hidden, wg) + jnp.concatenate([bg0[...], bg1[...]], axis=1).astype(F32)
        up = mm(hidden, wu) + jnp.concatenate([bu0[...], bu1[...]], axis=1).astype(F32)
        grad_product = mm_nt(grad_feed, wd)
        sig = 1.0 / (1.0 + jnp.exp(-gate))
        active = gate * sig
        product = (active * up).astype(BF16)
        grad_gate = (grad_product * up * sig * (1.0 + gate * (1.0 - sig))).astype(BF16)
        grad_up = (grad_product * active).astype(BF16)
        feed_ref[...] += mm(product, wd)
        gh_ref[...] += mm_nt(grad_gate, wg) + mm_nt(grad_up, wu)
        for e, grad in enumerate((grad_gate, grad_up)):
            total = col_sum(grad.astype(F32))
            for i in range(2):
                row = 16 * e + (2 * half + i) * 4 + place.flipped(owner)
                bias_ref[pl.ds(row, 1), :] = total[:, i * unit : (i + 1) * unit]

        @pl.when(step >= 2)
        def _():
            pair_copy(step - 2).wait_send()

        for e, grad in enumerate((grad_gate, grad_up)):
            made[slot, e, :g_rows] = mm(h2t_ref[...], grad).astype(BF16)
        product_t = product.T
        for b in range(3):
            d = mm(product_t, grad_feed[:, 256 * b : 256 * b + 256]).astype(BF16)
            for i in range(2):
                for c in range(2):
                    made[slot, c, pl.ds(g_rows + b * 128 + i * 64, 64)] = d[
                        i * 128 + c * 64 : i * 128 + c * 64 + 64
                    ]

    @pl.when(step >= 1)
    def _():
        of = step - 1
        copy = pair_copy(of)
        copy.wait_recv()
        late = (of == 4) | (of == 5)

        @pl.when(jnp.logical_not(late))
        def _():
            paired[of] = (made[1 - slot, core].astype(F32) + paired[of].astype(F32)).astype(BF16)

        @pl.when(late)
        def _():
            near_copy(of - 4, 1).wait_recv()
            paired[of] = (
                made[1 - slot, core].astype(F32)
                + paired[of].astype(F32)
                + near[of - 4].astype(F32)
            ).astype(BF16)

        @pl.when((of == 0) | (of == 2) | (of == 5))
        def _():
            near_copy(of, 2).start()

        @pl.when((of == 1) | (of == 3) | (of == 4))
        def _():
            near_copy(of, 1).start()

    @pl.when(step == 8)
    def _():
        half = width // 2
        dy = dy_ref[...].astype(F32)
        feed = feed_ref[...] + dbias_ref[...].astype(F32)
        middle = mid_ref[...]
        out_ref[...] = (middle + mod_ref[:, 5 * width :] * feed).astype(BF16)
        factor = lax.rsqrt(jnp.mean(middle * middle, axis=-1, keepdims=True) + NORM_EPSILON)
        normed = middle * factor
        grad_hidden = gh_ref[...]
        product = grad_hidden * normed
        grad_normed = grad_hidden * (1.0 + mod_ref[:, 4 * width : 5 * width])
        back = factor * (
            grad_normed - normed * jnp.mean(grad_normed * normed, axis=-1, keepdims=True)
        )
        grad_middle = dy + back
        gmid_ref[...] = grad_middle
        grad_attended = (mod_ref[:, 2 * width : 3 * width] * grad_middle).astype(BF16)
        sums_ref[0, 0:1, :] = col_sum(grad_middle * att_ref[...].astype(F32))
        sums_ref[0, 1:2, :] = col_sum(grad_hidden)
        sums_ref[0, 2:3, :] = col_sum(product)
        sums_ref[0, 3:4, :] = col_sum(dy * feed)
        sums_ref[0, 4:5, :] = col_sum(grad_attended.astype(F32))
        sums_ref[0, 5:6, :] = col_sum(gf_ref[...].astype(F32))
        sums_ref[0, 6:8, :] = known_ref[...]
        for row in range(32):
            col = (row % 6) * unit
            sums_ref[1, row // 6 : row // 6 + 1, col : col + unit] = bias_ref[row : row + 1, :]
        gmix_ref[...] = mm_nt(grad_attended, weight_ref[...]).astype(BF16)
        mixed_t = mix_ref[...].T
        dw_ref[0] = mm(mixed_t, grad_attended[:, :half]).astype(BF16)
        dw_ref[1] = mm(mixed_t, grad_attended[:, half:]).astype(BF16)
        for of in (6, 7):
            pair_copy(of).wait_send()
        for of in (2, 3, 4, 5):
            near_copy(of, 1).wait_recv()
        for of in range(6):
            near_copy(of, 1).wait_send()
        rows = width // 4
        for f in range(2):
            for z in range(4):
                span = slice(z * rows, (z + 1) * rows)
                total_ref[z, f] = sum(
                    part.astype(F32)
                    for part in (paired[6 + f, span], near[2 + f, span], near[4 + f, span])
                ).astype(BF16)
            for i in range(2):
                for b in range(3):
                    span = slice(g_rows + b * 128 + i * 64, g_rows + b * 128 + i * 64 + 64)
                    total_ref[2 * f + i, 2, b * 64 : b * 64 + 64] = sum(
                        part.astype(F32)
                        for part in (paired[6 + f, span], near[2 + f, span], near[4 + f, span])
                    ).astype(BF16)


def once(shape):
    return pl.BlockSpec(shape, lambda *_: (0,) * len(shape), pipeline_mode=pl.Buffered(1))


def feed_turn_call(
    hidden, hidden_t, grad_feed, gate_up, gate_up_bias, down, middle, attended, dy, mixed, mod,
    weight, down_bias, known,
):
    rows, width = hidden.shape
    low = jax.ShapeDtypeStruct((rows, width), BF16)
    wide = jax.ShapeDtypeStruct((rows, width), F32)
    cols = lambda i, e: pl.BlockSpec((width, 128), lambda s: (0, 16 * e + feed_block(s, i)))
    bias = lambda i, e: pl.BlockSpec((1, 128), lambda s: (0, 16 * e + feed_block(s, i)))
    deep = lambda i: pl.BlockSpec((128, width), lambda s: (feed_block(s, i), 0))
    piece = (width + 384, 256)
    out_shape = [
        low, wide, low,
        jax.ShapeDtypeStruct((2, width, width // 2), BF16),
        jax.ShapeDtypeStruct((2, 8, width), F32),
        jax.ShapeDtypeStruct((4, 3, width // 4, 256), BF16),
    ]
    return pl.pallas_call(
        feed_turn_kernel,
        grid=(9,),
        in_specs=[once((rows, width)), once((width, rows)), once((rows, width))]
        + [cols(0, 0), cols(1, 0), cols(0, 1), cols(1, 1)]
        + [bias(0, 0), bias(1, 0), bias(0, 1), bias(1, 1)]
        + [deep(0), deep(1)]
        + [once((rows, width))] * 4
        + [once(each.shape) for each in (mod, weight, down_bias, known)],
        out_specs=[full(shape.shape) for shape in out_shape],
        out_shape=out_shape,
        scratch_shapes=[
            pltpu.VMEM((rows, width), F32),
            pltpu.VMEM((rows, width), F32),
            pltpu.VMEM((32, 128), F32),
            pltpu.VMEM((2, 2) + piece, BF16),
            pltpu.VMEM((8,) + piece, BF16),
            pltpu.VMEM((6,) + piece, BF16),
            pltpu.SemaphoreType.DMA((2,)),
            pltpu.SemaphoreType.DMA((8,)),
            pltpu.SemaphoreType.DMA((6,)),
            pltpu.SemaphoreType.DMA((6,)),
        ],
        compiler_params=pltpu.CompilerParams(
            vmem_limit_bytes=VMEM_LIMIT, collective_id=1, has_side_effects=True
        ),
        name="feed_turn",
    )(
        hidden, hidden_t, grad_feed, gate_up, gate_up, gate_up, gate_up, gate_up_bias,
        gate_up_bias, gate_up_bias, gate_up_bias, down, down, middle, attended, dy, mixed, mod,
        weight, down_bias, known,
    )


Z_FIRST = (False, False, False, False)
GROUPS = 4


def back_kernel(
    head, q_ref, k0_ref, k1_ref, v0_ref, v1_ref, gm_ref, mix_ref, rl_ref, e_ref,
    mod_ref, qgain_ref, kgain_ref, cos_ref, sin_ref, dout_ref, totals_ref, early_ref,
    raw_hbm, hid_hbm, x_hbm, gmid_hbm, weight_hbm, rows_hbm,
    output_ref, gtok_ref, feeds_hbm, projs_hbm, early_hbm, late_hbm,
    feeds_ref, projs_ref, early_all, late_all, raw_ref, hid_ref, x_ref, gmid_ref, weight_ref, hidt_ref, gh_ref, gx_ref, late_ref,
    dq_s, dk0_s, dv0_s, dk1_s, dv1_s, dk_in, dv_in,
    made, paired, first_out, first_in, second_out, second_in, z_in, early_in, late_in,
    load_sem, own_sem, kv_send, kv_recv, pair_send, pair_recv, first_send, first_recv,
    second_send, second_recv, z_send, z_recv, tok_send, tok_recv, feed_send, feed_recv,
    proj_send, proj_recv, small_send, small_recv,
):
    place = Place()
    core, chip, z = place.core, place.chip, place.z
    step = pl.program_id(0)
    rows, width = x_ref.shape
    cells = rows // 4
    scale = head**-0.5
    lane = lax.broadcasted_iota(jnp.int32, (1, 128), 1)

    loads = [
        pltpu.make_async_copy(source, target, load_sem.at[i])
        for i, (source, target) in enumerate(
            (
                (hid_hbm, hid_ref), (raw_hbm, raw_ref), (weight_hbm, weight_ref),
                (x_hbm, x_ref), (gmid_hbm, gmid_ref),
            )
        )
    ]

    stores = [
        pltpu.make_async_copy(source, target, load_sem.at[5 + i])
        for i, (source, target) in enumerate(
            (
                (early_all, early_hbm), (late_all, late_hbm), (feeds_ref, feeds_hbm),
                (projs_ref, projs_hbm),
            )
        )
    ]

    def z_copy(d):
        return send(
            totals_ref.at[place.flipped_z(d)], z_in.at[d - 1], z_send.at[d - 1], z_recv.at[d - 1],
            place.depth(d),
        )

    def token_copy(which, k):
        source, target = ((rows_hbm, output_ref), (gx_ref, gtok_ref))[which]
        return send(
            source.at[pl.ds(k * cells, cells)], target.at[chip], tok_send.at[which, k - 1],
            tok_recv.at[which, k - 1], place.plane(k),
        )

    def own_tokens(which):
        source, target = ((rows_hbm, output_ref), (gx_ref, gtok_ref))[which]
        return pltpu.make_async_copy(source.at[pl.ds(0, cells)], target.at[chip], own_sem.at[which])

    def kv_copy(which, p):
        source, target = ((dk1_s, dk_in), (dv1_s, dv_in))[which]
        return send(
            source.at[p], target.at[p], kv_send.at[which, p], kv_recv.at[which, p], place.pair()
        )

    def pair_copy(g):
        source = dout_ref.at[1 - core] if g == 3 else made.at[g % 2, 1 - core]
        return send(source, paired.at[g], pair_send.at[g], pair_recv.at[g], place.pair())

    def first_copy(g, k):
        other = place.flipped_z(k) if Z_FIRST[g] else place.flipped(k)
        device = place.depth(k) if Z_FIRST[g] else place.plane(k)
        return send(
            first_out.at[g, other], first_in.at[g, k - 1], first_send.at[g, k - 1],
            first_recv.at[g, k - 1], device,
        )

    def second_copy(g, k):
        other = place.flipped(k) if Z_FIRST[g] else place.flipped_z(k)
        device = place.plane(k) if Z_FIRST[g] else place.depth(k)
        return send(
            second_out.at[g, other], second_in.at[g, k - 1], second_send.at[g, k - 1],
            second_recv.at[g, k - 1], device,
        )

    def feed_copy(k):
        here = feeds_ref.at[core, chip]
        return send(here, here, feed_send.at[k - 1], feed_recv.at[k - 1], place.plane(k))

    def feed_pair():
        here = feeds_ref.at[core]
        return send(here, here, feed_send.at[3], feed_recv.at[3], place.pair())

    def proj_copy(k):
        here = projs_ref.at[core, chip]
        return send(here, here, proj_send.at[k - 1], proj_recv.at[k - 1], place.plane(k))

    def proj_pair():
        here = projs_ref.at[core]
        return send(here, here, proj_send.at[3], proj_recv.at[3], place.pair())

    smalls = ((early_ref, early_in, early_all, 8), (late_ref, late_in, late_all, 4))
    hops = [place.plane(1), place.plane(2), place.depth(1), place.depth(2)]

    def small_pair(which):
        source, target, _, count = smalls[which]
        return send(
            source.at[1 - core], target, small_send.at[which, 0], small_recv.at[which, 0],
            place.pair(),
        )

    def small_hop(which, i):
        _, _, full_ref, _ = smalls[which]
        have = 1 << i
        return send(
            full_ref.at[core, pl.ds(0, have)], full_ref.at[core, pl.ds(have, have)],
            small_send.at[which, 1 + i], small_recv.at[which, 1 + i], hops[i],
        )

    def small_last(which):
        here = smalls[which][2].at[core]
        return send(
            here, here, small_send.at[which, 5], small_recv.at[which, 5], place.pair()
        )

    def small_begin(which):
        source, target, full_ref, _ = smalls[which]
        small_pair(which).wait_recv()
        full_ref[core, 0] = source[core] + target[...]
        small_hop(which, 0).start()

    def small_next(which, i):
        small_hop(which, i).wait_recv()
        (small_hop(which, i + 1) if i < 3 else small_last(which)).start()

    def start_group(g):
        pair_copy(g).wait_recv()
        mine = dout_ref.at[core] if g == 3 else made.at[g % 2, core]
        part = width // 16
        for a in range(4):
            for b in range(4):
                span = pl.ds((a * 4 + b) * part, part)
                total = (mine[span, :].astype(F32) + paired[g, span].astype(F32)).astype(BF16)
                if Z_FIRST[g]:
                    first_out[g, a, b] = total
                else:
                    first_out[g, b, a] = total
        for k in (1, 2, 3):
            first_copy(g, k).start()

    def go_on(g):
        for k in (1, 2, 3):
            first_copy(g, k).wait_recv()
        here = z if Z_FIRST[g] else chip
        second_out[g] = (
            first_out[g, here].astype(F32)
            + first_in[g, 0].astype(F32)
            + first_in[g, 1].astype(F32)
            + first_in[g, 2].astype(F32)
        ).astype(BF16)
        for k in (1, 2, 3):
            second_copy(g, k).start()

    def finish(g):
        for k in (1, 2, 3):
            second_copy(g, k).wait_recv()
        here = chip if Z_FIRST[g] else z
        projs_ref[core, chip, g] = (
            second_out[g, here].astype(F32)
            + second_in[g, 0].astype(F32)
            + second_in[g, 1].astype(F32)
            + second_in[g, 2].astype(F32)
        ).astype(BF16)

    @pl.when(step == 0)
    def _():
        for load in loads:
            load.start()
        meet(
            [place.pair()]
            + [place.plane(k) for k in (1, 2, 3)]
            + [place.depth(d) for d in (1, 2, 3)]
        )
        pair_copy(3).start()
        small_pair(0).start()
        for d in (1, 2, 3):
            z_copy(d).start()
        for k in (1, 2, 3):
            token_copy(0, k).start()
        own_tokens(0).start()
        gh_ref[...] = jnp.zeros_like(gh_ref)

    @pl.when(step >= 1)
    def _():
        for which in (0, 1):
            kv_copy(which, step - 1).start()

    @pl.when(step == 3)
    def _():
        pair_copy(0).start()

    @pl.when(step == 5)
    def _():
        pair_copy(1).start()

    @pl.when(step < 6)
    def _():
        keys = jnp.concatenate([k0_ref[...], k1_ref[...]], axis=0)
        values = jnp.concatenate([v0_ref[...], v1_ref[...]], axis=0)
        scaled = gm_ref[...].astype(F32) * rl_ref[...]
        products = scaled * mix_ref[...].astype(F32)
        scaled = scaled.astype(BF16)
        q_t = q_ref[...].T
        scaled_t = scaled.T
        dqs, dks, dvs = [], [], []
        for h in range(2):
            mine = (lane >= 64) if h else (lane < 64)
            inner = jnp.sum(jnp.where(mine, products, 0.0), axis=1, keepdims=True)
            grad_probs = mm_nt(jnp.where(mine, scaled, jnp.zeros_like(scaled)), values)
            grown = e_ref[h]
            grad_scores = (grown.astype(F32) * (grad_probs - inner) * scale).astype(BF16)
            dqs.append(mm(grad_scores, keys))
            dks.append(mm(q_t[64 * h : 64 * h + 64], grad_scores))
            dvs.append(mm(scaled_t[64 * h : 64 * h + 64], grown))
        dq_s[step] = jnp.where(lane < 64, dqs[0], dqs[1]).astype(BF16)
        dk = jnp.concatenate(dks, axis=0).T.astype(BF16)
        dv = jnp.concatenate(dvs, axis=0).T.astype(BF16)
        dk0_s[step] = dk[:rows]
        dk1_s[step] = dk[rows:]
        dv0_s[step] = dv[:rows]
        dv1_s[step] = dv[rows:]

    @pl.when(step == 0)
    def _():
        loads[0].wait()
        hidt_ref[...] = hid_ref[...].T

    @pl.when(step == 1)
    def _():
        loads[1].wait()
        loads[2].wait()
        start_group(3)
        small_begin(0)

    for i in range(4):

        @pl.when(step == 2 + i)
        def _(i=i):
            small_next(0, i)

    @pl.when(step == 3)
    def _():
        start_group(0)

    @pl.when(step == 5)
    def _():
        start_group(1)
        go_on(3)

    @pl.when(step == 6)
    def _():
        for d in (1, 2, 3):
            z_copy(d).wait_recv()
        for i in range(3):
            feeds_ref[core, chip, i] = (
                totals_ref[z, i].astype(F32)
                + z_in[0, i].astype(F32)
                + z_in[1, i].astype(F32)
                + z_in[2, i].astype(F32)
            ).astype(BF16)
        for k in (1, 2, 3):
            feed_copy(k).start()

    @pl.when((step >= 2) & (lax.rem(step, 2) == 0))
    def _():
        g = (step - 2) // 2
        slot = lax.rem(g, 2)
        cosine, sine = cos_ref[...], -sin_ref[...]
        for i in range(2):
            for which in (0, 1):
                kv_copy(which, 2 * g + i).wait_recv()

        def both(ref):
            return jnp.concatenate([ref[2 * g], ref[2 * g + 1]], axis=1).astype(F32)

        lows = []
        for part in range(3):
            span = pl.ds(pl.multiple_of(part * width + g * 256, 256), 256)
            if part == 2:
                grad = both(dv0_s) + both(dv_in)
            else:
                grad = both(dq_s) if part == 0 else both(dk0_s) + both(dk_in)
                gain = (qgain_ref, kgain_ref)[part][:, :256]
                raw = raw_ref[:, span].astype(F32)
                factor = lax.rsqrt(head_sum(raw * raw, head) * (1.0 / head) + NORM_EPSILON)
                normed = raw * factor
                turned = turn(grad, cosine, sine, head)
                late_ref[1, part : part + 1, pl.ds(pl.multiple_of(g * 256, 256), 256)] = col_sum(
                    turned * normed
                )
                turned = turned * gain
                mean = head_sum(turned * normed, head) * (1.0 / head)
                grad = factor * (turned - normed * mean)
            low = grad.astype(BF16)
            lows.append(low)
            total = col_sum(low.astype(F32))
            where = pl.ds(pl.multiple_of(g * 256, 256), 256)
            if part < 2:
                late_ref[0, 2 + part : 3 + part, where] = total
            else:
                late_ref[1, 2:3, where] = total
            gh_ref[...] += mm_nt(low, weight_ref[:, span])
        grads = jnp.concatenate(
            [low[:, 128 * c : 128 * c + 128] for c in range(2) for low in lows], axis=1
        )

        @pl.when(step == 6)
        def _():
            pair_copy(0).wait_send()

        half = width // 2
        made[slot, 0] = mm(hidt_ref[...], grads[:, :half]).astype(BF16)
        made[slot, 1] = mm(hidt_ref[...], grads[:, half:]).astype(BF16)

    @pl.when(step == 6)
    def _():
        pair_copy(2).start()
        go_on(0)
        go_on(1)
        loads[3].wait()
        loads[4].wait()
        grad_hidden = gh_ref[...]
        x = x_ref[...].astype(F32)
        factor = lax.rsqrt(jnp.mean(x * x, axis=-1, keepdims=True) + NORM_EPSILON)
        normed = x * factor
        late_ref[0, 0:1, :] = col_sum(grad_hidden)
        late_ref[0, 1:2, :] = col_sum(grad_hidden * normed)
        late_ref[1, 3:4, :] = jnp.zeros((1, width), F32)
        grad_normed = grad_hidden * (1.0 + mod_ref[:, width : 2 * width])
        back = factor * (
            grad_normed - normed * jnp.mean(grad_normed * normed, axis=-1, keepdims=True)
        )
        small_pair(1).start()
        start_group(2)
        gx_ref[...] = (gmid_ref[...] + back).astype(BF16)
        small_begin(1)
        for k in (1, 2, 3):
            token_copy(1, k).start()
        own_tokens(1).start()
        finish(3)
        small_next(1, 0)
        finish(0)
        finish(1)
        small_next(1, 1)
        go_on(2)
        small_next(1, 2)
        for k in (1, 2, 3):
            feed_copy(k).wait_recv()
        for k in (1, 2, 3):
            feed_copy(k).wait_send()
        feed_pair().start()
        finish(2)
        for k in (1, 2, 3):
            proj_copy(k).start()
        small_next(1, 3)
        for k in (1, 2, 3):
            proj_copy(k).wait()
        proj_pair().start()
        for which in (0, 1):
            own_tokens(which).wait()
            for k in (1, 2, 3):
                token_copy(which, k).wait()
            small_pair(which).wait_send()
            for i in range(4):
                small_hop(which, i).wait_send()
            small_last(which).wait()
            stores[which].start()
            for p in range(6):
                kv_copy(which, p).wait_send()
        for k in (1, 2, 3):
            z_copy(k).wait_send()
            for g in range(4):
                first_copy(g, k).wait_send()
                second_copy(g, k).wait_send()
        for g in (1, 2, 3):
            pair_copy(g).wait_send()
        feed_pair().wait()
        stores[2].start()
        proj_pair().wait()
        stores[3].start()
        for store in stores:
            store.wait()


def back_call(
    q, k0, k1, v0, v1, grad_mixed, mixed, inverse, grown, mod, qgain, kgain, cosine, sine, d_out,
    totals, early, raw, hidden, x, grad_middle, weight, output_rows, head,
):
    rows, width = q.shape
    half, part = width // 2, width // 16
    low = lambda *shape: jax.ShapeDtypeStruct(shape, BF16)
    pair = pl.BlockSpec((rows, 128), lambda s: (0, jnp.minimum(s, 5)))
    anywhere = pl.BlockSpec(memory_space=pl.ANY)
    small = [mod, qgain, kgain, cosine, sine, d_out, totals, early]
    out_shape = [
        low(4, rows // 4, width), low(4, rows // 4, width),
        low(2, 4, 3, width // 4, 256), low(2, 4, GROUPS, part, half),
        jax.ShapeDtypeStruct((2, 16, 8, width), F32), jax.ShapeDtypeStruct((2, 16, 4, width), F32),
    ]
    vmem = lambda *shape: pltpu.VMEM(shape, BF16)
    sems = lambda *shape: pltpu.SemaphoreType.DMA(shape)
    return pl.pallas_call(
        functools.partial(back_kernel, head),
        grid=(7,),
        in_specs=[pair] * 8
        + [pl.BlockSpec((2, rows, 2 * rows), lambda s: (jnp.minimum(s, 5), 0, 0))]
        + [once(each.shape) for each in small]
        + [anywhere] * 6,
        out_specs=[anywhere] * 6,
        out_shape=out_shape,
        scratch_shapes=[pltpu.VMEM(shape.shape, shape.dtype) for shape in out_shape[2:]]
        + [
            vmem(rows, 2 * width), vmem(rows, width), vmem(rows, width),
            pltpu.VMEM((rows, width), F32), vmem(width, 3 * width), vmem(width, rows),
            pltpu.VMEM((rows, width), F32), vmem(rows, width), pltpu.VMEM((2, 4, width), F32),
        ]
        + [vmem(6, rows, 128)] * 7
        + [
            vmem(2, 2, width, half), vmem(GROUPS, width, half),
            vmem(GROUPS, 4, 4, part, half), vmem(GROUPS, 3, 4, part, half),
            vmem(GROUPS, 4, part, half), vmem(GROUPS, 3, part, half),
            vmem(3, 3, width // 4, 256),
            pltpu.VMEM((8, width), F32), pltpu.VMEM((4, width), F32),
            sems(9), sems(2), sems(2, 6), sems(2, 6), sems(GROUPS), sems(GROUPS),
            sems(GROUPS, 3), sems(GROUPS, 3), sems(GROUPS, 3), sems(GROUPS, 3),
            sems(3), sems(3), sems(2, 3), sems(2, 3), sems(4), sems(4), sems(4), sems(4),
            sems(2, 6), sems(2, 6),
        ],
        compiler_params=pltpu.CompilerParams(
            vmem_limit_bytes=VMEM_LIMIT, collective_id=2, has_side_effects=True
        ),
        name="back",
    )(
        q, k0, k1, v0, v1, grad_mixed, mixed, inverse, grown, *small, raw, hidden, x, grad_middle,
        weight, output_rows,
    )


def finish_kernel(
    head, feeds_ref, projs_ref, early_ref, late_ref, modw_hbm,
    cond_ref, table_hbm, gmodw_hbm, gmodb_ref, ginw_hbm, ginb_ref, gqg_ref, gkg_ref, goutw_hbm,
    goutb_ref, gguw_hbm, ggub_ref, gdownw_hbm, gdownb_ref,
    modw_ref, table_ref, gmodw_ref, ginw_ref, goutw_ref, gguw_ref, gdownw_ref, acts_ref, load_sem,
    store_sem,
):
    place = Place()
    width = early_ref.shape[3]
    part = projs_ref.shape[3]
    load = pltpu.make_async_copy(modw_hbm, modw_ref, load_sem)
    load.start()
    stores = [
        pltpu.make_async_copy(source, target, store_sem.at[i])
        for i, (source, target) in enumerate(
            (
                (gguw_ref, gguw_hbm), (gdownw_ref, gdownw_hbm), (ginw_ref, ginw_hbm),
                (goutw_ref, goutw_hbm), (gmodw_ref, gmodw_hbm), (table_ref, table_hbm),
            )
        )
    ]
    for c in range(2):
        for chip in range(4):
            for f in range(2):
                for i in range(2):
                    col = (((c * 2 + f) * 2 + i) * 4 + chip) * 128
                    gguw_ref[:, col : col + 128] = feeds_ref[
                        c, chip, f, :, i * 128 : (i + 1) * 128
                    ].astype(F32)
    stores[0].start()
    for c in range(2):
        for chip in range(4):
            row = chip * 128 + c * 64
            for b in range(3):
                gdownw_ref[row : row + 64, b * 256 : (b + 1) * 256] = feeds_ref[
                    c, chip, 2, b * 64 : (b + 1) * 64, :
                ].astype(F32)
    stores[1].start()
    for c in range(2):
        for chip in range(4):
            row = chip * part
            for g in range(3):
                for q in range(3):
                    col = q * width + g * 256 + c * 128
                    ginw_ref[row : row + part, col : col + 128] = projs_ref[
                        c, chip, g, :, q * 128 : (q + 1) * 128
                    ].astype(F32)
            half = width // 2
            goutw_ref[row : row + part, c * half : (c + 1) * half] = projs_ref[c, chip, 3].astype(F32)
    stores[2].start()
    stores[3].start()

    vectors = [late_ref[0, :, 0, :], late_ref[0, :, 1, :]]
    vectors += [early_ref[0, :, j, :] for j in range(4)]
    lows = [vector.astype(BF16) for vector in vectors]
    conditions = early_ref[0, :, 6, :]
    labels = early_ref[0, :, 7, :]
    sig = 1.0 / (1.0 + jnp.exp(-conditions))
    acts = (conditions * sig).astype(BF16)
    size = acts_ref.shape[1]
    for z in range(4):

        @pl.when(place.z == z)
        def _(z=z):
            acts_ref[...] = acts[:, z * size : (z + 1) * size]

    mine = acts_ref[...]
    for j, low in enumerate(lows):
        gmodw_ref[:, j * width : (j + 1) * width] = mm_tn(mine, low)
    stores[4].start()
    early_sum = jnp.sum(early_ref[0], axis=0)
    gate_sum = jnp.sum(early_ref[1], axis=0)
    late_sum = jnp.sum(late_ref[0], axis=0)
    gain_sum = jnp.sum(late_ref[1], axis=0)
    mod_b = jnp.concatenate(
        [late_sum[0:1], late_sum[1:2]] + [early_sum[j : j + 1] for j in range(4)], axis=1
    )
    in_b = jnp.concatenate([late_sum[2:3], late_sum[3:4], gain_sum[2:3]], axis=1)
    gate_b = jnp.concatenate(
        [gate_sum[n // 6 : n // 6 + 1, (n % 6) * 128 : (n % 6) * 128 + 128] for n in range(32)],
        axis=1,
    )
    gains = sum(gain_sum[0:2, i : i + 128] for i in range(0, width, 128))
    gains = gains[:, :head] + gains[:, head:]
    pieces = (
        (gmodb_ref, mod_b), (ginb_ref, in_b), (gqg_ref, gains[0:1]), (gkg_ref, gains[1:2]),
        (goutb_ref, early_sum[4:5]), (ggub_ref, gate_b), (gdownb_ref, early_sum[5:6]),
    )
    for z in range(4):

        @pl.when(place.z == z)
        def _(z=z):
            for ref, row in pieces:
                size = row.shape[1] // 4
                ref[...] = row[:, z * size : (z + 1) * size]

    load.wait()
    grad = sum(mm_nt(low, modw_ref[:, j * width : (j + 1) * width]) for j, low in enumerate(lows))
    grad = grad * sig * (1.0 + conditions * (1.0 - sig))
    for k in range(4):
        cond_ref[pl.ds(place.flipped(k), 1), :] = grad[k : k + 1]
    classes = table_ref.shape[0]
    wide = -(-classes // 128) * 128
    column = lax.broadcasted_iota(jnp.int32, (1, wide), 1).astype(F32)
    onehot = jnp.where(labels[:, 0:1] == column, 1.0, 0.0).astype(BF16)
    high = grad.astype(BF16)
    rest = grad - high.astype(F32)
    middle = rest.astype(BF16)
    last = (rest - middle.astype(F32)).astype(BF16)
    table = mm_tn(
        jnp.concatenate([onehot] * 3, axis=0), jnp.concatenate([high, middle, last], axis=0)
    )
    table_ref[...] = table[:classes]
    stores[5].start()
    for store in stores:
        store.wait()


def finish_call(feeds, projs, early, late, weight, head, classes, hidden_width):
    width = weight.shape[0]
    rows = width // 4
    whole = lambda *shape: jax.ShapeDtypeStruct(shape, F32)
    anywhere = pl.BlockSpec(memory_space=pl.ANY)
    out_shape = [
        whole(4, width), whole(classes, width), whole(rows, 6 * width), whole(1, 6 * width // 4),
        whole(rows, 3 * width), whole(1, 3 * width // 4), whole(1, head // 4), whole(1, head // 4),
        whole(rows, width), whole(1, rows), whole(rows, 2 * hidden_width),
        whole(1, 2 * hidden_width // 4), whole(hidden_width // 4, width), whole(1, rows),
    ]
    big = (1, 2, 4, 8, 10, 12)
    return pl.pallas_call(
        functools.partial(finish_kernel, head),
        in_specs=[pl.BlockSpec(memory_space=pltpu.VMEM)] * 4 + [anywhere],
        out_specs=[
            anywhere if i in big else pl.BlockSpec(memory_space=pltpu.VMEM)
            for i in range(len(out_shape))
        ],
        out_shape=out_shape,
        scratch_shapes=[pltpu.VMEM(weight.shape, BF16)]
        + [pltpu.VMEM(out_shape[i].shape, F32) for i in big]
        + [pltpu.VMEM((16, rows), BF16), pltpu.SemaphoreType.DMA, pltpu.SemaphoreType.DMA((6,))],
        compiler_params=params(),
        name="finish",
    )(feeds, projs, early, late, weight)


def take(array_in, index, axis=0):
    return lax.dynamic_index_in_dim(array_in, index, axis, keepdims=False)


def add(*terms):
    return sum(term.astype(F32) for term in terms)


class Moves:
    def __init__(self, mesh):
        self.sizes = tuple(mesh.shape[name] for name in AXES)

    def flip(self, value, batch=0, gy=0, gx=0):
        nb, ny, nx = self.sizes
        pairs = []
        for b in range(nb):
            for y in range(ny):
                for x in range(nx):
                    here = (b * ny + y) * nx + x
                    there = ((b ^ batch) * ny + (y ^ gy)) * nx + (x ^ gx)
                    pairs.append((here, there))
        return lax.ppermute(value, AXES, pairs)

    def plane(self, value, k):
        return self.flip(value, gy=k >> 1, gx=2 * (k & 1))

    def pair(self, value):
        return self.flip(value, gx=1)

    def gather(self, value):
        value = value[None]
        value = jnp.concatenate([value, self.plane(value, 1)], axis=0)
        value = jnp.concatenate([value, self.plane(value, 2)], axis=0)
        bit = 1
        while bit < self.sizes[0]:
            value = jnp.concatenate([value, self.flip(value, batch=bit)], axis=0)
            bit *= 2
        return value


def regroup(parts, place):
    stacked = jnp.stack(parts)
    return jnp.stack([take(stacked, place ^ k) for k in range(len(parts))])


def body(mesh, *operands):
    (
        tokens, timesteps, labels, class_table, modulate_weight, modulate_bias, inproj_weight,
        inproj_bias, query_gain, key_gain, outproj_weight, outproj_bias, gate_up_weight,
        gate_up_bias, down_weight, down_bias, cotangent,
    ) = operands
    image_count, tile_rows, tile_cols, width = tokens.shape
    cells = tile_rows * tile_cols
    rows = image_count * cells
    head = query_gain.shape[0]
    heads = width // head
    hidden_width = down_weight.shape[0]
    class_count = class_table.shape[0]
    highest = lax.Precision.HIGHEST
    moves = Moves(mesh)
    nb, ny, nx = moves.sizes
    assert ny == 2 and nx == 4 and image_count == 4
    z, gy, gx = (lax.axis_index(name) for name in AXES)
    side, core = gx // 2, gx % 2
    place = 2 * gy + side

    tiles = tokens.reshape(image_count, cells, width)
    grads = cotangent.reshape(image_count, cells, width)

    def exchange(blocks):
        return [take(blocks, place)] + [
            moves.plane(take(blocks, place ^ k), k) for k in range(1, 4)
        ]

    x = jnp.concatenate(exchange(tiles), axis=0)

    half_width = width // 2
    step = take(timesteps, place).astype(F32)
    label = take(labels, place)
    rates = jnp.exp(-math.log(10000.0) * jnp.arange(half_width, dtype=F32) / half_width)
    features = jnp.concatenate([jnp.cos(step * rates), jnp.sin(step * rates)])
    condition = features + take(class_table, label).astype(F32)
    cond_act = jax.nn.silu(condition).astype(BF16)
    mod = modulation_call(
        jnp.broadcast_to(cond_act[None], (16, width)), modulate_weight, modulate_bias[None]
    )[:1]

    quarter = head // 4
    cell = jnp.arange(cells, dtype=jnp.int32)
    row_places, col_places = [], []
    for k in range(4):
        there = place ^ k
        row_places.append((there // 2) * tile_rows + cell // tile_cols)
        col_places.append((2 * (there % 2) + core) * tile_cols + cell % tile_cols)
    row_places = jnp.concatenate(row_places).astype(F32)[:, None]
    col_places = jnp.concatenate(col_places).astype(F32)[:, None]
    lane = jnp.arange(128, dtype=jnp.int32)
    turn_rate = jnp.exp(-math.log(10000.0) * (lane % quarter).astype(F32) / quarter)[None]
    angles = jnp.where((lane % head)[None] < head // 2, row_places, col_places) * turn_rate
    cosine = jnp.cos(angles)
    sine = jnp.where((lane % (2 * quarter))[None] < quarter, -1.0, 1.0) * jnp.sin(angles)
    qgain = jnp.tile(query_gain.astype(F32), heads)[None]
    kgain = jnp.tile(key_gain.astype(F32), heads)[None]

    hidden_one, q, k0, v0, raw = project_call(
        x, mod, inproj_weight, inproj_bias[None], qgain, kgain, cosine, sine, head
    )
    k1, v1 = moves.pair(k0), moves.pair(v0)
    dy = jnp.concatenate(exchange(grads), axis=0)
    mixed, grown, inverse = attend_call(q, k0, k1, v0, v1, head)
    attended, middle, hidden_two, hidden_two_t, grad_feed = middle_call(
        mixed, x, dy, mod, outproj_weight, outproj_bias[None]
    )

    unit = 256
    blocks = hidden_width // unit
    quick = nb == 4 and hidden_width == 16 * 128
    if quick:
        known = jnp.stack([condition, jnp.broadcast_to(label.astype(F32), (width,))])
        known = jnp.where(core == 0, known, 0.0)
        output_rows, grad_middle, grad_mixed, d_out, sums_two, totals = feed_turn_call(
            hidden_two, hidden_two_t, grad_feed, gate_up_weight, gate_up_bias[None], down_weight,
            middle, attended, dy, mixed, mod, outproj_weight, down_bias[None], known,
        )
        output, grad_tokens, feeds, projs, early, late = back_call(
            q, k0, k1, v0, v1, grad_mixed, mixed, inverse, grown, mod, qgain, kgain, cosine, sine,
            d_out, totals, sums_two, raw, hidden_one, x, grad_middle, inproj_weight, output_rows,
            head,
        )
        (
            grad_condition, grad_table, grad_mod_w, grad_mod_b, grad_in_w, grad_in_b, grad_q_gain,
            grad_k_gain, grad_out_w, grad_out_b, grad_gu_w, grad_gu_b, grad_down_w, grad_down_b,
        ) = finish_call(
            feeds, projs, early, late, modulate_weight, head, class_count, hidden_width
        )
        return (
            output.reshape(tokens.shape), grad_tokens.reshape(tokens.shape), grad_condition,
            grad_table, grad_mod_w, grad_mod_b[0], grad_in_w, grad_in_b[0], grad_q_gain[0],
            grad_k_gain[0], grad_out_w, grad_out_b[0], grad_gu_w, grad_gu_b[0], grad_down_w,
            grad_down_b[0],
        )
    else:
        feed, grad_hidden, d_down, d_gate, d_bias = feed_call(
            hidden_two, hidden_two_t, grad_feed, gate_up_weight, gate_up_bias[None], down_weight,
            jnp.zeros((rows, width), F32), jnp.zeros((rows, width), F32), 0, 1, unit,
        )
        output_rows, grad_middle, grad_mixed, d_out, sums_two = turn_call(
            feed, grad_hidden, middle, attended, dy, grad_feed, mixed, mod, outproj_weight,
            down_bias[None],
        )
        gate_bias = d_bias.reshape(blocks, 2, unit).transpose(1, 0, 2)
        dq, dk0, dk1, dv0, dv1 = attend_back_call(
            q, k0, k1, v0, v1, grown, grad_mixed, mixed, inverse, head
        )
        dk1, dv1 = moves.pair(dk1), moves.pair(dv1)
        grad_x, d_in, sums_one, in_bias = project_back_call(
            dq, dk0, dk1, dv0, dv1, raw, hidden_one, x, grad_middle, mod, inproj_weight, qgain,
            kgain, cosine, sine, head,
        )

        def give_back(rows_out):
            parts = rows_out.reshape(4, cells, width)
            got = [parts[0]] + [moves.plane(parts[k], k) for k in range(1, 4)]
            return regroup(got, place).reshape(tokens.shape)

        output = give_back(output_rows)
        grad_tokens = give_back(grad_x)
        slice_rows = width // nb

        def scatter(d):
            d = lax.psum_scatter(d.astype(BF16), "batch", scatter_dimension=0, tiled=True)
            return lax.psum(d, ("gy", "gx")).astype(F32)

        def joined(d):
            return jnp.concatenate([d[0], d[1]], axis=1)

        grad_down_w = scatter(d_down.reshape(hidden_width, width))
        grad_gu_w = scatter(
            d_gate.transpose(2, 1, 0, 3).reshape(width, 2 * hidden_width)
        )
        grad_out_w = scatter(joined(d_out))
        grad_in_w = scatter(joined(d_in))
        gain_sums = sums_one[2:4].reshape(2, heads, head).sum(axis=1)
        early = jnp.concatenate([sums_two[:6].reshape(-1), gate_bias.reshape(-1)])
        late = jnp.concatenate(
            [sums_one[:2].reshape(-1), in_bias.reshape(-1), gain_sums.reshape(-1)]
        )

    def everywhere(vector):
        halves = vector.reshape(2, -1)
        half = add(take(halves, core), moves.pair(take(halves, 1 - core)))
        half = moves.gather(half)
        both = regroup([half, moves.pair(half)], core)
        return both.transpose(1, 0, 2).reshape(half.shape[0], -1)

    known = jnp.concatenate([condition, jnp.broadcast_to(label.astype(F32), (128,))])
    known = moves.gather(known)
    early, late = everywhere(early), everywhere(late)
    grad_modulation = jnp.concatenate([late[:, : 2 * width], early[:, : 4 * width]], axis=1)
    conditions = known[:, :width]
    all_labels = known[:, width].astype(jnp.int32)
    cond_acts = jax.nn.silu(conditions).astype(BF16)
    my_acts = lax.dynamic_slice_in_dim(cond_acts, z * slice_rows, slice_rows, axis=1)
    low_mod = grad_modulation.astype(BF16)
    grad_mod_w = mm_tn(my_acts, low_mod)
    wide = 6 * width
    grad_mod_b = lax.dynamic_slice_in_dim(
        jnp.sum(grad_modulation, axis=0), z * (wide // nb), wide // nb, axis=0
    )
    grad_cond_act = mm_nt(low_mod, modulate_weight)
    sig = jax.nn.sigmoid(conditions)
    grad_conditions = grad_cond_act * sig * (1.0 + conditions * (1.0 - sig))
    grad_condition = regroup([grad_conditions[k] for k in range(4)], place)
    onehot = (all_labels[:, None] == jnp.arange(class_count, dtype=jnp.int32)[None, :]).astype(F32)
    grad_table = lax.dot_general(
        onehot, grad_conditions, (((0,), (0,)), ((), ())), precision=highest,
        preferred_element_type=F32,
    )

    early_sum = jnp.sum(early, axis=0)
    late_sum = jnp.sum(late, axis=0)

    def part(vector, start, size):
        return lax.dynamic_slice_in_dim(vector, start + z * (size // nb), size // nb, axis=0)

    grad_out_b = part(early_sum, 4 * width, width)
    grad_down_b = part(early_sum, 5 * width, width)
    grad_gu_b = part(early_sum, 6 * width, 2 * hidden_width)
    grad_in_b = part(late_sum, 2 * width, 3 * width)
    grad_q_gain = part(late_sum, 5 * width, head)
    grad_k_gain = part(late_sum, 5 * width + head, head)
    return (
        output, grad_tokens, grad_condition, grad_table, grad_mod_w, grad_mod_b, grad_in_w,
        grad_in_b, grad_q_gain, grad_k_gain, grad_out_w, grad_out_b, grad_gu_w, grad_gu_b,
        grad_down_w, grad_down_b,
    )


def solution(mesh):
    grid = P("batch", "gy", "gx", None)
    by_batch = P("batch")
    rows = P("batch", None)
    placed = (grid, by_batch, by_batch) + (P(),) * 13 + (grid,)
    return jax.shard_map(
        functools.partial(body, mesh),
        mesh=mesh,
        in_specs=placed,
        out_specs=(
            grid, grid, rows, P(), rows, by_batch, rows, by_batch, by_batch, by_batch, rows,
            by_batch, rows, by_batch, rows, by_batch,
        ),
        check_vma=False,
    )
```

```python
import functools
import math

import jax
import jax.numpy as jnp
from jax import lax
from jax.experimental import pallas as pl
from jax.experimental.pallas import tpu as pltpu
from jax.sharding import PartitionSpec as P

NORM_EPSILON = 1e-06
AXES = ("batch", "gy", "gx")
BF16 = jnp.bfloat16
F32 = jnp.float32
VMEM_LIMIT = 60 * 1024 * 1024


def mm(left, right):
    return lax.dot_general(left, right, (((1,), (0,)), ((), ())), preferred_element_type=F32)


def mm_nt(left, right):
    return lax.dot_general(left, right, (((1,), (1,)), ((), ())), preferred_element_type=F32)


def mm_tn(left, right):
    return lax.dot_general(left, right, (((0,), (0,)), ((), ())), preferred_element_type=F32)


def params():
    return pltpu.CompilerParams(vmem_limit_bytes=VMEM_LIMIT)


def full(shape):
    return pl.BlockSpec(shape, lambda *_: (0,) * len(shape))


def col_sum(values):
    return jnp.sum(values, axis=0, keepdims=True)


def modulation_kernel(act_ref, weight_ref, bias_ref, out_ref):
    out_ref[...] = mm(act_ref[...], weight_ref[...]) + bias_ref[...].astype(F32)


def modulation_call(act, weight, bias):
    rows, width = act.shape
    wide = weight.shape[1]
    return pl.pallas_call(
        modulation_kernel,
        grid=(wide // width,),
        in_specs=[
            full((rows, width)),
            pl.BlockSpec((width, width), lambda j: (0, j)),
            pl.BlockSpec((1, width), lambda j: (0, j)),
        ],
        out_specs=pl.BlockSpec((rows, width), lambda j: (0, j)),
        out_shape=jax.ShapeDtypeStruct((rows, wide), F32),
        compiler_params=params(),
        name="modulation",
    )(act, weight, bias)


def head_sum(values, head):
    width = 256
    row = lax.broadcasted_iota(jnp.int32, (width, width), 0) // head
    col = lax.broadcasted_iota(jnp.int32, (width, width), 1) // head
    ones = jnp.where(row == col, 1.0, 0.0).astype(BF16)
    parts = [
        mm(values[:, i : i + width].astype(BF16), ones) for i in range(0, values.shape[1], width)
    ]
    return jnp.concatenate(parts, axis=1)


def turn(values, cosine, sine, head):
    quarter = head // 4
    lane = lax.broadcasted_iota(jnp.int32, (1, 128), 1)
    first = (lane % (2 * quarter)) < quarter
    parts = []
    for i in range(0, values.shape[1], 128):
        part = values[:, i : i + 128]
        partner = jnp.where(
            first, pltpu.roll(part, 128 - quarter, 1), pltpu.roll(part, quarter, 1)
        )
        parts.append(part * cosine + partner * sine)
    return jnp.concatenate(parts, axis=1)


def project_kernel(
    head, x_ref, mod_ref, weight_ref, bias_ref, qgain_ref, kgain_ref, cos_ref, sin_ref,
    hid_ref, q_ref, k_ref, v_ref, raw_ref,
):
    width = x_ref.shape[1]
    x = x_ref[...].astype(F32)
    normed = x * lax.rsqrt(jnp.mean(x * x, axis=-1, keepdims=True) + NORM_EPSILON)
    hidden = (normed * (1.0 + mod_ref[:, width : 2 * width]) + mod_ref[:, :width]).astype(BF16)
    hid_ref[...] = hidden
    for part, (out_ref, gain_ref) in enumerate(((q_ref, qgain_ref), (k_ref, kgain_ref))):
        raw = mm(hidden, weight_ref[:, part * width : (part + 1) * width])
        raw = raw + bias_ref[:, part * width : (part + 1) * width].astype(F32)
        raw_ref[:, part * width : (part + 1) * width] = raw.astype(BF16)
        factor = lax.rsqrt(head_sum(raw * raw, head) * (1.0 / head) + NORM_EPSILON)
        scaled = raw * factor * gain_ref[...]
        out_ref[...] = turn(scaled, cos_ref[...], sin_ref[...], head).astype(BF16)
    value = mm(hidden, weight_ref[:, 2 * width :]) + bias_ref[:, 2 * width :].astype(F32)
    v_ref[...] = value.astype(BF16)


def project_call(x, mod, weight, bias, qgain, kgain, cosine, sine, head):
    rows, width = x.shape
    block = rows // 2
    by_row = lambda wide: pl.BlockSpec((block, wide), lambda i: (i, 0))
    shape = jax.ShapeDtypeStruct((rows, width), BF16)
    return pl.pallas_call(
        functools.partial(project_kernel, head),
        grid=(2,),
        in_specs=[
            by_row(width),
            full(mod.shape),
            full(weight.shape),
            full(bias.shape),
            full(qgain.shape),
            full(kgain.shape),
            by_row(128),
            by_row(128),
        ],
        out_specs=[by_row(width)] * 4 + [by_row(2 * width)],
        out_shape=[shape] * 4 + [jax.ShapeDtypeStruct((rows, 2 * width), BF16)],
        compiler_params=params(),
        name="project",
    )(x, mod, weight, bias, qgain, kgain, cosine, sine)


def attend_kernel(scale, q_ref, k0_ref, k1_ref, v0_ref, v1_ref, mix_ref, e_ref, rl_ref):
    lane = lax.broadcasted_iota(jnp.int32, (1, 128), 1)
    q = q_ref[...]
    keys = jnp.concatenate([k0_ref[...], k1_ref[...]], axis=0)
    values = jnp.concatenate([v0_ref[...], v1_ref[...]], axis=0)
    values = jnp.concatenate([values, jnp.ones_like(values)], axis=1)
    outs = []
    for h in range(2):
        mine = (lane >= 64) if h else (lane < 64)
        scores = mm_nt(jnp.where(mine, q, jnp.zeros_like(q)), keys)
        grown = jnp.exp(scores * scale).astype(BF16)
        e_ref[h] = grown
        outs.append(mm(grown, values))
    inverse = 1.0 / jnp.where(lane < 64, outs[0][:, 128:], outs[1][:, 128:])
    mix_ref[...] = (jnp.where(lane < 64, outs[0][:, :128], outs[1][:, :128]) * inverse).astype(BF16)
    rl_ref[...] = inverse


def attend_call(q, k0, k1, v0, v1, head):
    rows, width = q.shape
    pair = pl.BlockSpec((rows, 128), lambda p: (0, p))
    return pl.pallas_call(
        functools.partial(attend_kernel, head**-0.5),
        grid=(width // 128,),
        in_specs=[pair] * 5,
        out_specs=[pair, pl.BlockSpec((2, rows, 2 * rows), lambda p: (p, 0, 0)), pair],
        out_shape=[
            jax.ShapeDtypeStruct((rows, width), BF16),
            jax.ShapeDtypeStruct((width // head, rows, 2 * rows), BF16),
            jax.ShapeDtypeStruct((rows, width), F32),
        ],
        compiler_params=params(),
        name="attend",
    )(q, k0, k1, v0, v1)


def attend_back_kernel(
    scale, q_ref, k0_ref, k1_ref, v0_ref, v1_ref, e_ref, gm_ref, mix_ref, rl_ref,
    dq_ref, dk0_ref, dk1_ref, dv0_ref, dv1_ref,
):
    rows = q_ref.shape[0]
    lane = lax.broadcasted_iota(jnp.int32, (1, 128), 1)
    keys = jnp.concatenate([k0_ref[...], k1_ref[...]], axis=0)
    values = jnp.concatenate([v0_ref[...], v1_ref[...]], axis=0)
    scaled = gm_ref[...].astype(F32) * rl_ref[...]
    products = scaled * mix_ref[...].astype(F32)
    scaled = scaled.astype(BF16)
    q_t = q_ref[...].T
    scaled_t = scaled.T
    dqs, dks, dvs = [], [], []
    for h in range(2):
        mine = (lane >= 64) if h else (lane < 64)
        inner = jnp.sum(jnp.where(mine, products, 0.0), axis=1, keepdims=True)
        grad_probs = mm_nt(jnp.where(mine, scaled, jnp.zeros_like(scaled)), values)
        grown = e_ref[h]
        grad_scores = (grown.astype(F32) * (grad_probs - inner) * scale).astype(BF16)
        dqs.append(mm(grad_scores, keys))
        dks.append(mm(q_t[64 * h : 64 * h + 64], grad_scores))
        dvs.append(mm(scaled_t[64 * h : 64 * h + 64], grown))
    dq_ref[...] = jnp.where(lane < 64, dqs[0], dqs[1]).astype(BF16)
    dk = jnp.concatenate(dks, axis=0).T.astype(BF16)
    dv = jnp.concatenate(dvs, axis=0).T.astype(BF16)
    dk0_ref[...] = dk[:rows]
    dk1_ref[...] = dk[rows:]
    dv0_ref[...] = dv[:rows]
    dv1_ref[...] = dv[rows:]


def attend_back_call(q, k0, k1, v0, v1, grown, grad_mixed, mixed, inverse, head):
    rows, width = q.shape
    pair = pl.BlockSpec((rows, 128), lambda p: (0, p))
    return pl.pallas_call(
        functools.partial(attend_back_kernel, head**-0.5),
        grid=(width // 128,),
        in_specs=[pair] * 5
        + [pl.BlockSpec((2, rows, 2 * rows), lambda p: (p, 0, 0))]
        + [pair] * 3,
        out_specs=[pair] * 5,
        out_shape=[jax.ShapeDtypeStruct((rows, width), BF16)] * 5,
        compiler_params=params(),
        name="attend_back",
    )(q, k0, k1, v0, v1, grown, grad_mixed, mixed, inverse)


def middle_kernel(
    mix_ref, x_ref, dy_ref, mod_ref, weight_ref, bias_ref, att_ref, mid_ref, h2_ref, h2t_ref, gf_ref
):
    width = x_ref.shape[1]
    attended = mm(mix_ref[...], weight_ref[...]) + bias_ref[...].astype(F32)
    middle = x_ref[...].astype(F32) + mod_ref[:, 2 * width : 3 * width] * attended
    normed = middle * lax.rsqrt(jnp.mean(middle * middle, axis=-1, keepdims=True) + NORM_EPSILON)
    hidden = normed * (1.0 + mod_ref[:, 4 * width : 5 * width]) + mod_ref[:, 3 * width : 4 * width]
    hidden = hidden.astype(BF16)
    att_ref[...] = attended.astype(BF16)
    mid_ref[...] = middle
    h2_ref[...] = hidden
    h2t_ref[...] = hidden.T
    gf_ref[...] = (mod_ref[:, 5 * width :] * dy_ref[...].astype(F32)).astype(BF16)


def middle_call(mixed, x, dy, mod, weight, bias, bias_at=0):
    rows, width = x.shape
    block = rows // 2
    by_row = pl.BlockSpec((block, width), lambda i: (i, 0))
    low = jax.ShapeDtypeStruct((rows, width), BF16)
    return pl.pallas_call(
        middle_kernel,
        grid=(2,),
        in_specs=[by_row] * 3
        + [full(mod.shape), full(weight.shape), pl.BlockSpec((1, width), lambda i: (0, bias_at))],
        out_specs=[by_row] * 3 + [pl.BlockSpec((width, block), lambda i: (0, i)), by_row],
        out_shape=[low, jax.ShapeDtypeStruct((rows, width), F32), low]
        + [jax.ShapeDtypeStruct((width, rows), BF16), low],
        compiler_params=params(),
        name="middle",
    )(mixed, x, dy, mod, weight, bias)


def feed_kernel(
    h2_ref, h2t_ref, gf_ref, wg_ref, wu_ref, bg_ref, bu_ref, wd_ref, feed_in_ref, gh_in_ref,
    feed_ref, gh_ref, dd_ref, dg_ref, db_ref,
):
    @pl.when(pl.program_id(0) == 0)
    def _():
        feed_ref[...] = feed_in_ref[...]
        gh_ref[...] = gh_in_ref[...]

    hidden = h2_ref[...]
    grad_feed = gf_ref[...]
    gate = mm(hidden, wg_ref[...]) + bg_ref[...].astype(F32)
    up = mm(hidden, wu_ref[...]) + bu_ref[...].astype(F32)
    grad_product = mm_nt(grad_feed, wd_ref[...])
    sig = 1.0 / (1.0 + jnp.exp(-gate))
    active = gate * sig
    product = (active * up).astype(BF16)
    grad_gate = (grad_product * up * sig * (1.0 + gate * (1.0 - sig))).astype(BF16)
    grad_up = (grad_product * active).astype(BF16)
    dd_ref[...] = mm_tn(product, grad_feed).astype(BF16)
    dg_ref[0] = mm(h2t_ref[...], grad_gate).astype(BF16)
    dg_ref[1] = mm(h2t_ref[...], grad_up).astype(BF16)
    db_ref[0] = col_sum(grad_gate.astype(F32))
    db_ref[1] = col_sum(grad_up.astype(F32))
    feed_ref[...] += mm(product, wd_ref[...])
    gh_ref[...] += mm_nt(grad_gate, wg_ref[...]) + mm_nt(grad_up, wu_ref[...])


def feed_call(hidden, hidden_t, grad_feed, weight, bias, down, feed, grad_hidden, first, step, unit):
    rows, width = hidden.shape
    blocks = down.shape[0] // unit
    steps = len(range(first, blocks, step))
    pick = lambda s: first + step * s
    acc = jax.ShapeDtypeStruct((rows, width), F32)
    return pl.pallas_call(
        feed_kernel,
        grid=(steps,),
        in_specs=[
            full((rows, width)),
            full((width, rows)),
            full((rows, width)),
            pl.BlockSpec((width, unit), lambda s: (0, pick(s))),
            pl.BlockSpec((width, unit), lambda s: (0, blocks + pick(s))),
            pl.BlockSpec((1, unit), lambda s: (0, pick(s))),
            pl.BlockSpec((1, unit), lambda s: (0, blocks + pick(s))),
            pl.BlockSpec((unit, width), lambda s: (pick(s), 0)),
            full((rows, width)),
            full((rows, width)),
        ],
        out_specs=[
            full((rows, width)),
            full((rows, width)),
            pl.BlockSpec((None, unit, width), lambda s: (s, 0, 0)),
            pl.BlockSpec((None, 2, width, unit), lambda s: (s, 0, 0, 0)),
            pl.BlockSpec((None, 2, 1, unit), lambda s: (s, 0, 0, 0)),
        ],
        out_shape=[
            acc,
            acc,
            jax.ShapeDtypeStruct((steps, unit, width), BF16),
            jax.ShapeDtypeStruct((steps, 2, width, unit), BF16),
            jax.ShapeDtypeStruct((steps, 2, 1, unit), F32),
        ],
        compiler_params=params(),
        name="feed",
    )(hidden, hidden_t, grad_feed, weight, weight, bias, bias, down, feed, grad_hidden)


def turn_kernel(
    feed_ref, gh_ref, mid_ref, att_ref, dy_ref, gf_ref, mix_ref, mod_ref, weight_ref, dbias_ref,
    out_ref, gmid_ref, gmix_ref, dw_ref, sums_ref,
):
    width = mid_ref.shape[1]
    half = width // 2
    dy = dy_ref[...].astype(F32)
    feed = feed_ref[...] + dbias_ref[...].astype(F32)
    middle = mid_ref[...]
    out_ref[...] = (middle + mod_ref[:, 5 * width :] * feed).astype(BF16)
    factor = lax.rsqrt(jnp.mean(middle * middle, axis=-1, keepdims=True) + NORM_EPSILON)
    normed = middle * factor
    grad_hidden = gh_ref[...]
    product = grad_hidden * normed
    grad_normed = grad_hidden * (1.0 + mod_ref[:, 4 * width : 5 * width])
    back = factor * (
        grad_normed - normed * jnp.mean(grad_normed * normed, axis=-1, keepdims=True)
    )
    grad_middle = dy + back
    gmid_ref[...] = grad_middle
    grad_attended = (mod_ref[:, 2 * width : 3 * width] * grad_middle).astype(BF16)
    sums_ref[0:1, :] = col_sum(grad_middle * att_ref[...].astype(F32))
    sums_ref[1:2, :] = col_sum(grad_hidden)
    sums_ref[2:3, :] = col_sum(product)
    sums_ref[3:4, :] = col_sum(dy * feed)
    sums_ref[4:5, :] = col_sum(grad_attended.astype(F32))
    sums_ref[5:6, :] = col_sum(gf_ref[...].astype(F32))
    sums_ref[6:8, :] = jnp.zeros((2, width), F32)
    gmix_ref[...] = mm_nt(grad_attended, weight_ref[...]).astype(BF16)
    mixed_t = mix_ref[...].T
    dw_ref[0] = mm(mixed_t, grad_attended[:, :half]).astype(BF16)
    dw_ref[1] = mm(mixed_t, grad_attended[:, half:]).astype(BF16)


def turn_call(feed, grad_hidden, middle, attended, dy, grad_feed, mixed, mod, weight, down_bias):
    rows, width = middle.shape
    low = jax.ShapeDtypeStruct((rows, width), BF16)
    return pl.pallas_call(
        turn_kernel,
        out_shape=[
            low,
            jax.ShapeDtypeStruct((rows, width), F32),
            low,
            jax.ShapeDtypeStruct((2, width, width // 2), BF16),
            jax.ShapeDtypeStruct((8, width), F32),
        ],
        compiler_params=params(),
        name="turn",
    )(feed, grad_hidden, middle, attended, dy, grad_feed, mixed, mod, weight, down_bias)


def project_back_kernel(
    head, dq_ref, dk0_ref, dk1_ref, dv0_ref, dv1_ref, raw_ref, hid_ref, x_ref, gmid_ref, mod_ref,
    weight_ref, qgain_ref, kgain_ref, cos_ref, sin_ref,
    gx_ref, dw_ref, sums_ref, bias_ref, proj_ref,
):
    width = x_ref.shape[1]
    cosine, sine = cos_ref[...], -sin_ref[...]
    for part in range(3):
        span = slice(part * width, (part + 1) * width)
        if part == 2:
            grad = dv0_ref[...].astype(F32) + dv1_ref[...].astype(F32)
        else:
            grad = dq_ref[...].astype(F32)
            if part == 1:
                grad = dk0_ref[...].astype(F32) + dk1_ref[...].astype(F32)
            gain = (qgain_ref, kgain_ref)[part][...]
            raw = raw_ref[:, span].astype(F32)
            factor = lax.rsqrt(head_sum(raw * raw, head) * (1.0 / head) + NORM_EPSILON)
            normed = raw * factor
            turned = turn(grad, cosine, sine, head)
            sums_ref[2 + part : 3 + part, :] = col_sum(turned * normed)
            turned = turned * gain
            mean = head_sum(turned * normed, head) * (1.0 / head)
            grad = factor * (turned - normed * mean)
        low = grad.astype(BF16)
        proj_ref[:, span] = low
        bias_ref[:, span] = col_sum(low.astype(F32))
    hidden_t = hid_ref[...].T
    half = 3 * width // 2
    dw_ref[0] = mm(hidden_t, proj_ref[:, :half]).astype(BF16)
    dw_ref[1] = mm(hidden_t, proj_ref[:, half:]).astype(BF16)
    grad_hidden = mm_nt(proj_ref[...], weight_ref[...])
    x = x_ref[...].astype(F32)
    factor = lax.rsqrt(jnp.mean(x * x, axis=-1, keepdims=True) + NORM_EPSILON)
    normed = x * factor
    sums_ref[0:1, :] = col_sum(grad_hidden)
    sums_ref[1:2, :] = col_sum(grad_hidden * normed)
    sums_ref[4:8, :] = jnp.zeros((4, width), F32)
    grad_normed = grad_hidden * (1.0 + mod_ref[:, width : 2 * width])
    back = factor * (
        grad_normed - normed * jnp.mean(grad_normed * normed, axis=-1, keepdims=True)
    )
    gx_ref[...] = (gmid_ref[...] + back).astype(BF16)


def project_back_call(
    dq, dk0, dk1, dv0, dv1, raw, hidden, x, grad_middle, mod, weight, qgain, kgain, cosine, sine, head
):
    rows, width = x.shape
    return pl.pallas_call(
        functools.partial(project_back_kernel, head),
        out_shape=[
            jax.ShapeDtypeStruct((rows, width), BF16),
            jax.ShapeDtypeStruct((2, width, 3 * width // 2), BF16),
            jax.ShapeDtypeStruct((8, width), F32),
            jax.ShapeDtypeStruct((1, 3 * width), F32),
        ],
        scratch_shapes=[pltpu.VMEM((rows, 3 * width), BF16)],
        compiler_params=params(),
        name="project_back",
    )(dq, dk0, dk1, dv0, dv1, raw, hidden, x, grad_middle, mod, weight, qgain, kgain, cosine, sine)


class Place:
    def __init__(self):
        self.z, self.gy, self.gx = (lax.axis_index(name) for name in AXES)
        self.core = lax.rem(self.gx, 2)
        self.side = self.gx // 2
        self.chip = 2 * self.gy + self.side

    def flipped(self, k):
        return 2 * lax.rem(self.gy + k // 2, 2) + lax.rem(self.side + lax.rem(k, 2), 2)

    def pair(self):
        return {"gx": self.gx + 1 - 2 * self.core}

    def plane(self, k):
        device = {}
        if k & 2:
            device["gy"] = 1 - self.gy
        if k & 1:
            device["gx"] = lax.rem(self.gx + 2, 4)
        return device

    def depth(self, d):
        return {"batch": self.flipped_z(d)}

    def flipped_z(self, d):
        return {1: self.z + 1 - 2 * lax.rem(self.z, 2), 2: lax.rem(self.z + 2, 4), 3: 3 - self.z}[d]


def meet(devices):
    barrier = pltpu.get_barrier_semaphore()
    for device in devices:
        pl.semaphore_signal(barrier, inc=1, device_id=device, device_id_type=pl.DeviceIdType.MESH)
    pl.semaphore_wait(barrier, len(devices))


def send(source, target, send_sem, recv_sem, device):
    return pltpu.make_async_remote_copy(
        src_ref=source, dst_ref=target, send_sem=send_sem, recv_sem=recv_sem, device_id=device,
        device_id_type=pl.DeviceIdType.MESH,
    )


def feed_order(step):
    owner = jnp.where(
        step < 2, 3, jnp.where((step == 2) | (step == 5), 2, jnp.where(step < 5, 1, 0))
    )
    return owner, lax.rem(step, 2)


def feed_block(step, i):
    step = jnp.minimum(step, 7)
    owner, half = feed_order(step)
    return (2 * half + i) * 4 + Place().flipped(owner)


def feed_turn_kernel(
    h2_ref, h2t_ref, gf_ref, wg0, wg1, wu0, wu1, bg0, bg1, bu0, bu1, wd0, wd1,
    mid_ref, att_ref, dy_ref, mix_ref, mod_ref, weight_ref, dbias_ref, known_ref,
    out_ref, gmid_ref, gmix_ref, dw_ref, sums_ref, total_ref,
    feed_ref, gh_ref, bias_ref, made, paired, near, pair_send, pair_recv, near_send, near_recv,
):
    place = Place()
    core = place.core
    step = pl.program_id(0)
    slot = lax.rem(step, 2)
    width = h2_ref.shape[1]
    unit = 128
    g_rows = width

    @pl.when(step == 0)
    def _():
        feed_ref[...] = jnp.zeros_like(feed_ref)
        sums_ref[1] = jnp.zeros((8, width), F32)
        gh_ref[...] = jnp.zeros_like(gh_ref)
        meet([place.pair(), place.plane(1), place.plane(2)])

    def pair_copy(of):
        return send(
            made.at[lax.rem(of, 2), 1 - core], paired.at[of], pair_send.at[lax.rem(of, 2)],
            pair_recv.at[of], place.pair(),
        )

    def near_copy(of, k):
        return send(paired.at[of], near.at[of], near_send.at[of], near_recv.at[of], place.plane(k))

    @pl.when(step >= 1)
    def _():
        pair_copy(step - 1).start()

    @pl.when(step < 8)
    def _():
        owner, half = feed_order(step)
        hidden = h2_ref[...]
        grad_feed = gf_ref[...]
        wg = jnp.concatenate([wg0[...], wg1[...]], axis=1)
        wu = jnp.concatenate([wu0[...], wu1[...]], axis=1)
        wd = jnp.concatenate([wd0[...], wd1[...]], axis=0)
        gate = mm(hidden, wg) + jnp.concatenate([bg0[...], bg1[...]], axis=1).astype(F32)
        up = mm(hidden, wu) + jnp.concatenate([bu0[...], bu1[...]], axis=1).astype(F32)
        grad_product = mm_nt(grad_feed, wd)
        sig = 1.0 / (1.0 + jnp.exp(-gate))
        active = gate * sig
        product = (active * up).astype(BF16)
        grad_gate = (grad_product * up * sig * (1.0 + gate * (1.0 - sig))).astype(BF16)
        grad_up = (grad_product * active).astype(BF16)
        feed_ref[...] += mm(product, wd)
        gh_ref[...] += mm_nt(grad_gate, wg) + mm_nt(grad_up, wu)
        for e, grad in enumerate((grad_gate, grad_up)):
            total = col_sum(grad.astype(F32))
            for i in range(2):
                row = 16 * e + (2 * half + i) * 4 + place.flipped(owner)
                bias_ref[pl.ds(row, 1), :] = total[:, i * unit : (i + 1) * unit]

        @pl.when(step >= 2)
        def _():
            pair_copy(step - 2).wait_send()

        for e, grad in enumerate((grad_gate, grad_up)):
            made[slot, e, :g_rows] = mm(h2t_ref[...], grad).astype(BF16)
        product_t = product.T
        for b in range(3):
            d = mm(product_t, grad_feed[:, 256 * b : 256 * b + 256]).astype(BF16)
            for i in range(2):
                for c in range(2):
                    made[slot, c, pl.ds(g_rows + b * 128 + i * 64, 64)] = d[
                        i * 128 + c * 64 : i * 128 + c * 64 + 64
                    ]

    @pl.when(step >= 1)
    def _():
        of = step - 1
        copy = pair_copy(of)
        copy.wait_recv()
        late = (of == 4) | (of == 5)

        @pl.when(jnp.logical_not(late))
        def _():
            paired[of] = (made[1 - slot, core].astype(F32) + paired[of].astype(F32)).astype(BF16)

        @pl.when(late)
        def _():
            near_copy(of - 4, 1).wait_recv()
            paired[of] = (
                made[1 - slot, core].astype(F32)
                + paired[of].astype(F32)
                + near[of - 4].astype(F32)
            ).astype(BF16)

        @pl.when((of == 0) | (of == 2) | (of == 5))
        def _():
            near_copy(of, 2).start()

        @pl.when((of == 1) | (of == 3) | (of == 4))
        def _():
            near_copy(of, 1).start()

    @pl.when(step == 8)
    def _():
        half = width // 2
        dy = dy_ref[...].astype(F32)
        feed = feed_ref[...] + dbias_ref[...].astype(F32)
        middle = mid_ref[...]
        out_ref[...] = (middle + mod_ref[:, 5 * width :] * feed).astype(BF16)
        factor = lax.rsqrt(jnp.mean(middle * middle, axis=-1, keepdims=True) + NORM_EPSILON)
        normed = middle * factor
        grad_hidden = gh_ref[...]
        product = grad_hidden * normed
        grad_normed = grad_hidden * (1.0 + mod_ref[:, 4 * width : 5 * width])
        back = factor * (
            grad_normed - normed * jnp.mean(grad_normed * normed, axis=-1, keepdims=True)
        )
        grad_middle = dy + back
        gmid_ref[...] = grad_middle
        grad_attended = (mod_ref[:, 2 * width : 3 * width] * grad_middle).astype(BF16)
        sums_ref[0, 0:1, :] = col_sum(grad_middle * att_ref[...].astype(F32))
        sums_ref[0, 1:2, :] = col_sum(grad_hidden)
        sums_ref[0, 2:3, :] = col_sum(product)
        sums_ref[0, 3:4, :] = col_sum(dy * feed)
        sums_ref[0, 4:5, :] = col_sum(grad_attended.astype(F32))
        sums_ref[0, 5:6, :] = col_sum(gf_ref[...].astype(F32))
        sums_ref[0, 6:8, :] = known_ref[...]
        for row in range(32):
            col = (row % 6) * unit
            sums_ref[1, row // 6 : row // 6 + 1, col : col + unit] = bias_ref[row : row + 1, :]
        gmix_ref[...] = mm_nt(grad_attended, weight_ref[...]).astype(BF16)
        mixed_t = mix_ref[...].T
        dw_ref[0] = mm(mixed_t, grad_attended[:, :half]).astype(BF16)
        dw_ref[1] = mm(mixed_t, grad_attended[:, half:]).astype(BF16)
        for of in (6, 7):
            pair_copy(of).wait_send()
        for of in (2, 3, 4, 5):
            near_copy(of, 1).wait_recv()
        for of in range(6):
            near_copy(of, 1).wait_send()
        rows = width // 4
        for f in range(2):
            for z in range(4):
                span = slice(z * rows, (z + 1) * rows)
                total_ref[z, f] = sum(
                    part.astype(F32)
                    for part in (paired[6 + f, span], near[2 + f, span], near[4 + f, span])
                ).astype(BF16)
            for i in range(2):
                for b in range(3):
                    span = slice(g_rows + b * 128 + i * 64, g_rows + b * 128 + i * 64 + 64)
                    total_ref[2 * f + i, 2, b * 64 : b * 64 + 64] = sum(
                        part.astype(F32)
                        for part in (paired[6 + f, span], near[2 + f, span], near[4 + f, span])
                    ).astype(BF16)


def once(shape):
    return pl.BlockSpec(shape, lambda *_: (0,) * len(shape), pipeline_mode=pl.Buffered(1))


def feed_turn_call(
    hidden, hidden_t, grad_feed, gate_up, down, middle, attended, dy, mixed, mod, weight, small,
    known,
):
    rows, width = hidden.shape
    low = jax.ShapeDtypeStruct((rows, width), BF16)
    wide = jax.ShapeDtypeStruct((rows, width), F32)
    cols = lambda i, e: pl.BlockSpec((width, 128), lambda s: (0, 16 * e + feed_block(s, i)))
    first = GATE_BIAS * width // 128
    bias = lambda i, e: pl.BlockSpec((1, 128), lambda s: (0, first + 16 * e + feed_block(s, i)))
    down_bias = pl.BlockSpec((1, width), lambda s: (0, DOWN_BIAS), pipeline_mode=pl.Buffered(1))
    deep = lambda i: pl.BlockSpec((128, width), lambda s: (feed_block(s, i), 0))
    piece = (width + 384, 256)
    out_shape = [
        low, wide, low,
        jax.ShapeDtypeStruct((2, width, width // 2), BF16),
        jax.ShapeDtypeStruct((2, 8, width), F32),
        jax.ShapeDtypeStruct((4, 3, width // 4, 256), BF16),
    ]
    return pl.pallas_call(
        feed_turn_kernel,
        grid=(9,),
        in_specs=[once((rows, width)), once((width, rows)), once((rows, width))]
        + [cols(0, 0), cols(1, 0), cols(0, 1), cols(1, 1)]
        + [bias(0, 0), bias(1, 0), bias(0, 1), bias(1, 1)]
        + [deep(0), deep(1)]
        + [once((rows, width))] * 4
        + [once(mod.shape), once(weight.shape), down_bias, once(known.shape)],
        out_specs=[full(shape.shape) for shape in out_shape],
        out_shape=out_shape,
        scratch_shapes=[
            pltpu.VMEM((rows, width), F32),
            pltpu.VMEM((rows, width), F32),
            pltpu.VMEM((32, 128), F32),
            pltpu.VMEM((2, 2) + piece, BF16),
            pltpu.VMEM((8,) + piece, BF16),
            pltpu.VMEM((6,) + piece, BF16),
            pltpu.SemaphoreType.DMA((2,)),
            pltpu.SemaphoreType.DMA((8,)),
            pltpu.SemaphoreType.DMA((6,)),
            pltpu.SemaphoreType.DMA((6,)),
        ],
        compiler_params=pltpu.CompilerParams(
            vmem_limit_bytes=VMEM_LIMIT, collective_id=1, has_side_effects=True
        ),
        name="feed_turn",
    )(
        hidden, hidden_t, grad_feed, gate_up, gate_up, gate_up, gate_up, small, small, small,
        small, down, down, middle, attended, dy, mixed, mod, weight, small, known,
    )


IN_BIAS, Q_GAIN, K_GAIN, OUT_BIAS, DOWN_BIAS, GATE_BIAS = 6, 9, 10, 11, 12, 13


def small_row(width, head, modulate, inproj, qgain, kgain, outproj, down, gate_up):
    heads = width // head
    return jnp.concatenate(
        [modulate, inproj, jnp.tile(qgain, heads), jnp.tile(kgain, heads), outproj, down, gate_up]
    )[None]


def front_kernel(
    head, tile_cols, tok_hbm, grad_hbm, act_ref, small_ref, modw_hbm, inw_hbm,
    x_hbm, dy_hbm, hid_hbm, q_hbm, k0_hbm, v0_hbm, k1_hbm, v1_hbm, raw_hbm, mod_ref, cos_ref,
    sin_ref,
    x_ref, own_ref, hid_ref, q_ref, k_ref, v_ref, raw_ref, modw_ref, inw_ref,
    load_sem, store_sem, tok_send, tok_recv, kv_send, kv_recv,
):
    place = Place()
    core, chip = place.core, place.chip
    rows, width = x_ref.shape
    cells = rows // 4
    loads = [
        pltpu.make_async_copy(source, target, load_sem.at[i])
        for i, (source, target) in enumerate(
            (
                (tok_hbm.at[chip], x_ref.at[pl.ds(0, cells)]), (modw_hbm, modw_ref),
                (inw_hbm, inw_ref), (grad_hbm.at[chip], own_ref),
            )
        )
    ]
    stores = [
        pltpu.make_async_copy(source, target, store_sem.at[i])
        for i, (source, target) in enumerate(
            (
                (own_ref, dy_hbm.at[pl.ds(0, cells)]), (x_ref, x_hbm), (hid_ref, hid_hbm),
                (k_ref, k0_hbm), (v_ref, v0_hbm), (q_ref, q_hbm), (raw_ref, raw_hbm),
            )
        )
    ]

    def token_copy(which, k):
        source, target = ((tok_hbm, x_ref), (grad_hbm, dy_hbm))[which]
        return send(
            source.at[place.flipped(k)], target.at[pl.ds(k * cells, cells)],
            tok_send.at[which, k - 1], tok_recv.at[which, k - 1], place.plane(k),
        )

    def kv_copy(which, chunk):
        source, target = ((k_ref, k1_hbm), (v_ref, v1_hbm))[which]
        span = pl.ds(chunk * cells, cells if chunk == 0 else rows - cells)
        return send(
            source.at[span], target.at[span], kv_send.at[which, chunk], kv_recv.at[which, chunk],
            place.pair(),
        )

    def vector(start, count=1):
        return small_ref[:, start * width : (start + count) * width].astype(F32)

    def project(start, size, chunk):
        span = slice(start, start + size)
        x = x_ref[span, :].astype(F32)
        normed = x * lax.rsqrt(jnp.mean(x * x, axis=-1, keepdims=True) + NORM_EPSILON)
        hidden = normed * (1.0 + mod_ref[:, width : 2 * width]) + mod_ref[:, :width]
        hidden = hidden.astype(BF16)
        hid_ref[span, :] = hidden
        for part in (1, 2, 0):
            raw = mm(hidden, inw_ref[:, part * width : (part + 1) * width]) + vector(IN_BIAS + part)
            if part == 2:
                v_ref[span, :] = raw.astype(BF16)
                for which in (0, 1):
                    kv_copy(which, chunk).start()
                continue
            raw_ref[span, part * width : (part + 1) * width] = raw.astype(BF16)
            factor = lax.rsqrt(head_sum(raw * raw, head) * (1.0 / head) + NORM_EPSILON)
            scaled = raw * factor * vector((Q_GAIN, K_GAIN)[part])
            turned = turn(scaled, cos_ref[span, :], sin_ref[span, :], head).astype(BF16)
            (q_ref, k_ref)[part][span, :] = turned

    for load in loads:
        load.start()
    meet([place.pair()] + [place.plane(k) for k in (1, 2, 3)])
    for k in (3, 1, 2):
        token_copy(0, k).start()

    quarter = head // 4
    lane = lax.broadcasted_iota(jnp.int32, (1, 128), 1)
    rate = jnp.exp(-math.log(10000.0) / quarter * lax.rem(lane, quarter).astype(F32))
    by_row = lax.rem(lane, head) < head // 2
    sign = jnp.where(lax.rem(lane, 2 * quarter) < quarter, -1.0, 1.0)
    cell = lax.broadcasted_iota(jnp.int32, (cells, 128), 0)
    row, col = cell // tile_cols, lax.rem(cell, tile_cols)
    for k in range(4):
        there = place.flipped(k)
        down = (there // 2) * (cells // tile_cols) + row
        across = (2 * lax.rem(there, 2) + core) * tile_cols + col
        angle = jnp.where(by_row, down, across).astype(F32) * rate
        cos_ref[k * cells : (k + 1) * cells, :] = jnp.cos(angle)
        sin_ref[k * cells : (k + 1) * cells, :] = sign * jnp.sin(angle)
    loads[1].wait()
    mod_ref[...] = mm(act_ref[...], modw_ref[...])[:1] + vector(0, 6)
    loads[0].wait()
    loads[2].wait()
    project(0, cells, 0)
    loads[3].wait()
    stores[0].start()
    for k in (1, 2, 3):
        token_copy(0, k).wait()
    for k in (3, 1, 2):
        token_copy(1, k).start()
    stores[1].start()
    project(cells, rows - cells, 1)
    for store in stores[2:]:
        store.start()
    for which in (0, 1):
        for chunk in (0, 1):
            kv_copy(which, chunk).wait()
    for k in (1, 2, 3):
        token_copy(1, k).wait()
    for store in stores:
        store.wait()


def front_call(tokens, grads, act, small, modw, inw, head, tile_cols):
    images, cells, width = tokens.shape
    rows = images * cells
    low = lambda *shape: jax.ShapeDtypeStruct(shape, BF16)
    vmem = lambda *shape: pltpu.VMEM(shape, BF16)
    anywhere = pl.BlockSpec(memory_space=pl.ANY)
    inside = pl.BlockSpec(memory_space=pltpu.VMEM)
    sems = lambda *shape: pltpu.SemaphoreType.DMA(shape)
    return pl.pallas_call(
        functools.partial(front_kernel, head, tile_cols),
        in_specs=[anywhere] * 2 + [inside] * 2 + [anywhere] * 2,
        out_specs=[anywhere] * 9 + [inside] * 3,
        out_shape=[low(rows, width)] * 8
        + [
            low(rows, 2 * width), jax.ShapeDtypeStruct((1, 6 * width), F32),
            jax.ShapeDtypeStruct((rows, 128), F32), jax.ShapeDtypeStruct((rows, 128), F32),
        ],
        scratch_shapes=[
            vmem(rows, width), vmem(cells, width), vmem(rows, width), vmem(rows, width),
            vmem(rows, width), vmem(rows, width), vmem(rows, 2 * width), vmem(*modw.shape),
            vmem(*inw.shape), sems(4), sems(7), sems(2, 3), sems(2, 3), sems(2, 2), sems(2, 2),
        ],
        compiler_params=pltpu.CompilerParams(
            vmem_limit_bytes=VMEM_LIMIT, collective_id=3, has_side_effects=True
        ),
        name="front",
    )(tokens, grads, act, small, modw, inw)


Z_FIRST = (False, False, False, False)
GROUPS = 4


def back_kernel(
    head, q_ref, k0_ref, k1_ref, v0_ref, v1_ref, gm_ref, mix_ref, rl_ref, e_ref,
    mod_ref, qgain_ref, kgain_ref, cos_ref, sin_ref, dout_ref, totals_ref, early_ref,
    raw_hbm, hid_hbm, x_hbm, gmid_hbm, weight_hbm, rows_hbm,
    output_ref, gtok_ref, feeds_hbm, projs_hbm, early_hbm, late_hbm,
    feeds_ref, projs_ref, early_all, late_all, raw_ref, hid_ref, x_ref, gmid_ref, weight_ref, hidt_ref, gh_ref, gx_ref, late_ref,
    dq_s, dk0_s, dv0_s, dk1_s, dv1_s, dk_in, dv_in,
    made, paired, first_out, first_in, second_out, second_in, z_in, early_in, late_in,
    load_sem, own_sem, kv_send, kv_recv, pair_send, pair_recv, first_send, first_recv,
    second_send, second_recv, z_send, z_recv, tok_send, tok_recv, feed_send, feed_recv,
    proj_send, proj_recv, small_send, small_recv,
):
    place = Place()
    core, chip, z = place.core, place.chip, place.z
    step = pl.program_id(0)
    rows, width = x_ref.shape
    cells = rows // 4
    scale = head**-0.5
    lane = lax.broadcasted_iota(jnp.int32, (1, 128), 1)

    loads = [
        pltpu.make_async_copy(source, target, load_sem.at[i])
        for i, (source, target) in enumerate(
            (
                (hid_hbm, hid_ref), (raw_hbm, raw_ref), (weight_hbm, weight_ref),
                (x_hbm, x_ref), (gmid_hbm, gmid_ref),
            )
        )
    ]

    stores = [
        pltpu.make_async_copy(source, target, load_sem.at[5 + i])
        for i, (source, target) in enumerate(
            (
                (early_all, early_hbm), (late_all, late_hbm), (feeds_ref, feeds_hbm),
                (projs_ref, projs_hbm),
            )
        )
    ]

    def z_copy(d):
        return send(
            totals_ref.at[place.flipped_z(d)], z_in.at[d - 1], z_send.at[d - 1], z_recv.at[d - 1],
            place.depth(d),
        )

    def token_copy(which, k):
        source, target = ((rows_hbm, output_ref), (gx_ref, gtok_ref))[which]
        return send(
            source.at[pl.ds(k * cells, cells)], target.at[chip], tok_send.at[which, k - 1],
            tok_recv.at[which, k - 1], place.plane(k),
        )

    def own_tokens(which):
        source, target = ((rows_hbm, output_ref), (gx_ref, gtok_ref))[which]
        return pltpu.make_async_copy(source.at[pl.ds(0, cells)], target.at[chip], own_sem.at[which])

    def kv_copy(which, p):
        source, target = ((dk1_s, dk_in), (dv1_s, dv_in))[which]
        return send(
            source.at[p], target.at[p], kv_send.at[which, p], kv_recv.at[which, p], place.pair()
        )

    def pair_copy(g):
        source = dout_ref.at[1 - core] if g == 3 else made.at[g % 2, 1 - core]
        return send(source, paired.at[g], pair_send.at[g], pair_recv.at[g], place.pair())

    def first_copy(g, k):
        other = place.flipped_z(k) if Z_FIRST[g] else place.flipped(k)
        device = place.depth(k) if Z_FIRST[g] else place.plane(k)
        return send(
            first_out.at[g, other], first_in.at[g, k - 1], first_send.at[g, k - 1],
            first_recv.at[g, k - 1], device,
        )

    def second_copy(g, k):
        other = place.flipped(k) if Z_FIRST[g] else place.flipped_z(k)
        device = place.plane(k) if Z_FIRST[g] else place.depth(k)
        return send(
            second_out.at[g, other], second_in.at[g, k - 1], second_send.at[g, k - 1],
            second_recv.at[g, k - 1], device,
        )

    def feed_copy(k):
        here = feeds_ref.at[core, chip]
        return send(here, here, feed_send.at[k - 1], feed_recv.at[k - 1], place.plane(k))

    def feed_pair():
        here = feeds_ref.at[core]
        return send(here, here, feed_send.at[3], feed_recv.at[3], place.pair())

    def proj_copy(k):
        here = projs_ref.at[core, chip]
        return send(here, here, proj_send.at[k - 1], proj_recv.at[k - 1], place.plane(k))

    def proj_pair():
        here = projs_ref.at[core]
        return send(here, here, proj_send.at[3], proj_recv.at[3], place.pair())

    smalls = ((early_ref, early_in, early_all, 8), (late_ref, late_in, late_all, 4))
    hops = [place.plane(1), place.plane(2), place.depth(1), place.depth(2)]

    def small_pair(which):
        source, target, _, count = smalls[which]
        return send(
            source.at[1 - core], target, small_send.at[which, 0], small_recv.at[which, 0],
            place.pair(),
        )

    def small_hop(which, i):
        _, _, full_ref, _ = smalls[which]
        have = 1 << i
        return send(
            full_ref.at[core, pl.ds(0, have)], full_ref.at[core, pl.ds(have, have)],
            small_send.at[which, 1 + i], small_recv.at[which, 1 + i], hops[i],
        )

    def small_last(which):
        here = smalls[which][2].at[core]
        return send(
            here, here, small_send.at[which, 5], small_recv.at[which, 5], place.pair()
        )

    def small_begin(which):
        source, target, full_ref, _ = smalls[which]
        small_pair(which).wait_recv()
        full_ref[core, 0] = source[core] + target[...]
        small_hop(which, 0).start()

    def small_next(which, i):
        small_hop(which, i).wait_recv()
        (small_hop(which, i + 1) if i < 3 else small_last(which)).start()

    def start_group(g):
        pair_copy(g).wait_recv()
        mine = dout_ref.at[core] if g == 3 else made.at[g % 2, core]
        part = width // 16
        for a in range(4):
            for b in range(4):
                span = pl.ds((a * 4 + b) * part, part)
                total = (mine[span, :].astype(F32) + paired[g, span].astype(F32)).astype(BF16)
                if Z_FIRST[g]:
                    first_out[g, a, b] = total
                else:
                    first_out[g, b, a] = total
        for k in (1, 2, 3):
            first_copy(g, k).start()

    def go_on(g):
        for k in (1, 2, 3):
            first_copy(g, k).wait_recv()
        here = z if Z_FIRST[g] else chip
        second_out[g] = (
            first_out[g, here].astype(F32)
            + first_in[g, 0].astype(F32)
            + first_in[g, 1].astype(F32)
            + first_in[g, 2].astype(F32)
        ).astype(BF16)
        for k in (1, 2, 3):
            second_copy(g, k).start()

    def finish(g):
        for k in (1, 2, 3):
            second_copy(g, k).wait_recv()
        here = chip if Z_FIRST[g] else z
        projs_ref[core, chip, g] = (
            second_out[g, here].astype(F32)
            + second_in[g, 0].astype(F32)
            + second_in[g, 1].astype(F32)
            + second_in[g, 2].astype(F32)
        ).astype(BF16)

    @pl.when(step == 0)
    def _():
        for load in loads:
            load.start()
        meet(
            [place.pair()]
            + [place.plane(k) for k in (1, 2, 3)]
            + [place.depth(d) for d in (1, 2, 3)]
        )
        pair_copy(3).start()
        small_pair(0).start()
        for d in (1, 2, 3):
            z_copy(d).start()
        for k in (1, 2, 3):
            token_copy(0, k).start()
        own_tokens(0).start()
        gh_ref[...] = jnp.zeros_like(gh_ref)

    @pl.when(step >= 1)
    def _():
        for which in (0, 1):
            kv_copy(which, step - 1).start()

    @pl.when(step == 3)
    def _():
        pair_copy(0).start()

    @pl.when(step == 5)
    def _():
        pair_copy(1).start()

    @pl.when(step < 6)
    def _():
        keys = jnp.concatenate([k0_ref[...], k1_ref[...]], axis=0)
        values = jnp.concatenate([v0_ref[...], v1_ref[...]], axis=0)
        scaled = gm_ref[...].astype(F32) * rl_ref[...]
        products = scaled * mix_ref[...].astype(F32)
        scaled = scaled.astype(BF16)
        q_t = q_ref[...].T
        scaled_t = scaled.T
        dqs, dks, dvs = [], [], []
        for h in range(2):
            mine = (lane >= 64) if h else (lane < 64)
            inner = jnp.sum(jnp.where(mine, products, 0.0), axis=1, keepdims=True)
            grad_probs = mm_nt(jnp.where(mine, scaled, jnp.zeros_like(scaled)), values)
            grown = e_ref[h]
            grad_scores = (grown.astype(F32) * (grad_probs - inner) * scale).astype(BF16)
            dqs.append(mm(grad_scores, keys))
            dks.append(mm(q_t[64 * h : 64 * h + 64], grad_scores))
            dvs.append(mm(scaled_t[64 * h : 64 * h + 64], grown))
        dq_s[step] = jnp.where(lane < 64, dqs[0], dqs[1]).astype(BF16)
        dk = jnp.concatenate(dks, axis=0).T.astype(BF16)
        dv = jnp.concatenate(dvs, axis=0).T.astype(BF16)
        dk0_s[step] = dk[:rows]
        dk1_s[step] = dk[rows:]
        dv0_s[step] = dv[:rows]
        dv1_s[step] = dv[rows:]

    @pl.when(step == 0)
    def _():
        loads[0].wait()
        hidt_ref[...] = hid_ref[...].T

    @pl.when(step == 1)
    def _():
        loads[1].wait()
        loads[2].wait()
        start_group(3)
        small_begin(0)

    for i in range(4):

        @pl.when(step == 2 + i)
        def _(i=i):
            small_next(0, i)

    @pl.when(step == 3)
    def _():
        start_group(0)

    @pl.when(step == 5)
    def _():
        start_group(1)
        go_on(3)

    @pl.when(step == 6)
    def _():
        for d in (1, 2, 3):
            z_copy(d).wait_recv()
        for i in range(3):
            feeds_ref[core, chip, i] = (
                totals_ref[z, i].astype(F32)
                + z_in[0, i].astype(F32)
                + z_in[1, i].astype(F32)
                + z_in[2, i].astype(F32)
            ).astype(BF16)
        for k in (1, 2, 3):
            feed_copy(k).start()

    @pl.when((step >= 2) & (lax.rem(step, 2) == 0))
    def _():
        g = (step - 2) // 2
        slot = lax.rem(g, 2)
        cosine, sine = cos_ref[...], -sin_ref[...]
        for i in range(2):
            for which in (0, 1):
                kv_copy(which, 2 * g + i).wait_recv()

        def both(ref):
            return jnp.concatenate([ref[2 * g], ref[2 * g + 1]], axis=1).astype(F32)

        lows = []
        for part in range(3):
            span = pl.ds(pl.multiple_of(part * width + g * 256, 256), 256)
            if part == 2:
                grad = both(dv0_s) + both(dv_in)
            else:
                grad = both(dq_s) if part == 0 else both(dk0_s) + both(dk_in)
                gain = (qgain_ref, kgain_ref)[part][:, :256].astype(F32)
                raw = raw_ref[:, span].astype(F32)
                factor = lax.rsqrt(head_sum(raw * raw, head) * (1.0 / head) + NORM_EPSILON)
                normed = raw * factor
                turned = turn(grad, cosine, sine, head)
                late_ref[1, part : part + 1, pl.ds(pl.multiple_of(g * 256, 256), 256)] = col_sum(
                    turned * normed
                )
                turned = turned * gain
                mean = head_sum(turned * normed, head) * (1.0 / head)
                grad = factor * (turned - normed * mean)
            low = grad.astype(BF16)
            lows.append(low)
            total = col_sum(low.astype(F32))
            where = pl.ds(pl.multiple_of(g * 256, 256), 256)
            if part < 2:
                late_ref[0, 2 + part : 3 + part, where] = total
            else:
                late_ref[1, 2:3, where] = total
            gh_ref[...] += mm_nt(low, weight_ref[:, span])
        grads = jnp.concatenate(
            [low[:, 128 * c : 128 * c + 128] for c in range(2) for low in lows], axis=1
        )

        @pl.when(step == 6)
        def _():
            pair_copy(0).wait_send()

        half = width // 2
        made[slot, 0] = mm(hidt_ref[...], grads[:, :half]).astype(BF16)
        made[slot, 1] = mm(hidt_ref[...], grads[:, half:]).astype(BF16)

    @pl.when(step == 6)
    def _():
        pair_copy(2).start()
        go_on(0)
        go_on(1)
        loads[3].wait()
        loads[4].wait()
        grad_hidden = gh_ref[...]
        x = x_ref[...].astype(F32)
        factor = lax.rsqrt(jnp.mean(x * x, axis=-1, keepdims=True) + NORM_EPSILON)
        normed = x * factor
        late_ref[0, 0:1, :] = col_sum(grad_hidden)
        late_ref[0, 1:2, :] = col_sum(grad_hidden * normed)
        late_ref[1, 3:4, :] = jnp.zeros((1, width), F32)
        grad_normed = grad_hidden * (1.0 + mod_ref[:, width : 2 * width])
        back = factor * (
            grad_normed - normed * jnp.mean(grad_normed * normed, axis=-1, keepdims=True)
        )
        small_pair(1).start()
        start_group(2)
        gx_ref[...] = (gmid_ref[...] + back).astype(BF16)
        small_begin(1)
        for k in (1, 2, 3):
            token_copy(1, k).start()
        own_tokens(1).start()
        finish(3)
        small_next(1, 0)
        finish(0)
        finish(1)
        small_next(1, 1)
        go_on(2)
        small_next(1, 2)
        for k in (1, 2, 3):
            feed_copy(k).wait_recv()
        for k in (1, 2, 3):
            feed_copy(k).wait_send()
        feed_pair().start()
        finish(2)
        for k in (1, 2, 3):
            proj_copy(k).start()
        small_next(1, 3)
        for k in (1, 2, 3):
            proj_copy(k).wait()
        proj_pair().start()
        for which in (0, 1):
            own_tokens(which).wait()
            for k in (1, 2, 3):
                token_copy(which, k).wait()
            small_pair(which).wait_send()
            for i in range(4):
                small_hop(which, i).wait_send()
            small_last(which).wait()
            stores[which].start()
            for p in range(6):
                kv_copy(which, p).wait_send()
        for k in (1, 2, 3):
            z_copy(k).wait_send()
            for g in range(4):
                first_copy(g, k).wait_send()
                second_copy(g, k).wait_send()
        for g in (1, 2, 3):
            pair_copy(g).wait_send()
        feed_pair().wait()
        stores[2].start()
        proj_pair().wait()
        stores[3].start()
        for store in stores:
            store.wait()


def back_call(
    q, k0, k1, v0, v1, grad_mixed, mixed, inverse, grown, mod, small_vectors, cosine, sine, d_out,
    totals, early, raw, hidden, x, grad_middle, weight, output_rows, head,
):
    rows, width = q.shape
    half, part = width // 2, width // 16
    low = lambda *shape: jax.ShapeDtypeStruct(shape, BF16)
    pair = pl.BlockSpec((rows, 128), lambda s: (0, jnp.minimum(s, 5)))
    anywhere = pl.BlockSpec(memory_space=pl.ANY)
    small = [mod, small_vectors, small_vectors, cosine, sine, d_out, totals, early]
    gain = lambda at: pl.BlockSpec((1, width), lambda s: (0, at), pipeline_mode=pl.Buffered(1))
    out_shape = [
        low(4, rows // 4, width), low(4, rows // 4, width),
        low(2, 4, 3, width // 4, 256), low(2, 4, GROUPS, part, half),
        jax.ShapeDtypeStruct((2, 16, 8, width), F32), jax.ShapeDtypeStruct((2, 16, 4, width), F32),
    ]
    vmem = lambda *shape: pltpu.VMEM(shape, BF16)
    sems = lambda *shape: pltpu.SemaphoreType.DMA(shape)
    return pl.pallas_call(
        functools.partial(back_kernel, head),
        grid=(7,),
        in_specs=[pair] * 8
        + [pl.BlockSpec((2, rows, 2 * rows), lambda s: (jnp.minimum(s, 5), 0, 0))]
        + [once(mod.shape), gain(Q_GAIN), gain(K_GAIN)]
        + [once(each.shape) for each in small[3:]]
        + [anywhere] * 6,
        out_specs=[anywhere] * 6,
        out_shape=out_shape,
        scratch_shapes=[pltpu.VMEM(shape.shape, shape.dtype) for shape in out_shape[2:]]
        + [
            vmem(rows, 2 * width), vmem(rows, width), vmem(rows, width),
            pltpu.VMEM((rows, width), F32), vmem(width, 3 * width), vmem(width, rows),
            pltpu.VMEM((rows, width), F32), vmem(rows, width), pltpu.VMEM((2, 4, width), F32),
        ]
        + [vmem(6, rows, 128)] * 7
        + [
            vmem(2, 2, width, half), vmem(GROUPS, width, half),
            vmem(GROUPS, 4, 4, part, half), vmem(GROUPS, 3, 4, part, half),
            vmem(GROUPS, 4, part, half), vmem(GROUPS, 3, part, half),
            vmem(3, 3, width // 4, 256),
            pltpu.VMEM((8, width), F32), pltpu.VMEM((4, width), F32),
            sems(9), sems(2), sems(2, 6), sems(2, 6), sems(GROUPS), sems(GROUPS),
            sems(GROUPS, 3), sems(GROUPS, 3), sems(GROUPS, 3), sems(GROUPS, 3),
            sems(3), sems(3), sems(2, 3), sems(2, 3), sems(4), sems(4), sems(4), sems(4),
            sems(2, 6), sems(2, 6),
        ],
        compiler_params=pltpu.CompilerParams(
            vmem_limit_bytes=VMEM_LIMIT, collective_id=2, has_side_effects=True
        ),
        name="back",
    )(
        q, k0, k1, v0, v1, grad_mixed, mixed, inverse, grown, *small, raw, hidden, x, grad_middle,
        weight, output_rows,
    )


def finish_kernel(
    head, feeds_ref, projs_ref, early_ref, late_ref, modw_hbm,
    cond_ref, table_hbm, gmodw_hbm, gmodb_ref, ginw_hbm, ginb_ref, gqg_ref, gkg_ref, goutw_hbm,
    goutb_ref, gguw_hbm, ggub_ref, gdownw_hbm, gdownb_ref,
    modw_ref, table_ref, gmodw_ref, ginw_ref, goutw_ref, gguw_ref, gdownw_ref, acts_ref, load_sem,
    store_sem,
):
    place = Place()
    width = early_ref.shape[3]
    part = projs_ref.shape[3]
    load = pltpu.make_async_copy(modw_hbm, modw_ref, load_sem)
    load.start()
    stores = [
        pltpu.make_async_copy(source, target, store_sem.at[i])
        for i, (source, target) in enumerate(
            (
                (gguw_ref, gguw_hbm), (gdownw_ref, gdownw_hbm), (ginw_ref, ginw_hbm),
                (goutw_ref, goutw_hbm), (gmodw_ref, gmodw_hbm), (table_ref, table_hbm),
            )
        )
    ]
    for c in range(2):
        for chip in range(4):
            for f in range(2):
                for i in range(2):
                    col = (((c * 2 + f) * 2 + i) * 4 + chip) * 128
                    gguw_ref[:, col : col + 128] = feeds_ref[
                        c, chip, f, :, i * 128 : (i + 1) * 128
                    ].astype(F32)
    stores[0].start()
    for c in range(2):
        for chip in range(4):
            row = chip * 128 + c * 64
            for b in range(3):
                gdownw_ref[row : row + 64, b * 256 : (b + 1) * 256] = feeds_ref[
                    c, chip, 2, b * 64 : (b + 1) * 64, :
                ].astype(F32)
    stores[1].start()
    for c in range(2):
        for chip in range(4):
            row = chip * part
            for g in range(3):
                for q in range(3):
                    col = q * width + g * 256 + c * 128
                    ginw_ref[row : row + part, col : col + 128] = projs_ref[
                        c, chip, g, :, q * 128 : (q + 1) * 128
                    ].astype(F32)
            half = width // 2
            goutw_ref[row : row + part, c * half : (c + 1) * half] = projs_ref[c, chip, 3].astype(F32)
    stores[2].start()
    stores[3].start()

    vectors = [late_ref[0, :, 0, :], late_ref[0, :, 1, :]]
    vectors += [early_ref[0, :, j, :] for j in range(4)]
    lows = [vector.astype(BF16) for vector in vectors]
    conditions = early_ref[0, :, 6, :]
    labels = early_ref[0, :, 7, :]
    sig = 1.0 / (1.0 + jnp.exp(-conditions))
    acts = (conditions * sig).astype(BF16)
    size = acts_ref.shape[1]
    for z in range(4):

        @pl.when(place.z == z)
        def _(z=z):
            acts_ref[...] = acts[:, z * size : (z + 1) * size]

    mine = acts_ref[...]
    for j, low in enumerate(lows):
        gmodw_ref[:, j * width : (j + 1) * width] = mm_tn(mine, low)
    stores[4].start()
    early_sum = jnp.sum(early_ref[0], axis=0)
    gate_sum = jnp.sum(early_ref[1], axis=0)
    late_sum = jnp.sum(late_ref[0], axis=0)
    gain_sum = jnp.sum(late_ref[1], axis=0)
    mod_b = jnp.concatenate(
        [late_sum[0:1], late_sum[1:2]] + [early_sum[j : j + 1] for j in range(4)], axis=1
    )
    in_b = jnp.concatenate([late_sum[2:3], late_sum[3:4], gain_sum[2:3]], axis=1)
    gate_b = jnp.concatenate(
        [gate_sum[n // 6 : n // 6 + 1, (n % 6) * 128 : (n % 6) * 128 + 128] for n in range(32)],
        axis=1,
    )
    gains = sum(gain_sum[0:2, i : i + 128] for i in range(0, width, 128))
    gains = gains[:, :head] + gains[:, head:]
    pieces = (
        (gmodb_ref, mod_b), (ginb_ref, in_b), (gqg_ref, gains[0:1]), (gkg_ref, gains[1:2]),
        (goutb_ref, early_sum[4:5]), (ggub_ref, gate_b), (gdownb_ref, early_sum[5:6]),
    )
    for z in range(4):

        @pl.when(place.z == z)
        def _(z=z):
            for ref, row in pieces:
                size = row.shape[1] // 4
                ref[...] = row[:, z * size : (z + 1) * size]

    load.wait()
    grad = sum(mm_nt(low, modw_ref[:, j * width : (j + 1) * width]) for j, low in enumerate(lows))
    grad = grad * sig * (1.0 + conditions * (1.0 - sig))
    for k in range(4):
        cond_ref[pl.ds(place.flipped(k), 1), :] = grad[k : k + 1]
    classes = table_ref.shape[0]
    wide = -(-classes // 128) * 128
    column = lax.broadcasted_iota(jnp.int32, (1, wide), 1).astype(F32)
    onehot = jnp.where(labels[:, 0:1] == column, 1.0, 0.0).astype(BF16)
    high = grad.astype(BF16)
    rest = grad - high.astype(F32)
    middle = rest.astype(BF16)
    last = (rest - middle.astype(F32)).astype(BF16)
    table = mm_tn(
        jnp.concatenate([onehot] * 3, axis=0), jnp.concatenate([high, middle, last], axis=0)
    )
    table_ref[...] = table[:classes]
    stores[5].start()
    for store in stores:
        store.wait()


def finish_call(feeds, projs, early, late, weight, head, classes, hidden_width):
    width = weight.shape[0]
    rows = width // 4
    whole = lambda *shape: jax.ShapeDtypeStruct(shape, F32)
    anywhere = pl.BlockSpec(memory_space=pl.ANY)
    out_shape = [
        whole(4, width), whole(classes, width), whole(rows, 6 * width), whole(1, 6 * width // 4),
        whole(rows, 3 * width), whole(1, 3 * width // 4), whole(1, head // 4), whole(1, head // 4),
        whole(rows, width), whole(1, rows), whole(rows, 2 * hidden_width),
        whole(1, 2 * hidden_width // 4), whole(hidden_width // 4, width), whole(1, rows),
    ]
    big = (1, 2, 4, 8, 10, 12)
    return pl.pallas_call(
        functools.partial(finish_kernel, head),
        in_specs=[pl.BlockSpec(memory_space=pltpu.VMEM)] * 4 + [anywhere],
        out_specs=[
            anywhere if i in big else pl.BlockSpec(memory_space=pltpu.VMEM)
            for i in range(len(out_shape))
        ],
        out_shape=out_shape,
        scratch_shapes=[pltpu.VMEM(weight.shape, BF16)]
        + [pltpu.VMEM(out_shape[i].shape, F32) for i in big]
        + [pltpu.VMEM((16, rows), BF16), pltpu.SemaphoreType.DMA, pltpu.SemaphoreType.DMA((6,))],
        compiler_params=params(),
        name="finish",
    )(feeds, projs, early, late, weight)


def take(array_in, index, axis=0):
    return lax.dynamic_index_in_dim(array_in, index, axis, keepdims=False)


def add(*terms):
    return sum(term.astype(F32) for term in terms)


class Moves:
    def __init__(self, mesh):
        self.sizes = tuple(mesh.shape[name] for name in AXES)

    def flip(self, value, batch=0, gy=0, gx=0):
        nb, ny, nx = self.sizes
        pairs = []
        for b in range(nb):
            for y in range(ny):
                for x in range(nx):
                    here = (b * ny + y) * nx + x
                    there = ((b ^ batch) * ny + (y ^ gy)) * nx + (x ^ gx)
                    pairs.append((here, there))
        return lax.ppermute(value, AXES, pairs)

    def plane(self, value, k):
        return self.flip(value, gy=k >> 1, gx=2 * (k & 1))

    def pair(self, value):
        return self.flip(value, gx=1)

    def gather(self, value):
        value = value[None]
        value = jnp.concatenate([value, self.plane(value, 1)], axis=0)
        value = jnp.concatenate([value, self.plane(value, 2)], axis=0)
        bit = 1
        while bit < self.sizes[0]:
            value = jnp.concatenate([value, self.flip(value, batch=bit)], axis=0)
            bit *= 2
        return value


def regroup(parts, place):
    stacked = jnp.stack(parts)
    return jnp.stack([take(stacked, place ^ k) for k in range(len(parts))])


def body(mesh, *operands):
    (
        tokens, timesteps, labels, class_table, modulate_weight, modulate_bias, inproj_weight,
        inproj_bias, query_gain, key_gain, outproj_weight, outproj_bias, gate_up_weight,
        gate_up_bias, down_weight, down_bias, cotangent,
    ) = operands
    image_count, tile_rows, tile_cols, width = tokens.shape
    cells = tile_rows * tile_cols
    rows = image_count * cells
    head = query_gain.shape[0]
    heads = width // head
    hidden_width = down_weight.shape[0]
    class_count = class_table.shape[0]
    highest = lax.Precision.HIGHEST
    moves = Moves(mesh)
    nb, ny, nx = moves.sizes
    assert ny == 2 and nx == 4 and image_count == 4
    z, gy, gx = (lax.axis_index(name) for name in AXES)
    side, core = gx // 2, gx % 2
    place = 2 * gy + side

    tiles = tokens.reshape(image_count, cells, width)
    grads = cotangent.reshape(image_count, cells, width)

    half_width = width // 2
    step = take(timesteps, place).astype(F32)
    label = take(labels, place)
    rates = jnp.exp(-math.log(10000.0) * jnp.arange(half_width, dtype=F32) / half_width)
    features = jnp.concatenate([jnp.cos(step * rates), jnp.sin(step * rates)])
    condition = features + take(class_table, label).astype(F32)
    cond_act = jax.nn.silu(condition).astype(BF16)
    if nb == 4 and hidden_width == 16 * 128:
        act = jnp.broadcast_to(cond_act[None], (16, width))
        small = small_row(
            width, head, modulate_bias, inproj_bias, query_gain, key_gain, outproj_bias, down_bias,
            gate_up_bias,
        )
        known = jnp.stack([condition, jnp.broadcast_to(label.astype(F32), (width,))])
        known = jnp.where(core == 0, known, 0.0)
        x, dy, hidden_one, q, k0, v0, k1, v1, raw, mod, cosine, sine = front_call(
            tiles, grads, act, small, modulate_weight, inproj_weight, head, tile_cols
        )
        mixed, grown, inverse = attend_call(q, k0, k1, v0, v1, head)
        attended, middle, hidden_two, hidden_two_t, grad_feed = middle_call(
            mixed, x, dy, mod, outproj_weight, small, OUT_BIAS
        )
        output_rows, grad_middle, grad_mixed, d_out, sums_two, totals = feed_turn_call(
            hidden_two, hidden_two_t, grad_feed, gate_up_weight, down_weight, middle, attended, dy,
            mixed, mod, outproj_weight, small, known,
        )
        output, grad_tokens, feeds, projs, early, late = back_call(
            q, k0, k1, v0, v1, grad_mixed, mixed, inverse, grown, mod, small, cosine, sine, d_out,
            totals, sums_two, raw, hidden_one, x, grad_middle, inproj_weight, output_rows, head,
        )
        (
            grad_condition, grad_table, grad_mod_w, grad_mod_b, grad_in_w, grad_in_b, grad_q_gain,
            grad_k_gain, grad_out_w, grad_out_b, grad_gu_w, grad_gu_b, grad_down_w, grad_down_b,
        ) = finish_call(
            feeds, projs, early, late, modulate_weight, head, class_count, hidden_width
        )
        return (
            output.reshape(tokens.shape), grad_tokens.reshape(tokens.shape), grad_condition,
            grad_table, grad_mod_w, grad_mod_b[0], grad_in_w, grad_in_b[0], grad_q_gain[0],
            grad_k_gain[0], grad_out_w, grad_out_b[0], grad_gu_w, grad_gu_b[0], grad_down_w,
            grad_down_b[0],
        )

    def exchange(blocks):
        return [take(blocks, place)] + [
            moves.plane(take(blocks, place ^ k), k) for k in range(1, 4)
        ]

    x = jnp.concatenate(exchange(tiles), axis=0)

    mod = modulation_call(
        jnp.broadcast_to(cond_act[None], (16, width)), modulate_weight, modulate_bias[None]
    )[:1]

    quarter = head // 4
    cell = jnp.arange(cells, dtype=jnp.int32)
    row_places, col_places = [], []
    for k in range(4):
        there = place ^ k
        row_places.append((there // 2) * tile_rows + cell // tile_cols)
        col_places.append((2 * (there % 2) + core) * tile_cols + cell % tile_cols)
    row_places = jnp.concatenate(row_places).astype(F32)[:, None]
    col_places = jnp.concatenate(col_places).astype(F32)[:, None]
    lane = jnp.arange(128, dtype=jnp.int32)
    turn_rate = jnp.exp(-math.log(10000.0) * (lane % quarter).astype(F32) / quarter)[None]
    angles = jnp.where((lane % head)[None] < head // 2, row_places, col_places) * turn_rate
    cosine = jnp.cos(angles)
    sine = jnp.where((lane % (2 * quarter))[None] < quarter, -1.0, 1.0) * jnp.sin(angles)
    qgain = jnp.tile(query_gain.astype(F32), heads)[None]
    kgain = jnp.tile(key_gain.astype(F32), heads)[None]

    hidden_one, q, k0, v0, raw = project_call(
        x, mod, inproj_weight, inproj_bias[None], qgain, kgain, cosine, sine, head
    )
    k1, v1 = moves.pair(k0), moves.pair(v0)
    dy = jnp.concatenate(exchange(grads), axis=0)
    mixed, grown, inverse = attend_call(q, k0, k1, v0, v1, head)
    attended, middle, hidden_two, hidden_two_t, grad_feed = middle_call(
        mixed, x, dy, mod, outproj_weight, outproj_bias[None]
    )

    unit = 256
    blocks = hidden_width // unit
    feed, grad_hidden, d_down, d_gate, d_bias = feed_call(
        hidden_two, hidden_two_t, grad_feed, gate_up_weight, gate_up_bias[None], down_weight,
        jnp.zeros((rows, width), F32), jnp.zeros((rows, width), F32), 0, 1, unit,
    )
    output_rows, grad_middle, grad_mixed, d_out, sums_two = turn_call(
        feed, grad_hidden, middle, attended, dy, grad_feed, mixed, mod, outproj_weight,
        down_bias[None],
    )
    gate_bias = d_bias.reshape(blocks, 2, unit).transpose(1, 0, 2)
    dq, dk0, dk1, dv0, dv1 = attend_back_call(
        q, k0, k1, v0, v1, grown, grad_mixed, mixed, inverse, head
    )
    dk1, dv1 = moves.pair(dk1), moves.pair(dv1)
    grad_x, d_in, sums_one, in_bias = project_back_call(
        dq, dk0, dk1, dv0, dv1, raw, hidden_one, x, grad_middle, mod, inproj_weight, qgain,
        kgain, cosine, sine, head,
    )

    def give_back(rows_out):
        parts = rows_out.reshape(4, cells, width)
        got = [parts[0]] + [moves.plane(parts[k], k) for k in range(1, 4)]
        return regroup(got, place).reshape(tokens.shape)

    output = give_back(output_rows)
    grad_tokens = give_back(grad_x)
    slice_rows = width // nb

    def scatter(d):
        d = lax.psum_scatter(d.astype(BF16), "batch", scatter_dimension=0, tiled=True)
        return lax.psum(d, ("gy", "gx")).astype(F32)

    def joined(d):
        return jnp.concatenate([d[0], d[1]], axis=1)

    grad_down_w = scatter(d_down.reshape(hidden_width, width))
    grad_gu_w = scatter(
        d_gate.transpose(2, 1, 0, 3).reshape(width, 2 * hidden_width)
    )
    grad_out_w = scatter(joined(d_out))
    grad_in_w = scatter(joined(d_in))
    gain_sums = sums_one[2:4].reshape(2, heads, head).sum(axis=1)
    early = jnp.concatenate([sums_two[:6].reshape(-1), gate_bias.reshape(-1)])
    late = jnp.concatenate(
        [sums_one[:2].reshape(-1), in_bias.reshape(-1), gain_sums.reshape(-1)]
    )

    def everywhere(vector):
        halves = vector.reshape(2, -1)
        half = add(take(halves, core), moves.pair(take(halves, 1 - core)))
        half = moves.gather(half)
        both = regroup([half, moves.pair(half)], core)
        return both.transpose(1, 0, 2).reshape(half.shape[0], -1)

    known = jnp.concatenate([condition, jnp.broadcast_to(label.astype(F32), (128,))])
    known = moves.gather(known)
    early, late = everywhere(early), everywhere(late)
    grad_modulation = jnp.concatenate([late[:, : 2 * width], early[:, : 4 * width]], axis=1)
    conditions = known[:, :width]
    all_labels = known[:, width].astype(jnp.int32)
    cond_acts = jax.nn.silu(conditions).astype(BF16)
    my_acts = lax.dynamic_slice_in_dim(cond_acts, z * slice_rows, slice_rows, axis=1)
    low_mod = grad_modulation.astype(BF16)
    grad_mod_w = mm_tn(my_acts, low_mod)
    wide = 6 * width
    grad_mod_b = lax.dynamic_slice_in_dim(
        jnp.sum(grad_modulation, axis=0), z * (wide // nb), wide // nb, axis=0
    )
    grad_cond_act = mm_nt(low_mod, modulate_weight)
    sig = jax.nn.sigmoid(conditions)
    grad_conditions = grad_cond_act * sig * (1.0 + conditions * (1.0 - sig))
    grad_condition = regroup([grad_conditions[k] for k in range(4)], place)
    onehot = (all_labels[:, None] == jnp.arange(class_count, dtype=jnp.int32)[None, :]).astype(F32)
    grad_table = lax.dot_general(
        onehot, grad_conditions, (((0,), (0,)), ((), ())), precision=highest,
        preferred_element_type=F32,
    )

    early_sum = jnp.sum(early, axis=0)
    late_sum = jnp.sum(late, axis=0)

    def part(vector, start, size):
        return lax.dynamic_slice_in_dim(vector, start + z * (size // nb), size // nb, axis=0)

    grad_out_b = part(early_sum, 4 * width, width)
    grad_down_b = part(early_sum, 5 * width, width)
    grad_gu_b = part(early_sum, 6 * width, 2 * hidden_width)
    grad_in_b = part(late_sum, 2 * width, 3 * width)
    grad_q_gain = part(late_sum, 5 * width, head)
    grad_k_gain = part(late_sum, 5 * width + head, head)
    return (
        output, grad_tokens, grad_condition, grad_table, grad_mod_w, grad_mod_b, grad_in_w,
        grad_in_b, grad_q_gain, grad_k_gain, grad_out_w, grad_out_b, grad_gu_w, grad_gu_b,
        grad_down_w, grad_down_b,
    )


def solution(mesh):
    grid = P("batch", "gy", "gx", None)
    by_batch = P("batch")
    rows = P("batch", None)
    placed = (grid, by_batch, by_batch) + (P(),) * 13 + (grid,)
    return jax.shard_map(
        functools.partial(body, mesh),
        mesh=mesh,
        in_specs=placed,
        out_specs=(
            grid, grid, rows, P(), rows, by_batch, rows, by_batch, by_batch, by_batch, rows,
            by_batch, rows, by_batch, rows, by_batch,
        ),
        check_vma=False,
    )
```

```python
import functools
import math

import jax
import jax.numpy as jnp
from jax import lax
from jax.experimental import pallas as pl
from jax.experimental.pallas import tpu as pltpu
from jax.sharding import PartitionSpec as P

NORM_EPSILON = 1e-06
AXES = ("batch", "gy", "gx")
BF16 = jnp.bfloat16
F32 = jnp.float32
VMEM_LIMIT = 60 * 1024 * 1024


def mm(left, right):
    return lax.dot_general(left, right, (((1,), (0,)), ((), ())), preferred_element_type=F32)


def mm_nt(left, right):
    return lax.dot_general(left, right, (((1,), (1,)), ((), ())), preferred_element_type=F32)


def mm_tn(left, right):
    return lax.dot_general(left, right, (((0,), (0,)), ((), ())), preferred_element_type=F32)


def params():
    return pltpu.CompilerParams(vmem_limit_bytes=VMEM_LIMIT)


def full(shape):
    return pl.BlockSpec(shape, lambda *_: (0,) * len(shape))


def col_sum(values):
    return jnp.sum(values, axis=0, keepdims=True)


def modulation_kernel(act_ref, weight_ref, bias_ref, out_ref):
    out_ref[...] = mm(act_ref[...], weight_ref[...]) + bias_ref[...].astype(F32)


def modulation_call(act, weight, bias):
    rows, width = act.shape
    wide = weight.shape[1]
    return pl.pallas_call(
        modulation_kernel,
        grid=(wide // width,),
        in_specs=[
            full((rows, width)),
            pl.BlockSpec((width, width), lambda j: (0, j)),
            pl.BlockSpec((1, width), lambda j: (0, j)),
        ],
        out_specs=pl.BlockSpec((rows, width), lambda j: (0, j)),
        out_shape=jax.ShapeDtypeStruct((rows, wide), F32),
        compiler_params=params(),
        name="modulation",
    )(act, weight, bias)


def head_sum(values, head):
    width = 256
    row = lax.broadcasted_iota(jnp.int32, (width, width), 0) // head
    col = lax.broadcasted_iota(jnp.int32, (width, width), 1) // head
    ones = jnp.where(row == col, 1.0, 0.0).astype(BF16)
    parts = [
        mm(values[:, i : i + width].astype(BF16), ones) for i in range(0, values.shape[1], width)
    ]
    return jnp.concatenate(parts, axis=1)


def turn(values, cosine, sine, head):
    quarter = head // 4
    lane = lax.broadcasted_iota(jnp.int32, (1, 128), 1)
    first = (lane % (2 * quarter)) < quarter
    parts = []
    for i in range(0, values.shape[1], 128):
        part = values[:, i : i + 128]
        partner = jnp.where(
            first, pltpu.roll(part, 128 - quarter, 1), pltpu.roll(part, quarter, 1)
        )
        parts.append(part * cosine + partner * sine)
    return jnp.concatenate(parts, axis=1)


def project_kernel(
    head, x_ref, mod_ref, weight_ref, bias_ref, qgain_ref, kgain_ref, cos_ref, sin_ref,
    hid_ref, q_ref, k_ref, v_ref, raw_ref,
):
    width = x_ref.shape[1]
    x = x_ref[...].astype(F32)
    normed = x * lax.rsqrt(jnp.mean(x * x, axis=-1, keepdims=True) + NORM_EPSILON)
    hidden = (normed * (1.0 + mod_ref[:, width : 2 * width]) + mod_ref[:, :width]).astype(BF16)
    hid_ref[...] = hidden
    for part, (out_ref, gain_ref) in enumerate(((q_ref, qgain_ref), (k_ref, kgain_ref))):
        raw = mm(hidden, weight_ref[:, part * width : (part + 1) * width])
        raw = raw + bias_ref[:, part * width : (part + 1) * width].astype(F32)
        raw_ref[:, part * width : (part + 1) * width] = raw.astype(BF16)
        factor = lax.rsqrt(head_sum(raw * raw, head) * (1.0 / head) + NORM_EPSILON)
        scaled = raw * factor * gain_ref[...]
        out_ref[...] = turn(scaled, cos_ref[...], sin_ref[...], head).astype(BF16)
    value = mm(hidden, weight_ref[:, 2 * width :]) + bias_ref[:, 2 * width :].astype(F32)
    v_ref[...] = value.astype(BF16)


def project_call(x, mod, weight, bias, qgain, kgain, cosine, sine, head):
    rows, width = x.shape
    block = rows // 2
    by_row = lambda wide: pl.BlockSpec((block, wide), lambda i: (i, 0))
    shape = jax.ShapeDtypeStruct((rows, width), BF16)
    return pl.pallas_call(
        functools.partial(project_kernel, head),
        grid=(2,),
        in_specs=[
            by_row(width),
            full(mod.shape),
            full(weight.shape),
            full(bias.shape),
            full(qgain.shape),
            full(kgain.shape),
            by_row(128),
            by_row(128),
        ],
        out_specs=[by_row(width)] * 4 + [by_row(2 * width)],
        out_shape=[shape] * 4 + [jax.ShapeDtypeStruct((rows, 2 * width), BF16)],
        compiler_params=params(),
        name="project",
    )(x, mod, weight, bias, qgain, kgain, cosine, sine)


def attend_kernel(scale, q_ref, k0_ref, k1_ref, v0_ref, v1_ref, mix_ref, e_ref, rl_ref):
    lane = lax.broadcasted_iota(jnp.int32, (1, 128), 1)
    q = q_ref[...]
    keys = jnp.concatenate([k0_ref[...], k1_ref[...]], axis=0)
    values = jnp.concatenate([v0_ref[...], v1_ref[...]], axis=0)
    values = jnp.concatenate([values, jnp.ones_like(values)], axis=1)
    outs = []
    for h in range(2):
        mine = (lane >= 64) if h else (lane < 64)
        scores = mm_nt(jnp.where(mine, q, jnp.zeros_like(q)), keys)
        grown = jnp.exp(scores * scale).astype(BF16)
        e_ref[h] = grown
        outs.append(mm(grown, values))
    inverse = 1.0 / jnp.where(lane < 64, outs[0][:, 128:], outs[1][:, 128:])
    mix_ref[...] = (jnp.where(lane < 64, outs[0][:, :128], outs[1][:, :128]) * inverse).astype(BF16)
    rl_ref[...] = inverse


def attend_call(q, k0, k1, v0, v1, head):
    rows, width = q.shape
    pair = pl.BlockSpec((rows, 128), lambda p: (0, p))
    return pl.pallas_call(
        functools.partial(attend_kernel, head**-0.5),
        grid=(width // 128,),
        in_specs=[pair] * 5,
        out_specs=[pair, pl.BlockSpec((2, rows, 2 * rows), lambda p: (p, 0, 0)), pair],
        out_shape=[
            jax.ShapeDtypeStruct((rows, width), BF16),
            jax.ShapeDtypeStruct((width // head, rows, 2 * rows), BF16),
            jax.ShapeDtypeStruct((rows, width), F32),
        ],
        compiler_params=params(),
        name="attend",
    )(q, k0, k1, v0, v1)


def attend_back_kernel(
    scale, q_ref, k0_ref, k1_ref, v0_ref, v1_ref, e_ref, gm_ref, mix_ref, rl_ref,
    dq_ref, dk0_ref, dk1_ref, dv0_ref, dv1_ref,
):
    rows = q_ref.shape[0]
    lane = lax.broadcasted_iota(jnp.int32, (1, 128), 1)
    keys = jnp.concatenate([k0_ref[...], k1_ref[...]], axis=0)
    values = jnp.concatenate([v0_ref[...], v1_ref[...]], axis=0)
    scaled = gm_ref[...].astype(F32) * rl_ref[...]
    products = scaled * mix_ref[...].astype(F32)
    scaled = scaled.astype(BF16)
    q_t = q_ref[...].T
    scaled_t = scaled.T
    dqs, dks, dvs = [], [], []
    for h in range(2):
        mine = (lane >= 64) if h else (lane < 64)
        inner = jnp.sum(jnp.where(mine, products, 0.0), axis=1, keepdims=True)
        grad_probs = mm_nt(jnp.where(mine, scaled, jnp.zeros_like(scaled)), values)
        grown = e_ref[h]
        grad_scores = (grown.astype(F32) * (grad_probs - inner) * scale).astype(BF16)
        dqs.append(mm(grad_scores, keys))
        dks.append(mm(q_t[64 * h : 64 * h + 64], grad_scores))
        dvs.append(mm(scaled_t[64 * h : 64 * h + 64], grown))
    dq_ref[...] = jnp.where(lane < 64, dqs[0], dqs[1]).astype(BF16)
    dk = jnp.concatenate(dks, axis=0).T.astype(BF16)
    dv = jnp.concatenate(dvs, axis=0).T.astype(BF16)
    dk0_ref[...] = dk[:rows]
    dk1_ref[...] = dk[rows:]
    dv0_ref[...] = dv[:rows]
    dv1_ref[...] = dv[rows:]


def attend_back_call(q, k0, k1, v0, v1, grown, grad_mixed, mixed, inverse, head):
    rows, width = q.shape
    pair = pl.BlockSpec((rows, 128), lambda p: (0, p))
    return pl.pallas_call(
        functools.partial(attend_back_kernel, head**-0.5),
        grid=(width // 128,),
        in_specs=[pair] * 5
        + [pl.BlockSpec((2, rows, 2 * rows), lambda p: (p, 0, 0))]
        + [pair] * 3,
        out_specs=[pair] * 5,
        out_shape=[jax.ShapeDtypeStruct((rows, width), BF16)] * 5,
        compiler_params=params(),
        name="attend_back",
    )(q, k0, k1, v0, v1, grown, grad_mixed, mixed, inverse)


def middle_kernel(
    mix_ref, x_ref, dy_ref, mod_ref, weight_ref, bias_ref, att_ref, mid_ref, h2_ref, h2t_ref, gf_ref
):
    width = x_ref.shape[1]
    attended = mm(mix_ref[...], weight_ref[...]) + bias_ref[...].astype(F32)
    middle = x_ref[...].astype(F32) + mod_ref[:, 2 * width : 3 * width] * attended
    normed = middle * lax.rsqrt(jnp.mean(middle * middle, axis=-1, keepdims=True) + NORM_EPSILON)
    hidden = normed * (1.0 + mod_ref[:, 4 * width : 5 * width]) + mod_ref[:, 3 * width : 4 * width]
    hidden = hidden.astype(BF16)
    att_ref[...] = attended.astype(BF16)
    mid_ref[...] = middle
    h2_ref[...] = hidden
    h2t_ref[...] = hidden.T
    gf_ref[...] = (mod_ref[:, 5 * width :] * dy_ref[...].astype(F32)).astype(BF16)


def middle_call(mixed, x, dy, mod, weight, bias, bias_at=0):
    rows, width = x.shape
    block = rows // 2
    by_row = pl.BlockSpec((block, width), lambda i: (i, 0))
    low = jax.ShapeDtypeStruct((rows, width), BF16)
    return pl.pallas_call(
        middle_kernel,
        grid=(2,),
        in_specs=[by_row] * 3
        + [full(mod.shape), full(weight.shape), pl.BlockSpec((1, width), lambda i: (0, bias_at))],
        out_specs=[by_row] * 3 + [pl.BlockSpec((width, block), lambda i: (0, i)), by_row],
        out_shape=[low, jax.ShapeDtypeStruct((rows, width), F32), low]
        + [jax.ShapeDtypeStruct((width, rows), BF16), low],
        compiler_params=params(),
        name="middle",
    )(mixed, x, dy, mod, weight, bias)


def feed_kernel(
    h2_ref, h2t_ref, gf_ref, wg_ref, wu_ref, bg_ref, bu_ref, wd_ref, feed_in_ref, gh_in_ref,
    feed_ref, gh_ref, dd_ref, dg_ref, db_ref,
):
    @pl.when(pl.program_id(0) == 0)
    def _():
        feed_ref[...] = feed_in_ref[...]
        gh_ref[...] = gh_in_ref[...]

    hidden = h2_ref[...]
    grad_feed = gf_ref[...]
    gate = mm(hidden, wg_ref[...]) + bg_ref[...].astype(F32)
    up = mm(hidden, wu_ref[...]) + bu_ref[...].astype(F32)
    grad_product = mm_nt(grad_feed, wd_ref[...])
    sig = 1.0 / (1.0 + jnp.exp(-gate))
    active = gate * sig
    product = (active * up).astype(BF16)
    grad_gate = (grad_product * up * sig * (1.0 + gate * (1.0 - sig))).astype(BF16)
    grad_up = (grad_product * active).astype(BF16)
    dd_ref[...] = mm_tn(product, grad_feed).astype(BF16)
    dg_ref[0] = mm(h2t_ref[...], grad_gate).astype(BF16)
    dg_ref[1] = mm(h2t_ref[...], grad_up).astype(BF16)
    db_ref[0] = col_sum(grad_gate.astype(F32))
    db_ref[1] = col_sum(grad_up.astype(F32))
    feed_ref[...] += mm(product, wd_ref[...])
    gh_ref[...] += mm_nt(grad_gate, wg_ref[...]) + mm_nt(grad_up, wu_ref[...])


def feed_call(hidden, hidden_t, grad_feed, weight, bias, down, feed, grad_hidden, first, step, unit):
    rows, width = hidden.shape
    blocks = down.shape[0] // unit
    steps = len(range(first, blocks, step))
    pick = lambda s: first + step * s
    acc = jax.ShapeDtypeStruct((rows, width), F32)
    return pl.pallas_call(
        feed_kernel,
        grid=(steps,),
        in_specs=[
            full((rows, width)),
            full((width, rows)),
            full((rows, width)),
            pl.BlockSpec((width, unit), lambda s: (0, pick(s))),
            pl.BlockSpec((width, unit), lambda s: (0, blocks + pick(s))),
            pl.BlockSpec((1, unit), lambda s: (0, pick(s))),
            pl.BlockSpec((1, unit), lambda s: (0, blocks + pick(s))),
            pl.BlockSpec((unit, width), lambda s: (pick(s), 0)),
            full((rows, width)),
            full((rows, width)),
        ],
        out_specs=[
            full((rows, width)),
            full((rows, width)),
            pl.BlockSpec((None, unit, width), lambda s: (s, 0, 0)),
            pl.BlockSpec((None, 2, width, unit), lambda s: (s, 0, 0, 0)),
            pl.BlockSpec((None, 2, 1, unit), lambda s: (s, 0, 0, 0)),
        ],
        out_shape=[
            acc,
            acc,
            jax.ShapeDtypeStruct((steps, unit, width), BF16),
            jax.ShapeDtypeStruct((steps, 2, width, unit), BF16),
            jax.ShapeDtypeStruct((steps, 2, 1, unit), F32),
        ],
        compiler_params=params(),
        name="feed",
    )(hidden, hidden_t, grad_feed, weight, weight, bias, bias, down, feed, grad_hidden)


def turn_kernel(
    feed_ref, gh_ref, mid_ref, att_ref, dy_ref, gf_ref, mix_ref, mod_ref, weight_ref, dbias_ref,
    out_ref, gmid_ref, gmix_ref, dw_ref, sums_ref,
):
    width = mid_ref.shape[1]
    half = width // 2
    dy = dy_ref[...].astype(F32)
    feed = feed_ref[...] + dbias_ref[...].astype(F32)
    middle = mid_ref[...]
    out_ref[...] = (middle + mod_ref[:, 5 * width :] * feed).astype(BF16)
    factor = lax.rsqrt(jnp.mean(middle * middle, axis=-1, keepdims=True) + NORM_EPSILON)
    normed = middle * factor
    grad_hidden = gh_ref[...]
    product = grad_hidden * normed
    grad_normed = grad_hidden * (1.0 + mod_ref[:, 4 * width : 5 * width])
    back = factor * (
        grad_normed - normed * jnp.mean(grad_normed * normed, axis=-1, keepdims=True)
    )
    grad_middle = dy + back
    gmid_ref[...] = grad_middle
    grad_attended = (mod_ref[:, 2 * width : 3 * width] * grad_middle).astype(BF16)
    sums_ref[0:1, :] = col_sum(grad_middle * att_ref[...].astype(F32))
    sums_ref[1:2, :] = col_sum(grad_hidden)
    sums_ref[2:3, :] = col_sum(product)
    sums_ref[3:4, :] = col_sum(dy * feed)
    sums_ref[4:5, :] = col_sum(grad_attended.astype(F32))
    sums_ref[5:6, :] = col_sum(gf_ref[...].astype(F32))
    sums_ref[6:8, :] = jnp.zeros((2, width), F32)
    gmix_ref[...] = mm_nt(grad_attended, weight_ref[...]).astype(BF16)
    mixed_t = mix_ref[...].T
    dw_ref[0] = mm(mixed_t, grad_attended[:, :half]).astype(BF16)
    dw_ref[1] = mm(mixed_t, grad_attended[:, half:]).astype(BF16)


def turn_call(feed, grad_hidden, middle, attended, dy, grad_feed, mixed, mod, weight, down_bias):
    rows, width = middle.shape
    low = jax.ShapeDtypeStruct((rows, width), BF16)
    return pl.pallas_call(
        turn_kernel,
        out_shape=[
            low,
            jax.ShapeDtypeStruct((rows, width), F32),
            low,
            jax.ShapeDtypeStruct((2, width, width // 2), BF16),
            jax.ShapeDtypeStruct((8, width), F32),
        ],
        compiler_params=params(),
        name="turn",
    )(feed, grad_hidden, middle, attended, dy, grad_feed, mixed, mod, weight, down_bias)


def project_back_kernel(
    head, dq_ref, dk0_ref, dk1_ref, dv0_ref, dv1_ref, raw_ref, hid_ref, x_ref, gmid_ref, mod_ref,
    weight_ref, qgain_ref, kgain_ref, cos_ref, sin_ref,
    gx_ref, dw_ref, sums_ref, bias_ref, proj_ref,
):
    width = x_ref.shape[1]
    cosine, sine = cos_ref[...], -sin_ref[...]
    for part in range(3):
        span = slice(part * width, (part + 1) * width)
        if part == 2:
            grad = dv0_ref[...].astype(F32) + dv1_ref[...].astype(F32)
        else:
            grad = dq_ref[...].astype(F32)
            if part == 1:
                grad = dk0_ref[...].astype(F32) + dk1_ref[...].astype(F32)
            gain = (qgain_ref, kgain_ref)[part][...]
            raw = raw_ref[:, span].astype(F32)
            factor = lax.rsqrt(head_sum(raw * raw, head) * (1.0 / head) + NORM_EPSILON)
            normed = raw * factor
            turned = turn(grad, cosine, sine, head)
            sums_ref[2 + part : 3 + part, :] = col_sum(turned * normed)
            turned = turned * gain
            mean = head_sum(turned * normed, head) * (1.0 / head)
            grad = factor * (turned - normed * mean)
        low = grad.astype(BF16)
        proj_ref[:, span] = low
        bias_ref[:, span] = col_sum(low.astype(F32))
    hidden_t = hid_ref[...].T
    half = 3 * width // 2
    dw_ref[0] = mm(hidden_t, proj_ref[:, :half]).astype(BF16)
    dw_ref[1] = mm(hidden_t, proj_ref[:, half:]).astype(BF16)
    grad_hidden = mm_nt(proj_ref[...], weight_ref[...])
    x = x_ref[...].astype(F32)
    factor = lax.rsqrt(jnp.mean(x * x, axis=-1, keepdims=True) + NORM_EPSILON)
    normed = x * factor
    sums_ref[0:1, :] = col_sum(grad_hidden)
    sums_ref[1:2, :] = col_sum(grad_hidden * normed)
    sums_ref[4:8, :] = jnp.zeros((4, width), F32)
    grad_normed = grad_hidden * (1.0 + mod_ref[:, width : 2 * width])
    back = factor * (
        grad_normed - normed * jnp.mean(grad_normed * normed, axis=-1, keepdims=True)
    )
    gx_ref[...] = (gmid_ref[...] + back).astype(BF16)


def project_back_call(
    dq, dk0, dk1, dv0, dv1, raw, hidden, x, grad_middle, mod, weight, qgain, kgain, cosine, sine, head
):
    rows, width = x.shape
    return pl.pallas_call(
        functools.partial(project_back_kernel, head),
        out_shape=[
            jax.ShapeDtypeStruct((rows, width), BF16),
            jax.ShapeDtypeStruct((2, width, 3 * width // 2), BF16),
            jax.ShapeDtypeStruct((8, width), F32),
            jax.ShapeDtypeStruct((1, 3 * width), F32),
        ],
        scratch_shapes=[pltpu.VMEM((rows, 3 * width), BF16)],
        compiler_params=params(),
        name="project_back",
    )(dq, dk0, dk1, dv0, dv1, raw, hidden, x, grad_middle, mod, weight, qgain, kgain, cosine, sine)


class Place:
    def __init__(self):
        self.z, self.gy, self.gx = (lax.axis_index(name) for name in AXES)
        self.core = lax.rem(self.gx, 2)
        self.side = self.gx // 2
        self.chip = 2 * self.gy + self.side

    def flipped(self, k):
        return 2 * lax.rem(self.gy + k // 2, 2) + lax.rem(self.side + lax.rem(k, 2), 2)

    def pair(self):
        return {"gx": self.gx + 1 - 2 * self.core}

    def plane(self, k):
        device = {}
        if k & 2:
            device["gy"] = 1 - self.gy
        if k & 1:
            device["gx"] = lax.rem(self.gx + 2, 4)
        return device

    def depth(self, d):
        return {"batch": self.flipped_z(d)}

    def flipped_z(self, d):
        return {1: self.z + 1 - 2 * lax.rem(self.z, 2), 2: lax.rem(self.z + 2, 4), 3: 3 - self.z}[d]


def meet(devices):
    barrier = pltpu.get_barrier_semaphore()
    for device in devices:
        pl.semaphore_signal(barrier, inc=1, device_id=device, device_id_type=pl.DeviceIdType.MESH)
    pl.semaphore_wait(barrier, len(devices))


def send(source, target, send_sem, recv_sem, device):
    return pltpu.make_async_remote_copy(
        src_ref=source, dst_ref=target, send_sem=send_sem, recv_sem=recv_sem, device_id=device,
        device_id_type=pl.DeviceIdType.MESH,
    )


def feed_order(step):
    owner = jnp.where(
        step < 2, 3, jnp.where((step == 2) | (step == 5), 2, jnp.where(step < 5, 1, 0))
    )
    return owner, lax.rem(step, 2)


def feed_block(step, i):
    step = jnp.minimum(step, 7)
    owner, half = feed_order(step)
    return (2 * half + i) * 4 + Place().flipped(owner)


def feed_turn_kernel(
    h2_ref, h2t_ref, gf_ref, wg0, wg1, wu0, wu1, bg0, bg1, bu0, bu1, wd0, wd1,
    mid_ref, att_ref, dy_ref, mix_ref, mod_ref, weight_ref, dbias_ref, known_ref,
    out_ref, gmid_ref, gmix_ref, dw_ref, sums_ref, total_ref,
    feed_ref, gh_ref, bias_ref, made, paired, near, pair_send, pair_recv, near_send, near_recv,
):
    place = Place()
    core = place.core
    step = pl.program_id(0)
    slot = lax.rem(step, 2)
    width = h2_ref.shape[1]
    unit = 128
    g_rows = width

    @pl.when(step == 0)
    def _():
        feed_ref[...] = jnp.zeros_like(feed_ref)
        sums_ref[1] = jnp.zeros((8, width), F32)
        gh_ref[...] = jnp.zeros_like(gh_ref)
        meet([place.pair(), place.plane(1), place.plane(2)])

    def pair_copy(of):
        return send(
            made.at[lax.rem(of, 2), 1 - core], paired.at[of], pair_send.at[lax.rem(of, 2)],
            pair_recv.at[of], place.pair(),
        )

    def near_copy(of, k):
        return send(paired.at[of], near.at[of], near_send.at[of], near_recv.at[of], place.plane(k))

    @pl.when(step >= 1)
    def _():
        pair_copy(step - 1).start()

    @pl.when(step < 8)
    def _():
        owner, half = feed_order(step)
        hidden = h2_ref[...]
        grad_feed = gf_ref[...]
        wg = jnp.concatenate([wg0[...], wg1[...]], axis=1)
        wu = jnp.concatenate([wu0[...], wu1[...]], axis=1)
        wd = jnp.concatenate([wd0[...], wd1[...]], axis=0)
        gate = mm(hidden, wg) + jnp.concatenate([bg0[...], bg1[...]], axis=1).astype(F32)
        up = mm(hidden, wu) + jnp.concatenate([bu0[...], bu1[...]], axis=1).astype(F32)
        grad_product = mm_nt(grad_feed, wd)
        sig = 1.0 / (1.0 + jnp.exp(-gate))
        active = gate * sig
        product = (active * up).astype(BF16)
        grad_gate = (grad_product * up * sig * (1.0 + gate * (1.0 - sig))).astype(BF16)
        grad_up = (grad_product * active).astype(BF16)
        feed_ref[...] += mm(product, wd)
        gh_ref[...] += mm_nt(grad_gate, wg) + mm_nt(grad_up, wu)
        for e, grad in enumerate((grad_gate, grad_up)):
            total = col_sum(grad.astype(F32))
            for i in range(2):
                row = 16 * e + (2 * half + i) * 4 + place.flipped(owner)
                bias_ref[pl.ds(row, 1), :] = total[:, i * unit : (i + 1) * unit]

        @pl.when(step >= 2)
        def _():
            pair_copy(step - 2).wait_send()

        for e, grad in enumerate((grad_gate, grad_up)):
            made[slot, e, :g_rows] = mm(h2t_ref[...], grad).astype(BF16)
        product_t = product.T
        for b in range(3):
            d = mm(product_t, grad_feed[:, 256 * b : 256 * b + 256]).astype(BF16)
            for i in range(2):
                for c in range(2):
                    made[slot, c, pl.ds(g_rows + b * 128 + i * 64, 64)] = d[
                        i * 128 + c * 64 : i * 128 + c * 64 + 64
                    ]

    @pl.when(step >= 1)
    def _():
        of = step - 1
        copy = pair_copy(of)
        copy.wait_recv()
        late = (of == 4) | (of == 5)

        @pl.when(jnp.logical_not(late))
        def _():
            paired[of] = (made[1 - slot, core].astype(F32) + paired[of].astype(F32)).astype(BF16)

        @pl.when(late)
        def _():
            near_copy(of - 4, 1).wait_recv()
            paired[of] = (
                made[1 - slot, core].astype(F32)
                + paired[of].astype(F32)
                + near[of - 4].astype(F32)
            ).astype(BF16)

        @pl.when((of == 0) | (of == 2) | (of == 5))
        def _():
            near_copy(of, 2).start()

        @pl.when((of == 1) | (of == 3) | (of == 4))
        def _():
            near_copy(of, 1).start()

    @pl.when(step == 8)
    def _():
        half = width // 2
        dy = dy_ref[...].astype(F32)
        feed = feed_ref[...] + dbias_ref[...].astype(F32)
        middle = mid_ref[...]
        out_ref[...] = (middle + mod_ref[:, 5 * width :] * feed).astype(BF16)
        factor = lax.rsqrt(jnp.mean(middle * middle, axis=-1, keepdims=True) + NORM_EPSILON)
        normed = middle * factor
        grad_hidden = gh_ref[...]
        product = grad_hidden * normed
        grad_normed = grad_hidden * (1.0 + mod_ref[:, 4 * width : 5 * width])
        back = factor * (
            grad_normed - normed * jnp.mean(grad_normed * normed, axis=-1, keepdims=True)
        )
        grad_middle = dy + back
        gmid_ref[...] = grad_middle
        grad_attended = (mod_ref[:, 2 * width : 3 * width] * grad_middle).astype(BF16)
        sums_ref[0, 0:1, :] = col_sum(grad_middle * att_ref[...].astype(F32))
        sums_ref[0, 1:2, :] = col_sum(grad_hidden)
        sums_ref[0, 2:3, :] = col_sum(product)
        sums_ref[0, 3:4, :] = col_sum(dy * feed)
        sums_ref[0, 4:5, :] = col_sum(grad_attended.astype(F32))
        sums_ref[0, 5:6, :] = col_sum(gf_ref[...].astype(F32))
        sums_ref[0, 6:8, :] = known_ref[...]
        for row in range(32):
            col = (row % 6) * unit
            sums_ref[1, row // 6 : row // 6 + 1, col : col + unit] = bias_ref[row : row + 1, :]
        gmix_ref[...] = mm_nt(grad_attended, weight_ref[...]).astype(BF16)
        mixed_t = mix_ref[...].T
        dw_ref[0] = mm(mixed_t, grad_attended[:, :half]).astype(BF16)
        dw_ref[1] = mm(mixed_t, grad_attended[:, half:]).astype(BF16)
        for of in (6, 7):
            pair_copy(of).wait_send()
        for of in (2, 3, 4, 5):
            near_copy(of, 1).wait_recv()
        for of in range(6):
            near_copy(of, 1).wait_send()
        rows = width // 4
        for f in range(2):
            for z in range(4):
                span = slice(z * rows, (z + 1) * rows)
                total_ref[z, f] = sum(
                    part.astype(F32)
                    for part in (paired[6 + f, span], near[2 + f, span], near[4 + f, span])
                ).astype(BF16)
            for i in range(2):
                for b in range(3):
                    span = slice(g_rows + b * 128 + i * 64, g_rows + b * 128 + i * 64 + 64)
                    total_ref[2 * f + i, 2, b * 64 : b * 64 + 64] = sum(
                        part.astype(F32)
                        for part in (paired[6 + f, span], near[2 + f, span], near[4 + f, span])
                    ).astype(BF16)


def once(shape):
    return pl.BlockSpec(shape, lambda *_: (0,) * len(shape), pipeline_mode=pl.Buffered(1))


def feed_turn_call(
    hidden, hidden_t, grad_feed, gate_up, down, middle, attended, dy, mixed, mod, weight, small,
    known,
):
    rows, width = hidden.shape
    low = jax.ShapeDtypeStruct((rows, width), BF16)
    wide = jax.ShapeDtypeStruct((rows, width), F32)
    cols = lambda i, e: pl.BlockSpec((width, 128), lambda s: (0, 16 * e + feed_block(s, i)))
    first = GATE_BIAS * width // 128
    bias = lambda i, e: pl.BlockSpec((1, 128), lambda s: (0, first + 16 * e + feed_block(s, i)))
    down_bias = pl.BlockSpec((1, width), lambda s: (0, DOWN_BIAS), pipeline_mode=pl.Buffered(1))
    deep = lambda i: pl.BlockSpec((128, width), lambda s: (feed_block(s, i), 0))
    piece = (width + 384, 256)
    out_shape = [
        low, wide, low,
        jax.ShapeDtypeStruct((2, width, width // 2), BF16),
        jax.ShapeDtypeStruct((2, 8, width), F32),
        jax.ShapeDtypeStruct((4, 3, width // 4, 256), BF16),
    ]
    return pl.pallas_call(
        feed_turn_kernel,
        grid=(9,),
        in_specs=[once((rows, width)), once((width, rows)), once((rows, width))]
        + [cols(0, 0), cols(1, 0), cols(0, 1), cols(1, 1)]
        + [bias(0, 0), bias(1, 0), bias(0, 1), bias(1, 1)]
        + [deep(0), deep(1)]
        + [once((rows, width))] * 4
        + [once(mod.shape), once(weight.shape), down_bias, once(known.shape)],
        out_specs=[full(shape.shape) for shape in out_shape],
        out_shape=out_shape,
        scratch_shapes=[
            pltpu.VMEM((rows, width), F32),
            pltpu.VMEM((rows, width), F32),
            pltpu.VMEM((32, 128), F32),
            pltpu.VMEM((2, 2) + piece, BF16),
            pltpu.VMEM((8,) + piece, BF16),
            pltpu.VMEM((6,) + piece, BF16),
            pltpu.SemaphoreType.DMA((2,)),
            pltpu.SemaphoreType.DMA((8,)),
            pltpu.SemaphoreType.DMA((6,)),
            pltpu.SemaphoreType.DMA((6,)),
        ],
        compiler_params=pltpu.CompilerParams(
            vmem_limit_bytes=VMEM_LIMIT, collective_id=1, has_side_effects=True
        ),
        name="feed_turn",
    )(
        hidden, hidden_t, grad_feed, gate_up, gate_up, gate_up, gate_up, small, small, small,
        small, down, down, middle, attended, dy, mixed, mod, weight, small, known,
    )


IN_BIAS, Q_GAIN, K_GAIN, OUT_BIAS, DOWN_BIAS, GATE_BIAS = 6, 9, 10, 11, 12, 13


def small_row(width, head, modulate, inproj, qgain, kgain, outproj, down, gate_up):
    heads = width // head
    return jnp.concatenate(
        [modulate, inproj, jnp.tile(qgain, heads), jnp.tile(kgain, heads), outproj, down, gate_up]
    )[None]


def front_kernel(
    head, tile_cols, tok_hbm, grad_hbm, act_ref, small_ref, modw_hbm, inw_hbm,
    x_hbm, dy_hbm, hid_hbm, q_hbm, k0_hbm, v0_hbm, k1_hbm, v1_hbm, raw_hbm, mod_ref, cos_ref,
    sin_ref,
    x_ref, own_ref, hid_ref, q_ref, k_ref, v_ref, raw_ref, modw_ref, inw_ref,
    load_sem, store_sem, tok_send, tok_recv, kv_send, kv_recv,
):
    place = Place()
    core, chip = place.core, place.chip
    rows, width = x_ref.shape
    cells = rows // 4
    loads = [
        pltpu.make_async_copy(source, target, load_sem.at[i])
        for i, (source, target) in enumerate(
            (
                (tok_hbm.at[chip], x_ref.at[pl.ds(0, cells)]), (modw_hbm, modw_ref),
                (inw_hbm, inw_ref), (grad_hbm.at[chip], own_ref),
            )
        )
    ]
    stores = [
        pltpu.make_async_copy(source, target, store_sem.at[i])
        for i, (source, target) in enumerate(
            (
                (own_ref, dy_hbm.at[pl.ds(0, cells)]), (x_ref, x_hbm), (hid_ref, hid_hbm),
                (k_ref, k0_hbm), (v_ref, v0_hbm), (q_ref, q_hbm), (raw_ref, raw_hbm),
            )
        )
    ]

    def token_copy(which, k):
        source, target = ((tok_hbm, x_ref), (grad_hbm, dy_hbm))[which]
        return send(
            source.at[place.flipped(k)], target.at[pl.ds(k * cells, cells)],
            tok_send.at[which, k - 1], tok_recv.at[which, k - 1], place.plane(k),
        )

    def kv_copy(which, chunk):
        source, target = ((k_ref, k1_hbm), (v_ref, v1_hbm))[which]
        span = pl.ds(chunk * cells, cells if chunk == 0 else rows - cells)
        return send(
            source.at[span], target.at[span], kv_send.at[which, chunk], kv_recv.at[which, chunk],
            place.pair(),
        )

    def vector(start, count=1):
        return small_ref[:, start * width : (start + count) * width].astype(F32)

    def project(start, size, chunk):
        span = slice(start, start + size)
        x = x_ref[span, :].astype(F32)
        normed = x * lax.rsqrt(jnp.mean(x * x, axis=-1, keepdims=True) + NORM_EPSILON)
        hidden = normed * (1.0 + mod_ref[:, width : 2 * width]) + mod_ref[:, :width]
        hidden = hidden.astype(BF16)
        hid_ref[span, :] = hidden
        for part in (1, 2, 0):
            raw = mm(hidden, inw_ref[:, part * width : (part + 1) * width]) + vector(IN_BIAS + part)
            if part == 2:
                v_ref[span, :] = raw.astype(BF16)
                for which in (0, 1):
                    kv_copy(which, chunk).start()
                continue
            raw_ref[span, part * width : (part + 1) * width] = raw.astype(BF16)
            factor = lax.rsqrt(head_sum(raw * raw, head) * (1.0 / head) + NORM_EPSILON)
            scaled = raw * factor * vector((Q_GAIN, K_GAIN)[part])
            turned = turn(scaled, cos_ref[span, :], sin_ref[span, :], head).astype(BF16)
            (q_ref, k_ref)[part][span, :] = turned

    for load in loads:
        load.start()
    meet([place.pair()] + [place.plane(k) for k in (1, 2, 3)])
    for k in (3, 1, 2):
        token_copy(0, k).start()

    quarter = head // 4
    lane = lax.broadcasted_iota(jnp.int32, (1, 128), 1)
    rate = jnp.exp(-math.log(10000.0) / quarter * lax.rem(lane, quarter).astype(F32))
    by_row = lax.rem(lane, head) < head // 2
    sign = jnp.where(lax.rem(lane, 2 * quarter) < quarter, -1.0, 1.0)
    cell = lax.broadcasted_iota(jnp.int32, (cells, 128), 0)
    row, col = cell // tile_cols, lax.rem(cell, tile_cols)
    for k in range(4):
        there = place.flipped(k)
        down = (there // 2) * (cells // tile_cols) + row
        across = (2 * lax.rem(there, 2) + core) * tile_cols + col
        angle = jnp.where(by_row, down, across).astype(F32) * rate
        cos_ref[k * cells : (k + 1) * cells, :] = jnp.cos(angle)
        sin_ref[k * cells : (k + 1) * cells, :] = sign * jnp.sin(angle)
    loads[1].wait()
    mod_ref[...] = mm(act_ref[...], modw_ref[...])[:1] + vector(0, 6)
    loads[0].wait()
    loads[2].wait()
    project(0, cells, 0)
    loads[3].wait()
    stores[0].start()
    for k in (1, 2, 3):
        token_copy(0, k).wait()
    for k in (3, 1, 2):
        token_copy(1, k).start()
    stores[1].start()
    project(cells, rows - cells, 1)
    for store in stores[2:]:
        store.start()
    for which in (0, 1):
        for chunk in (0, 1):
            kv_copy(which, chunk).wait()
    for k in (1, 2, 3):
        token_copy(1, k).wait()
    for store in stores:
        store.wait()


def front_call(tokens, grads, act, small, modw, inw, head, tile_cols):
    images, cells, width = tokens.shape
    rows = images * cells
    low = lambda *shape: jax.ShapeDtypeStruct(shape, BF16)
    vmem = lambda *shape: pltpu.VMEM(shape, BF16)
    anywhere = pl.BlockSpec(memory_space=pl.ANY)
    inside = pl.BlockSpec(memory_space=pltpu.VMEM)
    sems = lambda *shape: pltpu.SemaphoreType.DMA(shape)
    return pl.pallas_call(
        functools.partial(front_kernel, head, tile_cols),
        in_specs=[anywhere] * 2 + [inside] * 2 + [anywhere] * 2,
        out_specs=[anywhere] * 9 + [inside] * 3,
        out_shape=[low(rows, width)] * 8
        + [
            low(rows, 2 * width), jax.ShapeDtypeStruct((1, 6 * width), F32),
            jax.ShapeDtypeStruct((rows, 128), F32), jax.ShapeDtypeStruct((rows, 128), F32),
        ],
        scratch_shapes=[
            vmem(rows, width), vmem(cells, width), vmem(rows, width), vmem(rows, width),
            vmem(rows, width), vmem(rows, width), vmem(rows, 2 * width), vmem(*modw.shape),
            vmem(*inw.shape), sems(4), sems(7), sems(2, 3), sems(2, 3), sems(2, 2), sems(2, 2),
        ],
        compiler_params=pltpu.CompilerParams(
            vmem_limit_bytes=VMEM_LIMIT, collective_id=3, has_side_effects=True
        ),
        name="front",
    )(tokens, grads, act, small, modw, inw)


Z_FIRST = (False, False, True, False)
GROUPS = 4


def back_kernel(
    head, q_ref, k0_ref, k1_ref, v0_ref, v1_ref, gm_ref, mix_ref, rl_ref, e_ref,
    mod_ref, qgain_ref, kgain_ref, cos_ref, sin_ref, dout_ref, totals_ref, early_ref,
    raw_hbm, hid_hbm, x_hbm, gmid_hbm, weight_hbm, rows_hbm,
    output_ref, gtok_ref, feeds_hbm, projs_hbm, early_hbm, late_hbm,
    feeds_ref, projs_ref, early_all, late_all, raw_ref, hid_ref, x_ref, gmid_ref, weight_ref, hidt_ref, gh_ref, gx_ref, late_ref,
    dq_s, dk0_s, dv0_s, dk1_s, dv1_s, dk_in, dv_in,
    made, paired, first_out, first_in, second_out, second_in, z_in, early_in, late_in,
    load_sem, own_sem, kv_send, kv_recv, pair_send, pair_recv, first_send, first_recv,
    second_send, second_recv, z_send, z_recv, tok_send, tok_recv, feed_send, feed_recv,
    proj_send, proj_recv, small_send, small_recv,
):
    place = Place()
    core, chip, z = place.core, place.chip, place.z
    step = pl.program_id(0)
    rows, width = x_ref.shape
    cells = rows // 4
    scale = head**-0.5
    lane = lax.broadcasted_iota(jnp.int32, (1, 128), 1)

    loads = [
        pltpu.make_async_copy(source, target, load_sem.at[i])
        for i, (source, target) in enumerate(
            (
                (hid_hbm, hid_ref), (raw_hbm, raw_ref), (weight_hbm, weight_ref),
                (x_hbm, x_ref), (gmid_hbm, gmid_ref),
            )
        )
    ]

    stores = [
        pltpu.make_async_copy(source, target, load_sem.at[5 + i])
        for i, (source, target) in enumerate(
            (
                (early_all, early_hbm), (late_all, late_hbm), (feeds_ref, feeds_hbm),
                (projs_ref, projs_hbm),
            )
        )
    ]

    def z_copy(d):
        return send(
            totals_ref.at[place.flipped_z(d)], z_in.at[d - 1], z_send.at[d - 1], z_recv.at[d - 1],
            place.depth(d),
        )

    def token_copy(which, k):
        source, target = ((rows_hbm, output_ref), (gx_ref, gtok_ref))[which]
        return send(
            source.at[pl.ds(k * cells, cells)], target.at[chip], tok_send.at[which, k - 1],
            tok_recv.at[which, k - 1], place.plane(k),
        )

    def own_tokens(which):
        source, target = ((rows_hbm, output_ref), (gx_ref, gtok_ref))[which]
        return pltpu.make_async_copy(source.at[pl.ds(0, cells)], target.at[chip], own_sem.at[which])

    def kv_copy(which, p):
        source, target = ((dk1_s, dk_in), (dv1_s, dv_in))[which]
        return send(
            source.at[p], target.at[p], kv_send.at[which, p], kv_recv.at[which, p], place.pair()
        )

    def pair_copy(g):
        source = dout_ref.at[1 - core] if g == 3 else made.at[g % 2, 1 - core]
        return send(source, paired.at[g], pair_send.at[g], pair_recv.at[g], place.pair())

    def first_copy(g, k):
        other = place.flipped_z(k) if Z_FIRST[g] else place.flipped(k)
        device = place.depth(k) if Z_FIRST[g] else place.plane(k)
        return send(
            first_out.at[g, other], first_in.at[g, k - 1], first_send.at[g, k - 1],
            first_recv.at[g, k - 1], device,
        )

    def second_copy(g, k):
        other = place.flipped(k) if Z_FIRST[g] else place.flipped_z(k)
        device = place.plane(k) if Z_FIRST[g] else place.depth(k)
        return send(
            second_out.at[g, other], second_in.at[g, k - 1], second_send.at[g, k - 1],
            second_recv.at[g, k - 1], device,
        )

    def feed_copy(k):
        here = feeds_ref.at[core, chip]
        return send(here, here, feed_send.at[k - 1], feed_recv.at[k - 1], place.plane(k))

    def feed_pair():
        here = feeds_ref.at[core]
        return send(here, here, feed_send.at[3], feed_recv.at[3], place.pair())

    def proj_copy(k):
        here = projs_ref.at[core, chip]
        return send(here, here, proj_send.at[k - 1], proj_recv.at[k - 1], place.plane(k))

    def proj_pair():
        here = projs_ref.at[core]
        return send(here, here, proj_send.at[3], proj_recv.at[3], place.pair())

    smalls = ((early_ref, early_in, early_all, 8), (late_ref, late_in, late_all, 4))

    def small_pair(which):
        source, target, _, count = smalls[which]
        return send(
            source.at[1 - core], target, small_send.at[which, 0], small_recv.at[which, 0],
            place.pair(),
        )

    def small_plane(which, k):
        full_ref = smalls[which][2]
        return send(
            full_ref.at[core, pl.ds(0, 1)], full_ref.at[core, pl.ds(k, 1)],
            small_send.at[which, k], small_recv.at[which, k], place.plane(k),
        )

    def small_depth(which, d):
        full_ref = smalls[which][2]
        have = 4 * d
        return send(
            full_ref.at[core, pl.ds(0, have)], full_ref.at[core, pl.ds(have, have)],
            small_send.at[which, 3 + d], small_recv.at[which, 3 + d], place.depth(d),
        )

    def small_last(which):
        here = smalls[which][2].at[core]
        return send(
            here, here, small_send.at[which, 6], small_recv.at[which, 6], place.pair()
        )

    def small_begin(which):
        source, target, full_ref, _ = smalls[which]
        small_pair(which).wait_recv()
        full_ref[core, 0] = source[core] + target[...]
        for k in (1, 2, 3):
            small_plane(which, k).start()

    def small_next(which, i):
        if i == 0:
            for k in (1, 2, 3):
                small_plane(which, k).wait_recv()
            small_depth(which, 1).start()
        elif i == 1:
            small_depth(which, 1).wait_recv()
            small_depth(which, 2).start()
        else:
            small_depth(which, 2).wait_recv()
            small_last(which).start()

    def start_group(g):
        pair_copy(g).wait_recv()
        mine = dout_ref.at[core] if g == 3 else made.at[g % 2, core]
        part = width // 16
        for a in range(4):
            for b in range(4):
                span = pl.ds((a * 4 + b) * part, part)
                total = (mine[span, :].astype(F32) + paired[g, span].astype(F32)).astype(BF16)
                if Z_FIRST[g]:
                    first_out[g, a, b] = total
                else:
                    first_out[g, b, a] = total
        for k in (1, 2, 3):
            first_copy(g, k).start()

    def go_on(g):
        for k in (1, 2, 3):
            first_copy(g, k).wait_recv()
        here = z if Z_FIRST[g] else chip
        second_out[g] = (
            first_out[g, here].astype(F32)
            + first_in[g, 0].astype(F32)
            + first_in[g, 1].astype(F32)
            + first_in[g, 2].astype(F32)
        ).astype(BF16)
        for k in (1, 2, 3):
            second_copy(g, k).start()

    def finish(g):
        for k in (1, 2, 3):
            second_copy(g, k).wait_recv()
        here = chip if Z_FIRST[g] else z
        projs_ref[core, chip, g] = (
            second_out[g, here].astype(F32)
            + second_in[g, 0].astype(F32)
            + second_in[g, 1].astype(F32)
            + second_in[g, 2].astype(F32)
        ).astype(BF16)

    @pl.when(step == 0)
    def _():
        for load in loads:
            load.start()
        meet(
            [place.pair()]
            + [place.plane(k) for k in (1, 2, 3)]
            + [place.depth(d) for d in (1, 2, 3)]
        )
        pair_copy(3).start()
        small_pair(0).start()
        for d in (1, 2, 3):
            z_copy(d).start()
        for k in (1, 2, 3):
            token_copy(0, k).start()
        own_tokens(0).start()
        gh_ref[...] = jnp.zeros_like(gh_ref)

    @pl.when(step >= 1)
    def _():
        for which in (0, 1):
            kv_copy(which, step - 1).start()

    @pl.when(step == 3)
    def _():
        pair_copy(0).start()

    @pl.when(step == 5)
    def _():
        pair_copy(1).start()

    @pl.when(step < 6)
    def _():
        keys = jnp.concatenate([k0_ref[...], k1_ref[...]], axis=0)
        values = jnp.concatenate([v0_ref[...], v1_ref[...]], axis=0)
        scaled = gm_ref[...].astype(F32) * rl_ref[...]
        products = scaled * mix_ref[...].astype(F32)
        scaled = scaled.astype(BF16)
        q_t = q_ref[...].T
        scaled_t = scaled.T
        dqs, dks, dvs = [], [], []
        for h in range(2):
            mine = (lane >= 64) if h else (lane < 64)
            inner = jnp.sum(jnp.where(mine, products, 0.0), axis=1, keepdims=True)
            grad_probs = mm_nt(jnp.where(mine, scaled, jnp.zeros_like(scaled)), values)
            grown = e_ref[h]
            grad_scores = (grown.astype(F32) * (grad_probs - inner) * scale).astype(BF16)
            dqs.append(mm(grad_scores, keys))
            dks.append(mm(q_t[64 * h : 64 * h + 64], grad_scores))
            dvs.append(mm(scaled_t[64 * h : 64 * h + 64], grown))
        dq_s[step] = jnp.where(lane < 64, dqs[0], dqs[1]).astype(BF16)
        dk = jnp.concatenate(dks, axis=0).T.astype(BF16)
        dv = jnp.concatenate(dvs, axis=0).T.astype(BF16)
        dk0_s[step] = dk[:rows]
        dk1_s[step] = dk[rows:]
        dv0_s[step] = dv[:rows]
        dv1_s[step] = dv[rows:]

    @pl.when(step == 0)
    def _():
        loads[0].wait()
        hidt_ref[...] = hid_ref[...].T

    @pl.when(step == 1)
    def _():
        loads[1].wait()
        loads[2].wait()
        start_group(3)
        small_begin(0)

    for i in range(3):

        @pl.when(step == 3 + i)
        def _(i=i):
            small_next(0, i)

    @pl.when(step == 3)
    def _():
        start_group(0)

    @pl.when(step == 5)
    def _():
        start_group(1)
        go_on(3)

    @pl.when(step == 6)
    def _():
        for d in (1, 2, 3):
            z_copy(d).wait_recv()
        for i in range(3):
            feeds_ref[core, chip, i] = (
                totals_ref[z, i].astype(F32)
                + z_in[0, i].astype(F32)
                + z_in[1, i].astype(F32)
                + z_in[2, i].astype(F32)
            ).astype(BF16)

    @pl.when((step >= 2) & (lax.rem(step, 2) == 0))
    def _():
        g = (step - 2) // 2
        slot = lax.rem(g, 2)
        cosine, sine = cos_ref[...], -sin_ref[...]
        for i in range(2):
            for which in (0, 1):
                kv_copy(which, 2 * g + i).wait_recv()

        def both(ref):
            return jnp.concatenate([ref[2 * g], ref[2 * g + 1]], axis=1).astype(F32)

        lows = []
        for part in range(3):
            span = pl.ds(pl.multiple_of(part * width + g * 256, 256), 256)
            if part == 2:
                grad = both(dv0_s) + both(dv_in)
            else:
                grad = both(dq_s) if part == 0 else both(dk0_s) + both(dk_in)
                gain = (qgain_ref, kgain_ref)[part][:, :256].astype(F32)
                raw = raw_ref[:, span].astype(F32)
                factor = lax.rsqrt(head_sum(raw * raw, head) * (1.0 / head) + NORM_EPSILON)
                normed = raw * factor
                turned = turn(grad, cosine, sine, head)
                late_ref[1, part : part + 1, pl.ds(pl.multiple_of(g * 256, 256), 256)] = col_sum(
                    turned * normed
                )
                turned = turned * gain
                mean = head_sum(turned * normed, head) * (1.0 / head)
                grad = factor * (turned - normed * mean)
            low = grad.astype(BF16)
            lows.append(low)
            total = col_sum(low.astype(F32))
            where = pl.ds(pl.multiple_of(g * 256, 256), 256)
            if part < 2:
                late_ref[0, 2 + part : 3 + part, where] = total
            else:
                late_ref[1, 2:3, where] = total
            gh_ref[...] += mm_nt(low, weight_ref[:, span])
        grads = jnp.concatenate(
            [low[:, 128 * c : 128 * c + 128] for c in range(2) for low in lows], axis=1
        )

        @pl.when(step == 6)
        def _():
            pair_copy(0).wait_send()

        half = width // 2
        made[slot, 0] = mm(hidt_ref[...], grads[:, :half]).astype(BF16)
        made[slot, 1] = mm(hidt_ref[...], grads[:, half:]).astype(BF16)

    @pl.when(step == 6)
    def _():
        pair_copy(2).start()
        grad_hidden = gh_ref[...]
        loads[3].wait()
        loads[4].wait()
        x = x_ref[...].astype(F32)
        factor = lax.rsqrt(jnp.mean(x * x, axis=-1, keepdims=True) + NORM_EPSILON)
        normed = x * factor
        late_ref[0, 0:1, :] = col_sum(grad_hidden)
        late_ref[0, 1:2, :] = col_sum(grad_hidden * normed)
        late_ref[1, 3:4, :] = jnp.zeros((1, width), F32)
        small_pair(1).start()
        go_on(0)
        go_on(1)
        small_begin(1)
        start_group(2)
        grad_normed = grad_hidden * (1.0 + mod_ref[:, width : 2 * width])
        back = factor * (
            grad_normed - normed * jnp.mean(grad_normed * normed, axis=-1, keepdims=True)
        )
        gx_ref[...] = (gmid_ref[...] + back).astype(BF16)
        for k in (1, 2, 3):
            token_copy(1, k).start()
        own_tokens(1).start()
        for k in (1, 2, 3):
            feed_copy(k).start()
        small_next(1, 0)
        finish(3)
        finish(0)
        small_next(1, 1)
        finish(1)
        small_next(1, 2)
        go_on(2)
        finish(2)
        for k in (1, 2, 3):
            proj_copy(k).start()
        for k in (1, 2, 3):
            feed_copy(k).wait_recv()
        for k in (1, 2, 3):
            feed_copy(k).wait_send()
        feed_pair().start()
        for k in (1, 2, 3):
            proj_copy(k).wait()
        proj_pair().start()
        for which in (0, 1):
            own_tokens(which).wait()
            for k in (1, 2, 3):
                token_copy(which, k).wait()
            small_pair(which).wait_send()
            for k in (1, 2, 3):
                small_plane(which, k).wait_send()
            for d in (1, 2):
                small_depth(which, d).wait_send()
            small_last(which).wait()
            stores[which].start()
            for p in range(6):
                kv_copy(which, p).wait_send()
        for k in (1, 2, 3):
            z_copy(k).wait_send()
            for g in range(4):
                first_copy(g, k).wait_send()
                second_copy(g, k).wait_send()
        for g in (1, 2, 3):
            pair_copy(g).wait_send()
        feed_pair().wait()
        stores[2].start()
        proj_pair().wait()
        stores[3].start()
        for store in stores:
            store.wait()


def back_call(
    q, k0, k1, v0, v1, grad_mixed, mixed, inverse, grown, mod, small_vectors, cosine, sine, d_out,
    totals, early, raw, hidden, x, grad_middle, weight, output_rows, head,
):
    rows, width = q.shape
    half, part = width // 2, width // 16
    low = lambda *shape: jax.ShapeDtypeStruct(shape, BF16)
    pair = pl.BlockSpec((rows, 128), lambda s: (0, jnp.minimum(s, 5)))
    anywhere = pl.BlockSpec(memory_space=pl.ANY)
    small = [mod, small_vectors, small_vectors, cosine, sine, d_out, totals, early]
    gain = lambda at: pl.BlockSpec((1, width), lambda s: (0, at), pipeline_mode=pl.Buffered(1))
    out_shape = [
        low(4, rows // 4, width), low(4, rows // 4, width),
        low(2, 4, 3, width // 4, 256), low(2, 4, GROUPS, part, half),
        jax.ShapeDtypeStruct((2, 16, 8, width), F32), jax.ShapeDtypeStruct((2, 16, 4, width), F32),
    ]
    vmem = lambda *shape: pltpu.VMEM(shape, BF16)
    sems = lambda *shape: pltpu.SemaphoreType.DMA(shape)
    return pl.pallas_call(
        functools.partial(back_kernel, head),
        grid=(7,),
        in_specs=[pair] * 8
        + [pl.BlockSpec((2, rows, 2 * rows), lambda s: (jnp.minimum(s, 5), 0, 0))]
        + [once(mod.shape), gain(Q_GAIN), gain(K_GAIN)]
        + [once(each.shape) for each in small[3:]]
        + [anywhere] * 6,
        out_specs=[anywhere] * 6,
        out_shape=out_shape,
        scratch_shapes=[pltpu.VMEM(shape.shape, shape.dtype) for shape in out_shape[2:]]
        + [
            vmem(rows, 2 * width), vmem(rows, width), vmem(rows, width),
            pltpu.VMEM((rows, width), F32), vmem(width, 3 * width), vmem(width, rows),
            pltpu.VMEM((rows, width), F32), vmem(rows, width), pltpu.VMEM((2, 4, width), F32),
        ]
        + [vmem(6, rows, 128)] * 7
        + [
            vmem(2, 2, width, half), vmem(GROUPS, width, half),
            vmem(GROUPS, 4, 4, part, half), vmem(GROUPS, 3, 4, part, half),
            vmem(GROUPS, 4, part, half), vmem(GROUPS, 3, part, half),
            vmem(3, 3, width // 4, 256),
            pltpu.VMEM((8, width), F32), pltpu.VMEM((4, width), F32),
            sems(9), sems(2), sems(2, 6), sems(2, 6), sems(GROUPS), sems(GROUPS),
            sems(GROUPS, 3), sems(GROUPS, 3), sems(GROUPS, 3), sems(GROUPS, 3),
            sems(3), sems(3), sems(2, 3), sems(2, 3), sems(4), sems(4), sems(4), sems(4),
            sems(2, 7), sems(2, 7),
        ],
        compiler_params=pltpu.CompilerParams(
            vmem_limit_bytes=VMEM_LIMIT, collective_id=2, has_side_effects=True
        ),
        name="back",
    )(
        q, k0, k1, v0, v1, grad_mixed, mixed, inverse, grown, *small, raw, hidden, x, grad_middle,
        weight, output_rows,
    )


def finish_kernel(
    head, feeds_ref, projs_ref, early_ref, late_ref, modw_hbm,
    cond_ref, table_hbm, gmodw_hbm, gmodb_ref, ginw_hbm, ginb_ref, gqg_ref, gkg_ref, goutw_hbm,
    goutb_ref, gguw_hbm, ggub_ref, gdownw_hbm, gdownb_ref,
    modw_ref, table_ref, gmodw_ref, ginw_ref, goutw_ref, gguw_ref, gdownw_ref, acts_ref, load_sem,
    store_sem,
):
    place = Place()
    width = early_ref.shape[3]
    part = projs_ref.shape[3]
    load = pltpu.make_async_copy(modw_hbm, modw_ref, load_sem)
    load.start()
    stores = [
        pltpu.make_async_copy(source, target, store_sem.at[i])
        for i, (source, target) in enumerate(
            (
                (gguw_ref, gguw_hbm), (gdownw_ref, gdownw_hbm), (ginw_ref, ginw_hbm),
                (goutw_ref, goutw_hbm), (gmodw_ref, gmodw_hbm), (table_ref, table_hbm),
            )
        )
    ]
    for c in range(2):
        for chip in range(4):
            for f in range(2):
                for i in range(2):
                    col = (((c * 2 + f) * 2 + i) * 4 + chip) * 128
                    gguw_ref[:, col : col + 128] = feeds_ref[
                        c, chip, f, :, i * 128 : (i + 1) * 128
                    ].astype(F32)
    stores[0].start()
    for c in range(2):
        for chip in range(4):
            row = chip * 128 + c * 64
            for b in range(3):
                gdownw_ref[row : row + 64, b * 256 : (b + 1) * 256] = feeds_ref[
                    c, chip, 2, b * 64 : (b + 1) * 64, :
                ].astype(F32)
    stores[1].start()
    for c in range(2):
        for chip in range(4):
            row = chip * part
            for g in range(3):
                for q in range(3):
                    col = q * width + g * 256 + c * 128
                    ginw_ref[row : row + part, col : col + 128] = projs_ref[
                        c, chip, g, :, q * 128 : (q + 1) * 128
                    ].astype(F32)
            half = width // 2
            goutw_ref[row : row + part, c * half : (c + 1) * half] = projs_ref[c, chip, 3].astype(F32)
    stores[2].start()
    stores[3].start()

    vectors = [late_ref[0, :, 0, :], late_ref[0, :, 1, :]]
    vectors += [early_ref[0, :, j, :] for j in range(4)]
    lows = [vector.astype(BF16) for vector in vectors]
    conditions = early_ref[0, :, 6, :]
    labels = early_ref[0, :, 7, :]
    sig = 1.0 / (1.0 + jnp.exp(-conditions))
    acts = (conditions * sig).astype(BF16)
    size = acts_ref.shape[1]
    for z in range(4):

        @pl.when(place.z == z)
        def _(z=z):
            acts_ref[...] = acts[:, z * size : (z + 1) * size]

    mine = acts_ref[...]
    for j, low in enumerate(lows):
        gmodw_ref[:, j * width : (j + 1) * width] = mm_tn(mine, low)
    stores[4].start()
    early_sum = jnp.sum(early_ref[0], axis=0)
    gate_sum = jnp.sum(early_ref[1], axis=0)
    late_sum = jnp.sum(late_ref[0], axis=0)
    gain_sum = jnp.sum(late_ref[1], axis=0)
    mod_b = jnp.concatenate(
        [late_sum[0:1], late_sum[1:2]] + [early_sum[j : j + 1] for j in range(4)], axis=1
    )
    in_b = jnp.concatenate([late_sum[2:3], late_sum[3:4], gain_sum[2:3]], axis=1)
    gate_b = jnp.concatenate(
        [gate_sum[n // 6 : n // 6 + 1, (n % 6) * 128 : (n % 6) * 128 + 128] for n in range(32)],
        axis=1,
    )
    gains = sum(gain_sum[0:2, i : i + 128] for i in range(0, width, 128))
    gains = gains[:, :head] + gains[:, head:]
    pieces = (
        (gmodb_ref, mod_b), (ginb_ref, in_b), (gqg_ref, gains[0:1]), (gkg_ref, gains[1:2]),
        (goutb_ref, early_sum[4:5]), (ggub_ref, gate_b), (gdownb_ref, early_sum[5:6]),
    )
    for z in range(4):

        @pl.when(place.z == z)
        def _(z=z):
            for ref, row in pieces:
                size = row.shape[1] // 4
                ref[...] = row[:, z * size : (z + 1) * size]

    load.wait()
    grad = sum(mm_nt(low, modw_ref[:, j * width : (j + 1) * width]) for j, low in enumerate(lows))
    grad = grad * sig * (1.0 + conditions * (1.0 - sig))
    for k in range(4):
        cond_ref[pl.ds(place.flipped(k), 1), :] = grad[k : k + 1]
    classes = table_ref.shape[0]
    wide = -(-classes // 128) * 128
    column = lax.broadcasted_iota(jnp.int32, (1, wide), 1).astype(F32)
    onehot = jnp.where(labels[:, 0:1] == column, 1.0, 0.0).astype(BF16)
    high = grad.astype(BF16)
    rest = grad - high.astype(F32)
    middle = rest.astype(BF16)
    last = (rest - middle.astype(F32)).astype(BF16)
    table = mm_tn(
        jnp.concatenate([onehot] * 3, axis=0), jnp.concatenate([high, middle, last], axis=0)
    )
    table_ref[...] = table[:classes]
    stores[5].start()
    for store in stores:
        store.wait()


def finish_call(feeds, projs, early, late, weight, head, classes, hidden_width):
    width = weight.shape[0]
    rows = width // 4
    whole = lambda *shape: jax.ShapeDtypeStruct(shape, F32)
    anywhere = pl.BlockSpec(memory_space=pl.ANY)
    out_shape = [
        whole(4, width), whole(classes, width), whole(rows, 6 * width), whole(1, 6 * width // 4),
        whole(rows, 3 * width), whole(1, 3 * width // 4), whole(1, head // 4), whole(1, head // 4),
        whole(rows, width), whole(1, rows), whole(rows, 2 * hidden_width),
        whole(1, 2 * hidden_width // 4), whole(hidden_width // 4, width), whole(1, rows),
    ]
    big = (1, 2, 4, 8, 10, 12)
    return pl.pallas_call(
        functools.partial(finish_kernel, head),
        in_specs=[pl.BlockSpec(memory_space=pltpu.VMEM)] * 4 + [anywhere],
        out_specs=[
            anywhere if i in big else pl.BlockSpec(memory_space=pltpu.VMEM)
            for i in range(len(out_shape))
        ],
        out_shape=out_shape,
        scratch_shapes=[pltpu.VMEM(weight.shape, BF16)]
        + [pltpu.VMEM(out_shape[i].shape, F32) for i in big]
        + [pltpu.VMEM((16, rows), BF16), pltpu.SemaphoreType.DMA, pltpu.SemaphoreType.DMA((6,))],
        compiler_params=params(),
        name="finish",
    )(feeds, projs, early, late, weight)


def take(array_in, index, axis=0):
    return lax.dynamic_index_in_dim(array_in, index, axis, keepdims=False)


def add(*terms):
    return sum(term.astype(F32) for term in terms)


class Moves:
    def __init__(self, mesh):
        self.sizes = tuple(mesh.shape[name] for name in AXES)

    def flip(self, value, batch=0, gy=0, gx=0):
        nb, ny, nx = self.sizes
        pairs = []
        for b in range(nb):
            for y in range(ny):
                for x in range(nx):
                    here = (b * ny + y) * nx + x
                    there = ((b ^ batch) * ny + (y ^ gy)) * nx + (x ^ gx)
                    pairs.append((here, there))
        return lax.ppermute(value, AXES, pairs)

    def plane(self, value, k):
        return self.flip(value, gy=k >> 1, gx=2 * (k & 1))

    def pair(self, value):
        return self.flip(value, gx=1)

    def gather(self, value):
        value = value[None]
        value = jnp.concatenate([value, self.plane(value, 1)], axis=0)
        value = jnp.concatenate([value, self.plane(value, 2)], axis=0)
        bit = 1
        while bit < self.sizes[0]:
            value = jnp.concatenate([value, self.flip(value, batch=bit)], axis=0)
            bit *= 2
        return value


def regroup(parts, place):
    stacked = jnp.stack(parts)
    return jnp.stack([take(stacked, place ^ k) for k in range(len(parts))])


def body(mesh, *operands):
    (
        tokens, timesteps, labels, class_table, modulate_weight, modulate_bias, inproj_weight,
        inproj_bias, query_gain, key_gain, outproj_weight, outproj_bias, gate_up_weight,
        gate_up_bias, down_weight, down_bias, cotangent,
    ) = operands
    image_count, tile_rows, tile_cols, width = tokens.shape
    cells = tile_rows * tile_cols
    rows = image_count * cells
    head = query_gain.shape[0]
    heads = width // head
    hidden_width = down_weight.shape[0]
    class_count = class_table.shape[0]
    highest = lax.Precision.HIGHEST
    moves = Moves(mesh)
    nb, ny, nx = moves.sizes
    assert ny == 2 and nx == 4 and image_count == 4
    z, gy, gx = (lax.axis_index(name) for name in AXES)
    side, core = gx // 2, gx % 2
    place = 2 * gy + side

    tiles = tokens.reshape(image_count, cells, width)
    grads = cotangent.reshape(image_count, cells, width)

    half_width = width // 2
    step = take(timesteps, place).astype(F32)
    label = take(labels, place)
    rates = jnp.exp(-math.log(10000.0) * jnp.arange(half_width, dtype=F32) / half_width)
    features = jnp.concatenate([jnp.cos(step * rates), jnp.sin(step * rates)])
    condition = features + take(class_table, label).astype(F32)
    cond_act = jax.nn.silu(condition).astype(BF16)
    if nb == 4 and hidden_width == 16 * 128:
        act = jnp.broadcast_to(cond_act[None], (16, width))
        small = small_row(
            width, head, modulate_bias, inproj_bias, query_gain, key_gain, outproj_bias, down_bias,
            gate_up_bias,
        )
        known = jnp.stack([condition, jnp.broadcast_to(label.astype(F32), (width,))])
        known = jnp.where(core == 0, known, 0.0)
        x, dy, hidden_one, q, k0, v0, k1, v1, raw, mod, cosine, sine = front_call(
            tiles, grads, act, small, modulate_weight, inproj_weight, head, tile_cols
        )
        mixed, grown, inverse = attend_call(q, k0, k1, v0, v1, head)
        attended, middle, hidden_two, hidden_two_t, grad_feed = middle_call(
            mixed, x, dy, mod, outproj_weight, small, OUT_BIAS
        )
        output_rows, grad_middle, grad_mixed, d_out, sums_two, totals = feed_turn_call(
            hidden_two, hidden_two_t, grad_feed, gate_up_weight, down_weight, middle, attended, dy,
            mixed, mod, outproj_weight, small, known,
        )
        output, grad_tokens, feeds, projs, early, late = back_call(
            q, k0, k1, v0, v1, grad_mixed, mixed, inverse, grown, mod, small, cosine, sine, d_out,
            totals, sums_two, raw, hidden_one, x, grad_middle, inproj_weight, output_rows, head,
        )
        (
            grad_condition, grad_table, grad_mod_w, grad_mod_b, grad_in_w, grad_in_b, grad_q_gain,
            grad_k_gain, grad_out_w, grad_out_b, grad_gu_w, grad_gu_b, grad_down_w, grad_down_b,
        ) = finish_call(
            feeds, projs, early, late, modulate_weight, head, class_count, hidden_width
        )
        return (
            output.reshape(tokens.shape), grad_tokens.reshape(tokens.shape), grad_condition,
            grad_table, grad_mod_w, grad_mod_b[0], grad_in_w, grad_in_b[0], grad_q_gain[0],
            grad_k_gain[0], grad_out_w, grad_out_b[0], grad_gu_w, grad_gu_b[0], grad_down_w,
            grad_down_b[0],
        )

    def exchange(blocks):
        return [take(blocks, place)] + [
            moves.plane(take(blocks, place ^ k), k) for k in range(1, 4)
        ]

    x = jnp.concatenate(exchange(tiles), axis=0)

    mod = modulation_call(
        jnp.broadcast_to(cond_act[None], (16, width)), modulate_weight, modulate_bias[None]
    )[:1]

    quarter = head // 4
    cell = jnp.arange(cells, dtype=jnp.int32)
    row_places, col_places = [], []
    for k in range(4):
        there = place ^ k
        row_places.append((there // 2) * tile_rows + cell // tile_cols)
        col_places.append((2 * (there % 2) + core) * tile_cols + cell % tile_cols)
    row_places = jnp.concatenate(row_places).astype(F32)[:, None]
    col_places = jnp.concatenate(col_places).astype(F32)[:, None]
    lane = jnp.arange(128, dtype=jnp.int32)
    turn_rate = jnp.exp(-math.log(10000.0) * (lane % quarter).astype(F32) / quarter)[None]
    angles = jnp.where((lane % head)[None] < head // 2, row_places, col_places) * turn_rate
    cosine = jnp.cos(angles)
    sine = jnp.where((lane % (2 * quarter))[None] < quarter, -1.0, 1.0) * jnp.sin(angles)
    qgain = jnp.tile(query_gain.astype(F32), heads)[None]
    kgain = jnp.tile(key_gain.astype(F32), heads)[None]

    hidden_one, q, k0, v0, raw = project_call(
        x, mod, inproj_weight, inproj_bias[None], qgain, kgain, cosine, sine, head
    )
    k1, v1 = moves.pair(k0), moves.pair(v0)
    dy = jnp.concatenate(exchange(grads), axis=0)
    mixed, grown, inverse = attend_call(q, k0, k1, v0, v1, head)
    attended, middle, hidden_two, hidden_two_t, grad_feed = middle_call(
        mixed, x, dy, mod, outproj_weight, outproj_bias[None]
    )

    unit = 256
    blocks = hidden_width // unit
    feed, grad_hidden, d_down, d_gate, d_bias = feed_call(
        hidden_two, hidden_two_t, grad_feed, gate_up_weight, gate_up_bias[None], down_weight,
        jnp.zeros((rows, width), F32), jnp.zeros((rows, width), F32), 0, 1, unit,
    )
    output_rows, grad_middle, grad_mixed, d_out, sums_two = turn_call(
        feed, grad_hidden, middle, attended, dy, grad_feed, mixed, mod, outproj_weight,
        down_bias[None],
    )
    gate_bias = d_bias.reshape(blocks, 2, unit).transpose(1, 0, 2)
    dq, dk0, dk1, dv0, dv1 = attend_back_call(
        q, k0, k1, v0, v1, grown, grad_mixed, mixed, inverse, head
    )
    dk1, dv1 = moves.pair(dk1), moves.pair(dv1)
    grad_x, d_in, sums_one, in_bias = project_back_call(
        dq, dk0, dk1, dv0, dv1, raw, hidden_one, x, grad_middle, mod, inproj_weight, qgain,
        kgain, cosine, sine, head,
    )

    def give_back(rows_out):
        parts = rows_out.reshape(4, cells, width)
        got = [parts[0]] + [moves.plane(parts[k], k) for k in range(1, 4)]
        return regroup(got, place).reshape(tokens.shape)

    output = give_back(output_rows)
    grad_tokens = give_back(grad_x)
    slice_rows = width // nb

    def scatter(d):
        d = lax.psum_scatter(d.astype(BF16), "batch", scatter_dimension=0, tiled=True)
        return lax.psum(d, ("gy", "gx")).astype(F32)

    def joined(d):
        return jnp.concatenate([d[0], d[1]], axis=1)

    grad_down_w = scatter(d_down.reshape(hidden_width, width))
    grad_gu_w = scatter(
        d_gate.transpose(2, 1, 0, 3).reshape(width, 2 * hidden_width)
    )
    grad_out_w = scatter(joined(d_out))
    grad_in_w = scatter(joined(d_in))
    gain_sums = sums_one[2:4].reshape(2, heads, head).sum(axis=1)
    early = jnp.concatenate([sums_two[:6].reshape(-1), gate_bias.reshape(-1)])
    late = jnp.concatenate(
        [sums_one[:2].reshape(-1), in_bias.reshape(-1), gain_sums.reshape(-1)]
    )

    def everywhere(vector):
        halves = vector.reshape(2, -1)
        half = add(take(halves, core), moves.pair(take(halves, 1 - core)))
        half = moves.gather(half)
        both = regroup([half, moves.pair(half)], core)
        return both.transpose(1, 0, 2).reshape(half.shape[0], -1)

    known = jnp.concatenate([condition, jnp.broadcast_to(label.astype(F32), (128,))])
    known = moves.gather(known)
    early, late = everywhere(early), everywhere(late)
    grad_modulation = jnp.concatenate([late[:, : 2 * width], early[:, : 4 * width]], axis=1)
    conditions = known[:, :width]
    all_labels = known[:, width].astype(jnp.int32)
    cond_acts = jax.nn.silu(conditions).astype(BF16)
    my_acts = lax.dynamic_slice_in_dim(cond_acts, z * slice_rows, slice_rows, axis=1)
    low_mod = grad_modulation.astype(BF16)
    grad_mod_w = mm_tn(my_acts, low_mod)
    wide = 6 * width
    grad_mod_b = lax.dynamic_slice_in_dim(
        jnp.sum(grad_modulation, axis=0), z * (wide // nb), wide // nb, axis=0
    )
    grad_cond_act = mm_nt(low_mod, modulate_weight)
    sig = jax.nn.sigmoid(conditions)
    grad_conditions = grad_cond_act * sig * (1.0 + conditions * (1.0 - sig))
    grad_condition = regroup([grad_conditions[k] for k in range(4)], place)
    onehot = (all_labels[:, None] == jnp.arange(class_count, dtype=jnp.int32)[None, :]).astype(F32)
    grad_table = lax.dot_general(
        onehot, grad_conditions, (((0,), (0,)), ((), ())), precision=highest,
        preferred_element_type=F32,
    )

    early_sum = jnp.sum(early, axis=0)
    late_sum = jnp.sum(late, axis=0)

    def part(vector, start, size):
        return lax.dynamic_slice_in_dim(vector, start + z * (size // nb), size // nb, axis=0)

    grad_out_b = part(early_sum, 4 * width, width)
    grad_down_b = part(early_sum, 5 * width, width)
    grad_gu_b = part(early_sum, 6 * width, 2 * hidden_width)
    grad_in_b = part(late_sum, 2 * width, 3 * width)
    grad_q_gain = part(late_sum, 5 * width, head)
    grad_k_gain = part(late_sum, 5 * width + head, head)
    return (
        output, grad_tokens, grad_condition, grad_table, grad_mod_w, grad_mod_b, grad_in_w,
        grad_in_b, grad_q_gain, grad_k_gain, grad_out_w, grad_out_b, grad_gu_w, grad_gu_b,
        grad_down_w, grad_down_b,
    )


def solution(mesh):
    grid = P("batch", "gy", "gx", None)
    by_batch = P("batch")
    rows = P("batch", None)
    placed = (grid, by_batch, by_batch) + (P(),) * 13 + (grid,)
    return jax.shard_map(
        functools.partial(body, mesh),
        mesh=mesh,
        in_specs=placed,
        out_specs=(
            grid, grid, rows, P(), rows, by_batch, rows, by_batch, by_batch, by_batch, rows,
            by_batch, rows, by_batch, rows, by_batch,
        ),
        check_vma=False,
    )
```

```python
import functools
import math

import jax
import jax.numpy as jnp
from jax import lax
from jax.experimental import pallas as pl
from jax.experimental.pallas import tpu as pltpu
from jax.sharding import PartitionSpec as P

NORM_EPSILON = 1e-06
AXES = ("batch", "gy", "gx")
BF16 = jnp.bfloat16
F32 = jnp.float32
VMEM_LIMIT = 60 * 1024 * 1024


def mm(left, right):
    return lax.dot_general(left, right, (((1,), (0,)), ((), ())), preferred_element_type=F32)


def mm_nt(left, right):
    return lax.dot_general(left, right, (((1,), (1,)), ((), ())), preferred_element_type=F32)


def mm_tn(left, right):
    return lax.dot_general(left, right, (((0,), (0,)), ((), ())), preferred_element_type=F32)


def params():
    return pltpu.CompilerParams(vmem_limit_bytes=VMEM_LIMIT)


def full(shape):
    return pl.BlockSpec(shape, lambda *_: (0,) * len(shape))


def col_sum(values):
    return jnp.sum(values, axis=0, keepdims=True)


def modulation_kernel(act_ref, weight_ref, bias_ref, out_ref):
    out_ref[...] = mm(act_ref[...], weight_ref[...]) + bias_ref[...].astype(F32)


def modulation_call(act, weight, bias):
    rows, width = act.shape
    wide = weight.shape[1]
    return pl.pallas_call(
        modulation_kernel,
        grid=(wide // width,),
        in_specs=[
            full((rows, width)),
            pl.BlockSpec((width, width), lambda j: (0, j)),
            pl.BlockSpec((1, width), lambda j: (0, j)),
        ],
        out_specs=pl.BlockSpec((rows, width), lambda j: (0, j)),
        out_shape=jax.ShapeDtypeStruct((rows, wide), F32),
        compiler_params=params(),
        name="modulation",
    )(act, weight, bias)


def head_sum(values, head):
    width = 256
    row = lax.broadcasted_iota(jnp.int32, (width, width), 0) // head
    col = lax.broadcasted_iota(jnp.int32, (width, width), 1) // head
    ones = jnp.where(row == col, 1.0, 0.0).astype(BF16)
    parts = [
        mm(values[:, i : i + width].astype(BF16), ones) for i in range(0, values.shape[1], width)
    ]
    return jnp.concatenate(parts, axis=1)


def turn(values, cosine, sine, head):
    quarter = head // 4
    lane = lax.broadcasted_iota(jnp.int32, (1, 128), 1)
    first = (lane % (2 * quarter)) < quarter
    parts = []
    for i in range(0, values.shape[1], 128):
        part = values[:, i : i + 128]
        partner = jnp.where(
            first, pltpu.roll(part, 128 - quarter, 1), pltpu.roll(part, quarter, 1)
        )
        parts.append(part * cosine + partner * sine)
    return jnp.concatenate(parts, axis=1)


def project_kernel(
    head, x_ref, mod_ref, weight_ref, bias_ref, qgain_ref, kgain_ref, cos_ref, sin_ref,
    hid_ref, q_ref, k_ref, v_ref, raw_ref,
):
    width = x_ref.shape[1]
    x = x_ref[...].astype(F32)
    normed = x * lax.rsqrt(jnp.mean(x * x, axis=-1, keepdims=True) + NORM_EPSILON)
    hidden = (normed * (1.0 + mod_ref[:, width : 2 * width]) + mod_ref[:, :width]).astype(BF16)
    hid_ref[...] = hidden
    for part, (out_ref, gain_ref) in enumerate(((q_ref, qgain_ref), (k_ref, kgain_ref))):
        raw = mm(hidden, weight_ref[:, part * width : (part + 1) * width])
        raw = raw + bias_ref[:, part * width : (part + 1) * width].astype(F32)
        raw_ref[:, part * width : (part + 1) * width] = raw.astype(BF16)
        factor = lax.rsqrt(head_sum(raw * raw, head) * (1.0 / head) + NORM_EPSILON)
        scaled = raw * factor * gain_ref[...]
        out_ref[...] = turn(scaled, cos_ref[...], sin_ref[...], head).astype(BF16)
    value = mm(hidden, weight_ref[:, 2 * width :]) + bias_ref[:, 2 * width :].astype(F32)
    v_ref[...] = value.astype(BF16)


def project_call(x, mod, weight, bias, qgain, kgain, cosine, sine, head):
    rows, width = x.shape
    block = rows // 2
    by_row = lambda wide: pl.BlockSpec((block, wide), lambda i: (i, 0))
    shape = jax.ShapeDtypeStruct((rows, width), BF16)
    return pl.pallas_call(
        functools.partial(project_kernel, head),
        grid=(2,),
        in_specs=[
            by_row(width),
            full(mod.shape),
            full(weight.shape),
            full(bias.shape),
            full(qgain.shape),
            full(kgain.shape),
            by_row(128),
            by_row(128),
        ],
        out_specs=[by_row(width)] * 4 + [by_row(2 * width)],
        out_shape=[shape] * 4 + [jax.ShapeDtypeStruct((rows, 2 * width), BF16)],
        compiler_params=params(),
        name="project",
    )(x, mod, weight, bias, qgain, kgain, cosine, sine)


def attend_kernel(scale, q_ref, k0_ref, k1_ref, v0_ref, v1_ref, mix_ref, e_ref, rl_ref):
    lane = lax.broadcasted_iota(jnp.int32, (1, 128), 1)
    q = q_ref[...]
    keys = jnp.concatenate([k0_ref[...], k1_ref[...]], axis=0)
    values = jnp.concatenate([v0_ref[...], v1_ref[...]], axis=0)
    values = jnp.concatenate([values, jnp.ones_like(values)], axis=1)
    outs = []
    for h in range(2):
        mine = (lane >= 64) if h else (lane < 64)
        scores = mm_nt(jnp.where(mine, q, jnp.zeros_like(q)), keys)
        grown = jnp.exp(scores * scale).astype(BF16)
        e_ref[h] = grown
        outs.append(mm(grown, values))
    inverse = 1.0 / jnp.where(lane < 64, outs[0][:, 128:], outs[1][:, 128:])
    mix_ref[...] = (jnp.where(lane < 64, outs[0][:, :128], outs[1][:, :128]) * inverse).astype(BF16)
    rl_ref[...] = inverse


def attend_call(q, k0, k1, v0, v1, head):
    rows, width = q.shape
    pair = pl.BlockSpec((rows, 128), lambda p: (0, p))
    return pl.pallas_call(
        functools.partial(attend_kernel, head**-0.5),
        grid=(width // 128,),
        in_specs=[pair] * 5,
        out_specs=[pair, pl.BlockSpec((2, rows, 2 * rows), lambda p: (p, 0, 0)), pair],
        out_shape=[
            jax.ShapeDtypeStruct((rows, width), BF16),
            jax.ShapeDtypeStruct((width // head, rows, 2 * rows), BF16),
            jax.ShapeDtypeStruct((rows, width), F32),
        ],
        compiler_params=params(),
        name="attend",
    )(q, k0, k1, v0, v1)


def attend_back_kernel(
    scale, q_ref, k0_ref, k1_ref, v0_ref, v1_ref, e_ref, gm_ref, mix_ref, rl_ref,
    dq_ref, dk0_ref, dk1_ref, dv0_ref, dv1_ref,
):
    rows = q_ref.shape[0]
    lane = lax.broadcasted_iota(jnp.int32, (1, 128), 1)
    keys = jnp.concatenate([k0_ref[...], k1_ref[...]], axis=0)
    values = jnp.concatenate([v0_ref[...], v1_ref[...]], axis=0)
    scaled = gm_ref[...].astype(F32) * rl_ref[...]
    products = scaled * mix_ref[...].astype(F32)
    scaled = scaled.astype(BF16)
    q_t = q_ref[...].T
    scaled_t = scaled.T
    dqs, dks, dvs = [], [], []
    for h in range(2):
        mine = (lane >= 64) if h else (lane < 64)
        inner = jnp.sum(jnp.where(mine, products, 0.0), axis=1, keepdims=True)
        grad_probs = mm_nt(jnp.where(mine, scaled, jnp.zeros_like(scaled)), values)
        grown = e_ref[h]
        grad_scores = (grown.astype(F32) * (grad_probs - inner) * scale).astype(BF16)
        dqs.append(mm(grad_scores, keys))
        dks.append(mm(q_t[64 * h : 64 * h + 64], grad_scores))
        dvs.append(mm(scaled_t[64 * h : 64 * h + 64], grown))
    dq_ref[...] = jnp.where(lane < 64, dqs[0], dqs[1]).astype(BF16)
    dk = jnp.concatenate(dks, axis=0).T.astype(BF16)
    dv = jnp.concatenate(dvs, axis=0).T.astype(BF16)
    dk0_ref[...] = dk[:rows]
    dk1_ref[...] = dk[rows:]
    dv0_ref[...] = dv[:rows]
    dv1_ref[...] = dv[rows:]


def attend_back_call(q, k0, k1, v0, v1, grown, grad_mixed, mixed, inverse, head):
    rows, width = q.shape
    pair = pl.BlockSpec((rows, 128), lambda p: (0, p))
    return pl.pallas_call(
        functools.partial(attend_back_kernel, head**-0.5),
        grid=(width // 128,),
        in_specs=[pair] * 5
        + [pl.BlockSpec((2, rows, 2 * rows), lambda p: (p, 0, 0))]
        + [pair] * 3,
        out_specs=[pair] * 5,
        out_shape=[jax.ShapeDtypeStruct((rows, width), BF16)] * 5,
        compiler_params=params(),
        name="attend_back",
    )(q, k0, k1, v0, v1, grown, grad_mixed, mixed, inverse)


def middle_kernel(
    mix_ref, x_ref, dy_ref, mod_ref, weight_ref, bias_ref, att_ref, mid_ref, h2_ref, h2t_ref, gf_ref
):
    width = x_ref.shape[1]
    attended = mm(mix_ref[...], weight_ref[...]) + bias_ref[...].astype(F32)
    middle = x_ref[...].astype(F32) + mod_ref[:, 2 * width : 3 * width] * attended
    normed = middle * lax.rsqrt(jnp.mean(middle * middle, axis=-1, keepdims=True) + NORM_EPSILON)
    hidden = normed * (1.0 + mod_ref[:, 4 * width : 5 * width]) + mod_ref[:, 3 * width : 4 * width]
    hidden = hidden.astype(BF16)
    att_ref[...] = attended.astype(BF16)
    mid_ref[...] = middle
    h2_ref[...] = hidden
    h2t_ref[...] = hidden.T
    gf_ref[...] = (mod_ref[:, 5 * width :] * dy_ref[...].astype(F32)).astype(BF16)


def middle_call(mixed, x, dy, mod, weight, bias, bias_at=0):
    rows, width = x.shape
    block = rows // 2
    by_row = pl.BlockSpec((block, width), lambda i: (i, 0))
    low = jax.ShapeDtypeStruct((rows, width), BF16)
    return pl.pallas_call(
        middle_kernel,
        grid=(2,),
        in_specs=[by_row] * 3
        + [full(mod.shape), full(weight.shape), pl.BlockSpec((1, width), lambda i: (0, bias_at))],
        out_specs=[by_row] * 3 + [pl.BlockSpec((width, block), lambda i: (0, i)), by_row],
        out_shape=[low, jax.ShapeDtypeStruct((rows, width), F32), low]
        + [jax.ShapeDtypeStruct((width, rows), BF16), low],
        compiler_params=params(),
        name="middle",
    )(mixed, x, dy, mod, weight, bias)


def feed_kernel(
    h2_ref, h2t_ref, gf_ref, wg_ref, wu_ref, bg_ref, bu_ref, wd_ref, feed_in_ref, gh_in_ref,
    feed_ref, gh_ref, dd_ref, dg_ref, db_ref,
):
    @pl.when(pl.program_id(0) == 0)
    def _():
        feed_ref[...] = feed_in_ref[...]
        gh_ref[...] = gh_in_ref[...]

    hidden = h2_ref[...]
    grad_feed = gf_ref[...]
    gate = mm(hidden, wg_ref[...]) + bg_ref[...].astype(F32)
    up = mm(hidden, wu_ref[...]) + bu_ref[...].astype(F32)
    grad_product = mm_nt(grad_feed, wd_ref[...])
    sig = 1.0 / (1.0 + jnp.exp(-gate))
    active = gate * sig
    product = (active * up).astype(BF16)
    grad_gate = (grad_product * up * sig * (1.0 + gate * (1.0 - sig))).astype(BF16)
    grad_up = (grad_product * active).astype(BF16)
    dd_ref[...] = mm_tn(product, grad_feed).astype(BF16)
    dg_ref[0] = mm(h2t_ref[...], grad_gate).astype(BF16)
    dg_ref[1] = mm(h2t_ref[...], grad_up).astype(BF16)
    db_ref[0] = col_sum(grad_gate.astype(F32))
    db_ref[1] = col_sum(grad_up.astype(F32))
    feed_ref[...] += mm(product, wd_ref[...])
    gh_ref[...] += mm_nt(grad_gate, wg_ref[...]) + mm_nt(grad_up, wu_ref[...])


def feed_call(hidden, hidden_t, grad_feed, weight, bias, down, feed, grad_hidden, first, step, unit):
    rows, width = hidden.shape
    blocks = down.shape[0] // unit
    steps = len(range(first, blocks, step))
    pick = lambda s: first + step * s
    acc = jax.ShapeDtypeStruct((rows, width), F32)
    return pl.pallas_call(
        feed_kernel,
        grid=(steps,),
        in_specs=[
            full((rows, width)),
            full((width, rows)),
            full((rows, width)),
            pl.BlockSpec((width, unit), lambda s: (0, pick(s))),
            pl.BlockSpec((width, unit), lambda s: (0, blocks + pick(s))),
            pl.BlockSpec((1, unit), lambda s: (0, pick(s))),
            pl.BlockSpec((1, unit), lambda s: (0, blocks + pick(s))),
            pl.BlockSpec((unit, width), lambda s: (pick(s), 0)),
            full((rows, width)),
            full((rows, width)),
        ],
        out_specs=[
            full((rows, width)),
            full((rows, width)),
            pl.BlockSpec((None, unit, width), lambda s: (s, 0, 0)),
            pl.BlockSpec((None, 2, width, unit), lambda s: (s, 0, 0, 0)),
            pl.BlockSpec((None, 2, 1, unit), lambda s: (s, 0, 0, 0)),
        ],
        out_shape=[
            acc,
            acc,
            jax.ShapeDtypeStruct((steps, unit, width), BF16),
            jax.ShapeDtypeStruct((steps, 2, width, unit), BF16),
            jax.ShapeDtypeStruct((steps, 2, 1, unit), F32),
        ],
        compiler_params=params(),
        name="feed",
    )(hidden, hidden_t, grad_feed, weight, weight, bias, bias, down, feed, grad_hidden)


def turn_kernel(
    feed_ref, gh_ref, mid_ref, att_ref, dy_ref, gf_ref, mix_ref, mod_ref, weight_ref, dbias_ref,
    out_ref, gmid_ref, gmix_ref, dw_ref, sums_ref,
):
    width = mid_ref.shape[1]
    half = width // 2
    dy = dy_ref[...].astype(F32)
    feed = feed_ref[...] + dbias_ref[...].astype(F32)
    middle = mid_ref[...]
    out_ref[...] = (middle + mod_ref[:, 5 * width :] * feed).astype(BF16)
    factor = lax.rsqrt(jnp.mean(middle * middle, axis=-1, keepdims=True) + NORM_EPSILON)
    normed = middle * factor
    grad_hidden = gh_ref[...]
    product = grad_hidden * normed
    grad_normed = grad_hidden * (1.0 + mod_ref[:, 4 * width : 5 * width])
    back = factor * (
        grad_normed - normed * jnp.mean(grad_normed * normed, axis=-1, keepdims=True)
    )
    grad_middle = dy + back
    gmid_ref[...] = grad_middle
    grad_attended = (mod_ref[:, 2 * width : 3 * width] * grad_middle).astype(BF16)
    sums_ref[0:1, :] = col_sum(grad_middle * att_ref[...].astype(F32))
    sums_ref[1:2, :] = col_sum(grad_hidden)
    sums_ref[2:3, :] = col_sum(product)
    sums_ref[3:4, :] = col_sum(dy * feed)
    sums_ref[4:5, :] = col_sum(grad_attended.astype(F32))
    sums_ref[5:6, :] = col_sum(gf_ref[...].astype(F32))
    sums_ref[6:8, :] = jnp.zeros((2, width), F32)
    gmix_ref[...] = mm_nt(grad_attended, weight_ref[...]).astype(BF16)
    mixed_t = mix_ref[...].T
    dw_ref[0] = mm(mixed_t, grad_attended[:, :half]).astype(BF16)
    dw_ref[1] = mm(mixed_t, grad_attended[:, half:]).astype(BF16)


def turn_call(feed, grad_hidden, middle, attended, dy, grad_feed, mixed, mod, weight, down_bias):
    rows, width = middle.shape
    low = jax.ShapeDtypeStruct((rows, width), BF16)
    return pl.pallas_call(
        turn_kernel,
        out_shape=[
            low,
            jax.ShapeDtypeStruct((rows, width), F32),
            low,
            jax.ShapeDtypeStruct((2, width, width // 2), BF16),
            jax.ShapeDtypeStruct((8, width), F32),
        ],
        compiler_params=params(),
        name="turn",
    )(feed, grad_hidden, middle, attended, dy, grad_feed, mixed, mod, weight, down_bias)


def project_back_kernel(
    head, dq_ref, dk0_ref, dk1_ref, dv0_ref, dv1_ref, raw_ref, hid_ref, x_ref, gmid_ref, mod_ref,
    weight_ref, qgain_ref, kgain_ref, cos_ref, sin_ref,
    gx_ref, dw_ref, sums_ref, bias_ref, proj_ref,
):
    width = x_ref.shape[1]
    cosine, sine = cos_ref[...], -sin_ref[...]
    for part in range(3):
        span = slice(part * width, (part + 1) * width)
        if part == 2:
            grad = dv0_ref[...].astype(F32) + dv1_ref[...].astype(F32)
        else:
            grad = dq_ref[...].astype(F32)
            if part == 1:
                grad = dk0_ref[...].astype(F32) + dk1_ref[...].astype(F32)
            gain = (qgain_ref, kgain_ref)[part][...]
            raw = raw_ref[:, span].astype(F32)
            factor = lax.rsqrt(head_sum(raw * raw, head) * (1.0 / head) + NORM_EPSILON)
            normed = raw * factor
            turned = turn(grad, cosine, sine, head)
            sums_ref[2 + part : 3 + part, :] = col_sum(turned * normed)
            turned = turned * gain
            mean = head_sum(turned * normed, head) * (1.0 / head)
            grad = factor * (turned - normed * mean)
        low = grad.astype(BF16)
        proj_ref[:, span] = low
        bias_ref[:, span] = col_sum(low.astype(F32))
    hidden_t = hid_ref[...].T
    half = 3 * width // 2
    dw_ref[0] = mm(hidden_t, proj_ref[:, :half]).astype(BF16)
    dw_ref[1] = mm(hidden_t, proj_ref[:, half:]).astype(BF16)
    grad_hidden = mm_nt(proj_ref[...], weight_ref[...])
    x = x_ref[...].astype(F32)
    factor = lax.rsqrt(jnp.mean(x * x, axis=-1, keepdims=True) + NORM_EPSILON)
    normed = x * factor
    sums_ref[0:1, :] = col_sum(grad_hidden)
    sums_ref[1:2, :] = col_sum(grad_hidden * normed)
    sums_ref[4:8, :] = jnp.zeros((4, width), F32)
    grad_normed = grad_hidden * (1.0 + mod_ref[:, width : 2 * width])
    back = factor * (
        grad_normed - normed * jnp.mean(grad_normed * normed, axis=-1, keepdims=True)
    )
    gx_ref[...] = (gmid_ref[...] + back).astype(BF16)


def project_back_call(
    dq, dk0, dk1, dv0, dv1, raw, hidden, x, grad_middle, mod, weight, qgain, kgain, cosine, sine, head
):
    rows, width = x.shape
    return pl.pallas_call(
        functools.partial(project_back_kernel, head),
        out_shape=[
            jax.ShapeDtypeStruct((rows, width), BF16),
            jax.ShapeDtypeStruct((2, width, 3 * width // 2), BF16),
            jax.ShapeDtypeStruct((8, width), F32),
            jax.ShapeDtypeStruct((1, 3 * width), F32),
        ],
        scratch_shapes=[pltpu.VMEM((rows, 3 * width), BF16)],
        compiler_params=params(),
        name="project_back",
    )(dq, dk0, dk1, dv0, dv1, raw, hidden, x, grad_middle, mod, weight, qgain, kgain, cosine, sine)


class Place:
    def __init__(self):
        self.z, self.gy, self.gx = (lax.axis_index(name) for name in AXES)
        self.core = lax.rem(self.gx, 2)
        self.side = self.gx // 2
        self.chip = 2 * self.gy + self.side

    def flipped(self, k):
        return 2 * lax.rem(self.gy + k // 2, 2) + lax.rem(self.side + lax.rem(k, 2), 2)

    def pair(self):
        return {"gx": self.gx + 1 - 2 * self.core}

    def plane(self, k):
        device = {}
        if k & 2:
            device["gy"] = 1 - self.gy
        if k & 1:
            device["gx"] = lax.rem(self.gx + 2, 4)
        return device

    def depth(self, d):
        return {"batch": self.flipped_z(d)}

    def flipped_z(self, d):
        return {1: self.z + 1 - 2 * lax.rem(self.z, 2), 2: lax.rem(self.z + 2, 4), 3: 3 - self.z}[d]


def meet(devices):
    barrier = pltpu.get_barrier_semaphore()
    for device in devices:
        pl.semaphore_signal(barrier, inc=1, device_id=device, device_id_type=pl.DeviceIdType.MESH)
    pl.semaphore_wait(barrier, len(devices))


def send(source, target, send_sem, recv_sem, device):
    return pltpu.make_async_remote_copy(
        src_ref=source, dst_ref=target, send_sem=send_sem, recv_sem=recv_sem, device_id=device,
        device_id_type=pl.DeviceIdType.MESH,
    )


def feed_order(step):
    owner = jnp.where(
        step < 2, 3, jnp.where((step == 2) | (step == 5), 2, jnp.where(step < 5, 1, 0))
    )
    return owner, lax.rem(step, 2)


def feed_block(step, i):
    step = jnp.minimum(step, 7)
    owner, half = feed_order(step)
    return (2 * half + i) * 4 + Place().flipped(owner)


def feed_turn_kernel(
    h2_ref, h2t_ref, gf_ref, wg0, wg1, wu0, wu1, bg0, bg1, bu0, bu1, wd0, wd1,
    mid_ref, att_ref, dy_ref, mix_ref, mod_ref, weight_ref, dbias_ref, known_ref,
    out_ref, gmid_ref, gmix_ref, dw_ref, sums_ref, total_ref, passed_ref,
    feed_ref, gh_ref, bias_ref, made, paired, near, pair_send, pair_recv, near_send, near_recv,
):
    place = Place()
    core = place.core
    step = pl.program_id(0)
    slot = lax.rem(step, 2)
    width = h2_ref.shape[1]
    unit = 128
    g_rows = width

    @pl.when(step == 0)
    def _():
        feed_ref[...] = jnp.zeros_like(feed_ref)
        sums_ref[1] = jnp.zeros((8, width), F32)
        gh_ref[...] = jnp.zeros_like(gh_ref)
        meet([place.pair(), place.plane(1), place.plane(2)])

    def pair_copy(of):
        return send(
            made.at[lax.rem(of, 2), 1 - core], paired.at[of], pair_send.at[lax.rem(of, 2)],
            pair_recv.at[of], place.pair(),
        )

    def near_copy(of, k):
        return send(paired.at[of], near.at[of], near_send.at[of], near_recv.at[of], place.plane(k))

    @pl.when(step >= 1)
    def _():
        pair_copy(step - 1).start()

    @pl.when(step < 8)
    def _():
        owner, half = feed_order(step)
        hidden = h2_ref[...]
        grad_feed = gf_ref[...]
        wg = jnp.concatenate([wg0[...], wg1[...]], axis=1)
        wu = jnp.concatenate([wu0[...], wu1[...]], axis=1)
        wd = jnp.concatenate([wd0[...], wd1[...]], axis=0)
        gate = mm(hidden, wg) + jnp.concatenate([bg0[...], bg1[...]], axis=1).astype(F32)
        up = mm(hidden, wu) + jnp.concatenate([bu0[...], bu1[...]], axis=1).astype(F32)
        grad_product = mm_nt(grad_feed, wd)
        sig = 1.0 / (1.0 + jnp.exp(-gate))
        active = gate * sig
        product = (active * up).astype(BF16)
        grad_gate = (grad_product * up * sig * (1.0 + gate * (1.0 - sig))).astype(BF16)
        grad_up = (grad_product * active).astype(BF16)
        feed_ref[...] += mm(product, wd)
        gh_ref[...] += mm_nt(grad_gate, wg) + mm_nt(grad_up, wu)
        for e, grad in enumerate((grad_gate, grad_up)):
            total = col_sum(grad.astype(F32))
            for i in range(2):
                row = 16 * e + (2 * half + i) * 4 + place.flipped(owner)
                bias_ref[pl.ds(row, 1), :] = total[:, i * unit : (i + 1) * unit]

        @pl.when(step >= 2)
        def _():
            pair_copy(step - 2).wait_send()

        for e, grad in enumerate((grad_gate, grad_up)):
            made[slot, e, :g_rows] = mm(h2t_ref[...], grad).astype(BF16)
        product_t = product.T
        for b in range(3):
            d = mm(product_t, grad_feed[:, 256 * b : 256 * b + 256]).astype(BF16)
            for i in range(2):
                for c in range(2):
                    made[slot, c, pl.ds(g_rows + b * 128 + i * 64, 64)] = d[
                        i * 128 + c * 64 : i * 128 + c * 64 + 64
                    ]

    @pl.when(step >= 1)
    def _():
        of = step - 1
        copy = pair_copy(of)
        copy.wait_recv()
        paired[of] = (made[1 - slot, core].astype(F32) + paired[of].astype(F32)).astype(BF16)

        @pl.when((of == 0) | (of == 2))
        def _():
            near_copy(of, 2).start()

        @pl.when((of == 1) | (of == 3))
        def _():
            near_copy(of, 1).start()

    @pl.when(step == 8)
    def _():
        half = width // 2
        dy = dy_ref[...].astype(F32)
        feed = feed_ref[...] + dbias_ref[...].astype(F32)
        middle = mid_ref[...]
        out_ref[...] = (middle + mod_ref[:, 5 * width :] * feed).astype(BF16)
        factor = lax.rsqrt(jnp.mean(middle * middle, axis=-1, keepdims=True) + NORM_EPSILON)
        normed = middle * factor
        grad_hidden = gh_ref[...]
        product = grad_hidden * normed
        grad_normed = grad_hidden * (1.0 + mod_ref[:, 4 * width : 5 * width])
        back = factor * (
            grad_normed - normed * jnp.mean(grad_normed * normed, axis=-1, keepdims=True)
        )
        grad_middle = dy + back
        gmid_ref[...] = grad_middle
        grad_attended = (mod_ref[:, 2 * width : 3 * width] * grad_middle).astype(BF16)
        sums_ref[0, 0:1, :] = col_sum(grad_middle * att_ref[...].astype(F32))
        sums_ref[0, 1:2, :] = col_sum(grad_hidden)
        sums_ref[0, 2:3, :] = col_sum(product)
        sums_ref[0, 3:4, :] = col_sum(dy * feed)
        sums_ref[0, 4:5, :] = col_sum(grad_attended.astype(F32))
        sums_ref[0, 5:6, :] = col_sum(gf_ref[...].astype(F32))
        sums_ref[0, 6:8, :] = known_ref[...]
        for row in range(32):
            col = (row % 6) * unit
            sums_ref[1, row // 6 : row // 6 + 1, col : col + unit] = bias_ref[row : row + 1, :]
        gmix_ref[...] = mm_nt(grad_attended, weight_ref[...]).astype(BF16)
        mixed_t = mix_ref[...].T
        dw_ref[0] = mm(mixed_t, grad_attended[:, :half]).astype(BF16)
        dw_ref[1] = mm(mixed_t, grad_attended[:, half:]).astype(BF16)
        for of in (6, 7):
            pair_copy(of).wait_send()
        for of in range(4):
            near_copy(of, 1).wait()
        rows = width // 4
        for target, mine, there in ((total_ref, 6, 2), (passed_ref, 4, 0)):
            for f in range(2):

                def added(span, f=f, mine=mine, there=there):
                    both = paired[mine + f, span].astype(F32) + near[there + f, span].astype(F32)
                    return both.astype(BF16)

                for z in range(4):
                    target[z, f] = added(slice(z * rows, (z + 1) * rows))
                for i in range(2):
                    for b in range(3):
                        start = g_rows + b * 128 + i * 64
                        target[2 * f + i, 2, b * 64 : b * 64 + 64] = added(slice(start, start + 64))


def once(shape):
    return pl.BlockSpec(shape, lambda *_: (0,) * len(shape), pipeline_mode=pl.Buffered(1))


def feed_turn_call(
    hidden, hidden_t, grad_feed, gate_up, down, middle, attended, dy, mixed, mod, weight, small,
    known,
):
    rows, width = hidden.shape
    low = jax.ShapeDtypeStruct((rows, width), BF16)
    wide = jax.ShapeDtypeStruct((rows, width), F32)
    cols = lambda i, e: pl.BlockSpec((width, 128), lambda s: (0, 16 * e + feed_block(s, i)))
    first = GATE_BIAS * width // 128
    bias = lambda i, e: pl.BlockSpec((1, 128), lambda s: (0, first + 16 * e + feed_block(s, i)))
    down_bias = pl.BlockSpec((1, width), lambda s: (0, DOWN_BIAS), pipeline_mode=pl.Buffered(1))
    deep = lambda i: pl.BlockSpec((128, width), lambda s: (feed_block(s, i), 0))
    piece = (width + 384, 256)
    out_shape = [
        low, wide, low,
        jax.ShapeDtypeStruct((2, width, width // 2), BF16),
        jax.ShapeDtypeStruct((2, 8, width), F32),
        jax.ShapeDtypeStruct((4, 3, width // 4, 256), BF16),
        jax.ShapeDtypeStruct((4, 3, width // 4, 256), BF16),
    ]
    return pl.pallas_call(
        feed_turn_kernel,
        grid=(9,),
        in_specs=[once((rows, width)), once((width, rows)), once((rows, width))]
        + [cols(0, 0), cols(1, 0), cols(0, 1), cols(1, 1)]
        + [bias(0, 0), bias(1, 0), bias(0, 1), bias(1, 1)]
        + [deep(0), deep(1)]
        + [once((rows, width))] * 4
        + [once(mod.shape), once(weight.shape), down_bias, once(known.shape)],
        out_specs=[full(shape.shape) for shape in out_shape],
        out_shape=out_shape,
        scratch_shapes=[
            pltpu.VMEM((rows, width), F32),
            pltpu.VMEM((rows, width), F32),
            pltpu.VMEM((32, 128), F32),
            pltpu.VMEM((2, 2) + piece, BF16),
            pltpu.VMEM((8,) + piece, BF16),
            pltpu.VMEM((4,) + piece, BF16),
            pltpu.SemaphoreType.DMA((2,)),
            pltpu.SemaphoreType.DMA((8,)),
            pltpu.SemaphoreType.DMA((4,)),
            pltpu.SemaphoreType.DMA((4,)),
        ],
        compiler_params=pltpu.CompilerParams(
            vmem_limit_bytes=VMEM_LIMIT, collective_id=1, has_side_effects=True
        ),
        name="feed_turn",
    )(
        hidden, hidden_t, grad_feed, gate_up, gate_up, gate_up, gate_up, small, small, small,
        small, down, down, middle, attended, dy, mixed, mod, weight, small, known,
    )


Q_GAIN, K_GAIN, OUT_BIAS, DOWN_BIAS, GATE_BIAS = 0, 1, 2, 3, 4


def front_kernel(
    head, tile_cols, tok_hbm, grad_hbm, time_ref, label_ref, modb_ref, inb_ref, qgain_ref,
    kgain_ref, outb_ref, downb_ref, gateb_ref, table_hbm, modw_hbm, inw_hbm,
    x_hbm, dy_hbm, hid_hbm, q_hbm, k0_hbm, v0_hbm, k1_hbm, v1_hbm, raw_hbm, mod_ref, cos_ref,
    sin_ref, small_ref, known_ref,
    x_ref, own_ref, hid_ref, q_ref, k_ref, v_ref, raw_ref, table_ref, modw_ref, inw_ref,
    load_sem, store_sem, tok_send, tok_recv, kv_send, kv_recv,
):
    place = Place()
    core, chip = place.core, place.chip
    rows, width = x_ref.shape
    cells = rows // 4
    loads = [
        pltpu.make_async_copy(source, target, load_sem.at[i])
        for i, (source, target) in enumerate(
            (
                (tok_hbm.at[chip], x_ref.at[pl.ds(0, cells)]), (modw_hbm, modw_ref),
                (inw_hbm, inw_ref), (grad_hbm.at[chip], own_ref), (table_hbm, table_ref),
            )
        )
    ]
    stores = [
        pltpu.make_async_copy(source, target, store_sem.at[i])
        for i, (source, target) in enumerate(
            (
                (own_ref, dy_hbm.at[pl.ds(0, cells)]), (x_ref, x_hbm), (hid_ref, hid_hbm),
                (k_ref, k0_hbm), (v_ref, v0_hbm), (q_ref, q_hbm), (raw_ref, raw_hbm),
            )
        )
    ]

    def token_copy(which, k):
        source, target = ((tok_hbm, x_ref), (grad_hbm, dy_hbm))[which]
        return send(
            source.at[place.flipped(k)], target.at[pl.ds(k * cells, cells)],
            tok_send.at[which, k - 1], tok_recv.at[which, k - 1], place.plane(k),
        )

    def kv_copy(which, chunk):
        source, target = ((k_ref, k1_hbm), (v_ref, v1_hbm))[which]
        span = pl.ds(chunk * cells, cells if chunk == 0 else rows - cells)
        return send(
            source.at[span], target.at[span], kv_send.at[which, chunk], kv_recv.at[which, chunk],
            place.pair(),
        )

    def line(ref):
        return ref[...].astype(F32)[None, :]

    in_bias = line(inb_ref)

    def project(start, size, chunk):
        span = slice(start, start + size)
        x = x_ref[span, :].astype(F32)
        normed = x * lax.rsqrt(jnp.mean(x * x, axis=-1, keepdims=True) + NORM_EPSILON)
        hidden = normed * (1.0 + mod_ref[:, width : 2 * width]) + mod_ref[:, :width]
        hidden = hidden.astype(BF16)
        hid_ref[span, :] = hidden
        for part in (1, 2, 0):
            raw = mm(hidden, inw_ref[:, part * width : (part + 1) * width])
            raw = raw + in_bias[:, part * width : (part + 1) * width]
            if part == 2:
                v_ref[span, :] = raw.astype(BF16)
                for which in (0, 1):
                    kv_copy(which, chunk).start()
                continue
            raw_ref[span, part * width : (part + 1) * width] = raw.astype(BF16)
            factor = lax.rsqrt(head_sum(raw * raw, head) * (1.0 / head) + NORM_EPSILON)
            scaled = raw * factor * small_ref[:, part * width : (part + 1) * width]
            turned = turn(scaled, cos_ref[span, :], sin_ref[span, :], head).astype(BF16)
            (q_ref, k_ref)[part][span, :] = turned

    for i in (0, 4, 1, 2, 3):
        loads[i].start()
    meet([place.pair()] + [place.plane(k) for k in (1, 2, 3)])
    for k in (3, 1, 2):
        token_copy(0, k).start()

    for start, row in (
        (Q_GAIN, jnp.concatenate([line(qgain_ref)] * (width // head), axis=1)),
        (K_GAIN, jnp.concatenate([line(kgain_ref)] * (width // head), axis=1)),
        (OUT_BIAS, line(outb_ref)), (DOWN_BIAS, line(downb_ref)), (GATE_BIAS, line(gateb_ref)),
    ):
        small_ref[:, start * width : start * width + row.shape[1]] = row
    half = width // 2
    index = lax.broadcasted_iota(jnp.int32, (1, half), 1).astype(F32)
    phase = time_ref[chip].astype(F32) * jnp.exp(-math.log(10000.0) * index / half)
    features = jnp.concatenate([jnp.cos(phase), jnp.sin(phase)], axis=1)
    label = label_ref[chip]
    classes = lax.broadcasted_iota(jnp.int32, (16, table_ref.shape[0]), 1)
    loads[4].wait()
    chosen = mm(jnp.where(classes == label, 1.0, 0.0).astype(BF16), table_ref[...])
    condition = features + chosen[:1]
    known_ref[0:1, :] = jnp.where(core == 0, condition, 0.0)
    known_ref[1:2, :] = jnp.where(core == 0, jnp.zeros((1, width), F32) + label.astype(F32), 0.0)
    act = condition * (1.0 / (1.0 + jnp.exp(-condition)))
    act = jnp.broadcast_to(act, (16, width)).astype(BF16)

    quarter = head // 4
    lane = lax.broadcasted_iota(jnp.int32, (1, 128), 1)
    rate = jnp.exp(-math.log(10000.0) / quarter * lax.rem(lane, quarter).astype(F32))
    by_row = lax.rem(lane, head) < head // 2
    sign = jnp.where(lax.rem(lane, 2 * quarter) < quarter, -1.0, 1.0)
    cell = lax.broadcasted_iota(jnp.int32, (cells, 128), 0)
    row, col = cell // tile_cols, lax.rem(cell, tile_cols)
    for k in range(4):
        there = place.flipped(k)
        down = (there // 2) * (cells // tile_cols) + row
        across = (2 * lax.rem(there, 2) + core) * tile_cols + col
        angle = jnp.where(by_row, down, across).astype(F32) * rate
        cos_ref[k * cells : (k + 1) * cells, :] = jnp.cos(angle)
        sin_ref[k * cells : (k + 1) * cells, :] = sign * jnp.sin(angle)
    loads[1].wait()
    mod_ref[...] = mm(act, modw_ref[...])[:1] + line(modb_ref)
    loads[0].wait()
    loads[2].wait()
    project(0, cells, 0)
    loads[3].wait()
    stores[0].start()
    for k in (1, 2, 3):
        token_copy(0, k).wait()
    for k in (3, 1, 2):
        token_copy(1, k).start()
    stores[1].start()
    project(cells, rows - cells, 1)
    for store in stores[2:]:
        store.start()
    for which in (0, 1):
        for chunk in (0, 1):
            kv_copy(which, chunk).wait()
    for k in (1, 2, 3):
        token_copy(1, k).wait()
    for store in stores:
        store.wait()


def front_call(
    tokens, grads, timesteps, labels, vectors, class_table, modw, inw, head, tile_cols
):
    images, cells, width = tokens.shape
    rows = images * cells
    low = lambda *shape: jax.ShapeDtypeStruct(shape, BF16)
    vmem = lambda *shape: pltpu.VMEM(shape, BF16)
    anywhere = pl.BlockSpec(memory_space=pl.ANY)
    inside = pl.BlockSpec(memory_space=pltpu.VMEM)
    sems = lambda *shape: pltpu.SemaphoreType.DMA(shape)
    return pl.pallas_call(
        functools.partial(front_kernel, head, tile_cols),
        in_specs=[anywhere] * 2
        + [pl.BlockSpec(memory_space=pltpu.SMEM)] * 2
        + [inside] * len(vectors)
        + [anywhere] * 3,
        out_specs=[anywhere] * 9 + [inside] * 5,
        out_shape=[low(rows, width)] * 8
        + [
            low(rows, 2 * width), jax.ShapeDtypeStruct((1, 6 * width), F32),
            jax.ShapeDtypeStruct((rows, 128), F32), jax.ShapeDtypeStruct((rows, 128), F32),
            jax.ShapeDtypeStruct((1, GATE_BIAS * width + vectors[-1].shape[0]), F32),
            jax.ShapeDtypeStruct((2, width), F32),
        ],
        scratch_shapes=[
            vmem(rows, width), vmem(cells, width), vmem(rows, width), vmem(rows, width),
            vmem(rows, width), vmem(rows, width), vmem(rows, 2 * width), vmem(*class_table.shape),
            vmem(*modw.shape), vmem(*inw.shape), sems(5), sems(7), sems(2, 3), sems(2, 3), sems(2, 2), sems(2, 2),
        ],
        compiler_params=pltpu.CompilerParams(
            vmem_limit_bytes=VMEM_LIMIT, collective_id=3, has_side_effects=True
        ),
        name="front",
    )(tokens, grads, timesteps, labels, *vectors, class_table, modw, inw)


Z_FIRST = (False, False, False, False)
GROUPS = 4
TOKEN_STEP = 3
PASS_STEP = 4


def back_kernel(
    head, q_ref, k0_ref, k1_ref, v0_ref, v1_ref, gm_ref, mix_ref, rl_ref, e_ref,
    mod_ref, qgain_ref, kgain_ref, cos_ref, sin_ref, dout_ref, totals_ref, passed_ref, early_ref,
    raw_hbm, hid_hbm, x_hbm, gmid_hbm, weight_hbm, rows_hbm,
    output_ref, gtok_ref, feeds_hbm, projs_hbm, early_hbm, late_hbm,
    feeds_ref, projs_ref, early_all, late_all, raw_ref, hid_ref, x_ref, gmid_ref, weight_ref, hidt_ref, gh_ref, gx_ref, late_ref,
    dq_s, dk0_s, dv0_s, dk1_s, dv1_s, dk_in, dv_in,
    made, paired, first_out, first_in, second_out, second_in, landed, z_in, early_in, late_in,
    load_sem, own_sem, kv_send, kv_recv, pair_send, pair_recv, first_send, first_recv,
    second_send, second_recv, pass_send, pass_recv, z_send, z_recv, tok_send, tok_recv, feed_send, feed_recv,
    proj_send, proj_recv, small_send, small_recv,
):
    place = Place()
    core, chip, z = place.core, place.chip, place.z
    step = pl.program_id(0)
    rows, width = x_ref.shape
    cells = rows // 4
    scale = head**-0.5
    lane = lax.broadcasted_iota(jnp.int32, (1, 128), 1)

    loads = [
        pltpu.make_async_copy(source, target, load_sem.at[i])
        for i, (source, target) in enumerate(
            (
                (hid_hbm, hid_ref), (raw_hbm, raw_ref), (weight_hbm, weight_ref),
                (x_hbm, x_ref), (gmid_hbm, gmid_ref),
            )
        )
    ]

    stores = [
        pltpu.make_async_copy(source, target, load_sem.at[5 + i])
        for i, (source, target) in enumerate(
            (
                (early_all, early_hbm), (late_all, late_hbm), (feeds_ref, feeds_hbm),
                (projs_ref, projs_hbm),
            )
        )
    ]

    def pass_copy(f, i):
        part = (slice(None), f) if i == 0 else (pl.ds(2 * f, 2), 2)
        return send(
            passed_ref.at[part], landed.at[part], pass_send.at[f, i], pass_recv.at[f, i],
            place.plane(f + 1),
        )

    def z_copy(d):
        return send(
            landed.at[place.flipped_z(d)], z_in.at[d - 1], z_send.at[d - 1], z_recv.at[d - 1],
            place.depth(d),
        )

    def token_copy(which, k):
        source, target = ((rows_hbm, output_ref), (gx_ref, gtok_ref))[which]
        return send(
            source.at[pl.ds(k * cells, cells)], target.at[chip], tok_send.at[which, k - 1],
            tok_recv.at[which, k - 1], place.plane(k),
        )

    def own_tokens(which):
        source, target = ((rows_hbm, output_ref), (gx_ref, gtok_ref))[which]
        return pltpu.make_async_copy(source.at[pl.ds(0, cells)], target.at[chip], own_sem.at[which])

    def kv_copy(which, p):
        source, target = ((dk1_s, dk_in), (dv1_s, dv_in))[which]
        return send(
            source.at[p], target.at[p], kv_send.at[which, p], kv_recv.at[which, p], place.pair()
        )

    def pair_copy(g):
        source = dout_ref.at[1 - core] if g == 3 else made.at[g % 2, 1 - core]
        return send(source, paired.at[g], pair_send.at[g], pair_recv.at[g], place.pair())

    def first_copy(g, k):
        other = place.flipped_z(k) if Z_FIRST[g] else place.flipped(k)
        device = place.depth(k) if Z_FIRST[g] else place.plane(k)
        return send(
            first_out.at[g, other], first_in.at[g, k - 1], first_send.at[g, k - 1],
            first_recv.at[g, k - 1], device,
        )

    def second_copy(g, k):
        other = place.flipped(k) if Z_FIRST[g] else place.flipped_z(k)
        device = place.plane(k) if Z_FIRST[g] else place.depth(k)
        return send(
            second_out.at[g, other], second_in.at[g, k - 1], second_send.at[g, k - 1],
            second_recv.at[g, k - 1], device,
        )

    def feed_copy(k):
        here = feeds_ref.at[core, chip]
        return send(here, here, feed_send.at[k - 1], feed_recv.at[k - 1], place.plane(k))

    def feed_pair():
        here = feeds_ref.at[core]
        return send(here, here, feed_send.at[3], feed_recv.at[3], place.pair())

    def proj_copy(k):
        here = projs_ref.at[core, chip]
        return send(here, here, proj_send.at[k - 1], proj_recv.at[k - 1], place.plane(k))

    def proj_pair():
        here = projs_ref.at[core]
        return send(here, here, proj_send.at[3], proj_recv.at[3], place.pair())

    smalls = ((early_ref, early_in, early_all, 8), (late_ref, late_in, late_all, 4))

    def small_pair(which):
        source, target, _, count = smalls[which]
        return send(
            source.at[1 - core], target, small_send.at[which, 0], small_recv.at[which, 0],
            place.pair(),
        )

    def small_plane(which, k):
        full_ref = smalls[which][2]
        return send(
            full_ref.at[core, pl.ds(0, 1)], full_ref.at[core, pl.ds(k, 1)],
            small_send.at[which, k], small_recv.at[which, k], place.plane(k),
        )

    def small_depth(which, d):
        full_ref = smalls[which][2]
        have = 4 * d
        return send(
            full_ref.at[core, pl.ds(0, have)], full_ref.at[core, pl.ds(have, have)],
            small_send.at[which, 3 + d], small_recv.at[which, 3 + d], place.depth(d),
        )

    def small_last(which):
        here = smalls[which][2].at[core]
        return send(
            here, here, small_send.at[which, 6], small_recv.at[which, 6], place.pair()
        )

    def small_begin(which):
        source, target, full_ref, _ = smalls[which]
        small_pair(which).wait_recv()
        full_ref[core, 0] = source[core] + target[...]
        for k in (1, 2, 3):
            small_plane(which, k).start()

    def small_next(which, i):
        if i == 0:
            for k in (1, 2, 3):
                small_plane(which, k).wait_recv()
            small_depth(which, 1).start()
        elif i == 1:
            small_depth(which, 1).wait_recv()
            small_depth(which, 2).start()
        else:
            small_depth(which, 2).wait_recv()
            small_last(which).start()

    def start_group(g):
        pair_copy(g).wait_recv()
        mine = dout_ref.at[core] if g == 3 else made.at[g % 2, core]
        part = width // 16
        for a in range(4):
            for b in range(4):
                span = pl.ds((a * 4 + b) * part, part)
                total = (mine[span, :].astype(F32) + paired[g, span].astype(F32)).astype(BF16)
                if Z_FIRST[g]:
                    first_out[g, a, b] = total
                else:
                    first_out[g, b, a] = total
        for k in (1, 2, 3):
            first_copy(g, k).start()

    def go_on(g):
        for k in (1, 2, 3):
            first_copy(g, k).wait_recv()
        here = z if Z_FIRST[g] else chip
        second_out[g] = (
            first_out[g, here].astype(F32)
            + first_in[g, 0].astype(F32)
            + first_in[g, 1].astype(F32)
            + first_in[g, 2].astype(F32)
        ).astype(BF16)
        for k in (1, 2, 3):
            second_copy(g, k).start()

    def finish(g):
        for k in (1, 2, 3):
            second_copy(g, k).wait_recv()
        here = chip if Z_FIRST[g] else z
        projs_ref[core, chip, g] = (
            second_out[g, here].astype(F32)
            + second_in[g, 0].astype(F32)
            + second_in[g, 1].astype(F32)
            + second_in[g, 2].astype(F32)
        ).astype(BF16)

    @pl.when(step == 0)
    def _():
        for load in loads:
            load.start()
        meet(
            [place.pair()]
            + [place.plane(k) for k in (1, 2, 3)]
            + [place.depth(d) for d in (1, 2, 3)]
        )
        for f in (0, 1):
            for i in (0, 1):
                pass_copy(f, i).start()
        pair_copy(3).start()
        small_pair(0).start()
        gh_ref[...] = jnp.zeros_like(gh_ref)

    @pl.when(step >= 1)
    def _():
        for which in (0, 1):
            kv_copy(which, step - 1).start()

    @pl.when(step == 3)
    def _():
        pair_copy(0).start()

    @pl.when(step == 5)
    def _():
        pair_copy(1).start()

    @pl.when(step < 6)
    def _():
        keys = jnp.concatenate([k0_ref[...], k1_ref[...]], axis=0)
        values = jnp.concatenate([v0_ref[...], v1_ref[...]], axis=0)
        scaled = gm_ref[...].astype(F32) * rl_ref[...]
        products = scaled * mix_ref[...].astype(F32)
        scaled = scaled.astype(BF16)
        q_t = q_ref[...].T
        scaled_t = scaled.T
        dqs, dks, dvs = [], [], []
        for h in range(2):
            mine = (lane >= 64) if h else (lane < 64)
            inner = jnp.sum(jnp.where(mine, products, 0.0), axis=1, keepdims=True)
            grad_probs = mm_nt(jnp.where(mine, scaled, jnp.zeros_like(scaled)), values)
            grown = e_ref[h]
            grad_scores = (grown.astype(F32) * (grad_probs - inner) * scale).astype(BF16)
            dqs.append(mm(grad_scores, keys))
            dks.append(mm(q_t[64 * h : 64 * h + 64], grad_scores))
            dvs.append(mm(scaled_t[64 * h : 64 * h + 64], grown))
        dq_s[step] = jnp.where(lane < 64, dqs[0], dqs[1]).astype(BF16)
        dk = jnp.concatenate(dks, axis=0).T.astype(BF16)
        dv = jnp.concatenate(dvs, axis=0).T.astype(BF16)
        dk0_s[step] = dk[:rows]
        dk1_s[step] = dk[rows:]
        dv0_s[step] = dv[:rows]
        dv1_s[step] = dv[rows:]

    @pl.when(step == 0)
    def _():
        loads[0].wait()
        hidt_ref[...] = hid_ref[...].T

    @pl.when(step == 1)
    def _():
        loads[1].wait()
        loads[2].wait()
        start_group(3)
        small_begin(0)

    for i in range(3):

        @pl.when(step == 3 + i)
        def _(i=i):
            small_next(0, i)

    @pl.when(step == 3)
    def _():
        start_group(0)

    @pl.when(step == 5)
    def _():
        start_group(1)
        go_on(3)

    @pl.when(step == TOKEN_STEP)
    def _():
        for k in (1, 2, 3):
            token_copy(0, k).start()
        own_tokens(0).start()

    @pl.when(step == PASS_STEP)
    def _():
        for f in (0, 1):
            for i in (0, 1):
                pass_copy(f, i).wait_recv()
        landed[...] = (landed[...].astype(F32) + totals_ref[...].astype(F32)).astype(BF16)
        for d in (1, 2, 3):
            z_copy(d).start()

    @pl.when((step >= 2) & (lax.rem(step, 2) == 0))
    def _():
        g = (step - 2) // 2
        slot = lax.rem(g, 2)
        cosine, sine = cos_ref[...], -sin_ref[...]
        for i in range(2):
            for which in (0, 1):
                kv_copy(which, 2 * g + i).wait_recv()

        def both(ref):
            return jnp.concatenate([ref[2 * g], ref[2 * g + 1]], axis=1).astype(F32)

        lows = []
        for part in range(3):
            span = pl.ds(pl.multiple_of(part * width + g * 256, 256), 256)
            if part == 2:
                grad = both(dv0_s) + both(dv_in)
            else:
                grad = both(dq_s) if part == 0 else both(dk0_s) + both(dk_in)
                gain = (qgain_ref, kgain_ref)[part][:, :256].astype(F32)
                raw = raw_ref[:, span].astype(F32)
                factor = lax.rsqrt(head_sum(raw * raw, head) * (1.0 / head) + NORM_EPSILON)
                normed = raw * factor
                turned = turn(grad, cosine, sine, head)
                late_ref[1, part : part + 1, pl.ds(pl.multiple_of(g * 256, 256), 256)] = col_sum(
                    turned * normed
                )
                turned = turned * gain
                mean = head_sum(turned * normed, head) * (1.0 / head)
                grad = factor * (turned - normed * mean)
            low = grad.astype(BF16)
            lows.append(low)
            total = col_sum(low.astype(F32))
            where = pl.ds(pl.multiple_of(g * 256, 256), 256)
            if part < 2:
                late_ref[0, 2 + part : 3 + part, where] = total
            else:
                late_ref[1, 2:3, where] = total
            gh_ref[...] += mm_nt(low, weight_ref[:, span])
        grads = jnp.concatenate(
            [low[:, 128 * c : 128 * c + 128] for c in range(2) for low in lows], axis=1
        )

        @pl.when(step == 6)
        def _():
            pair_copy(0).wait_send()

        half = width // 2
        made[slot, 0] = mm(hidt_ref[...], grads[:, :half]).astype(BF16)
        made[slot, 1] = mm(hidt_ref[...], grads[:, half:]).astype(BF16)

    @pl.when(step == 6)
    def _():
        pair_copy(2).start()
        grad_hidden = gh_ref[...]
        loads[3].wait()
        loads[4].wait()
        x = x_ref[...].astype(F32)
        factor = lax.rsqrt(jnp.mean(x * x, axis=-1, keepdims=True) + NORM_EPSILON)
        normed = x * factor
        late_ref[0, 0:1, :] = col_sum(grad_hidden)
        late_ref[0, 1:2, :] = col_sum(grad_hidden * normed)
        late_ref[1, 3:4, :] = jnp.zeros((1, width), F32)
        small_pair(1).start()
        go_on(0)
        go_on(1)
        small_begin(1)
        start_group(2)
        grad_normed = grad_hidden * (1.0 + mod_ref[:, width : 2 * width])
        back = factor * (
            grad_normed - normed * jnp.mean(grad_normed * normed, axis=-1, keepdims=True)
        )
        gx_ref[...] = (gmid_ref[...] + back).astype(BF16)
        for k in (1, 2, 3):
            token_copy(1, k).start()
        own_tokens(1).start()
        for d in (1, 2, 3):
            z_copy(d).wait_recv()
        for i in range(3):
            feeds_ref[core, chip, i] = (
                landed[z, i].astype(F32)
                + z_in[0, i].astype(F32)
                + z_in[1, i].astype(F32)
                + z_in[2, i].astype(F32)
            ).astype(BF16)
        for k in (1, 2, 3):
            feed_copy(k).start()
        finish(3)
        finish(0)
        finish(1)
        go_on(2)
        small_next(1, 0)
        finish(2)
        for k in (1, 2, 3):
            proj_copy(k).start()
        small_next(1, 1)
        small_next(1, 2)
        for k in (1, 2, 3):
            feed_copy(k).wait_recv()
        for k in (1, 2, 3):
            feed_copy(k).wait_send()
        feed_pair().start()
        for k in (1, 2, 3):
            proj_copy(k).wait()
        proj_pair().start()
        for which in (0, 1):
            own_tokens(which).wait()
            for k in (1, 2, 3):
                token_copy(which, k).wait()
            small_pair(which).wait_send()
            for k in (1, 2, 3):
                small_plane(which, k).wait_send()
            for d in (1, 2):
                small_depth(which, d).wait_send()
            small_last(which).wait()
            stores[which].start()
            for p in range(6):
                kv_copy(which, p).wait_send()
        for f in (0, 1):
            for i in (0, 1):
                pass_copy(f, i).wait_send()
        for k in (1, 2, 3):
            z_copy(k).wait_send()
            for g in range(4):
                first_copy(g, k).wait_send()
                second_copy(g, k).wait_send()
        for g in (1, 2, 3):
            pair_copy(g).wait_send()
        feed_pair().wait()
        stores[2].start()
        proj_pair().wait()
        stores[3].start()
        for store in stores:
            store.wait()


def back_call(
    q, k0, k1, v0, v1, grad_mixed, mixed, inverse, grown, mod, small_vectors, cosine, sine, d_out,
    totals, passed, early, raw, hidden, x, grad_middle, weight, output_rows, head,
):
    rows, width = q.shape
    half, part = width // 2, width // 16
    low = lambda *shape: jax.ShapeDtypeStruct(shape, BF16)
    pair = pl.BlockSpec((rows, 128), lambda s: (0, jnp.minimum(s, 5)))
    anywhere = pl.BlockSpec(memory_space=pl.ANY)
    small = [mod, small_vectors, small_vectors, cosine, sine, d_out, totals, passed, early]
    gain = lambda at: pl.BlockSpec((1, width), lambda s: (0, at), pipeline_mode=pl.Buffered(1))
    out_shape = [
        low(4, rows // 4, width), low(4, rows // 4, width),
        low(2, 4, 3, width // 4, 256), low(2, 4, GROUPS, part, half),
        jax.ShapeDtypeStruct((2, 16, 8, width), F32), jax.ShapeDtypeStruct((2, 16, 4, width), F32),
    ]
    vmem = lambda *shape: pltpu.VMEM(shape, BF16)
    sems = lambda *shape: pltpu.SemaphoreType.DMA(shape)
    return pl.pallas_call(
        functools.partial(back_kernel, head),
        grid=(7,),
        in_specs=[pair] * 8
        + [pl.BlockSpec((2, rows, 2 * rows), lambda s: (jnp.minimum(s, 5), 0, 0))]
        + [once(mod.shape), gain(Q_GAIN), gain(K_GAIN)]
        + [once(each.shape) for each in small[3:]]
        + [anywhere] * 6,
        out_specs=[anywhere] * 6,
        out_shape=out_shape,
        scratch_shapes=[pltpu.VMEM(shape.shape, shape.dtype) for shape in out_shape[2:]]
        + [
            vmem(rows, 2 * width), vmem(rows, width), vmem(rows, width),
            pltpu.VMEM((rows, width), F32), vmem(width, 3 * width), vmem(width, rows),
            pltpu.VMEM((rows, width), F32), vmem(rows, width), pltpu.VMEM((2, 4, width), F32),
        ]
        + [vmem(6, rows, 128)] * 7
        + [
            vmem(2, 2, width, half), vmem(GROUPS, width, half),
            vmem(GROUPS, 4, 4, part, half), vmem(GROUPS, 3, 4, part, half),
            vmem(GROUPS, 4, part, half), vmem(GROUPS, 3, part, half),
            vmem(*totals.shape), vmem(3, 3, width // 4, 256),
            pltpu.VMEM((8, width), F32), pltpu.VMEM((4, width), F32),
            sems(9), sems(2), sems(2, 6), sems(2, 6), sems(GROUPS), sems(GROUPS),
            sems(GROUPS, 3), sems(GROUPS, 3), sems(GROUPS, 3), sems(GROUPS, 3),
            sems(2, 2), sems(2, 2), sems(3), sems(3), sems(2, 3), sems(2, 3), sems(4), sems(4),
            sems(4), sems(4),
            sems(2, 7), sems(2, 7),
        ],
        compiler_params=pltpu.CompilerParams(
            vmem_limit_bytes=VMEM_LIMIT, collective_id=2, has_side_effects=True
        ),
        name="back",
    )(
        q, k0, k1, v0, v1, grad_mixed, mixed, inverse, grown, *small, raw, hidden, x, grad_middle,
        weight, output_rows,
    )


def finish_kernel(
    head, feeds_ref, projs_ref, early_ref, late_ref, modw_hbm,
    cond_ref, table_hbm, gmodw_hbm, gmodb_ref, ginw_hbm, ginb_ref, gqg_ref, gkg_ref, goutw_hbm,
    goutb_ref, gguw_hbm, ggub_ref, gdownw_hbm, gdownb_ref,
    modw_ref, table_ref, gmodw_ref, ginw_ref, goutw_ref, gguw_ref, gdownw_ref, acts_ref, load_sem,
    store_sem,
):
    place = Place()
    width = early_ref.shape[3]
    part = projs_ref.shape[3]
    load = pltpu.make_async_copy(modw_hbm, modw_ref, load_sem)
    load.start()
    stores = [
        pltpu.make_async_copy(source, target, store_sem.at[i])
        for i, (source, target) in enumerate(
            (
                (gguw_ref, gguw_hbm), (gdownw_ref, gdownw_hbm), (ginw_ref, ginw_hbm),
                (goutw_ref, goutw_hbm), (gmodw_ref, gmodw_hbm), (table_ref, table_hbm),
            )
        )
    ]
    for c in range(2):
        for chip in range(4):
            for f in range(2):
                for i in range(2):
                    col = (((c * 2 + f) * 2 + i) * 4 + chip) * 128
                    gguw_ref[:, col : col + 128] = feeds_ref[
                        c, chip, f, :, i * 128 : (i + 1) * 128
                    ].astype(F32)
    stores[0].start()
    for c in range(2):
        for chip in range(4):
            row = chip * 128 + c * 64
            for b in range(3):
                gdownw_ref[row : row + 64, b * 256 : (b + 1) * 256] = feeds_ref[
                    c, chip, 2, b * 64 : (b + 1) * 64, :
                ].astype(F32)
    stores[1].start()
    for c in range(2):
        for chip in range(4):
            row = chip * part
            for g in range(3):
                for q in range(3):
                    col = q * width + g * 256 + c * 128
                    ginw_ref[row : row + part, col : col + 128] = projs_ref[
                        c, chip, g, :, q * 128 : (q + 1) * 128
                    ].astype(F32)
            half = width // 2
            goutw_ref[row : row + part, c * half : (c + 1) * half] = projs_ref[c, chip, 3].astype(F32)
    stores[2].start()
    stores[3].start()

    vectors = [late_ref[0, :, 0, :], late_ref[0, :, 1, :]]
    vectors += [early_ref[0, :, j, :] for j in range(4)]
    lows = [vector.astype(BF16) for vector in vectors]
    conditions = early_ref[0, :, 6, :]
    labels = early_ref[0, :, 7, :]
    sig = 1.0 / (1.0 + jnp.exp(-conditions))
    acts = (conditions * sig).astype(BF16)
    size = acts_ref.shape[1]
    for z in range(4):

        @pl.when(place.z == z)
        def _(z=z):
            acts_ref[...] = acts[:, z * size : (z + 1) * size]

    mine = acts_ref[...]
    for j, low in enumerate(lows):
        gmodw_ref[:, j * width : (j + 1) * width] = mm_tn(mine, low)
    stores[4].start()
    early_sum = jnp.sum(early_ref[0], axis=0)
    gate_sum = jnp.sum(early_ref[1], axis=0)
    late_sum = jnp.sum(late_ref[0], axis=0)
    gain_sum = jnp.sum(late_ref[1], axis=0)
    mod_b = jnp.concatenate(
        [late_sum[0:1], late_sum[1:2]] + [early_sum[j : j + 1] for j in range(4)], axis=1
    )
    in_b = jnp.concatenate([late_sum[2:3], late_sum[3:4], gain_sum[2:3]], axis=1)
    gate_b = jnp.concatenate(
        [gate_sum[n // 6 : n // 6 + 1, (n % 6) * 128 : (n % 6) * 128 + 128] for n in range(32)],
        axis=1,
    )
    gains = sum(gain_sum[0:2, i : i + 128] for i in range(0, width, 128))
    gains = gains[:, :head] + gains[:, head:]
    pieces = (
        (gmodb_ref, mod_b), (ginb_ref, in_b), (gqg_ref, gains[0:1]), (gkg_ref, gains[1:2]),
        (goutb_ref, early_sum[4:5]), (ggub_ref, gate_b), (gdownb_ref, early_sum[5:6]),
    )
    for z in range(4):

        @pl.when(place.z == z)
        def _(z=z):
            for ref, row in pieces:
                size = row.shape[1] // 4
                ref[...] = row[0, z * size : (z + 1) * size]

    load.wait()
    grad = sum(mm_nt(modw_ref[:, j * width : (j + 1) * width], low) for j, low in enumerate(lows)).T
    grad = grad * sig * (1.0 + conditions * (1.0 - sig))
    for k in range(4):
        cond_ref[pl.ds(place.flipped(k), 1), :] = grad[k : k + 1]
    classes = table_ref.shape[0]
    wide = -(-classes // 128) * 128
    column = lax.broadcasted_iota(jnp.int32, (1, wide), 1).astype(F32)
    onehot = jnp.where(labels[:, 0:1] == column, 1.0, 0.0).astype(BF16)
    high = grad.astype(BF16)
    rest = grad - high.astype(F32)
    middle = rest.astype(BF16)
    last = (rest - middle.astype(F32)).astype(BF16)
    table = mm_tn(
        jnp.concatenate([onehot] * 3, axis=0), jnp.concatenate([high, middle, last], axis=0)
    )
    table_ref[...] = table[:classes]
    stores[5].start()
    for store in stores:
        store.wait()


def finish_call(feeds, projs, early, late, weight, head, classes, hidden_width):
    width = weight.shape[0]
    rows = width // 4
    whole = lambda *shape: jax.ShapeDtypeStruct(shape, F32)
    anywhere = pl.BlockSpec(memory_space=pl.ANY)
    out_shape = [
        whole(4, width), whole(classes, width), whole(rows, 6 * width), whole(6 * width // 4),
        whole(rows, 3 * width), whole(3 * width // 4), whole(head // 4), whole(head // 4),
        whole(rows, width), whole(rows), whole(rows, 2 * hidden_width),
        whole(2 * hidden_width // 4), whole(hidden_width // 4, width), whole(rows),
    ]
    big = (1, 2, 4, 8, 10, 12)
    return pl.pallas_call(
        functools.partial(finish_kernel, head),
        in_specs=[pl.BlockSpec(memory_space=pltpu.VMEM)] * 4 + [anywhere],
        out_specs=[
            anywhere if i in big else pl.BlockSpec(memory_space=pltpu.VMEM)
            for i in range(len(out_shape))
        ],
        out_shape=out_shape,
        scratch_shapes=[pltpu.VMEM(weight.shape, BF16)]
        + [pltpu.VMEM(out_shape[i].shape, F32) for i in big]
        + [pltpu.VMEM((16, rows), BF16), pltpu.SemaphoreType.DMA, pltpu.SemaphoreType.DMA((6,))],
        compiler_params=params(),
        name="finish",
    )(feeds, projs, early, late, weight)


def take(array_in, index, axis=0):
    return lax.dynamic_index_in_dim(array_in, index, axis, keepdims=False)


def add(*terms):
    return sum(term.astype(F32) for term in terms)


class Moves:
    def __init__(self, mesh):
        self.sizes = tuple(mesh.shape[name] for name in AXES)

    def flip(self, value, batch=0, gy=0, gx=0):
        nb, ny, nx = self.sizes
        pairs = []
        for b in range(nb):
            for y in range(ny):
                for x in range(nx):
                    here = (b * ny + y) * nx + x
                    there = ((b ^ batch) * ny + (y ^ gy)) * nx + (x ^ gx)
                    pairs.append((here, there))
        return lax.ppermute(value, AXES, pairs)

    def plane(self, value, k):
        return self.flip(value, gy=k >> 1, gx=2 * (k & 1))

    def pair(self, value):
        return self.flip(value, gx=1)

    def gather(self, value):
        value = value[None]
        value = jnp.concatenate([value, self.plane(value, 1)], axis=0)
        value = jnp.concatenate([value, self.plane(value, 2)], axis=0)
        bit = 1
        while bit < self.sizes[0]:
            value = jnp.concatenate([value, self.flip(value, batch=bit)], axis=0)
            bit *= 2
        return value


def regroup(parts, place):
    stacked = jnp.stack(parts)
    return jnp.stack([take(stacked, place ^ k) for k in range(len(parts))])


def body(mesh, *operands):
    (
        tokens, timesteps, labels, class_table, modulate_weight, modulate_bias, inproj_weight,
        inproj_bias, query_gain, key_gain, outproj_weight, outproj_bias, gate_up_weight,
        gate_up_bias, down_weight, down_bias, cotangent,
    ) = operands
    image_count, tile_rows, tile_cols, width = tokens.shape
    cells = tile_rows * tile_cols
    rows = image_count * cells
    head = query_gain.shape[0]
    heads = width // head
    hidden_width = down_weight.shape[0]
    class_count = class_table.shape[0]
    highest = lax.Precision.HIGHEST
    moves = Moves(mesh)
    nb, ny, nx = moves.sizes
    assert ny == 2 and nx == 4 and image_count == 4
    z, gy, gx = (lax.axis_index(name) for name in AXES)
    side, core = gx // 2, gx % 2
    place = 2 * gy + side

    tiles = tokens.reshape(image_count, cells, width)
    grads = cotangent.reshape(image_count, cells, width)

    if nb == 4 and hidden_width == 16 * 128:
        vectors = (
            modulate_bias, inproj_bias, query_gain, key_gain, outproj_bias, down_bias, gate_up_bias
        )
        x, dy, hidden_one, q, k0, v0, k1, v1, raw, mod, cosine, sine, small, known = front_call(
            tiles, grads, timesteps, labels, vectors, class_table, modulate_weight, inproj_weight,
            head, tile_cols,
        )
        mixed, grown, inverse = attend_call(q, k0, k1, v0, v1, head)
        attended, middle, hidden_two, hidden_two_t, grad_feed = middle_call(
            mixed, x, dy, mod, outproj_weight, small, OUT_BIAS
        )
        output_rows, grad_middle, grad_mixed, d_out, sums_two, totals, passed = feed_turn_call(
            hidden_two, hidden_two_t, grad_feed, gate_up_weight, down_weight, middle, attended, dy,
            mixed, mod, outproj_weight, small, known,
        )
        output, grad_tokens, feeds, projs, early, late = back_call(
            q, k0, k1, v0, v1, grad_mixed, mixed, inverse, grown, mod, small, cosine, sine, d_out,
            totals, passed, sums_two, raw, hidden_one, x, grad_middle, inproj_weight, output_rows, head,
        )
        (
            grad_condition, grad_table, grad_mod_w, grad_mod_b, grad_in_w, grad_in_b, grad_q_gain,
            grad_k_gain, grad_out_w, grad_out_b, grad_gu_w, grad_gu_b, grad_down_w, grad_down_b,
        ) = finish_call(
            feeds, projs, early, late, modulate_weight, head, class_count, hidden_width
        )
        return (
            output.reshape(tokens.shape), grad_tokens.reshape(tokens.shape), grad_condition,
            grad_table, grad_mod_w, grad_mod_b, grad_in_w, grad_in_b, grad_q_gain, grad_k_gain,
            grad_out_w, grad_out_b, grad_gu_w, grad_gu_b, grad_down_w, grad_down_b,
        )

    def exchange(blocks):
        return [take(blocks, place)] + [
            moves.plane(take(blocks, place ^ k), k) for k in range(1, 4)
        ]

    x = jnp.concatenate(exchange(tiles), axis=0)

    half_width = width // 2
    step = take(timesteps, place).astype(F32)
    label = take(labels, place)
    rates = jnp.exp(-math.log(10000.0) * jnp.arange(half_width, dtype=F32) / half_width)
    features = jnp.concatenate([jnp.cos(step * rates), jnp.sin(step * rates)])
    condition = features + take(class_table, label).astype(F32)
    cond_act = jax.nn.silu(condition).astype(BF16)
    mod = modulation_call(
        jnp.broadcast_to(cond_act[None], (16, width)), modulate_weight, modulate_bias[None]
    )[:1]

    quarter = head // 4
    cell = jnp.arange(cells, dtype=jnp.int32)
    row_places, col_places = [], []
    for k in range(4):
        there = place ^ k
        row_places.append((there // 2) * tile_rows + cell // tile_cols)
        col_places.append((2 * (there % 2) + core) * tile_cols + cell % tile_cols)
    row_places = jnp.concatenate(row_places).astype(F32)[:, None]
    col_places = jnp.concatenate(col_places).astype(F32)[:, None]
    lane = jnp.arange(128, dtype=jnp.int32)
    turn_rate = jnp.exp(-math.log(10000.0) * (lane % quarter).astype(F32) / quarter)[None]
    angles = jnp.where((lane % head)[None] < head // 2, row_places, col_places) * turn_rate
    cosine = jnp.cos(angles)
    sine = jnp.where((lane % (2 * quarter))[None] < quarter, -1.0, 1.0) * jnp.sin(angles)
    qgain = jnp.tile(query_gain.astype(F32), heads)[None]
    kgain = jnp.tile(key_gain.astype(F32), heads)[None]

    hidden_one, q, k0, v0, raw = project_call(
        x, mod, inproj_weight, inproj_bias[None], qgain, kgain, cosine, sine, head
    )
    k1, v1 = moves.pair(k0), moves.pair(v0)
    dy = jnp.concatenate(exchange(grads), axis=0)
    mixed, grown, inverse = attend_call(q, k0, k1, v0, v1, head)
    attended, middle, hidden_two, hidden_two_t, grad_feed = middle_call(
        mixed, x, dy, mod, outproj_weight, outproj_bias[None]
    )

    unit = 256
    blocks = hidden_width // unit
    feed, grad_hidden, d_down, d_gate, d_bias = feed_call(
        hidden_two, hidden_two_t, grad_feed, gate_up_weight, gate_up_bias[None], down_weight,
        jnp.zeros((rows, width), F32), jnp.zeros((rows, width), F32), 0, 1, unit,
    )
    output_rows, grad_middle, grad_mixed, d_out, sums_two = turn_call(
        feed, grad_hidden, middle, attended, dy, grad_feed, mixed, mod, outproj_weight,
        down_bias[None],
    )
    gate_bias = d_bias.reshape(blocks, 2, unit).transpose(1, 0, 2)
    dq, dk0, dk1, dv0, dv1 = attend_back_call(
        q, k0, k1, v0, v1, grown, grad_mixed, mixed, inverse, head
    )
    dk1, dv1 = moves.pair(dk1), moves.pair(dv1)
    grad_x, d_in, sums_one, in_bias = project_back_call(
        dq, dk0, dk1, dv0, dv1, raw, hidden_one, x, grad_middle, mod, inproj_weight, qgain,
        kgain, cosine, sine, head,
    )

    def give_back(rows_out):
        parts = rows_out.reshape(4, cells, width)
        got = [parts[0]] + [moves.plane(parts[k], k) for k in range(1, 4)]
        return regroup(got, place).reshape(tokens.shape)

    output = give_back(output_rows)
    grad_tokens = give_back(grad_x)
    slice_rows = width // nb

    def scatter(d):
        d = lax.psum_scatter(d.astype(BF16), "batch", scatter_dimension=0, tiled=True)
        return lax.psum(d, ("gy", "gx")).astype(F32)

    def joined(d):
        return jnp.concatenate([d[0], d[1]], axis=1)

    grad_down_w = scatter(d_down.reshape(hidden_width, width))
    grad_gu_w = scatter(
        d_gate.transpose(2, 1, 0, 3).reshape(width, 2 * hidden_width)
    )
    grad_out_w = scatter(joined(d_out))
    grad_in_w = scatter(joined(d_in))
    gain_sums = sums_one[2:4].reshape(2, heads, head).sum(axis=1)
    early = jnp.concatenate([sums_two[:6].reshape(-1), gate_bias.reshape(-1)])
    late = jnp.concatenate(
        [sums_one[:2].reshape(-1), in_bias.reshape(-1), gain_sums.reshape(-1)]
    )

    def everywhere(vector):
        halves = vector.reshape(2, -1)
        half = add(take(halves, core), moves.pair(take(halves, 1 - core)))
        half = moves.gather(half)
        both = regroup([half, moves.pair(half)], core)
        return both.transpose(1, 0, 2).reshape(half.shape[0], -1)

    known = jnp.concatenate([condition, jnp.broadcast_to(label.astype(F32), (128,))])
    known = moves.gather(known)
    early, late = everywhere(early), everywhere(late)
    grad_modulation = jnp.concatenate([late[:, : 2 * width], early[:, : 4 * width]], axis=1)
    conditions = known[:, :width]
    all_labels = known[:, width].astype(jnp.int32)
    cond_acts = jax.nn.silu(conditions).astype(BF16)
    my_acts = lax.dynamic_slice_in_dim(cond_acts, z * slice_rows, slice_rows, axis=1)
    low_mod = grad_modulation.astype(BF16)
    grad_mod_w = mm_tn(my_acts, low_mod)
    wide = 6 * width
    grad_mod_b = lax.dynamic_slice_in_dim(
        jnp.sum(grad_modulation, axis=0), z * (wide // nb), wide // nb, axis=0
    )
    grad_cond_act = mm_nt(low_mod, modulate_weight)
    sig = jax.nn.sigmoid(conditions)
    grad_conditions = grad_cond_act * sig * (1.0 + conditions * (1.0 - sig))
    grad_condition = regroup([grad_conditions[k] for k in range(4)], place)
    onehot = (all_labels[:, None] == jnp.arange(class_count, dtype=jnp.int32)[None, :]).astype(F32)
    grad_table = lax.dot_general(
        onehot, grad_conditions, (((0,), (0,)), ((), ())), precision=highest,
        preferred_element_type=F32,
    )

    early_sum = jnp.sum(early, axis=0)
    late_sum = jnp.sum(late, axis=0)

    def part(vector, start, size):
        return lax.dynamic_slice_in_dim(vector, start + z * (size // nb), size // nb, axis=0)

    grad_out_b = part(early_sum, 4 * width, width)
    grad_down_b = part(early_sum, 5 * width, width)
    grad_gu_b = part(early_sum, 6 * width, 2 * hidden_width)
    grad_in_b = part(late_sum, 2 * width, 3 * width)
    grad_q_gain = part(late_sum, 5 * width, head)
    grad_k_gain = part(late_sum, 5 * width + head, head)
    return (
        output, grad_tokens, grad_condition, grad_table, grad_mod_w, grad_mod_b, grad_in_w,
        grad_in_b, grad_q_gain, grad_k_gain, grad_out_w, grad_out_b, grad_gu_w, grad_gu_b,
        grad_down_w, grad_down_b,
    )


def solution(mesh):
    grid = P("batch", "gy", "gx", None)
    by_batch = P("batch")
    rows = P("batch", None)
    placed = (grid, by_batch, by_batch) + (P(),) * 13 + (grid,)
    return jax.shard_map(
        functools.partial(body, mesh),
        mesh=mesh,
        in_specs=placed,
        out_specs=(
            grid, grid, rows, P(), rows, by_batch, rows, by_batch, by_batch, by_batch, rows,
            by_batch, rows, by_batch, rows, by_batch,
        ),
        check_vma=False,
    )
```

```python
import functools
import math

import jax
import jax.numpy as jnp
from jax import lax
from jax.experimental import pallas as pl
from jax.experimental.pallas import tpu as pltpu
from jax.sharding import PartitionSpec as P

NORM_EPSILON = 1e-06
AXES = ("batch", "gy", "gx")
BF16 = jnp.bfloat16
F32 = jnp.float32
VMEM_LIMIT = 60 * 1024 * 1024


def mm(left, right):
    return lax.dot_general(left, right, (((1,), (0,)), ((), ())), preferred_element_type=F32)


def mm_nt(left, right):
    return lax.dot_general(left, right, (((1,), (1,)), ((), ())), preferred_element_type=F32)


def mm_tn(left, right):
    return lax.dot_general(left, right, (((0,), (0,)), ((), ())), preferred_element_type=F32)


def params():
    return pltpu.CompilerParams(vmem_limit_bytes=VMEM_LIMIT)


def full(shape):
    return pl.BlockSpec(shape, lambda *_: (0,) * len(shape))


def col_sum(values):
    return jnp.sum(values, axis=0, keepdims=True)


def modulation_kernel(act_ref, weight_ref, bias_ref, out_ref):
    out_ref[...] = mm(act_ref[...], weight_ref[...]) + bias_ref[...].astype(F32)


def modulation_call(act, weight, bias):
    rows, width = act.shape
    wide = weight.shape[1]
    return pl.pallas_call(
        modulation_kernel,
        grid=(wide // width,),
        in_specs=[
            full((rows, width)),
            pl.BlockSpec((width, width), lambda j: (0, j)),
            pl.BlockSpec((1, width), lambda j: (0, j)),
        ],
        out_specs=pl.BlockSpec((rows, width), lambda j: (0, j)),
        out_shape=jax.ShapeDtypeStruct((rows, wide), F32),
        compiler_params=params(),
        name="modulation",
    )(act, weight, bias)


def head_sum(values, head):
    width = 256
    row = lax.broadcasted_iota(jnp.int32, (width, width), 0) // head
    col = lax.broadcasted_iota(jnp.int32, (width, width), 1) // head
    ones = jnp.where(row == col, 1.0, 0.0).astype(BF16)
    parts = [
        mm(values[:, i : i + width].astype(BF16), ones) for i in range(0, values.shape[1], width)
    ]
    return jnp.concatenate(parts, axis=1)


def turn(values, cosine, sine, head):
    quarter = head // 4
    lane = lax.broadcasted_iota(jnp.int32, (1, 128), 1)
    first = (lane % (2 * quarter)) < quarter
    parts = []
    for i in range(0, values.shape[1], 128):
        part = values[:, i : i + 128]
        partner = jnp.where(
            first, pltpu.roll(part, 128 - quarter, 1), pltpu.roll(part, quarter, 1)
        )
        parts.append(part * cosine + partner * sine)
    return jnp.concatenate(parts, axis=1)


def project_kernel(
    head, x_ref, mod_ref, weight_ref, bias_ref, qgain_ref, kgain_ref, cos_ref, sin_ref,
    hid_ref, q_ref, k_ref, v_ref, raw_ref,
):
    width = x_ref.shape[1]
    x = x_ref[...].astype(F32)
    normed = x * lax.rsqrt(jnp.mean(x * x, axis=-1, keepdims=True) + NORM_EPSILON)
    hidden = (normed * (1.0 + mod_ref[:, width : 2 * width]) + mod_ref[:, :width]).astype(BF16)
    hid_ref[...] = hidden
    for part, (out_ref, gain_ref) in enumerate(((q_ref, qgain_ref), (k_ref, kgain_ref))):
        raw = mm(hidden, weight_ref[:, part * width : (part + 1) * width])
        raw = raw + bias_ref[:, part * width : (part + 1) * width].astype(F32)
        raw_ref[:, part * width : (part + 1) * width] = raw.astype(BF16)
        factor = lax.rsqrt(head_sum(raw * raw, head) * (1.0 / head) + NORM_EPSILON)
        scaled = raw * factor * gain_ref[...]
        out_ref[...] = turn(scaled, cos_ref[...], sin_ref[...], head).astype(BF16)
    value = mm(hidden, weight_ref[:, 2 * width :]) + bias_ref[:, 2 * width :].astype(F32)
    v_ref[...] = value.astype(BF16)


def project_call(x, mod, weight, bias, qgain, kgain, cosine, sine, head):
    rows, width = x.shape
    block = rows // 2
    by_row = lambda wide: pl.BlockSpec((block, wide), lambda i: (i, 0))
    shape = jax.ShapeDtypeStruct((rows, width), BF16)
    return pl.pallas_call(
        functools.partial(project_kernel, head),
        grid=(2,),
        in_specs=[
            by_row(width),
            full(mod.shape),
            full(weight.shape),
            full(bias.shape),
            full(qgain.shape),
            full(kgain.shape),
            by_row(128),
            by_row(128),
        ],
        out_specs=[by_row(width)] * 4 + [by_row(2 * width)],
        out_shape=[shape] * 4 + [jax.ShapeDtypeStruct((rows, 2 * width), BF16)],
        compiler_params=params(),
        name="project",
    )(x, mod, weight, bias, qgain, kgain, cosine, sine)


def attend_kernel(scale, q_ref, k0_ref, k1_ref, v0_ref, v1_ref, mix_ref, e_ref, rl_ref):
    lane = lax.broadcasted_iota(jnp.int32, (1, 128), 1)
    q = q_ref[...]
    keys = jnp.concatenate([k0_ref[...], k1_ref[...]], axis=0)
    values = jnp.concatenate([v0_ref[...], v1_ref[...]], axis=0)
    values = jnp.concatenate([values, jnp.ones_like(values)], axis=1)
    outs = []
    for h in range(2):
        mine = (lane >= 64) if h else (lane < 64)
        scores = mm_nt(jnp.where(mine, q, jnp.zeros_like(q)), keys)
        grown = jnp.exp(scores * scale).astype(BF16)
        e_ref[h] = grown
        outs.append(mm(grown, values))
    inverse = 1.0 / jnp.where(lane < 64, outs[0][:, 128:], outs[1][:, 128:])
    mix_ref[...] = (jnp.where(lane < 64, outs[0][:, :128], outs[1][:, :128]) * inverse).astype(BF16)
    rl_ref[...] = inverse


def attend_call(q, k0, k1, v0, v1, head):
    rows, width = q.shape
    pair = pl.BlockSpec((rows, 128), lambda p: (0, p))
    return pl.pallas_call(
        functools.partial(attend_kernel, head**-0.5),
        grid=(width // 128,),
        in_specs=[pair] * 5,
        out_specs=[pair, pl.BlockSpec((2, rows, 2 * rows), lambda p: (p, 0, 0)), pair],
        out_shape=[
            jax.ShapeDtypeStruct((rows, width), BF16),
            jax.ShapeDtypeStruct((width // head, rows, 2 * rows), BF16),
            jax.ShapeDtypeStruct((rows, width), F32),
        ],
        compiler_params=params(),
        name="attend",
    )(q, k0, k1, v0, v1)


def attend_back_kernel(
    scale, q_ref, k0_ref, k1_ref, v0_ref, v1_ref, e_ref, gm_ref, mix_ref, rl_ref,
    dq_ref, dk0_ref, dk1_ref, dv0_ref, dv1_ref,
):
    rows = q_ref.shape[0]
    lane = lax.broadcasted_iota(jnp.int32, (1, 128), 1)
    keys = jnp.concatenate([k0_ref[...], k1_ref[...]], axis=0)
    values = jnp.concatenate([v0_ref[...], v1_ref[...]], axis=0)
    scaled = gm_ref[...].astype(F32) * rl_ref[...]
    products = scaled * mix_ref[...].astype(F32)
    scaled = scaled.astype(BF16)
    q_t = q_ref[...].T
    scaled_t = scaled.T
    dqs, dks, dvs = [], [], []
    for h in range(2):
        mine = (lane >= 64) if h else (lane < 64)
        inner = jnp.sum(jnp.where(mine, products, 0.0), axis=1, keepdims=True)
        grad_probs = mm_nt(jnp.where(mine, scaled, jnp.zeros_like(scaled)), values)
        grown = e_ref[h]
        grad_scores = (grown.astype(F32) * (grad_probs - inner) * scale).astype(BF16)
        dqs.append(mm(grad_scores, keys))
        dks.append(mm(q_t[64 * h : 64 * h + 64], grad_scores))
        dvs.append(mm(scaled_t[64 * h : 64 * h + 64], grown))
    dq_ref[...] = jnp.where(lane < 64, dqs[0], dqs[1]).astype(BF16)
    dk = jnp.concatenate(dks, axis=0).T.astype(BF16)
    dv = jnp.concatenate(dvs, axis=0).T.astype(BF16)
    dk0_ref[...] = dk[:rows]
    dk1_ref[...] = dk[rows:]
    dv0_ref[...] = dv[:rows]
    dv1_ref[...] = dv[rows:]


def attend_back_call(q, k0, k1, v0, v1, grown, grad_mixed, mixed, inverse, head):
    rows, width = q.shape
    pair = pl.BlockSpec((rows, 128), lambda p: (0, p))
    return pl.pallas_call(
        functools.partial(attend_back_kernel, head**-0.5),
        grid=(width // 128,),
        in_specs=[pair] * 5
        + [pl.BlockSpec((2, rows, 2 * rows), lambda p: (p, 0, 0))]
        + [pair] * 3,
        out_specs=[pair] * 5,
        out_shape=[jax.ShapeDtypeStruct((rows, width), BF16)] * 5,
        compiler_params=params(),
        name="attend_back",
    )(q, k0, k1, v0, v1, grown, grad_mixed, mixed, inverse)


def middle_kernel(
    mix_ref, x_ref, dy_ref, mod_ref, weight_ref, bias_ref, att_ref, mid_ref, h2_ref, h2t_ref, gf_ref
):
    width = x_ref.shape[1]
    attended = mm(mix_ref[...], weight_ref[...]) + bias_ref[...].astype(F32)
    middle = x_ref[...].astype(F32) + mod_ref[:, 2 * width : 3 * width] * attended
    normed = middle * lax.rsqrt(jnp.mean(middle * middle, axis=-1, keepdims=True) + NORM_EPSILON)
    hidden = normed * (1.0 + mod_ref[:, 4 * width : 5 * width]) + mod_ref[:, 3 * width : 4 * width]
    hidden = hidden.astype(BF16)
    att_ref[...] = attended.astype(BF16)
    mid_ref[...] = middle
    h2_ref[...] = hidden
    h2t_ref[...] = hidden.T
    gf_ref[...] = (mod_ref[:, 5 * width :] * dy_ref[...].astype(F32)).astype(BF16)


def middle_call(mixed, x, dy, mod, weight, bias, bias_at=0):
    rows, width = x.shape
    block = rows // 2
    by_row = pl.BlockSpec((block, width), lambda i: (i, 0))
    low = jax.ShapeDtypeStruct((rows, width), BF16)
    return pl.pallas_call(
        middle_kernel,
        grid=(2,),
        in_specs=[by_row] * 3
        + [full(mod.shape), full(weight.shape), pl.BlockSpec((1, width), lambda i: (0, bias_at))],
        out_specs=[by_row] * 3 + [pl.BlockSpec((width, block), lambda i: (0, i)), by_row],
        out_shape=[low, jax.ShapeDtypeStruct((rows, width), F32), low]
        + [jax.ShapeDtypeStruct((width, rows), BF16), low],
        compiler_params=params(),
        name="middle",
    )(mixed, x, dy, mod, weight, bias)


def feed_kernel(
    h2_ref, h2t_ref, gf_ref, wg_ref, wu_ref, bg_ref, bu_ref, wd_ref, feed_in_ref, gh_in_ref,
    feed_ref, gh_ref, dd_ref, dg_ref, db_ref,
):
    @pl.when(pl.program_id(0) == 0)
    def _():
        feed_ref[...] = feed_in_ref[...]
        gh_ref[...] = gh_in_ref[...]

    hidden = h2_ref[...]
    grad_feed = gf_ref[...]
    gate = mm(hidden, wg_ref[...]) + bg_ref[...].astype(F32)
    up = mm(hidden, wu_ref[...]) + bu_ref[...].astype(F32)
    grad_product = mm_nt(grad_feed, wd_ref[...])
    sig = 1.0 / (1.0 + jnp.exp(-gate))
    active = gate * sig
    product = (active * up).astype(BF16)
    grad_gate = (grad_product * up * sig * (1.0 + gate * (1.0 - sig))).astype(BF16)
    grad_up = (grad_product * active).astype(BF16)
    dd_ref[...] = mm_tn(product, grad_feed).astype(BF16)
    dg_ref[0] = mm(h2t_ref[...], grad_gate).astype(BF16)
    dg_ref[1] = mm(h2t_ref[...], grad_up).astype(BF16)
    db_ref[0] = col_sum(grad_gate.astype(F32))
    db_ref[1] = col_sum(grad_up.astype(F32))
    feed_ref[...] += mm(product, wd_ref[...])
    gh_ref[...] += mm_nt(grad_gate, wg_ref[...]) + mm_nt(grad_up, wu_ref[...])


def feed_call(hidden, hidden_t, grad_feed, weight, bias, down, feed, grad_hidden, first, step, unit):
    rows, width = hidden.shape
    blocks = down.shape[0] // unit
    steps = len(range(first, blocks, step))
    pick = lambda s: first + step * s
    acc = jax.ShapeDtypeStruct((rows, width), F32)
    return pl.pallas_call(
        feed_kernel,
        grid=(steps,),
        in_specs=[
            full((rows, width)),
            full((width, rows)),
            full((rows, width)),
            pl.BlockSpec((width, unit), lambda s: (0, pick(s))),
            pl.BlockSpec((width, unit), lambda s: (0, blocks + pick(s))),
            pl.BlockSpec((1, unit), lambda s: (0, pick(s))),
            pl.BlockSpec((1, unit), lambda s: (0, blocks + pick(s))),
            pl.BlockSpec((unit, width), lambda s: (pick(s), 0)),
            full((rows, width)),
            full((rows, width)),
        ],
        out_specs=[
            full((rows, width)),
            full((rows, width)),
            pl.BlockSpec((None, unit, width), lambda s: (s, 0, 0)),
            pl.BlockSpec((None, 2, width, unit), lambda s: (s, 0, 0, 0)),
            pl.BlockSpec((None, 2, 1, unit), lambda s: (s, 0, 0, 0)),
        ],
        out_shape=[
            acc,
            acc,
            jax.ShapeDtypeStruct((steps, unit, width), BF16),
            jax.ShapeDtypeStruct((steps, 2, width, unit), BF16),
            jax.ShapeDtypeStruct((steps, 2, 1, unit), F32),
        ],
        compiler_params=params(),
        name="feed",
    )(hidden, hidden_t, grad_feed, weight, weight, bias, bias, down, feed, grad_hidden)


def turn_kernel(
    feed_ref, gh_ref, mid_ref, att_ref, dy_ref, gf_ref, mix_ref, mod_ref, weight_ref, dbias_ref,
    out_ref, gmid_ref, gmix_ref, dw_ref, sums_ref,
):
    width = mid_ref.shape[1]
    half = width // 2
    dy = dy_ref[...].astype(F32)
    feed = feed_ref[...] + dbias_ref[...].astype(F32)
    middle = mid_ref[...]
    out_ref[...] = (middle + mod_ref[:, 5 * width :] * feed).astype(BF16)
    factor = lax.rsqrt(jnp.mean(middle * middle, axis=-1, keepdims=True) + NORM_EPSILON)
    normed = middle * factor
    grad_hidden = gh_ref[...]
    product = grad_hidden * normed
    grad_normed = grad_hidden * (1.0 + mod_ref[:, 4 * width : 5 * width])
    back = factor * (
        grad_normed - normed * jnp.mean(grad_normed * normed, axis=-1, keepdims=True)
    )
    grad_middle = dy + back
    gmid_ref[...] = grad_middle
    grad_attended = (mod_ref[:, 2 * width : 3 * width] * grad_middle).astype(BF16)
    sums_ref[0:1, :] = col_sum(grad_middle * att_ref[...].astype(F32))
    sums_ref[1:2, :] = col_sum(grad_hidden)
    sums_ref[2:3, :] = col_sum(product)
    sums_ref[3:4, :] = col_sum(dy * feed)
    sums_ref[4:5, :] = col_sum(grad_attended.astype(F32))
    sums_ref[5:6, :] = col_sum(gf_ref[...].astype(F32))
    sums_ref[6:8, :] = jnp.zeros((2, width), F32)
    gmix_ref[...] = mm_nt(grad_attended, weight_ref[...]).astype(BF16)
    mixed_t = mix_ref[...].T
    dw_ref[0] = mm(mixed_t, grad_attended[:, :half]).astype(BF16)
    dw_ref[1] = mm(mixed_t, grad_attended[:, half:]).astype(BF16)


def turn_call(feed, grad_hidden, middle, attended, dy, grad_feed, mixed, mod, weight, down_bias):
    rows, width = middle.shape
    low = jax.ShapeDtypeStruct((rows, width), BF16)
    return pl.pallas_call(
        turn_kernel,
        out_shape=[
            low,
            jax.ShapeDtypeStruct((rows, width), F32),
            low,
            jax.ShapeDtypeStruct((2, width, width // 2), BF16),
            jax.ShapeDtypeStruct((8, width), F32),
        ],
        compiler_params=params(),
        name="turn",
    )(feed, grad_hidden, middle, attended, dy, grad_feed, mixed, mod, weight, down_bias)


def project_back_kernel(
    head, dq_ref, dk0_ref, dk1_ref, dv0_ref, dv1_ref, raw_ref, hid_ref, x_ref, gmid_ref, mod_ref,
    weight_ref, qgain_ref, kgain_ref, cos_ref, sin_ref,
    gx_ref, dw_ref, sums_ref, bias_ref, proj_ref,
):
    width = x_ref.shape[1]
    cosine, sine = cos_ref[...], -sin_ref[...]
    for part in range(3):
        span = slice(part * width, (part + 1) * width)
        if part == 2:
            grad = dv0_ref[...].astype(F32) + dv1_ref[...].astype(F32)
        else:
            grad = dq_ref[...].astype(F32)
            if part == 1:
                grad = dk0_ref[...].astype(F32) + dk1_ref[...].astype(F32)
            gain = (qgain_ref, kgain_ref)[part][...]
            raw = raw_ref[:, span].astype(F32)
            factor = lax.rsqrt(head_sum(raw * raw, head) * (1.0 / head) + NORM_EPSILON)
            normed = raw * factor
            turned = turn(grad, cosine, sine, head)
            sums_ref[2 + part : 3 + part, :] = col_sum(turned * normed)
            turned = turned * gain
            mean = head_sum(turned * normed, head) * (1.0 / head)
            grad = factor * (turned - normed * mean)
        low = grad.astype(BF16)
        proj_ref[:, span] = low
        bias_ref[:, span] = col_sum(low.astype(F32))
    hidden_t = hid_ref[...].T
    half = 3 * width // 2
    dw_ref[0] = mm(hidden_t, proj_ref[:, :half]).astype(BF16)
    dw_ref[1] = mm(hidden_t, proj_ref[:, half:]).astype(BF16)
    grad_hidden = mm_nt(proj_ref[...], weight_ref[...])
    x = x_ref[...].astype(F32)
    factor = lax.rsqrt(jnp.mean(x * x, axis=-1, keepdims=True) + NORM_EPSILON)
    normed = x * factor
    sums_ref[0:1, :] = col_sum(grad_hidden)
    sums_ref[1:2, :] = col_sum(grad_hidden * normed)
    sums_ref[4:8, :] = jnp.zeros((4, width), F32)
    grad_normed = grad_hidden * (1.0 + mod_ref[:, width : 2 * width])
    back = factor * (
        grad_normed - normed * jnp.mean(grad_normed * normed, axis=-1, keepdims=True)
    )
    gx_ref[...] = (gmid_ref[...] + back).astype(BF16)


def project_back_call(
    dq, dk0, dk1, dv0, dv1, raw, hidden, x, grad_middle, mod, weight, qgain, kgain, cosine, sine, head
):
    rows, width = x.shape
    return pl.pallas_call(
        functools.partial(project_back_kernel, head),
        out_shape=[
            jax.ShapeDtypeStruct((rows, width), BF16),
            jax.ShapeDtypeStruct((2, width, 3 * width // 2), BF16),
            jax.ShapeDtypeStruct((8, width), F32),
            jax.ShapeDtypeStruct((1, 3 * width), F32),
        ],
        scratch_shapes=[pltpu.VMEM((rows, 3 * width), BF16)],
        compiler_params=params(),
        name="project_back",
    )(dq, dk0, dk1, dv0, dv1, raw, hidden, x, grad_middle, mod, weight, qgain, kgain, cosine, sine)


class Place:
    def __init__(self):
        self.z, self.gy, self.gx = (lax.axis_index(name) for name in AXES)
        self.core = lax.rem(self.gx, 2)
        self.side = self.gx // 2
        self.chip = 2 * self.gy + self.side

    def flipped(self, k):
        return 2 * lax.rem(self.gy + k // 2, 2) + lax.rem(self.side + lax.rem(k, 2), 2)

    def pair(self):
        return {"gx": self.gx + 1 - 2 * self.core}

    def plane(self, k):
        device = {}
        if k & 2:
            device["gy"] = 1 - self.gy
        if k & 1:
            device["gx"] = lax.rem(self.gx + 2, 4)
        return device

    def depth(self, d):
        return {"batch": self.flipped_z(d)}

    def flipped_z(self, d):
        return {1: self.z + 1 - 2 * lax.rem(self.z, 2), 2: lax.rem(self.z + 2, 4), 3: 3 - self.z}[d]


def meet(devices):
    barrier = pltpu.get_barrier_semaphore()
    for device in devices:
        pl.semaphore_signal(barrier, inc=1, device_id=device, device_id_type=pl.DeviceIdType.MESH)
    pl.semaphore_wait(barrier, len(devices))


def send(source, target, send_sem, recv_sem, device):
    return pltpu.make_async_remote_copy(
        src_ref=source, dst_ref=target, send_sem=send_sem, recv_sem=recv_sem, device_id=device,
        device_id_type=pl.DeviceIdType.MESH,
    )


def feed_order(step):
    owner = jnp.where(
        step < 2, 3, jnp.where((step == 2) | (step == 5), 2, jnp.where(step < 5, 1, 0))
    )
    return owner, lax.rem(step, 2)


def feed_block(step, i):
    step = jnp.minimum(step, 7)
    owner, half = feed_order(step)
    return (2 * half + i) * 4 + Place().flipped(owner)


def feed_turn_kernel(
    h2_ref, h2t_ref, gf_ref, wg0, wg1, wu0, wu1, bg0, bg1, bu0, bu1, wd0, wd1,
    mid_ref, att_ref, dy_ref, mix_ref, mod_ref, weight_ref, dbias_ref, known_ref,
    out_ref, gmid_ref, gmix_ref, dw_ref, sums_ref, total_ref, passed_ref,
    feed_ref, gh_ref, bias_ref, made, paired, near, pair_send, pair_recv, near_send, near_recv,
):
    place = Place()
    core = place.core
    step = pl.program_id(0)
    slot = lax.rem(step, 2)
    width = h2_ref.shape[1]
    unit = 128
    g_rows = width

    @pl.when(step == 0)
    def _():
        feed_ref[...] = jnp.zeros_like(feed_ref)
        sums_ref[1] = jnp.zeros((8, width), F32)
        gh_ref[...] = jnp.zeros_like(gh_ref)
        meet([place.pair(), place.plane(1), place.plane(2)])

    def pair_copy(of):
        return send(
            made.at[lax.rem(of, 2), 1 - core], paired.at[of], pair_send.at[lax.rem(of, 2)],
            pair_recv.at[of], place.pair(),
        )

    def near_copy(of, k):
        return send(paired.at[of], near.at[of], near_send.at[of], near_recv.at[of], place.plane(k))

    @pl.when(step >= 1)
    def _():
        pair_copy(step - 1).start()

    def join_pair(of):
        copy = pair_copy(of)
        copy.wait_recv()
        paired[of] = (made[1 - slot, core].astype(F32) + paired[of].astype(F32)).astype(BF16)

        @pl.when((of == 0) | (of == 2))
        def _():
            near_copy(of, 2).start()

        @pl.when((of == 1) | (of == 3))
        def _():
            near_copy(of, 1).start()

    @pl.when(step < 8)
    def _():
        owner, half = feed_order(step)
        hidden = h2_ref[...]
        grad_feed = gf_ref[...]
        wg = jnp.concatenate([wg0[...], wg1[...]], axis=1)
        wu = jnp.concatenate([wu0[...], wu1[...]], axis=1)
        wd = jnp.concatenate([wd0[...], wd1[...]], axis=0)
        gate = mm(hidden, wg) + jnp.concatenate([bg0[...], bg1[...]], axis=1).astype(F32)
        up = mm(hidden, wu) + jnp.concatenate([bu0[...], bu1[...]], axis=1).astype(F32)
        grad_product = mm_nt(grad_feed, wd)
        sig = 1.0 / (1.0 + jnp.exp(-gate))
        active = gate * sig
        product = (active * up).astype(BF16)
        grad_gate = (grad_product * up * sig * (1.0 + gate * (1.0 - sig))).astype(BF16)
        grad_up = (grad_product * active).astype(BF16)
        feed_ref[...] += mm(product, wd)
        gh_ref[...] += mm_nt(grad_gate, wg) + mm_nt(grad_up, wu)
        for e, grad in enumerate((grad_gate, grad_up)):
            total = col_sum(grad.astype(F32))
            for i in range(2):
                row = 16 * e + (2 * half + i) * 4 + place.flipped(owner)
                bias_ref[pl.ds(row, 1), :] = total[:, i * unit : (i + 1) * unit]

        @pl.when(step >= 1)
        def _():
            join_pair(step - 1)

        @pl.when(step >= 2)
        def _():
            pair_copy(step - 2).wait_send()

        for e, grad in enumerate((grad_gate, grad_up)):
            made[slot, e, :g_rows] = mm(h2t_ref[...], grad).astype(BF16)
        product_t = product.T
        for b in range(3):
            d = mm(product_t, grad_feed[:, 256 * b : 256 * b + 256]).astype(BF16)
            for i in range(2):
                for c in range(2):
                    made[slot, c, pl.ds(g_rows + b * 128 + i * 64, 64)] = d[
                        i * 128 + c * 64 : i * 128 + c * 64 + 64
                    ]

    @pl.when(step == 8)
    def _():
        join_pair(7)
        half = width // 2
        dy = dy_ref[...].astype(F32)
        feed = feed_ref[...] + dbias_ref[...].astype(F32)
        middle = mid_ref[...]
        out_ref[...] = (middle + mod_ref[:, 5 * width :] * feed).astype(BF16)
        factor = lax.rsqrt(jnp.mean(middle * middle, axis=-1, keepdims=True) + NORM_EPSILON)
        normed = middle * factor
        grad_hidden = gh_ref[...]
        product = grad_hidden * normed
        grad_normed = grad_hidden * (1.0 + mod_ref[:, 4 * width : 5 * width])
        back = factor * (
            grad_normed - normed * jnp.mean(grad_normed * normed, axis=-1, keepdims=True)
        )
        grad_middle = dy + back
        gmid_ref[...] = grad_middle
        grad_attended = (mod_ref[:, 2 * width : 3 * width] * grad_middle).astype(BF16)
        sums_ref[0, 0:1, :] = col_sum(grad_middle * att_ref[...].astype(F32))
        sums_ref[0, 1:2, :] = col_sum(grad_hidden)
        sums_ref[0, 2:3, :] = col_sum(product)
        sums_ref[0, 3:4, :] = col_sum(dy * feed)
        sums_ref[0, 4:5, :] = col_sum(grad_attended.astype(F32))
        sums_ref[0, 5:6, :] = col_sum(gf_ref[...].astype(F32))
        sums_ref[0, 6:8, :] = known_ref[...]
        for row in range(32):
            col = (row % 6) * unit
            sums_ref[1, row // 6 : row // 6 + 1, col : col + unit] = bias_ref[row : row + 1, :]
        gmix_ref[...] = mm_nt(grad_attended, weight_ref[...]).astype(BF16)
        mixed_t = mix_ref[...].T
        dw_ref[0] = mm(mixed_t, grad_attended[:, :half]).astype(BF16)
        dw_ref[1] = mm(mixed_t, grad_attended[:, half:]).astype(BF16)
        for of in (6, 7):
            pair_copy(of).wait_send()
        for of in range(4):
            near_copy(of, 1).wait()
        rows = width // 4
        for target, mine, there in ((total_ref, 6, 2), (passed_ref, 4, 0)):
            for f in range(2):

                def added(span, f=f, mine=mine, there=there):
                    both = paired[mine + f, span].astype(F32) + near[there + f, span].astype(F32)
                    return both.astype(BF16)

                for z in range(4):
                    target[z, f] = added(slice(z * rows, (z + 1) * rows))
                for i in range(2):
                    for b in range(3):
                        start = g_rows + b * 128 + i * 64
                        target[2 * f + i, 2, b * 64 : b * 64 + 64] = added(slice(start, start + 64))


def once(shape):
    return pl.BlockSpec(shape, lambda *_: (0,) * len(shape), pipeline_mode=pl.Buffered(1))


def feed_turn_call(
    hidden, hidden_t, grad_feed, gate_up, down, middle, attended, dy, mixed, mod, weight, small,
    known,
):
    rows, width = hidden.shape
    low = jax.ShapeDtypeStruct((rows, width), BF16)
    wide = jax.ShapeDtypeStruct((rows, width), F32)
    cols = lambda i, e: pl.BlockSpec((width, 128), lambda s: (0, 16 * e + feed_block(s, i)))
    first = GATE_BIAS * width // 128
    bias = lambda i, e: pl.BlockSpec((1, 128), lambda s: (0, first + 16 * e + feed_block(s, i)))
    down_bias = pl.BlockSpec((1, width), lambda s: (0, DOWN_BIAS), pipeline_mode=pl.Buffered(1))
    deep = lambda i: pl.BlockSpec((128, width), lambda s: (feed_block(s, i), 0))
    piece = (width + 384, 256)
    out_shape = [
        low, wide, low,
        jax.ShapeDtypeStruct((2, width, width // 2), BF16),
        jax.ShapeDtypeStruct((2, 8, width), F32),
        jax.ShapeDtypeStruct((4, 3, width // 4, 256), BF16),
        jax.ShapeDtypeStruct((4, 3, width // 4, 256), BF16),
    ]
    return pl.pallas_call(
        feed_turn_kernel,
        grid=(9,),
        in_specs=[once((rows, width)), once((width, rows)), once((rows, width))]
        + [cols(0, 0), cols(1, 0), cols(0, 1), cols(1, 1)]
        + [bias(0, 0), bias(1, 0), bias(0, 1), bias(1, 1)]
        + [deep(0), deep(1)]
        + [once((rows, width))] * 4
        + [once(mod.shape), once(weight.shape), down_bias, once(known.shape)],
        out_specs=[full(shape.shape) for shape in out_shape],
        out_shape=out_shape,
        scratch_shapes=[
            pltpu.VMEM((rows, width), F32),
            pltpu.VMEM((rows, width), F32),
            pltpu.VMEM((32, 128), F32),
            pltpu.VMEM((2, 2) + piece, BF16),
            pltpu.VMEM((8,) + piece, BF16),
            pltpu.VMEM((4,) + piece, BF16),
            pltpu.SemaphoreType.DMA((2,)),
            pltpu.SemaphoreType.DMA((8,)),
            pltpu.SemaphoreType.DMA((4,)),
            pltpu.SemaphoreType.DMA((4,)),
        ],
        compiler_params=pltpu.CompilerParams(
            vmem_limit_bytes=VMEM_LIMIT, collective_id=1, has_side_effects=True
        ),
        name="feed_turn",
    )(
        hidden, hidden_t, grad_feed, gate_up, gate_up, gate_up, gate_up, small, small, small,
        small, down, down, middle, attended, dy, mixed, mod, weight, small, known,
    )


def attend_tiles_kernel(
    scale, q_ref, k0_ref, k1_ref, v0_ref, v1_ref, grad_hbm, mix_ref, e_ref, rl_ref, dy_hbm,
    own_ref, own_sem, tok_send, tok_recv,
):
    place = Place()
    cells = own_ref.shape[0]
    step = pl.program_id(0)
    load = pltpu.make_async_copy(grad_hbm.at[place.chip], own_ref, own_sem.at[0])
    store = pltpu.make_async_copy(own_ref, dy_hbm.at[pl.ds(0, cells)], own_sem.at[1])

    def token_copy(k):
        return send(
            grad_hbm.at[place.flipped(k)], dy_hbm.at[pl.ds(k * cells, cells)], tok_send.at[k - 1],
            tok_recv.at[k - 1], place.plane(k),
        )

    @pl.when(step == 0)
    def _():
        load.start()
        meet([place.plane(k) for k in (1, 2, 3)])
        for k in (3, 1, 2):
            token_copy(k).start()

    attend_kernel(scale, q_ref, k0_ref, k1_ref, v0_ref, v1_ref, mix_ref, e_ref, rl_ref)

    @pl.when(step == 1)
    def _():
        load.wait()
        store.start()

    @pl.when(step == pl.num_programs(0) - 1)
    def _():
        store.wait()
        for k in (1, 2, 3):
            token_copy(k).wait()


def attend_tiles_call(q, k0, k1, v0, v1, grads, head):
    rows, width = q.shape
    pair = pl.BlockSpec((rows, 128), lambda p: (0, p))
    anywhere = pl.BlockSpec(memory_space=pl.ANY)
    return pl.pallas_call(
        functools.partial(attend_tiles_kernel, head**-0.5),
        grid=(width // 128,),
        in_specs=[pair] * 5 + [anywhere],
        out_specs=[pair, pl.BlockSpec((2, rows, 2 * rows), lambda p: (p, 0, 0)), pair, anywhere],
        out_shape=[
            jax.ShapeDtypeStruct((rows, width), BF16),
            jax.ShapeDtypeStruct((width // head, rows, 2 * rows), BF16),
            jax.ShapeDtypeStruct((rows, width), F32),
            jax.ShapeDtypeStruct((rows, width), BF16),
        ],
        scratch_shapes=[
            pltpu.VMEM((rows // 4, width), BF16), pltpu.SemaphoreType.DMA((2,)),
            pltpu.SemaphoreType.DMA((3,)), pltpu.SemaphoreType.DMA((3,)),
        ],
        compiler_params=pltpu.CompilerParams(
            vmem_limit_bytes=VMEM_LIMIT, collective_id=4, has_side_effects=True
        ),
        name="attend_tiles",
    )(q, k0, k1, v0, v1, grads)


Q_GAIN, K_GAIN, OUT_BIAS, DOWN_BIAS, GATE_BIAS = 0, 1, 2, 3, 4


def front_kernel(
    head, tile_cols, tok_hbm, time_ref, label_ref, modb_ref, inb_ref, qgain_ref,
    kgain_ref, outb_ref, downb_ref, gateb_ref, table_hbm, modw_hbm, inw_hbm,
    x_hbm, hid_hbm, q_hbm, k0_hbm, v0_hbm, k1_hbm, v1_hbm, raw_hbm, mod_ref, cos_ref,
    sin_ref, small_ref, known_ref,
    x_ref, hid_ref, q_ref, k_ref, v_ref, raw_ref, table_ref, modw_ref, inw_ref,
    load_sem, store_sem, tok_send, tok_recv, kv_send, kv_recv,
):
    place = Place()
    core, chip = place.core, place.chip
    rows, width = x_ref.shape
    cells = rows // 4
    loads = [
        pltpu.make_async_copy(source, target, load_sem.at[i])
        for i, (source, target) in enumerate(
            (
                (tok_hbm.at[chip], x_ref.at[pl.ds(0, cells)]), (modw_hbm, modw_ref),
                (inw_hbm, inw_ref), (table_hbm, table_ref),
            )
        )
    ]
    stores = [
        pltpu.make_async_copy(source, target, store_sem.at[i])
        for i, (source, target) in enumerate(
            (
                (x_ref, x_hbm), (hid_ref, hid_hbm), (k_ref, k0_hbm),
                (v_ref, v0_hbm), (q_ref, q_hbm), (raw_ref, raw_hbm),
            )
        )
    ]

    def token_copy(k):
        return send(
            tok_hbm.at[place.flipped(k)], x_ref.at[pl.ds(k * cells, cells)], tok_send.at[k - 1],
            tok_recv.at[k - 1], place.plane(k),
        )

    def kv_copy(which, chunk):
        source, target = ((k_ref, k1_hbm), (v_ref, v1_hbm))[which]
        span = pl.ds(chunk * cells, cells if chunk == 0 else rows - cells)
        return send(
            source.at[span], target.at[span], kv_send.at[which, chunk], kv_recv.at[which, chunk],
            place.pair(),
        )

    def line(ref):
        return ref[...].astype(F32)[None, :]

    in_bias = line(inb_ref)

    def project(start, size, chunk):
        span = slice(start, start + size)
        x = x_ref[span, :].astype(F32)
        normed = x * lax.rsqrt(jnp.mean(x * x, axis=-1, keepdims=True) + NORM_EPSILON)
        hidden = normed * (1.0 + mod_ref[:, width : 2 * width]) + mod_ref[:, :width]
        hidden = hidden.astype(BF16)
        hid_ref[span, :] = hidden
        for part in (1, 2, 0):
            raw = mm(hidden, inw_ref[:, part * width : (part + 1) * width])
            raw = raw + in_bias[:, part * width : (part + 1) * width]
            if part == 2:
                v_ref[span, :] = raw.astype(BF16)
                for which in (0, 1):
                    kv_copy(which, chunk).start()
                continue
            raw_ref[span, part * width : (part + 1) * width] = raw.astype(BF16)
            factor = lax.rsqrt(head_sum(raw * raw, head) * (1.0 / head) + NORM_EPSILON)
            scaled = raw * factor * small_ref[:, part * width : (part + 1) * width]
            turned = turn(scaled, cos_ref[span, :], sin_ref[span, :], head).astype(BF16)
            (q_ref, k_ref)[part][span, :] = turned

    for i in (0, 3, 1, 2):
        loads[i].start()
    meet([place.pair()] + [place.plane(k) for k in (1, 2, 3)])
    for k in (3, 1, 2):
        token_copy(k).start()

    for start, row in (
        (Q_GAIN, jnp.concatenate([line(qgain_ref)] * (width // head), axis=1)),
        (K_GAIN, jnp.concatenate([line(kgain_ref)] * (width // head), axis=1)),
        (OUT_BIAS, line(outb_ref)), (DOWN_BIAS, line(downb_ref)), (GATE_BIAS, line(gateb_ref)),
    ):
        small_ref[:, start * width : start * width + row.shape[1]] = row
    half = width // 2
    index = lax.broadcasted_iota(jnp.int32, (1, half), 1).astype(F32)
    phase = time_ref[chip].astype(F32) * jnp.exp(-math.log(10000.0) * index / half)
    features = jnp.concatenate([jnp.cos(phase), jnp.sin(phase)], axis=1)
    label = label_ref[chip]
    classes = lax.broadcasted_iota(jnp.int32, (16, table_ref.shape[0]), 1)
    loads[3].wait()
    chosen = mm(jnp.where(classes == label, 1.0, 0.0).astype(BF16), table_ref[...])
    condition = features + chosen[:1]
    known_ref[0:1, :] = jnp.where(core == 0, condition, 0.0)
    known_ref[1:2, :] = jnp.where(core == 0, jnp.zeros((1, width), F32) + label.astype(F32), 0.0)
    act = condition * (1.0 / (1.0 + jnp.exp(-condition)))
    act = jnp.broadcast_to(act, (16, width)).astype(BF16)

    quarter = head // 4
    lane = lax.broadcasted_iota(jnp.int32, (1, 128), 1)
    rate = jnp.exp(-math.log(10000.0) / quarter * lax.rem(lane, quarter).astype(F32))
    by_row = lax.rem(lane, head) < head // 2
    sign = jnp.where(lax.rem(lane, 2 * quarter) < quarter, -1.0, 1.0)
    cell = lax.broadcasted_iota(jnp.int32, (cells, 128), 0)
    row, col = cell // tile_cols, lax.rem(cell, tile_cols)
    for k in range(4):
        there = place.flipped(k)
        down = (there // 2) * (cells // tile_cols) + row
        across = (2 * lax.rem(there, 2) + core) * tile_cols + col
        angle = jnp.where(by_row, down, across).astype(F32) * rate
        cos_ref[k * cells : (k + 1) * cells, :] = jnp.cos(angle)
        sin_ref[k * cells : (k + 1) * cells, :] = sign * jnp.sin(angle)
    loads[1].wait()
    mod_ref[...] = mm(act, modw_ref[...])[:1] + line(modb_ref)
    loads[0].wait()
    loads[2].wait()
    project(0, cells, 0)
    for k in (1, 2, 3):
        token_copy(k).wait()
    stores[0].start()
    project(cells, rows - cells, 1)
    for store in stores[1:]:
        store.start()
    for which in (0, 1):
        for chunk in (0, 1):
            kv_copy(which, chunk).wait()
    for store in stores:
        store.wait()


def front_call(
    tokens, timesteps, labels, vectors, class_table, modw, inw, head, tile_cols
):
    images, cells, width = tokens.shape
    rows = images * cells
    low = lambda *shape: jax.ShapeDtypeStruct(shape, BF16)
    vmem = lambda *shape: pltpu.VMEM(shape, BF16)
    anywhere = pl.BlockSpec(memory_space=pl.ANY)
    inside = pl.BlockSpec(memory_space=pltpu.VMEM)
    sems = lambda *shape: pltpu.SemaphoreType.DMA(shape)
    return pl.pallas_call(
        functools.partial(front_kernel, head, tile_cols),
        in_specs=[anywhere]
        + [pl.BlockSpec(memory_space=pltpu.SMEM)] * 2
        + [inside] * len(vectors)
        + [anywhere] * 3,
        out_specs=[anywhere] * 8 + [inside] * 5,
        out_shape=[low(rows, width)] * 7
        + [
            low(rows, 2 * width), jax.ShapeDtypeStruct((1, 6 * width), F32),
            jax.ShapeDtypeStruct((rows, 128), F32), jax.ShapeDtypeStruct((rows, 128), F32),
            jax.ShapeDtypeStruct((1, GATE_BIAS * width + vectors[-1].shape[0]), F32),
            jax.ShapeDtypeStruct((2, width), F32),
        ],
        scratch_shapes=[
            vmem(rows, width), vmem(rows, width), vmem(rows, width), vmem(rows, width),
            vmem(rows, width), vmem(rows, 2 * width), vmem(*class_table.shape),
            vmem(*modw.shape), vmem(*inw.shape), sems(4), sems(6), sems(3), sems(3), sems(2, 2), sems(2, 2),
        ],
        compiler_params=pltpu.CompilerParams(
            vmem_limit_bytes=VMEM_LIMIT, collective_id=3, has_side_effects=True
        ),
        name="front",
    )(tokens, timesteps, labels, *vectors, class_table, modw, inw)


Z_FIRST = (False, False, False, True)
GROUPS = 4
TOKEN_STEP = 5
PASS_STEP = 4


def back_kernel(
    head, q_ref, k0_ref, k1_ref, v0_ref, v1_ref, gm_ref, mix_ref, rl_ref, e_ref,
    mod_ref, qgain_ref, kgain_ref, cos_ref, sin_ref, dout_ref, totals_ref, passed_ref, early_ref,
    raw_hbm, hid_hbm, x_hbm, gmid_hbm, weight_hbm, rows_hbm,
    output_ref, gtok_ref, feeds_hbm, projs_hbm, early_hbm, late_hbm,
    feeds_ref, projs_ref, early_all, late_all, raw_ref, hid_ref, x_ref, gmid_ref, weight_ref, hidt_ref, gh_ref, gx_ref, late_ref,
    dq_s, dk0_s, dv0_s, dk1_s, dv1_s, dk_in, dv_in,
    made, paired, first_out, first_in, second_out, second_in, landed, z_in, early_in, late_in,
    load_sem, own_sem, kv_send, kv_recv, pair_send, pair_recv, first_send, first_recv,
    second_send, second_recv, pass_send, pass_recv, z_send, z_recv, tok_send, tok_recv, feed_send, feed_recv,
    proj_send, proj_recv, small_send, small_recv,
):
    place = Place()
    core, chip, z = place.core, place.chip, place.z
    step = pl.program_id(0)
    rows, width = x_ref.shape
    cells = rows // 4
    scale = head**-0.5
    lane = lax.broadcasted_iota(jnp.int32, (1, 128), 1)

    loads = [
        pltpu.make_async_copy(source, target, load_sem.at[i])
        for i, (source, target) in enumerate(
            (
                (hid_hbm, hid_ref), (raw_hbm, raw_ref), (weight_hbm, weight_ref),
                (x_hbm, x_ref), (gmid_hbm, gmid_ref),
            )
        )
    ]

    stores = [
        pltpu.make_async_copy(source, target, load_sem.at[5 + i])
        for i, (source, target) in enumerate(
            (
                (early_all, early_hbm), (late_all, late_hbm), (feeds_ref, feeds_hbm),
                (projs_ref, projs_hbm),
            )
        )
    ]

    def pass_copy(f, i):
        part = (slice(None), f) if i == 0 else (pl.ds(2 * f, 2), 2)
        return send(
            passed_ref.at[part], landed.at[part], pass_send.at[f, i], pass_recv.at[f, i],
            place.plane(f + 1),
        )

    def z_copy(d):
        return send(
            landed.at[place.flipped_z(d)], z_in.at[d - 1], z_send.at[d - 1], z_recv.at[d - 1],
            place.depth(d),
        )

    def token_copy(which, k):
        source, target = ((rows_hbm, output_ref), (gx_ref, gtok_ref))[which]
        return send(
            source.at[pl.ds(k * cells, cells)], target.at[chip], tok_send.at[which, k - 1],
            tok_recv.at[which, k - 1], place.plane(k),
        )

    def own_tokens(which):
        source, target = ((rows_hbm, output_ref), (gx_ref, gtok_ref))[which]
        return pltpu.make_async_copy(source.at[pl.ds(0, cells)], target.at[chip], own_sem.at[which])

    def kv_copy(which, p):
        source, target = ((dk1_s, dk_in), (dv1_s, dv_in))[which]
        return send(
            source.at[p], target.at[p], kv_send.at[which, p], kv_recv.at[which, p], place.pair()
        )

    def pair_copy(g):
        source = dout_ref.at[1 - core] if g == 3 else made.at[g % 2, 1 - core]
        return send(source, paired.at[g], pair_send.at[g], pair_recv.at[g], place.pair())

    def first_copy(g, k):
        other = place.flipped_z(k) if Z_FIRST[g] else place.flipped(k)
        device = place.depth(k) if Z_FIRST[g] else place.plane(k)
        return send(
            first_out.at[g, other], first_in.at[g, k - 1], first_send.at[g, k - 1],
            first_recv.at[g, k - 1], device,
        )

    def second_copy(g, k):
        other = place.flipped(k) if Z_FIRST[g] else place.flipped_z(k)
        device = place.plane(k) if Z_FIRST[g] else place.depth(k)
        return send(
            second_out.at[g, other], second_in.at[g, k - 1], second_send.at[g, k - 1],
            second_recv.at[g, k - 1], device,
        )

    def gather_copy(which, k):
        full_ref, sends, recvs = gathers[which]
        here = full_ref.at[core, chip]
        return send(here, here, sends.at[k - 1], recvs.at[k - 1], place.plane(k))

    def pass_on(which, k):
        full_ref, sends, recvs = gathers[which]
        here = full_ref.at[core, place.flipped(k)]
        if which == 0:
            half = here.shape[1] // 2
            here = here.at[:, pl.ds((k - 1) * half, half)]
        else:
            half = here.shape[0] // 2
            here = here.at[pl.ds((k - 1) * half, half)]
        return send(here, here, sends.at[1 + k], recvs.at[1 + k], place.plane(3 - k))

    def gather_pair(which):
        full_ref, sends, recvs = gathers[which]
        here = full_ref.at[core]
        return send(here, here, sends.at[4], recvs.at[4], place.pair())

    gathers = ((feeds_ref, feed_send, feed_recv), (projs_ref, proj_send, proj_recv))
    smalls = ((early_ref, early_in, early_all, 8), (late_ref, late_in, late_all, 4))

    def small_pair(which):
        source, target, _, count = smalls[which]
        return send(
            source.at[1 - core], target, small_send.at[which, 0], small_recv.at[which, 0],
            place.pair(),
        )

    def small_plane(which, k):
        full_ref = smalls[which][2]
        return send(
            full_ref.at[core, pl.ds(0, 1)], full_ref.at[core, pl.ds(k, 1)],
            small_send.at[which, k], small_recv.at[which, k], place.plane(k),
        )

    def small_depth(which, d):
        full_ref = smalls[which][2]
        have = 4 * d
        return send(
            full_ref.at[core, pl.ds(0, have)], full_ref.at[core, pl.ds(have, have)],
            small_send.at[which, 3 + d], small_recv.at[which, 3 + d], place.depth(d),
        )

    def small_last(which):
        here = smalls[which][2].at[core]
        return send(
            here, here, small_send.at[which, 6], small_recv.at[which, 6], place.pair()
        )

    def small_begin(which):
        source, target, full_ref, _ = smalls[which]
        small_pair(which).wait_recv()
        full_ref[core, 0] = source[core] + target[...]
        for k in (1, 2, 3):
            small_plane(which, k).start()

    def small_next(which, i):
        if i == 0:
            for k in (1, 2, 3):
                small_plane(which, k).wait_recv()
            small_depth(which, 1).start()
        elif i == 1:
            small_depth(which, 1).wait_recv()
            small_depth(which, 2).start()
        else:
            small_depth(which, 2).wait_recv()
            small_last(which).start()

    def start_group(g):
        pair_copy(g).wait_recv()
        mine = dout_ref.at[core] if g == 3 else made.at[g % 2, core]
        part = width // 16
        for a in range(4):
            for b in range(4):
                span = pl.ds((a * 4 + b) * part, part)
                total = (mine[span, :].astype(F32) + paired[g, span].astype(F32)).astype(BF16)
                if Z_FIRST[g]:
                    first_out[g, a, b] = total
                else:
                    first_out[g, b, a] = total
        for k in (1, 2, 3):
            first_copy(g, k).start()

    def go_on(g):
        for k in (1, 2, 3):
            first_copy(g, k).wait_recv()
        here = z if Z_FIRST[g] else chip
        second_out[g] = (
            first_out[g, here].astype(F32)
            + first_in[g, 0].astype(F32)
            + first_in[g, 1].astype(F32)
            + first_in[g, 2].astype(F32)
        ).astype(BF16)
        for k in (1, 2, 3):
            second_copy(g, k).start()

    def finish(g):
        for k in (1, 2, 3):
            second_copy(g, k).wait_recv()
        here = chip if Z_FIRST[g] else z
        projs_ref[core, chip, g] = (
            second_out[g, here].astype(F32)
            + second_in[g, 0].astype(F32)
            + second_in[g, 1].astype(F32)
            + second_in[g, 2].astype(F32)
        ).astype(BF16)

    @pl.when(step == 0)
    def _():
        for load in loads:
            load.start()
        meet(
            [place.pair()]
            + [place.plane(k) for k in (1, 2, 3)]
            + [place.depth(d) for d in (1, 2, 3)]
        )
        for f in (0, 1):
            for i in (0, 1):
                pass_copy(f, i).start()
        pair_copy(3).start()
        small_pair(0).start()
        gh_ref[...] = jnp.zeros_like(gh_ref)

    @pl.when(step >= 1)
    def _():
        for which in (0, 1):
            kv_copy(which, step - 1).start()

    @pl.when(step == 3)
    def _():
        pair_copy(0).start()

    @pl.when(step == 5)
    def _():
        pair_copy(1).start()

    @pl.when(step < 6)
    def _():
        keys = jnp.concatenate([k0_ref[...], k1_ref[...]], axis=0)
        values = jnp.concatenate([v0_ref[...], v1_ref[...]], axis=0)
        scaled = gm_ref[...].astype(F32) * rl_ref[...]
        products = scaled * mix_ref[...].astype(F32)
        scaled = scaled.astype(BF16)
        q_t = q_ref[...].T
        scaled_t = scaled.T
        dqs, dks, dvs = [], [], []
        for h in range(2):
            mine = (lane >= 64) if h else (lane < 64)
            inner = jnp.sum(jnp.where(mine, products, 0.0), axis=1, keepdims=True)
            grad_probs = mm_nt(jnp.where(mine, scaled, jnp.zeros_like(scaled)), values)
            grown = e_ref[h]
            grad_scores = (grown.astype(F32) * (grad_probs - inner) * scale).astype(BF16)
            dqs.append(mm(grad_scores, keys))
            dks.append(mm(q_t[64 * h : 64 * h + 64], grad_scores))
            dvs.append(mm(scaled_t[64 * h : 64 * h + 64], grown))
        dq_s[step] = jnp.where(lane < 64, dqs[0], dqs[1]).astype(BF16)
        dk = jnp.concatenate(dks, axis=0).T.astype(BF16)
        dv = jnp.concatenate(dvs, axis=0).T.astype(BF16)
        dk0_s[step] = dk[:rows]
        dk1_s[step] = dk[rows:]
        dv0_s[step] = dv[:rows]
        dv1_s[step] = dv[rows:]

    @pl.when(step == 0)
    def _():
        loads[0].wait()
        hidt_ref[...] = hid_ref[...].T

    @pl.when(step == 1)
    def _():
        loads[1].wait()
        loads[2].wait()
        start_group(3)
        small_begin(0)

    for i in range(3):

        @pl.when(step == 3 + i)
        def _(i=i):
            small_next(0, i)

    @pl.when(step == 3)
    def _():
        start_group(0)

    @pl.when(step == 5)
    def _():
        start_group(1)
        go_on(3)

    @pl.when(step == TOKEN_STEP)
    def _():
        for k in (1, 2, 3):
            token_copy(0, k).start()
        own_tokens(0).start()

    @pl.when(step == PASS_STEP)
    def _():
        for f in (0, 1):
            for i in (0, 1):
                pass_copy(f, i).wait_recv()
        landed[...] = (landed[...].astype(F32) + totals_ref[...].astype(F32)).astype(BF16)
        for d in (1, 2, 3):
            z_copy(d).start()

    @pl.when((step >= 2) & (lax.rem(step, 2) == 0))
    def _():
        g = (step - 2) // 2
        slot = lax.rem(g, 2)
        cosine, sine = cos_ref[...], -sin_ref[...]
        for i in range(2):
            for which in (0, 1):
                kv_copy(which, 2 * g + i).wait_recv()

        def both(ref):
            return jnp.concatenate([ref[2 * g], ref[2 * g + 1]], axis=1).astype(F32)

        lows = []
        for part in range(3):
            span = pl.ds(pl.multiple_of(part * width + g * 256, 256), 256)
            if part == 2:
                grad = both(dv0_s) + both(dv_in)
            else:
                grad = both(dq_s) if part == 0 else both(dk0_s) + both(dk_in)
                gain = (qgain_ref, kgain_ref)[part][:, :256].astype(F32)
                raw = raw_ref[:, span].astype(F32)
                factor = lax.rsqrt(head_sum(raw * raw, head) * (1.0 / head) + NORM_EPSILON)
                normed = raw * factor
                turned = turn(grad, cosine, sine, head)
                late_ref[1, part : part + 1, pl.ds(pl.multiple_of(g * 256, 256), 256)] = col_sum(
                    turned * normed
                )
                turned = turned * gain
                mean = head_sum(turned * normed, head) * (1.0 / head)
                grad = factor * (turned - normed * mean)
            low = grad.astype(BF16)
            lows.append(low)
            total = col_sum(low.astype(F32))
            where = pl.ds(pl.multiple_of(g * 256, 256), 256)
            if part < 2:
                late_ref[0, 2 + part : 3 + part, where] = total
            else:
                late_ref[1, 2:3, where] = total
            gh_ref[...] += mm_nt(low, weight_ref[:, span])
        grads = jnp.concatenate(
            [low[:, 128 * c : 128 * c + 128] for c in range(2) for low in lows], axis=1
        )

        @pl.when(step == 6)
        def _():
            pair_copy(0).wait_send()

        half = width // 2
        made[slot, 0] = mm(hidt_ref[...], grads[:, :half]).astype(BF16)
        made[slot, 1] = mm(hidt_ref[...], grads[:, half:]).astype(BF16)

    @pl.when(step == 6)
    def _():
        pair_copy(2).start()
        grad_hidden = gh_ref[...]
        loads[3].wait()
        loads[4].wait()
        x = x_ref[...].astype(F32)
        factor = lax.rsqrt(jnp.mean(x * x, axis=-1, keepdims=True) + NORM_EPSILON)
        normed = x * factor
        late_ref[0, 0:1, :] = col_sum(grad_hidden)
        late_ref[0, 1:2, :] = col_sum(grad_hidden * normed)
        late_ref[1, 3:4, :] = jnp.zeros((1, width), F32)
        small_pair(1).start()
        small_begin(1)
        start_group(2)
        go_on(0)
        go_on(1)
        grad_normed = grad_hidden * (1.0 + mod_ref[:, width : 2 * width])
        back = factor * (
            grad_normed - normed * jnp.mean(grad_normed * normed, axis=-1, keepdims=True)
        )
        gx_ref[...] = (gmid_ref[...] + back).astype(BF16)
        for k in (1, 2, 3):
            token_copy(1, k).start()
        own_tokens(1).start()
        for d in (1, 2, 3):
            z_copy(d).wait_recv()
        for i in range(3):
            feeds_ref[core, chip, i] = (
                landed[z, i].astype(F32)
                + z_in[0, i].astype(F32)
                + z_in[1, i].astype(F32)
                + z_in[2, i].astype(F32)
            ).astype(BF16)
        for k in (1, 2):
            gather_copy(0, k).start()
        finish(3)
        finish(0)
        finish(1)
        go_on(2)
        small_next(1, 0)
        finish(2)
        for k in (1, 2):
            gather_copy(1, k).start()
        small_next(1, 1)
        for k in (1, 2):
            gather_copy(0, k).wait_recv()
            pass_on(0, k).start()
        small_next(1, 2)
        for k in (1, 2):
            gather_copy(1, k).wait_recv()
            pass_on(1, k).start()
        for which in (0, 1):
            for k in (1, 2):
                gather_copy(which, k).wait_send()
                pass_on(which, k).wait()
            gather_pair(which).start()
        for which in (0, 1):
            own_tokens(which).wait()
            for k in (1, 2, 3):
                token_copy(which, k).wait()
            small_pair(which).wait_send()
            for k in (1, 2, 3):
                small_plane(which, k).wait_send()
            for d in (1, 2):
                small_depth(which, d).wait_send()
            small_last(which).wait()
            stores[which].start()
            for p in range(6):
                kv_copy(which, p).wait_send()
        for f in (0, 1):
            for i in (0, 1):
                pass_copy(f, i).wait_send()
        for k in (1, 2, 3):
            z_copy(k).wait_send()
            for g in range(4):
                first_copy(g, k).wait_send()
                second_copy(g, k).wait_send()
        for g in (1, 2, 3):
            pair_copy(g).wait_send()
        for which in (0, 1):
            gather_pair(which).wait()
            stores[2 + which].start()
        for store in stores:
            store.wait()


def back_call(
    q, k0, k1, v0, v1, grad_mixed, mixed, inverse, grown, mod, small_vectors, cosine, sine, d_out,
    totals, passed, early, raw, hidden, x, grad_middle, weight, output_rows, head,
):
    rows, width = q.shape
    half, part = width // 2, width // 16
    low = lambda *shape: jax.ShapeDtypeStruct(shape, BF16)
    pair = pl.BlockSpec((rows, 128), lambda s: (0, jnp.minimum(s, 5)))
    anywhere = pl.BlockSpec(memory_space=pl.ANY)
    small = [mod, small_vectors, small_vectors, cosine, sine, d_out, totals, passed, early]
    gain = lambda at: pl.BlockSpec((1, width), lambda s: (0, at), pipeline_mode=pl.Buffered(1))
    out_shape = [
        low(4, rows // 4, width), low(4, rows // 4, width),
        low(2, 4, 3, width // 4, 256), low(2, 4, GROUPS, part, half),
        jax.ShapeDtypeStruct((2, 16, 8, width), F32), jax.ShapeDtypeStruct((2, 16, 4, width), F32),
    ]
    vmem = lambda *shape: pltpu.VMEM(shape, BF16)
    sems = lambda *shape: pltpu.SemaphoreType.DMA(shape)
    return pl.pallas_call(
        functools.partial(back_kernel, head),
        grid=(7,),
        in_specs=[pair] * 8
        + [pl.BlockSpec((2, rows, 2 * rows), lambda s: (jnp.minimum(s, 5), 0, 0))]
        + [once(mod.shape), gain(Q_GAIN), gain(K_GAIN)]
        + [once(each.shape) for each in small[3:]]
        + [anywhere] * 6,
        out_specs=[anywhere] * 6,
        out_shape=out_shape,
        scratch_shapes=[pltpu.VMEM(shape.shape, shape.dtype) for shape in out_shape[2:]]
        + [
            vmem(rows, 2 * width), vmem(rows, width), vmem(rows, width),
            pltpu.VMEM((rows, width), F32), vmem(width, 3 * width), vmem(width, rows),
            pltpu.VMEM((rows, width), F32), vmem(rows, width), pltpu.VMEM((2, 4, width), F32),
        ]
        + [vmem(6, rows, 128)] * 7
        + [
            vmem(2, 2, width, half), vmem(GROUPS, width, half),
            vmem(GROUPS, 4, 4, part, half), vmem(GROUPS, 3, 4, part, half),
            vmem(GROUPS, 4, part, half), vmem(GROUPS, 3, part, half),
            vmem(*totals.shape), vmem(3, 3, width // 4, 256),
            pltpu.VMEM((8, width), F32), pltpu.VMEM((4, width), F32),
            sems(9), sems(2), sems(2, 6), sems(2, 6), sems(GROUPS), sems(GROUPS),
            sems(GROUPS, 3), sems(GROUPS, 3), sems(GROUPS, 3), sems(GROUPS, 3),
            sems(2, 2), sems(2, 2), sems(3), sems(3), sems(2, 3), sems(2, 3), sems(5), sems(5),
            sems(5), sems(5),
            sems(2, 7), sems(2, 7),
        ],
        compiler_params=pltpu.CompilerParams(
            vmem_limit_bytes=VMEM_LIMIT, collective_id=2, has_side_effects=True
        ),
        name="back",
    )(
        q, k0, k1, v0, v1, grad_mixed, mixed, inverse, grown, *small, raw, hidden, x, grad_middle,
        weight, output_rows,
    )


def finish_kernel(
    head, feeds_ref, projs_ref, early_ref, late_ref, modw_hbm,
    cond_ref, table_hbm, gmodw_hbm, gmodb_ref, ginw_hbm, ginb_ref, gqg_ref, gkg_ref, goutw_hbm,
    goutb_ref, gguw_hbm, ggub_ref, gdownw_hbm, gdownb_ref,
    modw_ref, table_ref, gmodw_ref, ginw_ref, goutw_ref, gguw_ref, gdownw_ref, acts_ref, load_sem,
    store_sem,
):
    place = Place()
    width = early_ref.shape[3]
    part = projs_ref.shape[3]
    load = pltpu.make_async_copy(modw_hbm, modw_ref, load_sem)
    load.start()
    stores = [
        pltpu.make_async_copy(source, target, store_sem.at[i])
        for i, (source, target) in enumerate(
            (
                (gguw_ref, gguw_hbm), (gdownw_ref, gdownw_hbm), (ginw_ref, ginw_hbm),
                (goutw_ref, goutw_hbm), (gmodw_ref, gmodw_hbm), (table_ref, table_hbm),
            )
        )
    ]
    for c in range(2):
        for chip in range(4):
            for f in range(2):
                for i in range(2):
                    col = (((c * 2 + f) * 2 + i) * 4 + chip) * 128
                    gguw_ref[:, col : col + 128] = feeds_ref[
                        c, chip, f, :, i * 128 : (i + 1) * 128
                    ].astype(F32)
    stores[0].start()
    for c in range(2):
        for chip in range(4):
            row = chip * 128 + c * 64
            for b in range(3):
                gdownw_ref[row : row + 64, b * 256 : (b + 1) * 256] = feeds_ref[
                    c, chip, 2, b * 64 : (b + 1) * 64, :
                ].astype(F32)
    stores[1].start()
    for c in range(2):
        for chip in range(4):
            row = chip * part
            for g in range(3):
                for q in range(3):
                    col = q * width + g * 256 + c * 128
                    ginw_ref[row : row + part, col : col + 128] = projs_ref[
                        c, chip, g, :, q * 128 : (q + 1) * 128
                    ].astype(F32)
            half = width // 2
            goutw_ref[row : row + part, c * half : (c + 1) * half] = projs_ref[c, chip, 3].astype(F32)
    stores[2].start()
    stores[3].start()

    vectors = [late_ref[0, :, 0, :], late_ref[0, :, 1, :]]
    vectors += [early_ref[0, :, j, :] for j in range(4)]
    lows = [vector.astype(BF16) for vector in vectors]
    conditions = early_ref[0, :, 6, :]
    labels = early_ref[0, :, 7, :]
    sig = 1.0 / (1.0 + jnp.exp(-conditions))
    acts = (conditions * sig).astype(BF16)
    size = acts_ref.shape[1]
    for z in range(4):

        @pl.when(place.z == z)
        def _(z=z):
            acts_ref[...] = acts[:, z * size : (z + 1) * size]

    mine = acts_ref[...]
    for j, low in enumerate(lows):
        gmodw_ref[:, j * width : (j + 1) * width] = mm_tn(mine, low)
    stores[4].start()
    early_sum = jnp.sum(early_ref[0], axis=0)
    gate_sum = jnp.sum(early_ref[1], axis=0)
    late_sum = jnp.sum(late_ref[0], axis=0)
    gain_sum = jnp.sum(late_ref[1], axis=0)
    mod_b = jnp.concatenate(
        [late_sum[0:1], late_sum[1:2]] + [early_sum[j : j + 1] for j in range(4)], axis=1
    )
    in_b = jnp.concatenate([late_sum[2:3], late_sum[3:4], gain_sum[2:3]], axis=1)
    gate_b = jnp.concatenate(
        [gate_sum[n // 6 : n // 6 + 1, (n % 6) * 128 : (n % 6) * 128 + 128] for n in range(32)],
        axis=1,
    )
    gains = sum(gain_sum[0:2, i : i + 128] for i in range(0, width, 128))
    gains = gains[:, :head] + gains[:, head:]
    pieces = (
        (gmodb_ref, mod_b), (ginb_ref, in_b), (gqg_ref, gains[0:1]), (gkg_ref, gains[1:2]),
        (goutb_ref, early_sum[4:5]), (ggub_ref, gate_b), (gdownb_ref, early_sum[5:6]),
    )
    for z in range(4):

        @pl.when(place.z == z)
        def _(z=z):
            for ref, row in pieces:
                size = row.shape[1] // 4
                ref[...] = row[0, z * size : (z + 1) * size]

    load.wait()
    grad = sum(mm_nt(modw_ref[:, j * width : (j + 1) * width], low) for j, low in enumerate(lows)).T
    grad = grad * sig * (1.0 + conditions * (1.0 - sig))
    for k in range(4):
        cond_ref[pl.ds(place.flipped(k), 1), :] = grad[k : k + 1]
    classes = table_ref.shape[0]
    wide = -(-classes // 128) * 128
    column = lax.broadcasted_iota(jnp.int32, (1, wide), 1).astype(F32)
    onehot = jnp.where(labels[:, 0:1] == column, 1.0, 0.0).astype(BF16)
    high = grad.astype(BF16)
    rest = grad - high.astype(F32)
    middle = rest.astype(BF16)
    last = (rest - middle.astype(F32)).astype(BF16)
    table = mm_tn(
        jnp.concatenate([onehot] * 3, axis=0), jnp.concatenate([high, middle, last], axis=0)
    )
    table_ref[...] = table[:classes]
    stores[5].start()
    for store in stores:
        store.wait()


def finish_call(feeds, projs, early, late, weight, head, classes, hidden_width):
    width = weight.shape[0]
    rows = width // 4
    whole = lambda *shape: jax.ShapeDtypeStruct(shape, F32)
    anywhere = pl.BlockSpec(memory_space=pl.ANY)
    out_shape = [
        whole(4, width), whole(classes, width), whole(rows, 6 * width), whole(6 * width // 4),
        whole(rows, 3 * width), whole(3 * width // 4), whole(head // 4), whole(head // 4),
        whole(rows, width), whole(rows), whole(rows, 2 * hidden_width),
        whole(2 * hidden_width // 4), whole(hidden_width // 4, width), whole(rows),
    ]
    big = (1, 2, 4, 8, 10, 12)
    return pl.pallas_call(
        functools.partial(finish_kernel, head),
        in_specs=[pl.BlockSpec(memory_space=pltpu.VMEM)] * 4 + [anywhere],
        out_specs=[
            anywhere if i in big else pl.BlockSpec(memory_space=pltpu.VMEM)
            for i in range(len(out_shape))
        ],
        out_shape=out_shape,
        scratch_shapes=[pltpu.VMEM(weight.shape, BF16)]
        + [pltpu.VMEM(out_shape[i].shape, F32) for i in big]
        + [pltpu.VMEM((16, rows), BF16), pltpu.SemaphoreType.DMA, pltpu.SemaphoreType.DMA((6,))],
        compiler_params=params(),
        name="finish",
    )(feeds, projs, early, late, weight)


def take(array_in, index, axis=0):
    return lax.dynamic_index_in_dim(array_in, index, axis, keepdims=False)


def add(*terms):
    return sum(term.astype(F32) for term in terms)


class Moves:
    def __init__(self, mesh):
        self.sizes = tuple(mesh.shape[name] for name in AXES)

    def flip(self, value, batch=0, gy=0, gx=0):
        nb, ny, nx = self.sizes
        pairs = []
        for b in range(nb):
            for y in range(ny):
                for x in range(nx):
                    here = (b * ny + y) * nx + x
                    there = ((b ^ batch) * ny + (y ^ gy)) * nx + (x ^ gx)
                    pairs.append((here, there))
        return lax.ppermute(value, AXES, pairs)

    def plane(self, value, k):
        return self.flip(value, gy=k >> 1, gx=2 * (k & 1))

    def pair(self, value):
        return self.flip(value, gx=1)

    def gather(self, value):
        value = value[None]
        value = jnp.concatenate([value, self.plane(value, 1)], axis=0)
        value = jnp.concatenate([value, self.plane(value, 2)], axis=0)
        bit = 1
        while bit < self.sizes[0]:
            value = jnp.concatenate([value, self.flip(value, batch=bit)], axis=0)
            bit *= 2
        return value


def regroup(parts, place):
    stacked = jnp.stack(parts)
    return jnp.stack([take(stacked, place ^ k) for k in range(len(parts))])


def body(mesh, *operands):
    (
        tokens, timesteps, labels, class_table, modulate_weight, modulate_bias, inproj_weight,
        inproj_bias, query_gain, key_gain, outproj_weight, outproj_bias, gate_up_weight,
        gate_up_bias, down_weight, down_bias, cotangent,
    ) = operands
    image_count, tile_rows, tile_cols, width = tokens.shape
    cells = tile_rows * tile_cols
    rows = image_count * cells
    head = query_gain.shape[0]
    heads = width // head
    hidden_width = down_weight.shape[0]
    class_count = class_table.shape[0]
    highest = lax.Precision.HIGHEST
    moves = Moves(mesh)
    nb, ny, nx = moves.sizes
    assert ny == 2 and nx == 4 and image_count == 4
    z, gy, gx = (lax.axis_index(name) for name in AXES)
    side, core = gx // 2, gx % 2
    place = 2 * gy + side

    tiles = tokens.reshape(image_count, cells, width)
    grads = cotangent.reshape(image_count, cells, width)

    if nb == 4 and hidden_width == 16 * 128:
        vectors = (
            modulate_bias, inproj_bias, query_gain, key_gain, outproj_bias, down_bias, gate_up_bias
        )
        x, hidden_one, q, k0, v0, k1, v1, raw, mod, cosine, sine, small, known = front_call(
            tiles, timesteps, labels, vectors, class_table, modulate_weight, inproj_weight, head,
            tile_cols,
        )
        mixed, grown, inverse, dy = attend_tiles_call(q, k0, k1, v0, v1, grads, head)
        attended, middle, hidden_two, hidden_two_t, grad_feed = middle_call(
            mixed, x, dy, mod, outproj_weight, small, OUT_BIAS
        )
        output_rows, grad_middle, grad_mixed, d_out, sums_two, totals, passed = feed_turn_call(
            hidden_two, hidden_two_t, grad_feed, gate_up_weight, down_weight, middle, attended, dy,
            mixed, mod, outproj_weight, small, known,
        )
        output, grad_tokens, feeds, projs, early, late = back_call(
            q, k0, k1, v0, v1, grad_mixed, mixed, inverse, grown, mod, small, cosine, sine, d_out,
            totals, passed, sums_two, raw, hidden_one, x, grad_middle, inproj_weight, output_rows, head,
        )
        (
            grad_condition, grad_table, grad_mod_w, grad_mod_b, grad_in_w, grad_in_b, grad_q_gain,
            grad_k_gain, grad_out_w, grad_out_b, grad_gu_w, grad_gu_b, grad_down_w, grad_down_b,
        ) = finish_call(
            feeds, projs, early, late, modulate_weight, head, class_count, hidden_width
        )
        return (
            output.reshape(tokens.shape), grad_tokens.reshape(tokens.shape), grad_condition,
            grad_table, grad_mod_w, grad_mod_b, grad_in_w, grad_in_b, grad_q_gain, grad_k_gain,
            grad_out_w, grad_out_b, grad_gu_w, grad_gu_b, grad_down_w, grad_down_b,
        )

    def exchange(blocks):
        return [take(blocks, place)] + [
            moves.plane(take(blocks, place ^ k), k) for k in range(1, 4)
        ]

    x = jnp.concatenate(exchange(tiles), axis=0)

    half_width = width // 2
    step = take(timesteps, place).astype(F32)
    label = take(labels, place)
    rates = jnp.exp(-math.log(10000.0) * jnp.arange(half_width, dtype=F32) / half_width)
    features = jnp.concatenate([jnp.cos(step * rates), jnp.sin(step * rates)])
    condition = features + take(class_table, label).astype(F32)
    cond_act = jax.nn.silu(condition).astype(BF16)
    mod = modulation_call(
        jnp.broadcast_to(cond_act[None], (16, width)), modulate_weight, modulate_bias[None]
    )[:1]

    quarter = head // 4
    cell = jnp.arange(cells, dtype=jnp.int32)
    row_places, col_places = [], []
    for k in range(4):
        there = place ^ k
        row_places.append((there // 2) * tile_rows + cell // tile_cols)
        col_places.append((2 * (there % 2) + core) * tile_cols + cell % tile_cols)
    row_places = jnp.concatenate(row_places).astype(F32)[:, None]
    col_places = jnp.concatenate(col_places).astype(F32)[:, None]
    lane = jnp.arange(128, dtype=jnp.int32)
    turn_rate = jnp.exp(-math.log(10000.0) * (lane % quarter).astype(F32) / quarter)[None]
    angles = jnp.where((lane % head)[None] < head // 2, row_places, col_places) * turn_rate
    cosine = jnp.cos(angles)
    sine = jnp.where((lane % (2 * quarter))[None] < quarter, -1.0, 1.0) * jnp.sin(angles)
    qgain = jnp.tile(query_gain.astype(F32), heads)[None]
    kgain = jnp.tile(key_gain.astype(F32), heads)[None]

    hidden_one, q, k0, v0, raw = project_call(
        x, mod, inproj_weight, inproj_bias[None], qgain, kgain, cosine, sine, head
    )
    k1, v1 = moves.pair(k0), moves.pair(v0)
    dy = jnp.concatenate(exchange(grads), axis=0)
    mixed, grown, inverse = attend_call(q, k0, k1, v0, v1, head)
    attended, middle, hidden_two, hidden_two_t, grad_feed = middle_call(
        mixed, x, dy, mod, outproj_weight, outproj_bias[None]
    )

    unit = 256
    blocks = hidden_width // unit
    feed, grad_hidden, d_down, d_gate, d_bias = feed_call(
        hidden_two, hidden_two_t, grad_feed, gate_up_weight, gate_up_bias[None], down_weight,
        jnp.zeros((rows, width), F32), jnp.zeros((rows, width), F32), 0, 1, unit,
    )
    output_rows, grad_middle, grad_mixed, d_out, sums_two = turn_call(
        feed, grad_hidden, middle, attended, dy, grad_feed, mixed, mod, outproj_weight,
        down_bias[None],
    )
    gate_bias = d_bias.reshape(blocks, 2, unit).transpose(1, 0, 2)
    dq, dk0, dk1, dv0, dv1 = attend_back_call(
        q, k0, k1, v0, v1, grown, grad_mixed, mixed, inverse, head
    )
    dk1, dv1 = moves.pair(dk1), moves.pair(dv1)
    grad_x, d_in, sums_one, in_bias = project_back_call(
        dq, dk0, dk1, dv0, dv1, raw, hidden_one, x, grad_middle, mod, inproj_weight, qgain,
        kgain, cosine, sine, head,
    )

    def give_back(rows_out):
        parts = rows_out.reshape(4, cells, width)
        got = [parts[0]] + [moves.plane(parts[k], k) for k in range(1, 4)]
        return regroup(got, place).reshape(tokens.shape)

    output = give_back(output_rows)
    grad_tokens = give_back(grad_x)
    slice_rows = width // nb

    def scatter(d):
        d = lax.psum_scatter(d.astype(BF16), "batch", scatter_dimension=0, tiled=True)
        return lax.psum(d, ("gy", "gx")).astype(F32)

    def joined(d):
        return jnp.concatenate([d[0], d[1]], axis=1)

    grad_down_w = scatter(d_down.reshape(hidden_width, width))
    grad_gu_w = scatter(
        d_gate.transpose(2, 1, 0, 3).reshape(width, 2 * hidden_width)
    )
    grad_out_w = scatter(joined(d_out))
    grad_in_w = scatter(joined(d_in))
    gain_sums = sums_one[2:4].reshape(2, heads, head).sum(axis=1)
    early = jnp.concatenate([sums_two[:6].reshape(-1), gate_bias.reshape(-1)])
    late = jnp.concatenate(
        [sums_one[:2].reshape(-1), in_bias.reshape(-1), gain_sums.reshape(-1)]
    )

    def everywhere(vector):
        halves = vector.reshape(2, -1)
        half = add(take(halves, core), moves.pair(take(halves, 1 - core)))
        half = moves.gather(half)
        both = regroup([half, moves.pair(half)], core)
        return both.transpose(1, 0, 2).reshape(half.shape[0], -1)

    known = jnp.concatenate([condition, jnp.broadcast_to(label.astype(F32), (128,))])
    known = moves.gather(known)
    early, late = everywhere(early), everywhere(late)
    grad_modulation = jnp.concatenate([late[:, : 2 * width], early[:, : 4 * width]], axis=1)
    conditions = known[:, :width]
    all_labels = known[:, width].astype(jnp.int32)
    cond_acts = jax.nn.silu(conditions).astype(BF16)
    my_acts = lax.dynamic_slice_in_dim(cond_acts, z * slice_rows, slice_rows, axis=1)
    low_mod = grad_modulation.astype(BF16)
    grad_mod_w = mm_tn(my_acts, low_mod)
    wide = 6 * width
    grad_mod_b = lax.dynamic_slice_in_dim(
        jnp.sum(grad_modulation, axis=0), z * (wide // nb), wide // nb, axis=0
    )
    grad_cond_act = mm_nt(low_mod, modulate_weight)
    sig = jax.nn.sigmoid(conditions)
    grad_conditions = grad_cond_act * sig * (1.0 + conditions * (1.0 - sig))
    grad_condition = regroup([grad_conditions[k] for k in range(4)], place)
    onehot = (all_labels[:, None] == jnp.arange(class_count, dtype=jnp.int32)[None, :]).astype(F32)
    grad_table = lax.dot_general(
        onehot, grad_conditions, (((0,), (0,)), ((), ())), precision=highest,
        preferred_element_type=F32,
    )

    early_sum = jnp.sum(early, axis=0)
    late_sum = jnp.sum(late, axis=0)

    def part(vector, start, size):
        return lax.dynamic_slice_in_dim(vector, start + z * (size // nb), size // nb, axis=0)

    grad_out_b = part(early_sum, 4 * width, width)
    grad_down_b = part(early_sum, 5 * width, width)
    grad_gu_b = part(early_sum, 6 * width, 2 * hidden_width)
    grad_in_b = part(late_sum, 2 * width, 3 * width)
    grad_q_gain = part(late_sum, 5 * width, head)
    grad_k_gain = part(late_sum, 5 * width + head, head)
    return (
        output, grad_tokens, grad_condition, grad_table, grad_mod_w, grad_mod_b, grad_in_w,
        grad_in_b, grad_q_gain, grad_k_gain, grad_out_w, grad_out_b, grad_gu_w, grad_gu_b,
        grad_down_w, grad_down_b,
    )


def solution(mesh):
    grid = P("batch", "gy", "gx", None)
    by_batch = P("batch")
    rows = P("batch", None)
    placed = (grid, by_batch, by_batch) + (P(),) * 13 + (grid,)
    return jax.shard_map(
        functools.partial(body, mesh),
        mesh=mesh,
        in_specs=placed,
        out_specs=(
            grid, grid, rows, P(), rows, by_batch, rows, by_batch, by_batch, by_batch, rows,
            by_batch, rows, by_batch, rows, by_batch,
        ),
        check_vma=False,
    )
```

```python
import functools
import math

import jax
import jax.numpy as jnp
from jax import lax
from jax.experimental import pallas as pl
from jax.experimental.pallas import tpu as pltpu
from jax.sharding import PartitionSpec as P

NORM_EPSILON = 1e-06
AXES = ("batch", "gy", "gx")
BF16 = jnp.bfloat16
F32 = jnp.float32
VMEM_LIMIT = 60 * 1024 * 1024


def mm(left, right):
    return lax.dot_general(left, right, (((1,), (0,)), ((), ())), preferred_element_type=F32)


def mm_nt(left, right):
    return lax.dot_general(left, right, (((1,), (1,)), ((), ())), preferred_element_type=F32)


def mm_tn(left, right):
    return lax.dot_general(left, right, (((0,), (0,)), ((), ())), preferred_element_type=F32)


def params():
    return pltpu.CompilerParams(vmem_limit_bytes=VMEM_LIMIT)


def full(shape):
    return pl.BlockSpec(shape, lambda *_: (0,) * len(shape))


def col_sum(values):
    return jnp.sum(values, axis=0, keepdims=True)


def modulation_kernel(act_ref, weight_ref, bias_ref, out_ref):
    out_ref[...] = mm(act_ref[...], weight_ref[...]) + bias_ref[...].astype(F32)


def modulation_call(act, weight, bias):
    rows, width = act.shape
    wide = weight.shape[1]
    return pl.pallas_call(
        modulation_kernel,
        grid=(wide // width,),
        in_specs=[
            full((rows, width)),
            pl.BlockSpec((width, width), lambda j: (0, j)),
            pl.BlockSpec((1, width), lambda j: (0, j)),
        ],
        out_specs=pl.BlockSpec((rows, width), lambda j: (0, j)),
        out_shape=jax.ShapeDtypeStruct((rows, wide), F32),
        compiler_params=params(),
        name="modulation",
    )(act, weight, bias)


def head_sum(values, head):
    width = 256
    row = lax.broadcasted_iota(jnp.int32, (width, width), 0) // head
    col = lax.broadcasted_iota(jnp.int32, (width, width), 1) // head
    ones = jnp.where(row == col, 1.0, 0.0).astype(BF16)
    parts = [
        mm(values[:, i : i + width].astype(BF16), ones) for i in range(0, values.shape[1], width)
    ]
    return jnp.concatenate(parts, axis=1)


def turn(values, cosine, sine, head):
    quarter = head // 4
    lane = lax.broadcasted_iota(jnp.int32, (1, 128), 1)
    first = (lane % (2 * quarter)) < quarter
    parts = []
    for i in range(0, values.shape[1], 128):
        part = values[:, i : i + 128]
        partner = jnp.where(
            first, pltpu.roll(part, 128 - quarter, 1), pltpu.roll(part, quarter, 1)
        )
        parts.append(part * cosine + partner * sine)
    return jnp.concatenate(parts, axis=1)


def project_kernel(
    head, x_ref, mod_ref, weight_ref, bias_ref, qgain_ref, kgain_ref, cos_ref, sin_ref,
    hid_ref, q_ref, k_ref, v_ref, raw_ref,
):
    width = x_ref.shape[1]
    x = x_ref[...].astype(F32)
    normed = x * lax.rsqrt(jnp.mean(x * x, axis=-1, keepdims=True) + NORM_EPSILON)
    hidden = (normed * (1.0 + mod_ref[:, width : 2 * width]) + mod_ref[:, :width]).astype(BF16)
    hid_ref[...] = hidden
    for part, (out_ref, gain_ref) in enumerate(((q_ref, qgain_ref), (k_ref, kgain_ref))):
        raw = mm(hidden, weight_ref[:, part * width : (part + 1) * width])
        raw = raw + bias_ref[:, part * width : (part + 1) * width].astype(F32)
        raw_ref[:, part * width : (part + 1) * width] = raw.astype(BF16)
        factor = lax.rsqrt(head_sum(raw * raw, head) * (1.0 / head) + NORM_EPSILON)
        scaled = raw * factor * gain_ref[...]
        out_ref[...] = turn(scaled, cos_ref[...], sin_ref[...], head).astype(BF16)
    value = mm(hidden, weight_ref[:, 2 * width :]) + bias_ref[:, 2 * width :].astype(F32)
    v_ref[...] = value.astype(BF16)


def project_call(x, mod, weight, bias, qgain, kgain, cosine, sine, head):
    rows, width = x.shape
    block = rows // 2
    by_row = lambda wide: pl.BlockSpec((block, wide), lambda i: (i, 0))
    shape = jax.ShapeDtypeStruct((rows, width), BF16)
    return pl.pallas_call(
        functools.partial(project_kernel, head),
        grid=(2,),
        in_specs=[
            by_row(width),
            full(mod.shape),
            full(weight.shape),
            full(bias.shape),
            full(qgain.shape),
            full(kgain.shape),
            by_row(128),
            by_row(128),
        ],
        out_specs=[by_row(width)] * 4 + [by_row(2 * width)],
        out_shape=[shape] * 4 + [jax.ShapeDtypeStruct((rows, 2 * width), BF16)],
        compiler_params=params(),
        name="project",
    )(x, mod, weight, bias, qgain, kgain, cosine, sine)


def attend_kernel(scale, q_ref, k0_ref, k1_ref, v0_ref, v1_ref, mix_ref, e_ref, rl_ref):
    lane = lax.broadcasted_iota(jnp.int32, (1, 128), 1)
    q = q_ref[...]
    keys = jnp.concatenate([k0_ref[...], k1_ref[...]], axis=0)
    values = jnp.concatenate([v0_ref[...], v1_ref[...]], axis=0)
    values = jnp.concatenate([values, jnp.ones_like(values)], axis=1)
    outs = []
    for h in range(2):
        mine = (lane >= 64) if h else (lane < 64)
        scores = mm_nt(jnp.where(mine, q, jnp.zeros_like(q)), keys)
        grown = jnp.exp(scores * scale).astype(BF16)
        e_ref[h] = grown
        outs.append(mm(grown, values))
    inverse = 1.0 / jnp.where(lane < 64, outs[0][:, 128:], outs[1][:, 128:])
    mix_ref[...] = (jnp.where(lane < 64, outs[0][:, :128], outs[1][:, :128]) * inverse).astype(BF16)
    rl_ref[...] = inverse


def attend_call(q, k0, k1, v0, v1, head):
    rows, width = q.shape
    pair = pl.BlockSpec((rows, 128), lambda p: (0, p))
    return pl.pallas_call(
        functools.partial(attend_kernel, head**-0.5),
        grid=(width // 128,),
        in_specs=[pair] * 5,
        out_specs=[pair, pl.BlockSpec((2, rows, 2 * rows), lambda p: (p, 0, 0)), pair],
        out_shape=[
            jax.ShapeDtypeStruct((rows, width), BF16),
            jax.ShapeDtypeStruct((width // head, rows, 2 * rows), BF16),
            jax.ShapeDtypeStruct((rows, width), F32),
        ],
        compiler_params=params(),
        name="attend",
    )(q, k0, k1, v0, v1)


def attend_back_kernel(
    scale, q_ref, k0_ref, k1_ref, v0_ref, v1_ref, e_ref, gm_ref, mix_ref, rl_ref,
    dq_ref, dk0_ref, dk1_ref, dv0_ref, dv1_ref,
):
    rows = q_ref.shape[0]
    lane = lax.broadcasted_iota(jnp.int32, (1, 128), 1)
    keys = jnp.concatenate([k0_ref[...], k1_ref[...]], axis=0)
    values = jnp.concatenate([v0_ref[...], v1_ref[...]], axis=0)
    scaled = gm_ref[...].astype(F32) * rl_ref[...]
    products = scaled * mix_ref[...].astype(F32)
    scaled = scaled.astype(BF16)
    q_t = q_ref[...].T
    scaled_t = scaled.T
    dqs, dks, dvs = [], [], []
    for h in range(2):
        mine = (lane >= 64) if h else (lane < 64)
        inner = jnp.sum(jnp.where(mine, products, 0.0), axis=1, keepdims=True)
        grad_probs = mm_nt(jnp.where(mine, scaled, jnp.zeros_like(scaled)), values)
        grown = e_ref[h]
        grad_scores = (grown.astype(F32) * (grad_probs - inner) * scale).astype(BF16)
        dqs.append(mm(grad_scores, keys))
        dks.append(mm(q_t[64 * h : 64 * h + 64], grad_scores))
        dvs.append(mm(scaled_t[64 * h : 64 * h + 64], grown))
    dq_ref[...] = jnp.where(lane < 64, dqs[0], dqs[1]).astype(BF16)
    dk = jnp.concatenate(dks, axis=0).T.astype(BF16)
    dv = jnp.concatenate(dvs, axis=0).T.astype(BF16)
    dk0_ref[...] = dk[:rows]
    dk1_ref[...] = dk[rows:]
    dv0_ref[...] = dv[:rows]
    dv1_ref[...] = dv[rows:]


def attend_back_call(q, k0, k1, v0, v1, grown, grad_mixed, mixed, inverse, head):
    rows, width = q.shape
    pair = pl.BlockSpec((rows, 128), lambda p: (0, p))
    return pl.pallas_call(
        functools.partial(attend_back_kernel, head**-0.5),
        grid=(width // 128,),
        in_specs=[pair] * 5
        + [pl.BlockSpec((2, rows, 2 * rows), lambda p: (p, 0, 0))]
        + [pair] * 3,
        out_specs=[pair] * 5,
        out_shape=[jax.ShapeDtypeStruct((rows, width), BF16)] * 5,
        compiler_params=params(),
        name="attend_back",
    )(q, k0, k1, v0, v1, grown, grad_mixed, mixed, inverse)


def middle_kernel(
    mix_ref, x_ref, dy_ref, mod_ref, weight_ref, bias_ref, att_ref, mid_ref, h2_ref, h2t_ref, gf_ref
):
    width = x_ref.shape[1]
    attended = mm(mix_ref[...], weight_ref[...]) + bias_ref[...].astype(F32)
    middle = x_ref[...].astype(F32) + mod_ref[:, 2 * width : 3 * width] * attended
    normed = middle * lax.rsqrt(jnp.mean(middle * middle, axis=-1, keepdims=True) + NORM_EPSILON)
    hidden = normed * (1.0 + mod_ref[:, 4 * width : 5 * width]) + mod_ref[:, 3 * width : 4 * width]
    hidden = hidden.astype(BF16)
    att_ref[...] = attended.astype(BF16)
    mid_ref[...] = middle
    h2_ref[...] = hidden
    h2t_ref[...] = hidden.T
    gf_ref[...] = (mod_ref[:, 5 * width :] * dy_ref[...].astype(F32)).astype(BF16)


def middle_call(mixed, x, dy, mod, weight, bias, bias_at=0):
    rows, width = x.shape
    block = rows // 2
    by_row = pl.BlockSpec((block, width), lambda i: (i, 0))
    low = jax.ShapeDtypeStruct((rows, width), BF16)
    return pl.pallas_call(
        middle_kernel,
        grid=(2,),
        in_specs=[by_row] * 3
        + [full(mod.shape), full(weight.shape), pl.BlockSpec((1, width), lambda i: (0, bias_at))],
        out_specs=[by_row] * 3 + [pl.BlockSpec((width, block), lambda i: (0, i)), by_row],
        out_shape=[low, jax.ShapeDtypeStruct((rows, width), F32), low]
        + [jax.ShapeDtypeStruct((width, rows), BF16), low],
        compiler_params=params(),
        name="middle",
    )(mixed, x, dy, mod, weight, bias)


def feed_kernel(
    h2_ref, h2t_ref, gf_ref, wg_ref, wu_ref, bg_ref, bu_ref, wd_ref, feed_in_ref, gh_in_ref,
    feed_ref, gh_ref, dd_ref, dg_ref, db_ref,
):
    @pl.when(pl.program_id(0) == 0)
    def _():
        feed_ref[...] = feed_in_ref[...]
        gh_ref[...] = gh_in_ref[...]

    hidden = h2_ref[...]
    grad_feed = gf_ref[...]
    gate = mm(hidden, wg_ref[...]) + bg_ref[...].astype(F32)
    up = mm(hidden, wu_ref[...]) + bu_ref[...].astype(F32)
    grad_product = mm_nt(grad_feed, wd_ref[...])
    sig = 1.0 / (1.0 + jnp.exp(-gate))
    active = gate * sig
    product = (active * up).astype(BF16)
    grad_gate = (grad_product * up * sig * (1.0 + gate * (1.0 - sig))).astype(BF16)
    grad_up = (grad_product * active).astype(BF16)
    dd_ref[...] = mm_tn(product, grad_feed).astype(BF16)
    dg_ref[0] = mm(h2t_ref[...], grad_gate).astype(BF16)
    dg_ref[1] = mm(h2t_ref[...], grad_up).astype(BF16)
    db_ref[0] = col_sum(grad_gate.astype(F32))
    db_ref[1] = col_sum(grad_up.astype(F32))
    feed_ref[...] += mm(product, wd_ref[...])
    gh_ref[...] += mm_nt(grad_gate, wg_ref[...]) + mm_nt(grad_up, wu_ref[...])


def feed_call(hidden, hidden_t, grad_feed, weight, bias, down, feed, grad_hidden, first, step, unit):
    rows, width = hidden.shape
    blocks = down.shape[0] // unit
    steps = len(range(first, blocks, step))
    pick = lambda s: first + step * s
    acc = jax.ShapeDtypeStruct((rows, width), F32)
    return pl.pallas_call(
        feed_kernel,
        grid=(steps,),
        in_specs=[
            full((rows, width)),
            full((width, rows)),
            full((rows, width)),
            pl.BlockSpec((width, unit), lambda s: (0, pick(s))),
            pl.BlockSpec((width, unit), lambda s: (0, blocks + pick(s))),
            pl.BlockSpec((1, unit), lambda s: (0, pick(s))),
            pl.BlockSpec((1, unit), lambda s: (0, blocks + pick(s))),
            pl.BlockSpec((unit, width), lambda s: (pick(s), 0)),
            full((rows, width)),
            full((rows, width)),
        ],
        out_specs=[
            full((rows, width)),
            full((rows, width)),
            pl.BlockSpec((None, unit, width), lambda s: (s, 0, 0)),
            pl.BlockSpec((None, 2, width, unit), lambda s: (s, 0, 0, 0)),
            pl.BlockSpec((None, 2, 1, unit), lambda s: (s, 0, 0, 0)),
        ],
        out_shape=[
            acc,
            acc,
            jax.ShapeDtypeStruct((steps, unit, width), BF16),
            jax.ShapeDtypeStruct((steps, 2, width, unit), BF16),
            jax.ShapeDtypeStruct((steps, 2, 1, unit), F32),
        ],
        compiler_params=params(),
        name="feed",
    )(hidden, hidden_t, grad_feed, weight, weight, bias, bias, down, feed, grad_hidden)


def turn_kernel(
    feed_ref, gh_ref, mid_ref, att_ref, dy_ref, gf_ref, mix_ref, mod_ref, weight_ref, dbias_ref,
    out_ref, gmid_ref, gmix_ref, dw_ref, sums_ref,
):
    width = mid_ref.shape[1]
    half = width // 2
    dy = dy_ref[...].astype(F32)
    feed = feed_ref[...] + dbias_ref[...].astype(F32)
    middle = mid_ref[...]
    out_ref[...] = (middle + mod_ref[:, 5 * width :] * feed).astype(BF16)
    factor = lax.rsqrt(jnp.mean(middle * middle, axis=-1, keepdims=True) + NORM_EPSILON)
    normed = middle * factor
    grad_hidden = gh_ref[...]
    product = grad_hidden * normed
    grad_normed = grad_hidden * (1.0 + mod_ref[:, 4 * width : 5 * width])
    back = factor * (
        grad_normed - normed * jnp.mean(grad_normed * normed, axis=-1, keepdims=True)
    )
    grad_middle = dy + back
    gmid_ref[...] = grad_middle
    grad_attended = (mod_ref[:, 2 * width : 3 * width] * grad_middle).astype(BF16)
    sums_ref[0:1, :] = col_sum(grad_middle * att_ref[...].astype(F32))
    sums_ref[1:2, :] = col_sum(grad_hidden)
    sums_ref[2:3, :] = col_sum(product)
    sums_ref[3:4, :] = col_sum(dy * feed)
    sums_ref[4:5, :] = col_sum(grad_attended.astype(F32))
    sums_ref[5:6, :] = col_sum(gf_ref[...].astype(F32))
    sums_ref[6:8, :] = jnp.zeros((2, width), F32)
    gmix_ref[...] = mm_nt(grad_attended, weight_ref[...]).astype(BF16)
    mixed_t = mix_ref[...].T
    dw_ref[0] = mm(mixed_t, grad_attended[:, :half]).astype(BF16)
    dw_ref[1] = mm(mixed_t, grad_attended[:, half:]).astype(BF16)


def turn_call(feed, grad_hidden, middle, attended, dy, grad_feed, mixed, mod, weight, down_bias):
    rows, width = middle.shape
    low = jax.ShapeDtypeStruct((rows, width), BF16)
    return pl.pallas_call(
        turn_kernel,
        out_shape=[
            low,
            jax.ShapeDtypeStruct((rows, width), F32),
            low,
            jax.ShapeDtypeStruct((2, width, width // 2), BF16),
            jax.ShapeDtypeStruct((8, width), F32),
        ],
        compiler_params=params(),
        name="turn",
    )(feed, grad_hidden, middle, attended, dy, grad_feed, mixed, mod, weight, down_bias)


def project_back_kernel(
    head, dq_ref, dk0_ref, dk1_ref, dv0_ref, dv1_ref, raw_ref, hid_ref, x_ref, gmid_ref, mod_ref,
    weight_ref, qgain_ref, kgain_ref, cos_ref, sin_ref,
    gx_ref, dw_ref, sums_ref, bias_ref, proj_ref,
):
    width = x_ref.shape[1]
    cosine, sine = cos_ref[...], -sin_ref[...]
    for part in range(3):
        span = slice(part * width, (part + 1) * width)
        if part == 2:
            grad = dv0_ref[...].astype(F32) + dv1_ref[...].astype(F32)
        else:
            grad = dq_ref[...].astype(F32)
            if part == 1:
                grad = dk0_ref[...].astype(F32) + dk1_ref[...].astype(F32)
            gain = (qgain_ref, kgain_ref)[part][...]
            raw = raw_ref[:, span].astype(F32)
            factor = lax.rsqrt(head_sum(raw * raw, head) * (1.0 / head) + NORM_EPSILON)
            normed = raw * factor
            turned = turn(grad, cosine, sine, head)
            sums_ref[2 + part : 3 + part, :] = col_sum(turned * normed)
            turned = turned * gain
            mean = head_sum(turned * normed, head) * (1.0 / head)
            grad = factor * (turned - normed * mean)
        low = grad.astype(BF16)
        proj_ref[:, span] = low
        bias_ref[:, span] = col_sum(low.astype(F32))
    hidden_t = hid_ref[...].T
    half = 3 * width // 2
    dw_ref[0] = mm(hidden_t, proj_ref[:, :half]).astype(BF16)
    dw_ref[1] = mm(hidden_t, proj_ref[:, half:]).astype(BF16)
    grad_hidden = mm_nt(proj_ref[...], weight_ref[...])
    x = x_ref[...].astype(F32)
    factor = lax.rsqrt(jnp.mean(x * x, axis=-1, keepdims=True) + NORM_EPSILON)
    normed = x * factor
    sums_ref[0:1, :] = col_sum(grad_hidden)
    sums_ref[1:2, :] = col_sum(grad_hidden * normed)
    sums_ref[4:8, :] = jnp.zeros((4, width), F32)
    grad_normed = grad_hidden * (1.0 + mod_ref[:, width : 2 * width])
    back = factor * (
        grad_normed - normed * jnp.mean(grad_normed * normed, axis=-1, keepdims=True)
    )
    gx_ref[...] = (gmid_ref[...] + back).astype(BF16)


def project_back_call(
    dq, dk0, dk1, dv0, dv1, raw, hidden, x, grad_middle, mod, weight, qgain, kgain, cosine, sine, head
):
    rows, width = x.shape
    return pl.pallas_call(
        functools.partial(project_back_kernel, head),
        out_shape=[
            jax.ShapeDtypeStruct((rows, width), BF16),
            jax.ShapeDtypeStruct((2, width, 3 * width // 2), BF16),
            jax.ShapeDtypeStruct((8, width), F32),
            jax.ShapeDtypeStruct((1, 3 * width), F32),
        ],
        scratch_shapes=[pltpu.VMEM((rows, 3 * width), BF16)],
        compiler_params=params(),
        name="project_back",
    )(dq, dk0, dk1, dv0, dv1, raw, hidden, x, grad_middle, mod, weight, qgain, kgain, cosine, sine)


class Place:
    def __init__(self):
        self.z, self.gy, self.gx = (lax.axis_index(name) for name in AXES)
        self.core = lax.rem(self.gx, 2)
        self.side = self.gx // 2
        self.chip = 2 * self.gy + self.side

    def flipped(self, k):
        return 2 * lax.rem(self.gy + k // 2, 2) + lax.rem(self.side + lax.rem(k, 2), 2)

    def pair(self):
        return {"gx": self.gx + 1 - 2 * self.core}

    def plane(self, k):
        device = {}
        if k & 2:
            device["gy"] = 1 - self.gy
        if k & 1:
            device["gx"] = lax.rem(self.gx + 2, 4)
        return device

    def depth(self, d):
        return {"batch": self.flipped_z(d)}

    def flipped_z(self, d):
        return {1: self.z + 1 - 2 * lax.rem(self.z, 2), 2: lax.rem(self.z + 2, 4), 3: 3 - self.z}[d]


def meet(devices):
    barrier = pltpu.get_barrier_semaphore()
    for device in devices:
        pl.semaphore_signal(barrier, inc=1, device_id=device, device_id_type=pl.DeviceIdType.MESH)
    pl.semaphore_wait(barrier, len(devices))


def send(source, target, send_sem, recv_sem, device):
    return pltpu.make_async_remote_copy(
        src_ref=source, dst_ref=target, send_sem=send_sem, recv_sem=recv_sem, device_id=device,
        device_id_type=pl.DeviceIdType.MESH,
    )


def feed_order(step):
    owner = jnp.where(
        step < 2, 3, jnp.where((step == 2) | (step == 5), 2, jnp.where(step < 5, 1, 0))
    )
    return owner, lax.rem(step, 2)


def feed_block(step, i):
    step = jnp.minimum(step, 7)
    owner, half = feed_order(step)
    return (2 * half + i) * 4 + Place().flipped(owner)


def feed_turn_kernel(
    h2_ref, h2t_ref, gf_ref, wg0, wg1, wu0, wu1, bg0, bg1, bu0, bu1, wd0, wd1,
    mid_ref, att_ref, dy_ref, mix_ref, mod_ref, weight_ref, dbias_ref, known_ref,
    out_ref, gmid_ref, gmix_ref, dw_ref, sums_ref, total_ref, passed_ref,
    feed_ref, gh_ref, bias_ref, made, paired, near, pair_send, pair_recv, near_send, near_recv,
):
    place = Place()
    core = place.core
    step = pl.program_id(0)
    slot = lax.rem(step, 2)
    width = h2_ref.shape[1]
    unit = 128
    g_rows = width

    @pl.when(step == 0)
    def _():
        feed_ref[...] = jnp.zeros_like(feed_ref)
        sums_ref[1] = jnp.zeros((8, width), F32)
        gh_ref[...] = jnp.zeros_like(gh_ref)
        meet([place.pair(), place.plane(1), place.plane(2)])

    def pair_copy(of):
        return send(
            made.at[lax.rem(of, 2), 1 - core], paired.at[of], pair_send.at[lax.rem(of, 2)],
            pair_recv.at[of], place.pair(),
        )

    def near_copy(of, k):
        return send(paired.at[of], near.at[of], near_send.at[of], near_recv.at[of], place.plane(k))

    @pl.when(step >= 1)
    def _():
        pair_copy(step - 1).start()

    def join_pair(of):
        copy = pair_copy(of)
        copy.wait_recv()
        paired[of] = (made[1 - slot, core].astype(F32) + paired[of].astype(F32)).astype(BF16)

        @pl.when((of == 0) | (of == 2))
        def _():
            near_copy(of, 2).start()

        @pl.when((of == 1) | (of == 3))
        def _():
            near_copy(of, 1).start()

    @pl.when(step < 8)
    def _():
        owner, half = feed_order(step)
        hidden = h2_ref[...]
        grad_feed = gf_ref[...]
        wg = jnp.concatenate([wg0[...], wg1[...]], axis=1)
        wu = jnp.concatenate([wu0[...], wu1[...]], axis=1)
        wd = jnp.concatenate([wd0[...], wd1[...]], axis=0)
        gate = mm(hidden, wg) + jnp.concatenate([bg0[...], bg1[...]], axis=1).astype(F32)
        up = mm(hidden, wu) + jnp.concatenate([bu0[...], bu1[...]], axis=1).astype(F32)
        grad_product = mm_nt(grad_feed, wd)
        sig = 1.0 / (1.0 + jnp.exp(-gate))
        active = gate * sig
        product = (active * up).astype(BF16)
        grad_gate = (grad_product * up * sig * (1.0 + gate * (1.0 - sig))).astype(BF16)
        grad_up = (grad_product * active).astype(BF16)
        feed_ref[...] += mm(product, wd)
        gh_ref[...] += mm_nt(grad_gate, wg) + mm_nt(grad_up, wu)
        for e, grad in enumerate((grad_gate, grad_up)):
            total = col_sum(grad.astype(F32))
            for i in range(2):
                row = 16 * e + (2 * half + i) * 4 + place.flipped(owner)
                bias_ref[pl.ds(row, 1), :] = total[:, i * unit : (i + 1) * unit]

        @pl.when(step >= 1)
        def _():
            join_pair(step - 1)

        @pl.when(step >= 2)
        def _():
            pair_copy(step - 2).wait_send()

        for e, grad in enumerate((grad_gate, grad_up)):
            made[slot, e, :g_rows] = mm(h2t_ref[...], grad).astype(BF16)
        product_t = product.T
        for b in range(3):
            d = mm(product_t, grad_feed[:, 256 * b : 256 * b + 256]).astype(BF16)
            for i in range(2):
                for c in range(2):
                    made[slot, c, pl.ds(g_rows + b * 128 + i * 64, 64)] = d[
                        i * 128 + c * 64 : i * 128 + c * 64 + 64
                    ]

    @pl.when(step == 8)
    def _():
        join_pair(7)
        half = width // 2
        dy = dy_ref[...].astype(F32)
        feed = feed_ref[...] + dbias_ref[...].astype(F32)
        middle = mid_ref[...]
        out_ref[...] = (middle + mod_ref[:, 5 * width :] * feed).astype(BF16)
        factor = lax.rsqrt(jnp.mean(middle * middle, axis=-1, keepdims=True) + NORM_EPSILON)
        normed = middle * factor
        grad_hidden = gh_ref[...]
        product = grad_hidden * normed
        grad_normed = grad_hidden * (1.0 + mod_ref[:, 4 * width : 5 * width])
        back = factor * (
            grad_normed - normed * jnp.mean(grad_normed * normed, axis=-1, keepdims=True)
        )
        grad_middle = dy + back
        gmid_ref[...] = grad_middle
        grad_attended = (mod_ref[:, 2 * width : 3 * width] * grad_middle).astype(BF16)
        sums_ref[0, 0:1, :] = col_sum(grad_middle * att_ref[...].astype(F32))
        sums_ref[0, 1:2, :] = col_sum(grad_hidden)
        sums_ref[0, 2:3, :] = col_sum(product)
        sums_ref[0, 3:4, :] = col_sum(dy * feed)
        sums_ref[0, 4:5, :] = col_sum(grad_attended.astype(F32))
        sums_ref[0, 5:6, :] = col_sum(gf_ref[...].astype(F32))
        sums_ref[0, 6:8, :] = known_ref[...]
        for row in range(32):
            col = (row % 6) * unit
            sums_ref[1, row // 6 : row // 6 + 1, col : col + unit] = bias_ref[row : row + 1, :]
        gmix_ref[...] = mm_nt(grad_attended, weight_ref[...]).astype(BF16)
        mixed_t = mix_ref[...].T
        dw_ref[0] = mm(mixed_t, grad_attended[:, :half]).astype(BF16)
        dw_ref[1] = mm(mixed_t, grad_attended[:, half:]).astype(BF16)
        for of in (6, 7):
            pair_copy(of).wait_send()
        for of in range(4):
            near_copy(of, 1).wait()
        rows = width // 4
        for target, mine, there in ((total_ref, 6, 2), (passed_ref, 4, 0)):
            for f in range(2):

                def added(span, f=f, mine=mine, there=there):
                    both = paired[mine + f, span].astype(F32) + near[there + f, span].astype(F32)
                    return both.astype(BF16)

                for z in range(4):
                    target[z, f] = added(slice(z * rows, (z + 1) * rows))
                for i in range(2):
                    for b in range(3):
                        start = g_rows + b * 128 + i * 64
                        target[2 * f + i, 2, b * 64 : b * 64 + 64] = added(slice(start, start + 64))


def once(shape):
    return pl.BlockSpec(shape, lambda *_: (0,) * len(shape), pipeline_mode=pl.Buffered(1))


def feed_turn_call(
    hidden, hidden_t, grad_feed, gate_up, down, middle, attended, dy, mixed, mod, weight, small,
    known,
):
    rows, width = hidden.shape
    low = jax.ShapeDtypeStruct((rows, width), BF16)
    wide = jax.ShapeDtypeStruct((rows, width), F32)
    cols = lambda i, e: pl.BlockSpec((width, 128), lambda s: (0, 16 * e + feed_block(s, i)))
    first = GATE_BIAS * width // 128
    bias = lambda i, e: pl.BlockSpec((1, 128), lambda s: (0, first + 16 * e + feed_block(s, i)))
    down_bias = pl.BlockSpec((1, width), lambda s: (0, DOWN_BIAS), pipeline_mode=pl.Buffered(1))
    deep = lambda i: pl.BlockSpec((128, width), lambda s: (feed_block(s, i), 0))
    piece = (width + 384, 256)
    out_shape = [
        low, wide, low,
        jax.ShapeDtypeStruct((2, width, width // 2), BF16),
        jax.ShapeDtypeStruct((2, 8, width), F32),
        jax.ShapeDtypeStruct((4, 3, width // 4, 256), BF16),
        jax.ShapeDtypeStruct((4, 3, width // 4, 256), BF16),
    ]
    return pl.pallas_call(
        feed_turn_kernel,
        grid=(9,),
        in_specs=[once((rows, width)), once((width, rows)), once((rows, width))]
        + [cols(0, 0), cols(1, 0), cols(0, 1), cols(1, 1)]
        + [bias(0, 0), bias(1, 0), bias(0, 1), bias(1, 1)]
        + [deep(0), deep(1)]
        + [once((rows, width))] * 4
        + [once(mod.shape), once(weight.shape), down_bias, once(known.shape)],
        out_specs=[full(shape.shape) for shape in out_shape],
        out_shape=out_shape,
        scratch_shapes=[
            pltpu.VMEM((rows, width), F32),
            pltpu.VMEM((rows, width), F32),
            pltpu.VMEM((32, 128), F32),
            pltpu.VMEM((2, 2) + piece, BF16),
            pltpu.VMEM((8,) + piece, BF16),
            pltpu.VMEM((4,) + piece, BF16),
            pltpu.SemaphoreType.DMA((2,)),
            pltpu.SemaphoreType.DMA((8,)),
            pltpu.SemaphoreType.DMA((4,)),
            pltpu.SemaphoreType.DMA((4,)),
        ],
        compiler_params=pltpu.CompilerParams(
            vmem_limit_bytes=VMEM_LIMIT, collective_id=1, has_side_effects=True
        ),
        name="feed_turn",
    )(
        hidden, hidden_t, grad_feed, gate_up, gate_up, gate_up, gate_up, small, small, small,
        small, down, down, middle, attended, dy, mixed, mod, weight, small, known,
    )


def attend_tiles_kernel(
    scale, q_ref, k0_ref, k1_ref, v0_ref, v1_ref, grad_hbm, mix_ref, e_ref, rl_ref, dy_hbm,
    own_ref, own_sem, tok_send, tok_recv,
):
    place = Place()
    cells = own_ref.shape[0]
    step = pl.program_id(0)
    load = pltpu.make_async_copy(grad_hbm.at[place.chip], own_ref, own_sem.at[0])
    store = pltpu.make_async_copy(own_ref, dy_hbm.at[pl.ds(0, cells)], own_sem.at[1])

    def token_copy(k):
        return send(
            grad_hbm.at[place.flipped(k)], dy_hbm.at[pl.ds(k * cells, cells)], tok_send.at[k - 1],
            tok_recv.at[k - 1], place.plane(k),
        )

    @pl.when(step == 0)
    def _():
        load.start()
        meet([place.plane(k) for k in (1, 2, 3)])
        for k in (3, 1, 2):
            token_copy(k).start()

    attend_kernel(scale, q_ref, k0_ref, k1_ref, v0_ref, v1_ref, mix_ref, e_ref, rl_ref)

    @pl.when(step == 1)
    def _():
        load.wait()
        store.start()

    @pl.when(step == pl.num_programs(0) - 1)
    def _():
        store.wait()
        for k in (1, 2, 3):
            token_copy(k).wait()


def attend_tiles_call(q, k0, k1, v0, v1, grads, head):
    rows, width = q.shape
    pair = pl.BlockSpec((rows, 128), lambda p: (0, p))
    anywhere = pl.BlockSpec(memory_space=pl.ANY)
    return pl.pallas_call(
        functools.partial(attend_tiles_kernel, head**-0.5),
        grid=(width // 128,),
        in_specs=[pair] * 5 + [anywhere],
        out_specs=[pair, pl.BlockSpec((2, rows, 2 * rows), lambda p: (p, 0, 0)), pair, anywhere],
        out_shape=[
            jax.ShapeDtypeStruct((rows, width), BF16),
            jax.ShapeDtypeStruct((width // head, rows, 2 * rows), BF16),
            jax.ShapeDtypeStruct((rows, width), F32),
            jax.ShapeDtypeStruct((rows, width), BF16),
        ],
        scratch_shapes=[
            pltpu.VMEM((rows // 4, width), BF16), pltpu.SemaphoreType.DMA((2,)),
            pltpu.SemaphoreType.DMA((3,)), pltpu.SemaphoreType.DMA((3,)),
        ],
        compiler_params=pltpu.CompilerParams(
            vmem_limit_bytes=VMEM_LIMIT, collective_id=4, has_side_effects=True
        ),
        name="attend_tiles",
    )(q, k0, k1, v0, v1, grads)


Q_GAIN, K_GAIN, OUT_BIAS, DOWN_BIAS, GATE_BIAS = 0, 1, 2, 3, 4


def front_kernel(
    head, tile_cols, tok_hbm, time_ref, label_ref, modb_ref, inb_ref, qgain_ref,
    kgain_ref, outb_ref, downb_ref, gateb_ref, table_hbm, modw_hbm, inw_hbm,
    x_hbm, hid_hbm, q_hbm, k0_hbm, v0_hbm, k1_hbm, v1_hbm, raw_hbm, mod_ref, cos_ref,
    sin_ref, small_ref, known_ref,
    x_ref, hid_ref, q_ref, k_ref, v_ref, raw_ref, table_ref, modw_ref, inw_ref,
    load_sem, store_sem, tok_send, tok_recv, kv_send, kv_recv,
):
    place = Place()
    core, chip = place.core, place.chip
    rows, width = x_ref.shape
    cells = rows // 4
    loads = [
        pltpu.make_async_copy(source, target, load_sem.at[i])
        for i, (source, target) in enumerate(
            (
                (tok_hbm.at[chip], x_ref.at[pl.ds(0, cells)]), (modw_hbm, modw_ref),
                (inw_hbm, inw_ref), (table_hbm, table_ref),
            )
        )
    ]
    stores = [
        pltpu.make_async_copy(source, target, store_sem.at[i])
        for i, (source, target) in enumerate(
            (
                (x_ref, x_hbm), (hid_ref, hid_hbm), (k_ref, k0_hbm),
                (v_ref, v0_hbm), (q_ref, q_hbm), (raw_ref, raw_hbm),
            )
        )
    ]

    def token_copy(k):
        return send(
            tok_hbm.at[place.flipped(k)], x_ref.at[pl.ds(k * cells, cells)], tok_send.at[k - 1],
            tok_recv.at[k - 1], place.plane(k),
        )

    def kv_copy(which, chunk):
        source, target = ((k_ref, k1_hbm), (v_ref, v1_hbm))[which]
        span = pl.ds(chunk * cells, cells if chunk == 0 else rows - cells)
        return send(
            source.at[span], target.at[span], kv_send.at[which, chunk], kv_recv.at[which, chunk],
            place.pair(),
        )

    def line(ref):
        return ref[...].astype(F32)[None, :]

    in_bias = line(inb_ref)

    def project(start, size, chunk):
        span = slice(start, start + size)
        x = x_ref[span, :].astype(F32)
        normed = x * lax.rsqrt(jnp.mean(x * x, axis=-1, keepdims=True) + NORM_EPSILON)
        hidden = normed * (1.0 + mod_ref[:, width : 2 * width]) + mod_ref[:, :width]
        hidden = hidden.astype(BF16)
        hid_ref[span, :] = hidden
        for part in (1, 2, 0):
            raw = mm(hidden, inw_ref[:, part * width : (part + 1) * width])
            raw = raw + in_bias[:, part * width : (part + 1) * width]
            if part == 2:
                v_ref[span, :] = raw.astype(BF16)
                for which in (0, 1):
                    kv_copy(which, chunk).start()
                continue
            raw_ref[span, part * width : (part + 1) * width] = raw.astype(BF16)
            factor = lax.rsqrt(head_sum(raw * raw, head) * (1.0 / head) + NORM_EPSILON)
            scaled = raw * factor * small_ref[:, part * width : (part + 1) * width]
            turned = turn(scaled, cos_ref[span, :], sin_ref[span, :], head).astype(BF16)
            (q_ref, k_ref)[part][span, :] = turned

    for i in (0, 3, 1, 2):
        loads[i].start()
    meet([place.pair()] + [place.plane(k) for k in (1, 2, 3)])
    for k in (3, 1, 2):
        token_copy(k).start()

    for start, row in (
        (Q_GAIN, jnp.concatenate([line(qgain_ref)] * (width // head), axis=1)),
        (K_GAIN, jnp.concatenate([line(kgain_ref)] * (width // head), axis=1)),
        (OUT_BIAS, line(outb_ref)), (DOWN_BIAS, line(downb_ref)), (GATE_BIAS, line(gateb_ref)),
    ):
        small_ref[:, start * width : start * width + row.shape[1]] = row
    half = width // 2
    index = lax.broadcasted_iota(jnp.int32, (1, half), 1).astype(F32)
    phase = time_ref[chip].astype(F32) * jnp.exp(-math.log(10000.0) * index / half)
    features = jnp.concatenate([jnp.cos(phase), jnp.sin(phase)], axis=1)
    label = label_ref[chip]
    classes = lax.broadcasted_iota(jnp.int32, (16, table_ref.shape[0]), 1)
    loads[3].wait()
    chosen = mm(jnp.where(classes == label, 1.0, 0.0).astype(BF16), table_ref[...])
    condition = features + chosen[:1]
    known_ref[0:1, :] = jnp.where(core == 0, condition, 0.0)
    known_ref[1:2, :] = jnp.where(core == 0, jnp.zeros((1, width), F32) + label.astype(F32), 0.0)
    act = condition * (1.0 / (1.0 + jnp.exp(-condition)))
    act = jnp.broadcast_to(act, (16, width)).astype(BF16)

    quarter = head // 4
    lane = lax.broadcasted_iota(jnp.int32, (1, 128), 1)
    rate = jnp.exp(-math.log(10000.0) / quarter * lax.rem(lane, quarter).astype(F32))
    by_row = lax.rem(lane, head) < head // 2
    sign = jnp.where(lax.rem(lane, 2 * quarter) < quarter, -1.0, 1.0)
    cell = lax.broadcasted_iota(jnp.int32, (cells, 128), 0)
    row, col = cell // tile_cols, lax.rem(cell, tile_cols)
    for k in range(4):
        there = place.flipped(k)
        down = (there // 2) * (cells // tile_cols) + row
        across = (2 * lax.rem(there, 2) + core) * tile_cols + col
        angle = jnp.where(by_row, down, across).astype(F32) * rate
        cos_ref[k * cells : (k + 1) * cells, :] = jnp.cos(angle)
        sin_ref[k * cells : (k + 1) * cells, :] = sign * jnp.sin(angle)
    loads[1].wait()
    mod_ref[...] = mm(act, modw_ref[...])[:1] + line(modb_ref)
    loads[0].wait()
    loads[2].wait()
    project(0, cells, 0)
    for k in (1, 2, 3):
        token_copy(k).wait()
    stores[0].start()
    project(cells, rows - cells, 1)
    for store in stores[1:]:
        store.start()
    for which in (0, 1):
        for chunk in (0, 1):
            kv_copy(which, chunk).wait()
    for store in stores:
        store.wait()


def front_call(
    tokens, timesteps, labels, vectors, class_table, modw, inw, head, tile_cols
):
    images, cells, width = tokens.shape
    rows = images * cells
    low = lambda *shape: jax.ShapeDtypeStruct(shape, BF16)
    vmem = lambda *shape: pltpu.VMEM(shape, BF16)
    anywhere = pl.BlockSpec(memory_space=pl.ANY)
    inside = pl.BlockSpec(memory_space=pltpu.VMEM)
    sems = lambda *shape: pltpu.SemaphoreType.DMA(shape)
    return pl.pallas_call(
        functools.partial(front_kernel, head, tile_cols),
        in_specs=[anywhere]
        + [pl.BlockSpec(memory_space=pltpu.SMEM)] * 2
        + [inside] * len(vectors)
        + [anywhere] * 3,
        out_specs=[anywhere] * 8 + [inside] * 5,
        out_shape=[low(rows, width)] * 7
        + [
            low(rows, 2 * width), jax.ShapeDtypeStruct((1, 6 * width), F32),
            jax.ShapeDtypeStruct((rows, 128), F32), jax.ShapeDtypeStruct((rows, 128), F32),
            jax.ShapeDtypeStruct((1, GATE_BIAS * width + vectors[-1].shape[0]), F32),
            jax.ShapeDtypeStruct((2, width), F32),
        ],
        scratch_shapes=[
            vmem(rows, width), vmem(rows, width), vmem(rows, width), vmem(rows, width),
            vmem(rows, width), vmem(rows, 2 * width), vmem(*class_table.shape),
            vmem(*modw.shape), vmem(*inw.shape), sems(4), sems(6), sems(3), sems(3), sems(2, 2), sems(2, 2),
        ],
        compiler_params=pltpu.CompilerParams(
            vmem_limit_bytes=VMEM_LIMIT, collective_id=3, has_side_effects=True
        ),
        name="front",
    )(tokens, timesteps, labels, *vectors, class_table, modw, inw)


Z_FIRST = (False, False, False, True)
GROUPS = 4
TOKEN_STEP = 5
PASS_STEP = 4


def back_kernel(
    head, q_ref, k0_ref, k1_ref, v0_ref, v1_ref, gm_ref, mix_ref, rl_ref, e_ref,
    mod_ref, qgain_ref, kgain_ref, cos_ref, sin_ref, dout_ref, totals_ref, passed_ref, early_ref,
    raw_hbm, hid_hbm, x_hbm, gmid_hbm, weight_hbm, rows_hbm,
    output_ref, gtok_ref, feeds_hbm, projs_hbm, early_hbm, late_hbm,
    feeds_ref, projs_ref, early_all, late_all, raw_ref, hid_ref, x_ref, gmid_ref, weight_ref, hidt_ref, gh_ref, gx_ref, late_ref,
    dq_s, dk0_s, dv0_s, dk1_s, dv1_s, dk_in, dv_in,
    made, paired, first_out, first_in, second_out, second_in, landed, z_in, early_in, late_in,
    load_sem, own_sem, kv_send, kv_recv, pair_send, pair_recv, first_send, first_recv,
    second_send, second_recv, pass_send, pass_recv, z_send, z_recv, tok_send, tok_recv, feed_send, feed_recv,
    proj_send, proj_recv, small_send, small_recv,
):
    place = Place()
    core, chip, z = place.core, place.chip, place.z
    step = pl.program_id(0)
    rows, width = x_ref.shape
    cells = rows // 4
    scale = head**-0.5
    lane = lax.broadcasted_iota(jnp.int32, (1, 128), 1)

    loads = [
        pltpu.make_async_copy(source, target, load_sem.at[i])
        for i, (source, target) in enumerate(
            (
                (hid_hbm, hid_ref), (raw_hbm, raw_ref), (weight_hbm, weight_ref),
                (x_hbm, x_ref), (gmid_hbm, gmid_ref),
            )
        )
    ]

    stores = [
        pltpu.make_async_copy(source, target, load_sem.at[5 + i])
        for i, (source, target) in enumerate(
            (
                (early_all, early_hbm), (late_all, late_hbm),
                (feeds_ref.at[core], feeds_hbm.at[core]), (projs_ref.at[core], projs_hbm.at[core]),
                (feeds_ref.at[1 - core], feeds_hbm.at[1 - core]),
                (projs_ref.at[1 - core], projs_hbm.at[1 - core]),
            )
        )
    ]

    def pass_copy(f, i):
        part = (slice(None), f) if i == 0 else (pl.ds(2 * f, 2), 2)
        return send(
            passed_ref.at[part], landed.at[part], pass_send.at[f, i], pass_recv.at[f, i],
            place.plane(f + 1),
        )

    def z_copy(d):
        return send(
            landed.at[place.flipped_z(d)], z_in.at[d - 1], z_send.at[d - 1], z_recv.at[d - 1],
            place.depth(d),
        )

    def token_copy(which, k):
        source, target = ((rows_hbm, output_ref), (gx_ref, gtok_ref))[which]
        return send(
            source.at[pl.ds(k * cells, cells)], target.at[chip], tok_send.at[which, k - 1],
            tok_recv.at[which, k - 1], place.plane(k),
        )

    def own_tokens(which):
        source, target = ((rows_hbm, output_ref), (gx_ref, gtok_ref))[which]
        return pltpu.make_async_copy(source.at[pl.ds(0, cells)], target.at[chip], own_sem.at[which])

    def kv_copy(which, p):
        source, target = ((dk1_s, dk_in), (dv1_s, dv_in))[which]
        return send(
            source.at[p], target.at[p], kv_send.at[which, p], kv_recv.at[which, p], place.pair()
        )

    def pair_copy(g):
        source = dout_ref.at[1 - core] if g == 3 else made.at[g % 2, 1 - core]
        return send(source, paired.at[g], pair_send.at[g], pair_recv.at[g], place.pair())

    def first_copy(g, k):
        other = place.flipped_z(k) if Z_FIRST[g] else place.flipped(k)
        device = place.depth(k) if Z_FIRST[g] else place.plane(k)
        return send(
            first_out.at[g, other], first_in.at[g, k - 1], first_send.at[g, k - 1],
            first_recv.at[g, k - 1], device,
        )

    def second_copy(g, k):
        other = place.flipped(k) if Z_FIRST[g] else place.flipped_z(k)
        device = place.plane(k) if Z_FIRST[g] else place.depth(k)
        return send(
            second_out.at[g, other], second_in.at[g, k - 1], second_send.at[g, k - 1],
            second_recv.at[g, k - 1], device,
        )

    def gather_copy(which, k):
        full_ref, sends, recvs = gathers[which]
        here = full_ref.at[core, chip]
        return send(here, here, sends.at[k - 1], recvs.at[k - 1], place.plane(k))

    def pass_on(which, k):
        full_ref, sends, recvs = gathers[which]
        here = full_ref.at[core, place.flipped(k)]
        if which == 0:
            half = here.shape[1] // 2
            here = here.at[:, pl.ds((k - 1) * half, half)]
        else:
            half = here.shape[0] // 2
            here = here.at[pl.ds((k - 1) * half, half)]
        return send(here, here, sends.at[1 + k], recvs.at[1 + k], place.plane(3 - k))

    def gather_pair(which, k):
        full_ref, sends, recvs = gathers[which]
        here = full_ref.at[core, place.flipped(k)]
        return send(here, here, sends.at[4 + k], recvs.at[4 + k], place.pair())

    gathers = ((feeds_ref, feed_send, feed_recv), (projs_ref, proj_send, proj_recv))
    smalls = ((early_ref, early_in, early_all, 8), (late_ref, late_in, late_all, 4))

    def small_pair(which):
        source, target, _, count = smalls[which]
        return send(
            source.at[1 - core], target, small_send.at[which, 0], small_recv.at[which, 0],
            place.pair(),
        )

    def small_plane(which, k):
        full_ref = smalls[which][2]
        return send(
            full_ref.at[core, pl.ds(0, 1)], full_ref.at[core, pl.ds(k, 1)],
            small_send.at[which, k], small_recv.at[which, k], place.plane(k),
        )

    def small_depth(which, d):
        full_ref = smalls[which][2]
        have = 4 * d
        return send(
            full_ref.at[core, pl.ds(0, have)], full_ref.at[core, pl.ds(have, have)],
            small_send.at[which, 3 + d], small_recv.at[which, 3 + d], place.depth(d),
        )

    def small_last(which):
        here = smalls[which][2].at[core]
        return send(
            here, here, small_send.at[which, 6], small_recv.at[which, 6], place.pair()
        )

    def small_begin(which):
        source, target, full_ref, _ = smalls[which]
        small_pair(which).wait_recv()
        full_ref[core, 0] = source[core] + target[...]
        for k in (1, 2, 3):
            small_plane(which, k).start()

    def small_next(which, i):
        if i == 0:
            for k in (1, 2, 3):
                small_plane(which, k).wait_recv()
            small_depth(which, 1).start()
        elif i == 1:
            small_depth(which, 1).wait_recv()
            small_depth(which, 2).start()
        else:
            small_depth(which, 2).wait_recv()
            small_last(which).start()

    def start_group(g):
        pair_copy(g).wait_recv()
        mine = dout_ref.at[core] if g == 3 else made.at[g % 2, core]
        part = width // 16
        for a in range(4):
            for b in range(4):
                span = pl.ds((a * 4 + b) * part, part)
                total = (mine[span, :].astype(F32) + paired[g, span].astype(F32)).astype(BF16)
                if Z_FIRST[g]:
                    first_out[g, a, b] = total
                else:
                    first_out[g, b, a] = total
        for k in (1, 2, 3):
            first_copy(g, k).start()

    def go_on(g):
        for k in (1, 2, 3):
            first_copy(g, k).wait_recv()
        here = z if Z_FIRST[g] else chip
        second_out[g] = (
            first_out[g, here].astype(F32)
            + first_in[g, 0].astype(F32)
            + first_in[g, 1].astype(F32)
            + first_in[g, 2].astype(F32)
        ).astype(BF16)
        for k in (1, 2, 3):
            second_copy(g, k).start()

    def finish(g):
        for k in (1, 2, 3):
            second_copy(g, k).wait_recv()
        here = chip if Z_FIRST[g] else z
        projs_ref[core, chip, g] = (
            second_out[g, here].astype(F32)
            + second_in[g, 0].astype(F32)
            + second_in[g, 1].astype(F32)
            + second_in[g, 2].astype(F32)
        ).astype(BF16)

    @pl.when(step == 0)
    def _():
        for load in loads:
            load.start()
        meet(
            [place.pair()]
            + [place.plane(k) for k in (1, 2, 3)]
            + [place.depth(d) for d in (1, 2, 3)]
        )
        for f in (0, 1):
            for i in (0, 1):
                pass_copy(f, i).start()
        pair_copy(3).start()
        small_pair(0).start()
        gh_ref[...] = jnp.zeros_like(gh_ref)

    @pl.when(step >= 1)
    def _():
        for which in (0, 1):
            kv_copy(which, step - 1).start()

    @pl.when(step == 3)
    def _():
        pair_copy(0).start()

    @pl.when(step == 5)
    def _():
        pair_copy(1).start()

    @pl.when(step < 6)
    def _():
        keys = jnp.concatenate([k0_ref[...], k1_ref[...]], axis=0)
        values = jnp.concatenate([v0_ref[...], v1_ref[...]], axis=0)
        scaled = gm_ref[...].astype(F32) * rl_ref[...]
        products = scaled * mix_ref[...].astype(F32)
        scaled = scaled.astype(BF16)
        q_t = q_ref[...].T
        scaled_t = scaled.T
        dqs, dks, dvs = [], [], []
        for h in range(2):
            mine = (lane >= 64) if h else (lane < 64)
            inner = jnp.sum(jnp.where(mine, products, 0.0), axis=1, keepdims=True)
            grad_probs = mm_nt(jnp.where(mine, scaled, jnp.zeros_like(scaled)), values)
            grown = e_ref[h]
            grad_scores = (grown.astype(F32) * (grad_probs - inner) * scale).astype(BF16)
            dqs.append(mm(grad_scores, keys))
            dks.append(mm(q_t[64 * h : 64 * h + 64], grad_scores))
            dvs.append(mm(scaled_t[64 * h : 64 * h + 64], grown))
        dq_s[step] = jnp.where(lane < 64, dqs[0], dqs[1]).astype(BF16)
        dk = jnp.concatenate(dks, axis=0).T.astype(BF16)
        dv = jnp.concatenate(dvs, axis=0).T.astype(BF16)
        dk0_s[step] = dk[:rows]
        dk1_s[step] = dk[rows:]
        dv0_s[step] = dv[:rows]
        dv1_s[step] = dv[rows:]

    @pl.when(step == 0)
    def _():
        loads[0].wait()
        hidt_ref[...] = hid_ref[...].T

    @pl.when(step == 1)
    def _():
        loads[1].wait()
        loads[2].wait()
        start_group(3)
        small_begin(0)

    for i in range(3):

        @pl.when(step == 3 + i)
        def _(i=i):
            small_next(0, i)

    @pl.when(step == 3)
    def _():
        start_group(0)

    @pl.when(step == 5)
    def _():
        start_group(1)
        go_on(3)

    @pl.when(step == TOKEN_STEP)
    def _():
        for k in (1, 2, 3):
            token_copy(0, k).start()
        own_tokens(0).start()

    @pl.when(step == PASS_STEP)
    def _():
        for f in (0, 1):
            for i in (0, 1):
                pass_copy(f, i).wait_recv()
        landed[...] = (landed[...].astype(F32) + totals_ref[...].astype(F32)).astype(BF16)
        for d in (1, 2, 3):
            z_copy(d).start()

    @pl.when((step >= 2) & (lax.rem(step, 2) == 0))
    def _():
        g = (step - 2) // 2
        slot = lax.rem(g, 2)
        cosine, sine = cos_ref[...], -sin_ref[...]
        for i in range(2):
            for which in (0, 1):
                kv_copy(which, 2 * g + i).wait_recv()

        def both(ref):
            return jnp.concatenate([ref[2 * g], ref[2 * g + 1]], axis=1).astype(F32)

        lows = []
        for part in range(3):
            span = pl.ds(pl.multiple_of(part * width + g * 256, 256), 256)
            if part == 2:
                grad = both(dv0_s) + both(dv_in)
            else:
                grad = both(dq_s) if part == 0 else both(dk0_s) + both(dk_in)
                gain = (qgain_ref, kgain_ref)[part][:, :256].astype(F32)
                raw = raw_ref[:, span].astype(F32)
                factor = lax.rsqrt(head_sum(raw * raw, head) * (1.0 / head) + NORM_EPSILON)
                normed = raw * factor
                turned = turn(grad, cosine, sine, head)
                late_ref[1, part : part + 1, pl.ds(pl.multiple_of(g * 256, 256), 256)] = col_sum(
                    turned * normed
                )
                turned = turned * gain
                mean = head_sum(turned * normed, head) * (1.0 / head)
                grad = factor * (turned - normed * mean)
            low = grad.astype(BF16)
            lows.append(low)
            total = col_sum(low.astype(F32))
            where = pl.ds(pl.multiple_of(g * 256, 256), 256)
            if part < 2:
                late_ref[0, 2 + part : 3 + part, where] = total
            else:
                late_ref[1, 2:3, where] = total
            gh_ref[...] += mm_nt(low, weight_ref[:, span])
        grads = jnp.concatenate(
            [low[:, 128 * c : 128 * c + 128] for c in range(2) for low in lows], axis=1
        )

        @pl.when(step == 6)
        def _():
            pair_copy(0).wait_send()

        half = width // 2
        made[slot, 0] = mm(hidt_ref[...], grads[:, :half]).astype(BF16)
        made[slot, 1] = mm(hidt_ref[...], grads[:, half:]).astype(BF16)

    @pl.when(step == 6)
    def _():
        pair_copy(2).start()
        grad_hidden = gh_ref[...]
        loads[3].wait()
        loads[4].wait()
        x = x_ref[...].astype(F32)
        factor = lax.rsqrt(jnp.mean(x * x, axis=-1, keepdims=True) + NORM_EPSILON)
        normed = x * factor
        late_ref[0, 0:1, :] = col_sum(grad_hidden)
        late_ref[0, 1:2, :] = col_sum(grad_hidden * normed)
        late_ref[1, 3:4, :] = jnp.zeros((1, width), F32)
        small_pair(1).start()
        small_begin(1)
        start_group(2)
        go_on(0)
        go_on(1)
        grad_normed = grad_hidden * (1.0 + mod_ref[:, width : 2 * width])
        back = factor * (
            grad_normed - normed * jnp.mean(grad_normed * normed, axis=-1, keepdims=True)
        )
        gx_ref[...] = (gmid_ref[...] + back).astype(BF16)
        for k in (1, 2, 3):
            token_copy(1, k).start()
        own_tokens(1).start()
        for d in (1, 2, 3):
            z_copy(d).wait_recv()
        for i in range(3):
            feeds_ref[core, chip, i] = (
                landed[z, i].astype(F32)
                + z_in[0, i].astype(F32)
                + z_in[1, i].astype(F32)
                + z_in[2, i].astype(F32)
            ).astype(BF16)
        for k in (1, 2):
            gather_copy(0, k).start()
        gather_pair(0, 0).start()
        finish(3)
        finish(0)
        finish(1)
        go_on(2)
        small_next(1, 0)
        finish(2)
        for k in (1, 2):
            gather_copy(1, k).start()
        gather_pair(1, 0).start()
        small_next(1, 1)
        for k in (1, 2):
            gather_copy(0, k).wait_recv()
            pass_on(0, k).start()
            gather_pair(0, k).start()
        small_next(1, 2)
        for k in (1, 2):
            gather_copy(1, k).wait_recv()
            pass_on(1, k).start()
            gather_pair(1, k).start()
        for which in (0, 1):
            for k in (1, 2):
                gather_copy(which, k).wait_send()
                pass_on(which, k).wait()
            gather_pair(which, 3).start()
            stores[2 + which].start()
        for which in (0, 1):
            own_tokens(which).wait()
            for k in (1, 2, 3):
                token_copy(which, k).wait()
            small_pair(which).wait_send()
            for k in (1, 2, 3):
                small_plane(which, k).wait_send()
            for d in (1, 2):
                small_depth(which, d).wait_send()
            small_last(which).wait()
            stores[which].start()
            for p in range(6):
                kv_copy(which, p).wait_send()
        for f in (0, 1):
            for i in (0, 1):
                pass_copy(f, i).wait_send()
        for k in (1, 2, 3):
            z_copy(k).wait_send()
            for g in range(4):
                first_copy(g, k).wait_send()
                second_copy(g, k).wait_send()
        for g in (1, 2, 3):
            pair_copy(g).wait_send()
        for which in (0, 1):
            for k in range(4):
                gather_pair(which, k).wait()
            stores[4 + which].start()
        for store in stores:
            store.wait()


def back_call(
    q, k0, k1, v0, v1, grad_mixed, mixed, inverse, grown, mod, small_vectors, cosine, sine, d_out,
    totals, passed, early, raw, hidden, x, grad_middle, weight, output_rows, head,
):
    rows, width = q.shape
    half, part = width // 2, width // 16
    low = lambda *shape: jax.ShapeDtypeStruct(shape, BF16)
    pair = pl.BlockSpec((rows, 128), lambda s: (0, jnp.minimum(s, 5)))
    anywhere = pl.BlockSpec(memory_space=pl.ANY)
    small = [mod, small_vectors, small_vectors, cosine, sine, d_out, totals, passed, early]
    gain = lambda at: pl.BlockSpec((1, width), lambda s: (0, at), pipeline_mode=pl.Buffered(1))
    out_shape = [
        low(4, rows // 4, width), low(4, rows // 4, width),
        low(2, 4, 3, width // 4, 256), low(2, 4, GROUPS, part, half),
        jax.ShapeDtypeStruct((2, 16, 8, width), F32), jax.ShapeDtypeStruct((2, 16, 4, width), F32),
    ]
    vmem = lambda *shape: pltpu.VMEM(shape, BF16)
    sems = lambda *shape: pltpu.SemaphoreType.DMA(shape)
    return pl.pallas_call(
        functools.partial(back_kernel, head),
        grid=(7,),
        in_specs=[pair] * 8
        + [pl.BlockSpec((2, rows, 2 * rows), lambda s: (jnp.minimum(s, 5), 0, 0))]
        + [once(mod.shape), gain(Q_GAIN), gain(K_GAIN)]
        + [once(each.shape) for each in small[3:]]
        + [anywhere] * 6,
        out_specs=[anywhere] * 6,
        out_shape=out_shape,
        scratch_shapes=[pltpu.VMEM(shape.shape, shape.dtype) for shape in out_shape[2:]]
        + [
            vmem(rows, 2 * width), vmem(rows, width), vmem(rows, width),
            pltpu.VMEM((rows, width), F32), vmem(width, 3 * width), vmem(width, rows),
            pltpu.VMEM((rows, width), F32), vmem(rows, width), pltpu.VMEM((2, 4, width), F32),
        ]
        + [vmem(6, rows, 128)] * 7
        + [
            vmem(2, 2, width, half), vmem(GROUPS, width, half),
            vmem(GROUPS, 4, 4, part, half), vmem(GROUPS, 3, 4, part, half),
            vmem(GROUPS, 4, part, half), vmem(GROUPS, 3, part, half),
            vmem(*totals.shape), vmem(3, 3, width // 4, 256),
            pltpu.VMEM((8, width), F32), pltpu.VMEM((4, width), F32),
            sems(11), sems(2), sems(2, 6), sems(2, 6), sems(GROUPS), sems(GROUPS),
            sems(GROUPS, 3), sems(GROUPS, 3), sems(GROUPS, 3), sems(GROUPS, 3),
            sems(2, 2), sems(2, 2), sems(3), sems(3), sems(2, 3), sems(2, 3), sems(8), sems(8),
            sems(8), sems(8),
            sems(2, 7), sems(2, 7),
        ],
        compiler_params=pltpu.CompilerParams(
            vmem_limit_bytes=VMEM_LIMIT, collective_id=2, has_side_effects=True
        ),
        name="back",
    )(
        q, k0, k1, v0, v1, grad_mixed, mixed, inverse, grown, *small, raw, hidden, x, grad_middle,
        weight, output_rows,
    )


def finish_kernel(
    head, feeds_ref, projs_ref, early_ref, late_ref, modw_hbm,
    cond_ref, table_hbm, gmodw_hbm, gmodb_ref, ginw_hbm, ginb_ref, gqg_ref, gkg_ref, goutw_hbm,
    goutb_ref, gguw_hbm, ggub_ref, gdownw_hbm, gdownb_ref,
    modw_ref, table_ref, gmodw_ref, ginw_ref, goutw_ref, gguw_ref, gdownw_ref, acts_ref, load_sem,
    store_sem,
):
    place = Place()
    width = early_ref.shape[3]
    part = projs_ref.shape[3]
    load = pltpu.make_async_copy(modw_hbm, modw_ref, load_sem)
    load.start()
    stores = [
        pltpu.make_async_copy(source, target, store_sem.at[i])
        for i, (source, target) in enumerate(
            (
                (gguw_ref, gguw_hbm), (gdownw_ref, gdownw_hbm), (ginw_ref, ginw_hbm),
                (goutw_ref, goutw_hbm), (gmodw_ref, gmodw_hbm), (table_ref, table_hbm),
            )
        )
    ]
    for c in range(2):
        for chip in range(4):
            for f in range(2):
                for i in range(2):
                    col = (((c * 2 + f) * 2 + i) * 4 + chip) * 128
                    gguw_ref[:, col : col + 128] = feeds_ref[
                        c, chip, f, :, i * 128 : (i + 1) * 128
                    ].astype(F32)
    stores[0].start()
    for c in range(2):
        for chip in range(4):
            row = chip * 128 + c * 64
            for b in range(3):
                gdownw_ref[row : row + 64, b * 256 : (b + 1) * 256] = feeds_ref[
                    c, chip, 2, b * 64 : (b + 1) * 64, :
                ].astype(F32)
    stores[1].start()
    for c in range(2):
        for chip in range(4):
            row = chip * part
            for g in range(3):
                for q in range(3):
                    col = q * width + g * 256 + c * 128
                    ginw_ref[row : row + part, col : col + 128] = projs_ref[
                        c, chip, g, :, q * 128 : (q + 1) * 128
                    ].astype(F32)
            half = width // 2
            goutw_ref[row : row + part, c * half : (c + 1) * half] = projs_ref[c, chip, 3].astype(F32)
    stores[2].start()
    stores[3].start()

    vectors = [late_ref[0, :, 0, :], late_ref[0, :, 1, :]]
    vectors += [early_ref[0, :, j, :] for j in range(4)]
    lows = [vector.astype(BF16) for vector in vectors]
    conditions = early_ref[0, :, 6, :]
    labels = early_ref[0, :, 7, :]
    sig = 1.0 / (1.0 + jnp.exp(-conditions))
    acts = (conditions * sig).astype(BF16)
    size = acts_ref.shape[1]
    for z in range(4):

        @pl.when(place.z == z)
        def _(z=z):
            acts_ref[...] = acts[:, z * size : (z + 1) * size]

    mine = acts_ref[...]
    for j, low in enumerate(lows):
        gmodw_ref[:, j * width : (j + 1) * width] = mm_tn(mine, low)
    stores[4].start()
    early_sum = jnp.sum(early_ref[0], axis=0)
    gate_sum = jnp.sum(early_ref[1], axis=0)
    late_sum = jnp.sum(late_ref[0], axis=0)
    gain_sum = jnp.sum(late_ref[1], axis=0)
    mod_b = jnp.concatenate(
        [late_sum[0:1], late_sum[1:2]] + [early_sum[j : j + 1] for j in range(4)], axis=1
    )
    in_b = jnp.concatenate([late_sum[2:3], late_sum[3:4], gain_sum[2:3]], axis=1)
    gate_b = jnp.concatenate(
        [gate_sum[n // 6 : n // 6 + 1, (n % 6) * 128 : (n % 6) * 128 + 128] for n in range(32)],
        axis=1,
    )
    gains = sum(gain_sum[0:2, i : i + 128] for i in range(0, width, 128))
    gains = gains[:, :head] + gains[:, head:]
    pieces = (
        (gmodb_ref, mod_b), (ginb_ref, in_b), (gqg_ref, gains[0:1]), (gkg_ref, gains[1:2]),
        (goutb_ref, early_sum[4:5]), (ggub_ref, gate_b), (gdownb_ref, early_sum[5:6]),
    )
    for z in range(4):

        @pl.when(place.z == z)
        def _(z=z):
            for ref, row in pieces:
                size = row.shape[1] // 4
                ref[...] = row[0, z * size : (z + 1) * size]

    load.wait()
    grad = sum(mm_nt(modw_ref[:, j * width : (j + 1) * width], low) for j, low in enumerate(lows)).T
    grad = grad * sig * (1.0 + conditions * (1.0 - sig))
    for k in range(4):
        cond_ref[pl.ds(place.flipped(k), 1), :] = grad[k : k + 1]
    classes = table_ref.shape[0]
    wide = -(-classes // 128) * 128
    column = lax.broadcasted_iota(jnp.int32, (1, wide), 1).astype(F32)
    onehot = jnp.where(labels[:, 0:1] == column, 1.0, 0.0).astype(BF16)
    high = grad.astype(BF16)
    rest = grad - high.astype(F32)
    middle = rest.astype(BF16)
    last = (rest - middle.astype(F32)).astype(BF16)
    table = mm_tn(
        jnp.concatenate([onehot] * 3, axis=0), jnp.concatenate([high, middle, last], axis=0)
    )
    table_ref[...] = table[:classes]
    stores[5].start()
    for store in stores:
        store.wait()


def finish_call(feeds, projs, early, late, weight, head, classes, hidden_width):
    width = weight.shape[0]
    rows = width // 4
    whole = lambda *shape: jax.ShapeDtypeStruct(shape, F32)
    anywhere = pl.BlockSpec(memory_space=pl.ANY)
    out_shape = [
        whole(4, width), whole(classes, width), whole(rows, 6 * width), whole(6 * width // 4),
        whole(rows, 3 * width), whole(3 * width // 4), whole(head // 4), whole(head // 4),
        whole(rows, width), whole(rows), whole(rows, 2 * hidden_width),
        whole(2 * hidden_width // 4), whole(hidden_width // 4, width), whole(rows),
    ]
    big = (1, 2, 4, 8, 10, 12)
    return pl.pallas_call(
        functools.partial(finish_kernel, head),
        in_specs=[pl.BlockSpec(memory_space=pltpu.VMEM)] * 4 + [anywhere],
        out_specs=[
            anywhere if i in big else pl.BlockSpec(memory_space=pltpu.VMEM)
            for i in range(len(out_shape))
        ],
        out_shape=out_shape,
        scratch_shapes=[pltpu.VMEM(weight.shape, BF16)]
        + [pltpu.VMEM(out_shape[i].shape, F32) for i in big]
        + [pltpu.VMEM((16, rows), BF16), pltpu.SemaphoreType.DMA, pltpu.SemaphoreType.DMA((6,))],
        compiler_params=params(),
        name="finish",
    )(feeds, projs, early, late, weight)


def take(array_in, index, axis=0):
    return lax.dynamic_index_in_dim(array_in, index, axis, keepdims=False)


def add(*terms):
    return sum(term.astype(F32) for term in terms)


class Moves:
    def __init__(self, mesh):
        self.sizes = tuple(mesh.shape[name] for name in AXES)

    def flip(self, value, batch=0, gy=0, gx=0):
        nb, ny, nx = self.sizes
        pairs = []
        for b in range(nb):
            for y in range(ny):
                for x in range(nx):
                    here = (b * ny + y) * nx + x
                    there = ((b ^ batch) * ny + (y ^ gy)) * nx + (x ^ gx)
                    pairs.append((here, there))
        return lax.ppermute(value, AXES, pairs)

    def plane(self, value, k):
        return self.flip(value, gy=k >> 1, gx=2 * (k & 1))

    def pair(self, value):
        return self.flip(value, gx=1)

    def gather(self, value):
        value = value[None]
        value = jnp.concatenate([value, self.plane(value, 1)], axis=0)
        value = jnp.concatenate([value, self.plane(value, 2)], axis=0)
        bit = 1
        while bit < self.sizes[0]:
            value = jnp.concatenate([value, self.flip(value, batch=bit)], axis=0)
            bit *= 2
        return value


def regroup(parts, place):
    stacked = jnp.stack(parts)
    return jnp.stack([take(stacked, place ^ k) for k in range(len(parts))])


def body(mesh, *operands):
    (
        tokens, timesteps, labels, class_table, modulate_weight, modulate_bias, inproj_weight,
        inproj_bias, query_gain, key_gain, outproj_weight, outproj_bias, gate_up_weight,
        gate_up_bias, down_weight, down_bias, cotangent,
    ) = operands
    image_count, tile_rows, tile_cols, width = tokens.shape
    cells = tile_rows * tile_cols
    rows = image_count * cells
    head = query_gain.shape[0]
    heads = width // head
    hidden_width = down_weight.shape[0]
    class_count = class_table.shape[0]
    highest = lax.Precision.HIGHEST
    moves = Moves(mesh)
    nb, ny, nx = moves.sizes
    assert ny == 2 and nx == 4 and image_count == 4
    z, gy, gx = (lax.axis_index(name) for name in AXES)
    side, core = gx // 2, gx % 2
    place = 2 * gy + side

    tiles = tokens.reshape(image_count, cells, width)
    grads = cotangent.reshape(image_count, cells, width)

    if nb == 4 and hidden_width == 16 * 128:
        vectors = (
            modulate_bias, inproj_bias, query_gain, key_gain, outproj_bias, down_bias, gate_up_bias
        )
        x, hidden_one, q, k0, v0, k1, v1, raw, mod, cosine, sine, small, known = front_call(
            tiles, timesteps, labels, vectors, class_table, modulate_weight, inproj_weight, head,
            tile_cols,
        )
        mixed, grown, inverse, dy = attend_tiles_call(q, k0, k1, v0, v1, grads, head)
        attended, middle, hidden_two, hidden_two_t, grad_feed = middle_call(
            mixed, x, dy, mod, outproj_weight, small, OUT_BIAS
        )
        output_rows, grad_middle, grad_mixed, d_out, sums_two, totals, passed = feed_turn_call(
            hidden_two, hidden_two_t, grad_feed, gate_up_weight, down_weight, middle, attended, dy,
            mixed, mod, outproj_weight, small, known,
        )
        output, grad_tokens, feeds, projs, early, late = back_call(
            q, k0, k1, v0, v1, grad_mixed, mixed, inverse, grown, mod, small, cosine, sine, d_out,
            totals, passed, sums_two, raw, hidden_one, x, grad_middle, inproj_weight, output_rows, head,
        )
        (
            grad_condition, grad_table, grad_mod_w, grad_mod_b, grad_in_w, grad_in_b, grad_q_gain,
            grad_k_gain, grad_out_w, grad_out_b, grad_gu_w, grad_gu_b, grad_down_w, grad_down_b,
        ) = finish_call(
            feeds, projs, early, late, modulate_weight, head, class_count, hidden_width
        )
        return (
            output.reshape(tokens.shape), grad_tokens.reshape(tokens.shape), grad_condition,
            grad_table, grad_mod_w, grad_mod_b, grad_in_w, grad_in_b, grad_q_gain, grad_k_gain,
            grad_out_w, grad_out_b, grad_gu_w, grad_gu_b, grad_down_w, grad_down_b,
        )

    def exchange(blocks):
        return [take(blocks, place)] + [
            moves.plane(take(blocks, place ^ k), k) for k in range(1, 4)
        ]

    x = jnp.concatenate(exchange(tiles), axis=0)

    half_width = width // 2
    step = take(timesteps, place).astype(F32)
    label = take(labels, place)
    rates = jnp.exp(-math.log(10000.0) * jnp.arange(half_width, dtype=F32) / half_width)
    features = jnp.concatenate([jnp.cos(step * rates), jnp.sin(step * rates)])
    condition = features + take(class_table, label).astype(F32)
    cond_act = jax.nn.silu(condition).astype(BF16)
    mod = modulation_call(
        jnp.broadcast_to(cond_act[None], (16, width)), modulate_weight, modulate_bias[None]
    )[:1]

    quarter = head // 4
    cell = jnp.arange(cells, dtype=jnp.int32)
    row_places, col_places = [], []
    for k in range(4):
        there = place ^ k
        row_places.append((there // 2) * tile_rows + cell // tile_cols)
        col_places.append((2 * (there % 2) + core) * tile_cols + cell % tile_cols)
    row_places = jnp.concatenate(row_places).astype(F32)[:, None]
    col_places = jnp.concatenate(col_places).astype(F32)[:, None]
    lane = jnp.arange(128, dtype=jnp.int32)
    turn_rate = jnp.exp(-math.log(10000.0) * (lane % quarter).astype(F32) / quarter)[None]
    angles = jnp.where((lane % head)[None] < head // 2, row_places, col_places) * turn_rate
    cosine = jnp.cos(angles)
    sine = jnp.where((lane % (2 * quarter))[None] < quarter, -1.0, 1.0) * jnp.sin(angles)
    qgain = jnp.tile(query_gain.astype(F32), heads)[None]
    kgain = jnp.tile(key_gain.astype(F32), heads)[None]

    hidden_one, q, k0, v0, raw = project_call(
        x, mod, inproj_weight, inproj_bias[None], qgain, kgain, cosine, sine, head
    )
    k1, v1 = moves.pair(k0), moves.pair(v0)
    dy = jnp.concatenate(exchange(grads), axis=0)
    mixed, grown, inverse = attend_call(q, k0, k1, v0, v1, head)
    attended, middle, hidden_two, hidden_two_t, grad_feed = middle_call(
        mixed, x, dy, mod, outproj_weight, outproj_bias[None]
    )

    unit = 256
    blocks = hidden_width // unit
    feed, grad_hidden, d_down, d_gate, d_bias = feed_call(
        hidden_two, hidden_two_t, grad_feed, gate_up_weight, gate_up_bias[None], down_weight,
        jnp.zeros((rows, width), F32), jnp.zeros((rows, width), F32), 0, 1, unit,
    )
    output_rows, grad_middle, grad_mixed, d_out, sums_two = turn_call(
        feed, grad_hidden, middle, attended, dy, grad_feed, mixed, mod, outproj_weight,
        down_bias[None],
    )
    gate_bias = d_bias.reshape(blocks, 2, unit).transpose(1, 0, 2)
    dq, dk0, dk1, dv0, dv1 = attend_back_call(
        q, k0, k1, v0, v1, grown, grad_mixed, mixed, inverse, head
    )
    dk1, dv1 = moves.pair(dk1), moves.pair(dv1)
    grad_x, d_in, sums_one, in_bias = project_back_call(
        dq, dk0, dk1, dv0, dv1, raw, hidden_one, x, grad_middle, mod, inproj_weight, qgain,
        kgain, cosine, sine, head,
    )

    def give_back(rows_out):
        parts = rows_out.reshape(4, cells, width)
        got = [parts[0]] + [moves.plane(parts[k], k) for k in range(1, 4)]
        return regroup(got, place).reshape(tokens.shape)

    output = give_back(output_rows)
    grad_tokens = give_back(grad_x)
    slice_rows = width // nb

    def scatter(d):
        d = lax.psum_scatter(d.astype(BF16), "batch", scatter_dimension=0, tiled=True)
        return lax.psum(d, ("gy", "gx")).astype(F32)

    def joined(d):
        return jnp.concatenate([d[0], d[1]], axis=1)

    grad_down_w = scatter(d_down.reshape(hidden_width, width))
    grad_gu_w = scatter(
        d_gate.transpose(2, 1, 0, 3).reshape(width, 2 * hidden_width)
    )
    grad_out_w = scatter(joined(d_out))
    grad_in_w = scatter(joined(d_in))
    gain_sums = sums_one[2:4].reshape(2, heads, head).sum(axis=1)
    early = jnp.concatenate([sums_two[:6].reshape(-1), gate_bias.reshape(-1)])
    late = jnp.concatenate(
        [sums_one[:2].reshape(-1), in_bias.reshape(-1), gain_sums.reshape(-1)]
    )

    def everywhere(vector):
        halves = vector.reshape(2, -1)
        half = add(take(halves, core), moves.pair(take(halves, 1 - core)))
        half = moves.gather(half)
        both = regroup([half, moves.pair(half)], core)
        return both.transpose(1, 0, 2).reshape(half.shape[0], -1)

    known = jnp.concatenate([condition, jnp.broadcast_to(label.astype(F32), (128,))])
    known = moves.gather(known)
    early, late = everywhere(early), everywhere(late)
    grad_modulation = jnp.concatenate([late[:, : 2 * width], early[:, : 4 * width]], axis=1)
    conditions = known[:, :width]
    all_labels = known[:, width].astype(jnp.int32)
    cond_acts = jax.nn.silu(conditions).astype(BF16)
    my_acts = lax.dynamic_slice_in_dim(cond_acts, z * slice_rows, slice_rows, axis=1)
    low_mod = grad_modulation.astype(BF16)
    grad_mod_w = mm_tn(my_acts, low_mod)
    wide = 6 * width
    grad_mod_b = lax.dynamic_slice_in_dim(
        jnp.sum(grad_modulation, axis=0), z * (wide // nb), wide // nb, axis=0
    )
    grad_cond_act = mm_nt(low_mod, modulate_weight)
    sig = jax.nn.sigmoid(conditions)
    grad_conditions = grad_cond_act * sig * (1.0 + conditions * (1.0 - sig))
    grad_condition = regroup([grad_conditions[k] for k in range(4)], place)
    onehot = (all_labels[:, None] == jnp.arange(class_count, dtype=jnp.int32)[None, :]).astype(F32)
    grad_table = lax.dot_general(
        onehot, grad_conditions, (((0,), (0,)), ((), ())), precision=highest,
        preferred_element_type=F32,
    )

    early_sum = jnp.sum(early, axis=0)
    late_sum = jnp.sum(late, axis=0)

    def part(vector, start, size):
        return lax.dynamic_slice_in_dim(vector, start + z * (size // nb), size // nb, axis=0)

    grad_out_b = part(early_sum, 4 * width, width)
    grad_down_b = part(early_sum, 5 * width, width)
    grad_gu_b = part(early_sum, 6 * width, 2 * hidden_width)
    grad_in_b = part(late_sum, 2 * width, 3 * width)
    grad_q_gain = part(late_sum, 5 * width, head)
    grad_k_gain = part(late_sum, 5 * width + head, head)
    return (
        output, grad_tokens, grad_condition, grad_table, grad_mod_w, grad_mod_b, grad_in_w,
        grad_in_b, grad_q_gain, grad_k_gain, grad_out_w, grad_out_b, grad_gu_w, grad_gu_b,
        grad_down_w, grad_down_b,
    )


def solution(mesh):
    grid = P("batch", "gy", "gx", None)
    by_batch = P("batch")
    rows = P("batch", None)
    placed = (grid, by_batch, by_batch) + (P(),) * 13 + (grid,)
    return jax.shard_map(
        functools.partial(body, mesh),
        mesh=mesh,
        in_specs=placed,
        out_specs=(
            grid, grid, rows, P(), rows, by_batch, rows, by_batch, by_batch, by_batch, rows,
            by_batch, rows, by_batch, rows, by_batch,
        ),
        check_vma=False,
    )
```
